32 devices in a mesh: seq: 16 (over z, x, core), head: 2 (over y).
Axes of the slice: x: 2, y: 2, z: 4, core: 2. Of those that a mesh axis runs over, the one named last changes fastest.
Arguments:
- frames: bfloat16 [6144, 1536], P('seq'), may hold values from -6 to 6
- time_token: bfloat16 [6, 1536], replicated, may hold values from -6 to 6
- prompt: bfloat16 [6, 128, 768], replicated, may hold values from -6 to 6
- clip_ids: int32 [6144], replicated, may hold values from 0 to 5, as said below
- norm1_gain: float32 [1536], P('seq'), may hold values from 0.5 to 1.5
- norm2_gain: float32 [1536], P('seq'), may hold values from 0.5 to 1.5
- norm3_gain: float32 [1536], P('seq'), may hold values from 0.5 to 1.5
- query_weight: float32 [1536, 1536], P('seq', 'head'), may hold values from -0.15625 to 0.15625
- key_weight: float32 [1536, 1536], P('seq', 'head'), may hold values from -0.15625 to 0.15625
- value_weight: float32 [1536, 1536], P('seq', 'head'), may hold values from -0.15625 to 0.15625
- out_weight: float32 [1536, 1536], P('seq', 'head'), may hold values from -1.75 to 1.75
- cross_query: float32 [1536, 1536], P('seq', 'head'), may hold values from -0.15625 to 0.15625
- cross_key: float32 [768, 1536], P('seq', 'head'), may hold values from -0.21875 to 0.21875
- cross_value: float32 [768, 1536], P('seq', 'head'), may hold values from -0.21875 to 0.21875
- cross_out: float32 [1536, 1536], P('seq', 'head'), may hold values from -1.25 to 1.25
- gate_weight: float32 [1536, 6144], P('seq', 'head'), may hold values from -0.15625 to 0.15625
- up_weight: float32 [1536, 6144], P('seq', 'head'), may hold values from -0.15625 to 0.15625
- down_weight: float32 [1536, 6144], P('seq', 'head'), may hold values from -0.078125 to 0.078125
- gate_bias: float32 [6144], P('head'), may hold values from -3 to 3
- up_bias: float32 [6144], P('head'), may hold values from -3 to 3
- down_bias: float32 [1536], P('seq'), may hold values from -2 to 2
- out_grad: bfloat16 [6144, 1536], P('seq'), may hold values from -6 to 6
Outputs:
- result: bfloat16 [6144, 1536], P('seq')
- frames_grad: bfloat16 [6144, 1536], P('seq')
- time_grad: float32 [6, 1536], replicated
- norm1_gain_grad: float32 [1536], P('seq')
- norm2_gain_grad: float32 [1536], P('seq')
- norm3_gain_grad: float32 [1536], P('seq')
- query_weight_grad: float32 [1536, 1536], P('seq', 'head')
- key_weight_grad: float32 [1536, 1536], P('seq', 'head')
- value_weight_grad: float32 [1536, 1536], P('seq', 'head')
- out_weight_grad: float32 [1536, 1536], P('seq', 'head')
- cross_query_grad: float32 [1536, 1536], P('seq', 'head')
- cross_key_grad: float32 [768, 1536], P('seq', 'head')
- cross_value_grad: float32 [768, 1536], P('seq', 'head')
- cross_out_grad: float32 [1536, 1536], P('seq', 'head')
- gate_weight_grad: float32 [1536, 6144], P('seq', 'head')
- up_weight_grad: float32 [1536, 6144], P('seq', 'head')
- down_weight_grad: float32 [1536, 6144], P('seq', 'head')
- gate_bias_grad: float32 [6144], P('head')
- up_bias_grad: float32 [6144], P('head')
- down_bias_grad: float32 [1536], P('seq')
The draws below stay inside these ranges and needn't reach their ends.
Inputs may be any that keep to these rules, and one draw needn't show every extreme that they name: `clip_ids`: never falls from one frame to the next, starts at 0 and takes every value up to 5; each clip covers 2 * 256 frames or more, and one covers exactly 512; no clip starts at a nonzero multiple of 384.
All inputs are finite; a program needn't handle non-finite values.
Results may differ from the reference program's by a relative error of at most 0.025.
Values may be sent and summed in bfloat16 or wider, within the bound.
A program may use at most 320 MiB of HBM per device.

```python
import jax
import jax.numpy as jnp
from jax import lax

D = 1536
HD = 64
CTXW = 768
FF = 6144
ROT = 32
CTX = 128
HALF = 256
FRAMES = 6144
CLIPS = 6


def draw_clip_ids(key, part):
    spacing = 4 * HALF
    clip_count = FRAMES // spacing
    jitter = 2 * jax.random.randint(jax.random.fold_in(key, 11), (clip_count - 1,), 0, HALF + 1) - 1
    pinned = jax.random.randint(jax.random.fold_in(key, 12), (), 0, clip_count - 2)
    ladder = jnp.arange(clip_count - 1, dtype=jnp.int32)
    jitter = jnp.where(ladder == pinned, 2 * HALF - 1, jnp.where(ladder == pinned + 1, -1, jitter))
    bounds = (ladder + 1) * spacing + jitter
    positions = jnp.arange(FRAMES, dtype=jnp.int32)
    return jnp.sum((positions[:, None] >= bounds[None, :]).astype(jnp.int32), axis=1).astype(jnp.int32)


def raised(entries, stream_key, source, target, parts, factor):
    owner, partner = [(jnp.arange(entries.shape[dim]) // (entries.shape[dim] // parts)).reshape([-1 if axis == dim else 1 for axis in range(entries.ndim)]) for dim in (source, target)]
    chosen = jax.random.permutation(stream_key, parts)[partner]
    strong = (owner == chosen) | (owner == (partner + parts // 2) % parts)
    return jnp.where(strong, factor * entries, entries)


def shard_levels(stream_key, shape, cuts, smallest, high):
    factor_of, own = 1.0, jax.random.fold_in(stream_key, 6)
    for axis_at, shards_of in cuts:
        heights = jnp.exp(jax.random.uniform(jax.random.fold_in(own, axis_at), (shards_of,), jnp.float32, smallest / len(cuts), high / len(cuts)))
        factor_of = factor_of * jnp.repeat(heights, shape[axis_at] // shards_of).reshape([-1 if axis == axis_at else 1 for axis in range(len(shape))])
    return factor_of


def bell_draw(stream_key, dims, scale, reach, shards=(), kind=jnp.bfloat16):
    level = shard_levels(stream_key, dims, shards, -0.22, 0.18) if shards else 1.0
    entries = jax.random.normal(stream_key, dims, jnp.float32) * scale * level
    return jnp.minimum(jnp.maximum(entries, -reach), reach).astype(kind)


def heavy_noise(key, extent, deviation, limit, split, heavy, kind=jnp.bfloat16):
    values = deviation * jax.random.normal(key, extent, jnp.float32)
    if split:
        values = values * shard_levels(key, extent, split, -0.22, 0.18)
    return jnp.clip(raised(values, jax.random.fold_in(key, 3), *heavy), -limit, limit).astype(kind)


def setup_inputs(seed: int = 0) -> dict:
    key_of = jax.random.split(jax.random.key(seed), 23)
    frames = heavy_noise(key_of[0], (FRAMES, D), 1.0, 6.0, ((0, 16),), (0, 1, 16, 2.0))
    time_token = bell_draw(key_of[1], (CLIPS, D), 1.0, 6.0)
    prompt = bell_draw(key_of[2], (CLIPS, CTX, CTXW), 1.0, 6.0)
    clip_ids = draw_clip_ids(jax.random.fold_in(key_of[22], 71), 0)
    norm1_gain = jnp.clip(1.0 + 0.1 * jax.random.normal(key_of[4], (D,), jnp.float32), 0.5, 1.5)
    norm2_gain = jnp.clip(1.0 + 0.1 * jax.random.normal(key_of[5], (D,), jnp.float32), 0.5, 1.5)
    norm3_gain = jnp.clip(1.0 + 0.1 * jax.random.normal(key_of[6], (D,), jnp.float32), 0.5, 1.5)
    query_weight = bell_draw(key_of[7], (D, D), D ** -0.5, 0.15625, ((0, 16), (1, 2)), jnp.float32)
    key_weight = bell_draw(key_of[8], (D, D), D ** -0.5, 0.15625, ((0, 16), (1, 2)), jnp.float32)
    value_weight = bell_draw(key_of[9], (D, D), D ** -0.5, 0.15625, ((0, 16), (1, 2)), jnp.float32)
    out_weight = bell_draw(key_of[10], (D, D), (D // (HALF // 2)) ** -0.5, 1.75, ((0, 16), (1, 2)), jnp.float32)
    cross_query = bell_draw(key_of[11], (D, D), D ** -0.5, 0.15625, ((0, 16), (1, 2)), jnp.float32)
    cross_key = bell_draw(key_of[12], (CTXW, D), CTXW ** -0.5, 0.21875, ((0, 16), (1, 2)), jnp.float32)
    cross_value = bell_draw(key_of[13], (CTXW, D), CTXW ** -0.5, 0.21875, ((0, 16), (1, 2)), jnp.float32)
    cross_out = bell_draw(key_of[14], (D, D), (D // (CTX // 2)) ** -0.5, 1.25, ((0, 16), (1, 2)), jnp.float32)
    gate_weight = bell_draw(key_of[15], (D, FF), D ** -0.5, 0.15625, ((0, 16), (1, 2)), jnp.float32)
    up_weight = bell_draw(key_of[16], (D, FF), D ** -0.5, 0.15625, ((0, 16), (1, 2)), jnp.float32)
    down_weight = bell_draw(key_of[17], (D, FF), FF ** -0.5, 0.078125, ((0, 16), (1, 2)), jnp.float32)
    gate_bias = bell_draw(key_of[18], (FF,), 0.5, 3.0, ((0, 2),), jnp.float32)
    up_bias = bell_draw(key_of[19], (FF,), 0.5, 3.0, ((0, 2),), jnp.float32)
    down_bias = bell_draw(key_of[20], (D,), 0.3, 2.0, ((0, 16),), jnp.float32)
    out_grad = heavy_noise(key_of[21], (FRAMES, D), 1.0, 6.0, ((0, 16),), (0, 1, 16, 2.0))
    return {"frames": frames, "time_token": time_token, "prompt": prompt, "clip_ids": clip_ids, "norm1_gain": norm1_gain, "norm2_gain": norm2_gain, "norm3_gain": norm3_gain, "query_weight": query_weight, "key_weight": key_weight, "value_weight": value_weight, "out_weight": out_weight, "cross_query": cross_query, "cross_key": cross_key, "cross_value": cross_value, "cross_out": cross_out, "gate_weight": gate_weight, "up_weight": up_weight, "down_weight": down_weight, "gate_bias": gate_bias, "up_bias": up_bias, "down_bias": down_bias, "out_grad": out_grad}


EPS = 1e-05
NEG = -1e+30
HIGHEST = lax.Precision.HIGHEST

@jax.custom_vjp
def low(v):
    return lax.optimization_barrier(v.astype(jnp.bfloat16)).astype(jnp.float32)

@jax.custom_vjp
def low_back(v):
    return v

def low_keep(v):
    return (low(v), None)

def low_pass(kept, grad):
    return (grad,)

def back_keep(v):
    return (v, None)

def back_low(kept, grad):
    return (low(grad),)
low.defvjp(low_keep, low_pass)
low_back.defvjp(back_keep, back_low)

def layer_norm(values, gain):
    average = lax.optimization_barrier(jnp.mean(values, axis=-1, keepdims=True))
    centered = values - average
    spread = lax.optimization_barrier(jnp.mean(centered * centered, axis=-1, keepdims=True))
    return centered * lax.rsqrt(spread + EPS) * gain

def matmul(matrix_a, matrix_b):
    return jnp.dot(matrix_a, matrix_b, precision=HIGHEST)

def angles(positions):
    ladder = jnp.arange(ROT // 2, dtype=jnp.float32)
    frequency = 10000.0 ** (-2.0 * ladder / ROT)
    phases = positions.astype(jnp.float32)[:, None] * frequency[None, :]
    return (jnp.cos(phases), jnp.sin(phases))

def rotate(values, cos_table, sin_table):
    shaped = values.reshape(values.shape[0], -1, HD)
    rot_half = ROT // 2
    leading = shaped[:, :, :rot_half]
    trailing = shaped[:, :, rot_half:ROT]
    cos_row = cos_table[:, None, :]
    sin_row = sin_table[:, None, :]
    turned = jnp.concatenate([leading * cos_row - trailing * sin_row, trailing * cos_row + leading * sin_row, shaped[:, :, ROT:]], axis=-1)
    return turned.reshape(values.shape)

def forward(params, frames, stamps, prompt, clip_ids):
    gain_one, gain_two, gain_three, w_query, w_key, w_value, w_out, c_query, c_key, c_value, c_out, w_gate, w_up, w_down, b_gate, b_up, b_down = params
    gain_one = low(gain_one)
    gain_two = low(gain_two)
    gain_three = low(gain_three)
    b_down = low(b_down)
    w_query = low(w_query)
    w_key = low(w_key)
    w_value = low(w_value)
    w_out = low(w_out)
    c_query = low(c_query)
    c_key = low(c_key)
    c_value = low(c_value)
    c_out = low(c_out)
    w_gate = low(w_gate)
    w_up = low(w_up)
    w_down = low(w_down)
    head_count = D // HD
    score_scale = HD ** (-0.5)
    block_rows = 2 * HALF
    window = block_rows + 2 * HALF
    block_count = FRAMES // block_rows
    indices = jnp.arange(block_count, dtype=jnp.int32)
    cos_table, sin_table = angles(jnp.arange(FRAMES, dtype=jnp.int32))

    def project(block_index):
        row_start = block_index * block_rows
        row_block = lax.dynamic_slice_in_dim(frames, row_start, block_rows, 0)
        cos_rows = lax.dynamic_slice_in_dim(cos_table, row_start, block_rows, 0)
        sin_rows = lax.dynamic_slice_in_dim(sin_table, row_start, block_rows, 0)
        normed = low(layer_norm(row_block, gain_one))
        query_rows = low(rotate(low_back(matmul(normed, w_query)), cos_rows, sin_rows))
        key_rows = low(rotate(low_back(matmul(normed, w_key)), cos_rows, sin_rows))
        value_rows = low(low_back(matmul(normed, w_value)))
        return (query_rows, key_rows, value_rows)
    queries, keys, values = lax.map(jax.checkpoint(project), indices)
    queries = queries.reshape(FRAMES, D)
    keys = keys.reshape(FRAMES, D)
    values = values.reshape(FRAMES, D)
    stamp_norm = low(layer_norm(stamps, gain_one))
    stamp_keys = low(matmul(stamp_norm, w_key))
    stamp_values = low(matmul(stamp_norm, w_value))
    keys_pad = jnp.pad(keys, ((HALF, HALF), (0, 0)))
    values_pad = jnp.pad(values, ((HALF, HALF), (0, 0)))
    ids_pad = jnp.pad(clip_ids, (HALF, HALF), constant_values=-1)

    def attend(block_index):
        row_start = block_index * block_rows
        query_h = lax.dynamic_slice_in_dim(queries, row_start, block_rows, 0).reshape(block_rows, head_count, HD)
        key_h = lax.dynamic_slice_in_dim(keys_pad, row_start, window, 0).reshape(window, head_count, HD)
        value_h = lax.dynamic_slice_in_dim(values_pad, row_start, window, 0).reshape(window, head_count, HD)
        query_ids = lax.dynamic_slice_in_dim(clip_ids, row_start, block_rows)
        key_ids = lax.dynamic_slice_in_dim(ids_pad, row_start, window)
        query_pos = row_start + jnp.arange(block_rows, dtype=jnp.int32)
        key_pos = row_start - HALF + jnp.arange(window, dtype=jnp.int32)
        visible = (query_ids[:, None] == key_ids[None, :]) & (jnp.abs(query_pos[:, None] - key_pos[None, :]) <= HALF)
        raw_scores = low_back(jnp.einsum('qhd,khd->hqk', query_h, key_h, precision=HIGHEST) * score_scale)
        scores = jnp.where(visible[None], raw_scores, NEG)
        stamp_key = jnp.take(stamp_keys, query_ids, axis=0).reshape(block_rows, head_count, HD)
        stamp_value = jnp.take(stamp_values, query_ids, axis=0).reshape(block_rows, head_count, HD)
        stamp_score = low_back(jnp.einsum('qhd,qhd->hq', query_h, stamp_key, precision=HIGHEST) * score_scale)
        row_peak = jnp.maximum(lax.optimization_barrier(jnp.max(scores, axis=-1)), stamp_score)
        exp_scores = jnp.exp(scores - row_peak[:, :, None])
        exp_stamp = jnp.exp(stamp_score - row_peak)
        row_total = lax.optimization_barrier(jnp.sum(exp_scores, axis=-1)) + exp_stamp
        probs = low(exp_scores / row_total[:, :, None])
        stamp_prob = low(exp_stamp / row_total)
        attn_mixed = jnp.einsum('hqk,khd->qhd', probs, value_h, precision=HIGHEST) + jnp.transpose(stamp_prob)[:, :, None] * stamp_value
        return low(low_back(attn_mixed.reshape(block_rows, D)))
    attn_out = lax.map(jax.checkpoint(attend), indices).reshape(FRAMES, D)
    h_one = frames + low_back(matmul(attn_out, w_out.T))
    prompt_keys = low(jnp.einsum('cti,io->cto', prompt, c_key, precision=HIGHEST))
    prompt_values = low(jnp.einsum('cti,io->cto', prompt, c_value, precision=HIGHEST))

    def finish(block_index):
        row_start = block_index * block_rows
        row_block = lax.dynamic_slice_in_dim(h_one, row_start, block_rows, 0)
        block_ids = lax.dynamic_slice_in_dim(clip_ids, row_start, block_rows)
        base_clip = jnp.minimum(block_ids[0], CLIPS - 2)
        block_slot = block_ids - base_clip
        normed = low(layer_norm(row_block, gain_two))
        query_h = low(low_back(matmul(normed, c_query))).reshape(block_rows, head_count, HD)
        ctx_key = lax.dynamic_slice_in_dim(prompt_keys, base_clip, 2, 0).reshape(2 * CTX, head_count, HD)
        ctx_value = lax.dynamic_slice_in_dim(prompt_values, base_clip, 2, 0).reshape(2 * CTX, head_count, HD)
        key_slot = jnp.arange(2 * CTX, dtype=jnp.int32) // CTX
        visible = block_slot[:, None] == key_slot[None, :]
        raw_scores = low_back(jnp.einsum('qhd,khd->hqk', query_h, ctx_key, precision=HIGHEST) * score_scale)
        scores = jnp.where(visible[None], raw_scores, NEG)
        row_peak = lax.optimization_barrier(jnp.max(scores, axis=-1))
        exp_scores = jnp.exp(scores - row_peak[:, :, None])
        row_total = lax.optimization_barrier(jnp.sum(exp_scores, axis=-1))
        probs = low(exp_scores / row_total[:, :, None])
        cross_mixed = low(low_back(jnp.einsum('hqk,khd->qhd', probs, ctx_value, precision=HIGHEST).reshape(block_rows, D)))
        middle = row_block + low_back(matmul(cross_mixed, c_out.T))
        normed_three = low(layer_norm(middle, gain_three))
        gate_pre = low_back(matmul(normed_three, w_gate) + b_gate)
        up_pre = low_back(matmul(normed_three, w_up) + b_up)
        hidden = low(low_back(jax.nn.silu(gate_pre) * up_pre))
        return middle + low_back(matmul(hidden, w_down.T)) + b_down
    return lax.map(jax.checkpoint(finish), indices).reshape(FRAMES, D)

def reference(frames, time_token, prompt, clip_ids, norm1_gain, norm2_gain, norm3_gain, query_weight, key_weight, value_weight, out_weight, cross_query, cross_key, cross_value, cross_out, gate_weight, up_weight, down_weight, gate_bias, up_bias, down_bias, out_grad):
    params = (norm1_gain, norm2_gain, norm3_gain, query_weight, key_weight, value_weight, out_weight, cross_query, cross_key, cross_value, cross_out, gate_weight, up_weight, down_weight, gate_bias, up_bias, down_bias)
    prompt_float = prompt.astype(jnp.float32)

    def run_layer(weights, inputs, stamps):
        return forward(weights, inputs, stamps, prompt_float, clip_ids)
    result, pullback = jax.vjp(run_layer, params, frames.astype(jnp.float32), time_token.astype(jnp.float32))
    weight_grads, frames_grad, time_grad = pullback(out_grad.astype(jnp.float32))
    return (result.astype(jnp.bfloat16), frames_grad.astype(jnp.bfloat16), time_grad, weight_grads[0], weight_grads[1], weight_grads[2], weight_grads[3], weight_grads[4], weight_grads[5], weight_grads[6], weight_grads[7], weight_grads[8], weight_grads[9], weight_grads[10], weight_grads[11], weight_grads[12], weight_grads[13], weight_grads[14], weight_grads[15], weight_grads[16])
```

```python
from functools import reduce

import jax
import jax.numpy as jnp
from jax import lax
from jax.sharding import PartitionSpec as P

HD = 64
ROT = 32
HALF = 256


EPS = 1e-05
NEG = -1e30


def extended(block, sides, width):
    for axis, dim in sides:
        count = lax.axis_size(axis)
        forward = [(i, i + 1) for i in range(count - 1)]
        backward = [(target, source) for source, target in forward]
        low = lax.ppermute(
            lax.slice_in_dim(block, block.shape[dim] - width, None, axis=dim), axis, forward
        )
        high = lax.ppermute(lax.slice_in_dim(block, 0, width, axis=dim), axis, backward)
        block = jnp.concatenate([low, block, high], axis=dim)
    return block


def passed_along(value, axis, steps):
    count = lax.axis_size(axis)
    first, last = (max(0, -steps), min(count, count - steps))
    return lax.ppermute(value, axis, [(source, source + steps) for source in range(first, last)])


def layer_norm_parts(values, gain):
    average = jnp.mean(values, axis=-1, keepdims=True)
    centered = values - average
    spread = jnp.mean(centered * centered, axis=-1, keepdims=True)
    inverse = lax.rsqrt(spread + EPS)
    normal = centered * inverse
    return (normal * gain, normal, inverse)


def norm_back(grad_out, normal, inverse, gain):
    shaped = grad_out * gain
    return (
        shaped
        - jnp.mean(shaped, axis=-1, keepdims=True)
        - normal * jnp.mean(shaped * normal, axis=-1, keepdims=True)
    ) * inverse


def angles(positions):
    ladder = jnp.arange(ROT // 2, dtype=jnp.float32)
    frequency = 10000.0 ** (-2.0 * ladder / ROT)
    phases = positions.astype(jnp.float32)[:, None] * frequency[None, :]
    return (jnp.cos(phases), jnp.sin(phases))


def rotate(values, cos_table, sin_table):
    shaped = values.reshape(values.shape[0], -1, HD)
    rot_half = ROT // 2
    leading = shaped[:, :, :rot_half]
    trailing = shaped[:, :, rot_half:ROT]
    cos_row = cos_table[:, None, :]
    sin_row = sin_table[:, None, :]
    turned = jnp.concatenate(
        [
            leading * cos_row - trailing * sin_row,
            trailing * cos_row + leading * sin_row,
            shaped[:, :, ROT:],
        ],
        axis=-1,
    )
    return turned.reshape(values.shape)


def product(matrix_a, matrix_b):
    return jnp.dot(matrix_a, matrix_b, preferred_element_type=jnp.float32)


def product_t(matrix_a, matrix_b):
    return lax.dot_general(
        matrix_a, matrix_b, (((1,), (1,)), ((), ())), preferred_element_type=jnp.float32
    )


def product_tn(matrix_a, matrix_b):
    return lax.dot_general(
        matrix_a, matrix_b, (((0,), (0,)), ((), ())), preferred_element_type=jnp.float32
    )


def exact_t(matrix_a, matrix_b):
    return lax.dot_general(
        matrix_a,
        matrix_b,
        (((1,), (1,)), ((), ())),
        precision=lax.Precision.HIGHEST,
        preferred_element_type=jnp.float32,
    )


def exact_tn(matrix_a, matrix_b):
    return lax.dot_general(
        matrix_a,
        matrix_b,
        (((0,), (0,)), ((), ())),
        precision=lax.Precision.HIGHEST,
        preferred_element_type=jnp.float32,
    )


def score_parts(query_h, key_parts, score_scale):
    return [
        jnp.where(
            visible[None],
            jnp.einsum("qhd,khd->hqk", query_h, key_h, preferred_element_type=jnp.float32)
            * score_scale,
            NEG,
        )
        for key_h, value_h, visible in key_parts
    ]


def attend_forward(query_h, key_parts, score_scale):
    scores = score_parts(query_h, key_parts, score_scale)
    row_peak = reduce(jnp.maximum, [jnp.max(score_part, axis=-1) for score_part in scores])
    exp_parts = [jnp.exp(score_part - row_peak[:, :, None]) for score_part in scores]
    row_total = reduce(jnp.add, [jnp.sum(exp_part, axis=-1) for exp_part in exp_parts])
    attn_mixed = reduce(
        jnp.add,
        [
            jnp.einsum(
                "hqk,khd->qhd",
                (exp_part / row_total[:, :, None]).astype(jnp.bfloat16),
                key_part[1],
                preferred_element_type=jnp.float32,
            )
            for exp_part, key_part in zip(exp_parts, key_parts)
        ],
    )
    return (attn_mixed, row_peak + jnp.log(row_total))


def attend_backward(query_h, key_parts, score_scale, log_total, grad_h):
    scores = score_parts(query_h, key_parts, score_scale)
    prob_parts = [jnp.exp(score_part - log_total[:, :, None]) for score_part in scores]
    dprob_parts = [
        jnp.einsum("qhd,khd->hqk", grad_h, key_part[1], preferred_element_type=jnp.float32)
        for key_part in key_parts
    ]
    row_dot = reduce(
        jnp.add,
        [
            jnp.sum(prob_part * dprob_part, axis=-1)
            for prob_part, dprob_part in zip(prob_parts, dprob_parts)
        ],
    )
    dscore_parts = [
        (prob_part * (dprob_part - row_dot[:, :, None])).astype(jnp.bfloat16)
        for prob_part, dprob_part in zip(prob_parts, dprob_parts)
    ]
    grad_query = (
        reduce(
            jnp.add,
            [
                jnp.einsum(
                    "hqk,khd->qhd", dscore_part, key_part[0], preferred_element_type=jnp.float32
                )
                for dscore_part, key_part in zip(dscore_parts, key_parts)
            ],
        )
        * score_scale
    )
    grad_keys = [
        jnp.einsum("hqk,qhd->khd", dscore_part, query_h, preferred_element_type=jnp.float32)
        * score_scale
        for dscore_part in dscore_parts
    ]
    grad_values = [
        jnp.einsum(
            "hqk,qhd->khd",
            prob_part.astype(jnp.bfloat16),
            grad_h,
            preferred_element_type=jnp.float32,
        )
        for prob_part in prob_parts
    ]
    return (grad_query, grad_keys, grad_values)


LANES = 128
RING_LIMIT = 16


def ring_place(chip, chips):
    return jnp.where(chip % 2 == 0, chip // 2, chips - 1 - chip // 2)


def ring_chip(place, chips):
    return jnp.where(2 * place < chips, 2 * place, 2 * (chips - 1 - place) + 1)


def static_chip(place, chips):
    return 2 * place if 2 * place < chips else 2 * (chips - 1 - place) + 1


def ring_pairs(chips, step):
    return [
        (2 * static_chip(place, chips) + core, 2 * static_chip((place + step) % chips, chips) + core)
        for place in range(chips)
        for core in range(2)
    ]


def owner_order(matrix, seq_index, seq_count):
    chips = seq_count // 2
    width = matrix.shape[-1] // seq_count
    core = seq_index % 2
    place = ring_place(seq_index // 2, chips)
    blocks = []
    for which in (core, 1 - core):
        for near in range(chips):
            chip = ring_chip((place + near) % chips, chips)
            blocks.append(
                lax.dynamic_slice_in_dim(matrix, (2 * chip + which) * width, width, axis=-1)
            )
    return jnp.concatenate(blocks, axis=-1)


def over_core(values, seq_count):
    return lax.ppermute(values, "seq", [(index, index ^ 1) for index in range(seq_count)])


def ring_sum(chunks, seq_count):
    chips = seq_count // 2
    far = chips // 2
    half = chunks[0].shape[-1] // 2
    ahead, behind = ring_pairs(chips, 1), ring_pairs(chips, -1)
    onward = lax.ppermute(chunks[far][..., :half], "seq", ahead)
    backward = lax.ppermute(chunks[far][..., half:], "seq", behind)

    def joined(term, arrived, low_side):
        term, arrived = term.astype(jnp.float32), arrived.astype(jnp.float32)
        if arrived.shape != term.shape:
            pads = (0, half) if low_side else (half, 0)
            arrived = jnp.pad(arrived, ((0, 0),) * (term.ndim - 1) + (pads,))
        return (term + arrived).astype(jnp.bfloat16)

    for near in range(1, far):
        onward = lax.ppermute(joined(chunks[far - near], onward, True), "seq", ahead)
        backward = lax.ppermute(joined(chunks[far + near], backward, False), "seq", behind)
    total = chunks[0].astype(jnp.float32)
    return total + onward.astype(jnp.float32) + backward.astype(jnp.float32)


def owned_sum(rows, columns, seq_count):
    chips = seq_count // 2
    if chips > RING_LIMIT:
        return None
    half = rows.shape[-1] // 2
    away = product_tn(rows[:, half:], columns).astype(jnp.bfloat16)
    arrived = over_core(away, seq_count)
    mine = (product_tn(rows[:, :half], columns) + arrived.astype(jnp.float32)).astype(jnp.bfloat16)
    width = half // chips
    return ring_sum(
        [mine[near * width : (near + 1) * width] for near in range(chips)], seq_count
    )


def weight_grad(rows, columns, seq_index, seq_count):
    if seq_count // 2 > RING_LIMIT:
        return lax.psum_scatter(
            product_tn(rows, columns).astype(jnp.bfloat16), "seq", scatter_dimension=0, tiled=True
        ).astype(jnp.float32)
    return owned_sum(owner_order(rows, seq_index, seq_count), columns, seq_count)


def head_total(partial_sum):
    low = lax.optimization_barrier(partial_sum.astype(jnp.bfloat16))
    count = lax.axis_size("head")
    total = low.astype(jnp.float32)
    for step in range(1, count):
        pairs = [(index, (index + step) % count) for index in range(count)]
        total = total + lax.ppermute(low, "head", pairs).astype(jnp.float32)
    return total


def low_gather(block):
    return lax.all_gather(block.astype(jnp.bfloat16), "seq", axis=0, tiled=True)


def per_device(
    frames,
    time_token,
    prompt,
    clip_ids,
    norm1_gain,
    norm2_gain,
    norm3_gain,
    query_weight,
    key_weight,
    value_weight,
    out_weight,
    cross_query,
    cross_key,
    cross_value,
    cross_out,
    gate_weight,
    up_weight,
    down_weight,
    gate_bias,
    up_bias,
    down_bias,
    out_grad,
):
    local_rows, width = frames.shape
    clip_total = time_token.shape[0]
    ctx_tokens = prompt.shape[1]
    slot_count = local_rows // (2 * HALF) + 2
    seq_count = lax.axis_size("seq")
    seq_index = lax.axis_index("seq")
    head_index = lax.axis_index("head")
    first_row = seq_index * local_rows
    score_scale = HD ** (-0.5)
    part = query_weight.shape[1]
    hidden_width = gate_weight.shape[1]
    gain_rows = norm1_gain.shape[0]
    ctx_rows = cross_key.shape[0]
    ctx_width = prompt.shape[2]
    head_count = part // HD

    vectors = jnp.stack([norm1_gain, norm2_gain, norm3_gain, down_bias], axis=1)
    vectors = jnp.pad(vectors, ((0, 0), (0, LANES - 4)))
    ctx_pair = jnp.concatenate([cross_key, cross_value], axis=0)
    attn_local = jnp.concatenate(
        [query_weight, key_weight, value_weight, out_weight, cross_query, cross_out, ctx_pair, vectors],
        axis=1,
    )
    attn_weights = low_gather(attn_local)
    glu_weights = low_gather(jnp.concatenate([gate_weight, up_weight, down_weight], axis=1))
    w_qkv = attn_weights[:, : 3 * part]
    w_out = attn_weights[:, 3 * part : 4 * part]
    c_query = attn_weights[:, 4 * part : 5 * part]
    c_out = attn_weights[:, 5 * part : 6 * part]
    ctx_weights = attn_weights[:, 6 * part : 7 * part].reshape(seq_count, 2, ctx_rows, part)
    c_key = ctx_weights[:, 0].reshape(ctx_width, part)
    c_value = ctx_weights[:, 1].reshape(ctx_width, part)
    rows_of = attn_weights[:, 7 * part : 7 * part + 8].astype(jnp.float32).T
    gain_one_f, gain_two_f, gain_three_f, bias_f = rows_of[0], rows_of[1], rows_of[2], rows_of[3]
    w_gate_up = glu_weights[:, : 2 * hidden_width]
    w_down = glu_weights[:, 2 * hidden_width :]

    positions = first_row + jnp.arange(local_rows, dtype=jnp.int32)
    cos_table, sin_table = angles(positions)
    padded_ids = jnp.pad(clip_ids, (HALF, HALF), constant_values=-1)
    own_ids = lax.dynamic_slice_in_dim(clip_ids, first_row, local_rows)
    near_ids = lax.dynamic_slice_in_dim(padded_ids, first_row, local_rows + 2 * HALF)
    base_clip = jnp.minimum(own_ids[0], clip_total - slot_count)
    own_slot = own_ids - base_clip
    slot_range = jnp.arange(slot_count, dtype=jnp.int32)
    pad_rows = -slot_count % 16
    stamp_end = local_rows + slot_count

    stamp_rows = lax.dynamic_slice_in_dim(time_token, base_clip, slot_count, 0)
    source = jnp.concatenate(
        [frames, jnp.pad(stamp_rows, ((0, pad_rows), (0, 0)))], axis=0
    ).astype(jnp.float32)
    normed_out, normal_one, inverse_one = layer_norm_parts(source, gain_one_f)
    normed_one = normed_out.astype(jnp.bfloat16)
    frames_f = source[:local_rows]
    qkv = product(normed_one, w_qkv)
    query_rows = rotate(qkv[:local_rows, :part], cos_table, sin_table).astype(jnp.bfloat16)
    key_rows = rotate(qkv[:local_rows, part : 2 * part], cos_table, sin_table).astype(jnp.bfloat16)
    value_rows = qkv[:local_rows, 2 * part :].astype(jnp.bfloat16)
    near = extended(jnp.stack([key_rows, value_rows]), (("seq", 1),), HALF)
    window = local_rows + 2 * HALF
    near_key_h = near[0].reshape(window, head_count, HD)
    near_value_h = near[1].reshape(window, head_count, HD)
    query_h = query_rows.reshape(local_rows, head_count, HD)
    stamps = qkv[local_rows:stamp_end].astype(jnp.bfloat16)
    stamp_key_h = stamps[:, part : 2 * part].reshape(slot_count, head_count, HD)
    stamp_value_h = stamps[:, 2 * part :].reshape(slot_count, head_count, HD)

    query_pos = jnp.arange(local_rows, dtype=jnp.int32)
    key_pos = jnp.arange(window, dtype=jnp.int32) - HALF
    visible = (own_ids[:, None] == near_ids[None, :]) & (
        jnp.abs(query_pos[:, None] - key_pos[None, :]) <= HALF
    )
    own_stamp = own_slot[:, None] == slot_range[None, :]
    self_keys = [(near_key_h, near_value_h, visible), (stamp_key_h, stamp_value_h, own_stamp)]
    attn_mix_h, self_logs = attend_forward(query_h, self_keys, score_scale)
    attn_mixed = attn_mix_h.reshape(local_rows, part).astype(jnp.bfloat16)
    h_one = frames_f + head_total(product_t(attn_mixed, w_out))
    middle_out, normal_two, inverse_two = layer_norm_parts(h_one, gain_two_f)
    normed_two = middle_out.astype(jnp.bfloat16)
    cross_h = product(normed_two, c_query).astype(jnp.bfloat16).reshape(local_rows, head_count, HD)
    context_rows = lax.dynamic_slice_in_dim(prompt, base_clip, slot_count, 0).reshape(
        slot_count * ctx_tokens, ctx_width
    )
    ctx_key_h = product(context_rows, c_key).astype(jnp.bfloat16)
    ctx_key_h = ctx_key_h.reshape(slot_count * ctx_tokens, head_count, HD)
    ctx_value_h = product(context_rows, c_value).astype(jnp.bfloat16)
    ctx_value_h = ctx_value_h.reshape(slot_count * ctx_tokens, head_count, HD)
    key_slot = jnp.arange(slot_count * ctx_tokens, dtype=jnp.int32) // ctx_tokens
    cross_keys = [(ctx_key_h, ctx_value_h, own_slot[:, None] == key_slot[None, :])]
    cross_mix_h, cross_logs = attend_forward(cross_h, cross_keys, score_scale)
    cross_mixed = cross_mix_h.reshape(local_rows, part).astype(jnp.bfloat16)
    h_two = h_one + head_total(product_t(cross_mixed, c_out))
    third_out, normal_three, inverse_three = layer_norm_parts(h_two, gain_three_f)
    normed_three = third_out.astype(jnp.bfloat16)

    gate_up = product(normed_three, w_gate_up)
    gate_pre = gate_up[:, :hidden_width] + gate_bias
    up_pre = gate_up[:, hidden_width:] + up_bias
    sigmoid_gate = jax.nn.sigmoid(gate_pre)
    hidden = (gate_pre * sigmoid_gate * up_pre).astype(jnp.bfloat16)
    result = (h_two + head_total(product_t(hidden, w_down)) + bias_f).astype(jnp.bfloat16)
    grad_top = out_grad.astype(jnp.float32)
    grad_hidden = product(out_grad, w_down)
    grad_up = (grad_hidden * gate_pre * sigmoid_gate).astype(jnp.bfloat16)
    grad_gate = (
        grad_hidden * up_pre * sigmoid_gate * (1.0 + gate_pre * (1.0 - sigmoid_gate))
    ).astype(jnp.bfloat16)
    grad_gate_up = jnp.concatenate([grad_gate, grad_up], axis=1)
    bias_local = jnp.sum(grad_gate_up.astype(jnp.float32), axis=0).reshape(2, hidden_width)
    grad_normed_three = head_total(product_t(grad_gate_up, w_gate_up))
    down_share = weight_grad(out_grad, hidden, seq_index, seq_count)
    gate_up_share = weight_grad(normed_three, grad_gate_up, seq_index, seq_count)
    gain_three_term = jnp.sum(grad_normed_three * normal_three, axis=0)
    down_bias_term = jnp.sum(grad_top, axis=0)

    grad_h_two = grad_top + norm_back(grad_normed_three, normal_three, inverse_three, gain_three_f)
    grad_two_low = grad_h_two.astype(jnp.bfloat16)
    grad_cross_h = product(grad_two_low, c_out).astype(jnp.bfloat16)
    grad_cross_h = grad_cross_h.reshape(local_rows, head_count, HD)
    cross_out_share = weight_grad(grad_two_low, cross_mixed, seq_index, seq_count)
    grad_cross_q, ctx_key_grads, ctx_value_grads = attend_backward(
        cross_h, cross_keys, score_scale, cross_logs, grad_cross_h
    )
    grad_cross_query = grad_cross_q.reshape(local_rows, part).astype(jnp.bfloat16)
    ctx_grads = jnp.concatenate(
        [ctx_key_grads[0].reshape(-1, part), ctx_value_grads[0].reshape(-1, part)], axis=1
    ).astype(jnp.bfloat16)
    grad_normed_two = head_total(product_t(grad_cross_query, c_query))
    ctx_share = weight_grad(context_rows, ctx_grads, seq_index, seq_count)
    cross_query_share = weight_grad(normed_two, grad_cross_query, seq_index, seq_count)
    gain_two_term = jnp.sum(grad_normed_two * normal_two, axis=0)
    grad_h_one = grad_h_two + norm_back(grad_normed_two, normal_two, inverse_two, gain_two_f)
    grad_one_low = grad_h_one.astype(jnp.bfloat16)
    grad_attn_h = product(grad_one_low, w_out).astype(jnp.bfloat16)
    grad_attn_h = grad_attn_h.reshape(local_rows, head_count, HD)
    out_share = weight_grad(grad_one_low, attn_mixed, seq_index, seq_count)

    grad_query, grad_keys, grad_values = attend_backward(
        query_h, self_keys, score_scale, self_logs, grad_attn_h
    )
    near_grads = jnp.stack([grad_keys[0], grad_values[0]]).reshape(2, window, part)
    from_above = passed_along(near_grads[:, :HALF].astype(jnp.bfloat16), "seq", -1).astype(
        jnp.float32
    )
    from_below = passed_along(
        near_grads[:, HALF + local_rows :].astype(jnp.bfloat16), "seq", 1
    ).astype(jnp.float32)
    own_grads = (
        near_grads[:, HALF : HALF + local_rows]
        + jnp.pad(from_below, ((0, 0), (0, local_rows - HALF), (0, 0)))
        + jnp.pad(from_above, ((0, 0), (local_rows - HALF, 0), (0, 0)))
    )
    grad_query_rows = rotate(grad_query.reshape(local_rows, part), cos_table, -sin_table)
    grad_key_rows = rotate(own_grads[0], cos_table, -sin_table)
    stamp_grads = jnp.concatenate(
        [
            jnp.zeros((slot_count, part), jnp.float32),
            grad_keys[1].reshape(slot_count, part),
            grad_values[1].reshape(slot_count, part),
        ],
        axis=1,
    )
    frame_grads = jnp.concatenate([grad_query_rows, grad_key_rows, own_grads[1]], axis=1)
    grad_qkv = jnp.concatenate(
        [
            frame_grads.astype(jnp.bfloat16),
            jnp.pad(stamp_grads, ((0, pad_rows), (0, 0))).astype(jnp.bfloat16),
        ],
        axis=0,
    )
    grad_normed_all = product_t(grad_qkv, w_qkv)
    grad_normed_one = head_total(grad_normed_all[:local_rows])
    qkv_share = weight_grad(normed_one, grad_qkv, seq_index, seq_count)
    gain_one_term = jnp.sum(grad_normed_one * normal_one[:local_rows], axis=0)
    frames_grad = (
        grad_h_one
        + norm_back(grad_normed_one, normal_one[:local_rows], inverse_one[:local_rows], gain_one_f)
    ).astype(jnp.bfloat16)

    stamp_full = lax.dynamic_update_slice_in_dim(
        jnp.zeros((clip_total, width), jnp.float32), grad_normed_all[local_rows:stamp_end], base_clip, 0
    )
    bias_full = lax.dynamic_update_slice_in_dim(
        jnp.zeros((2, hidden_width * lax.axis_size("head")), jnp.float32),
        bias_local,
        head_index * hidden_width,
        1,
    )
    share = 1.0 / lax.axis_size("head")
    gains_full = share * jnp.stack(
        [gain_one_term, gain_two_term, gain_three_term, down_bias_term]
    )
    stamp_sum, bias_sum, gains_sum = lax.psum((stamp_full, bias_full, gains_full), ("seq", "head"))
    every_out, every_normal, every_inverse = layer_norm_parts(
        time_token.astype(jnp.float32), gain_one_f
    )
    time_grad = norm_back(stamp_sum, every_normal, every_inverse, gain_one_f)
    time_gain = jnp.sum(stamp_sum * every_normal, axis=0)
    gains_own = lax.dynamic_slice_in_dim(
        gains_sum.at[0].add(time_gain), seq_index * gain_rows, gain_rows, 1
    )
    own_bias = lax.dynamic_slice_in_dim(bias_sum, head_index * hidden_width, hidden_width, 1)
    return (
        result,
        frames_grad,
        time_grad,
        gains_own[0],
        gains_own[1],
        gains_own[2],
        qkv_share[:, :part],
        qkv_share[:, part : 2 * part],
        qkv_share[:, 2 * part :],
        out_share,
        cross_query_share,
        ctx_share[:, :part],
        ctx_share[:, part:],
        cross_out_share,
        gate_up_share[:, :hidden_width],
        gate_up_share[:, hidden_width:],
        down_share,
        own_bias[0],
        own_bias[1],
        gains_own[3],
    )


def solution(mesh):
    in_specs = (
        P("seq", None),
        P(),
        P(),
        P(),
        P("seq"),
        P("seq"),
        P("seq"),
        P("seq", "head"),
        P("seq", "head"),
        P("seq", "head"),
        P("seq", "head"),
        P("seq", "head"),
        P("seq", "head"),
        P("seq", "head"),
        P("seq", "head"),
        P("seq", "head"),
        P("seq", "head"),
        P("seq", "head"),
        P("head"),
        P("head"),
        P("seq"),
        P("seq", None),
    )
    out_specs = (
        P("seq", None),
        P("seq", None),
        P(),
        P("seq"),
        P("seq"),
        P("seq"),
        P("seq", "head"),
        P("seq", "head"),
        P("seq", "head"),
        P("seq", "head"),
        P("seq", "head"),
        P("seq", "head"),
        P("seq", "head"),
        P("seq", "head"),
        P("seq", "head"),
        P("seq", "head"),
        P("seq", "head"),
        P("head"),
        P("head"),
        P("seq"),
    )
    return jax.shard_map(
        per_device, mesh=mesh, in_specs=in_specs, out_specs=out_specs, check_vma=False
    )
```

```python
import functools
from functools import reduce

import jax
import jax.numpy as jnp
from jax import lax
from jax.experimental import pallas as pl
from jax.experimental.pallas import tpu as pltpu
from jax.sharding import PartitionSpec as P

HD = 64
ROT = 32
HALF = 256


EPS = 1e-05
NEG = -1e30


def extended(block, sides, width):
    for axis, dim in sides:
        count = lax.axis_size(axis)
        forward = [(i, i + 1) for i in range(count - 1)]
        backward = [(target, source) for source, target in forward]
        low = lax.ppermute(
            lax.slice_in_dim(block, block.shape[dim] - width, None, axis=dim), axis, forward
        )
        high = lax.ppermute(lax.slice_in_dim(block, 0, width, axis=dim), axis, backward)
        block = jnp.concatenate([low, block, high], axis=dim)
    return block


def passed_along(value, axis, steps):
    count = lax.axis_size(axis)
    first, last = (max(0, -steps), min(count, count - steps))
    return lax.ppermute(value, axis, [(source, source + steps) for source in range(first, last)])


def layer_norm_parts(values, gain):
    average = jnp.mean(values, axis=-1, keepdims=True)
    centered = values - average
    spread = jnp.mean(centered * centered, axis=-1, keepdims=True)
    inverse = lax.rsqrt(spread + EPS)
    normal = centered * inverse
    return (normal * gain, normal, inverse)


def norm_back(grad_out, normal, inverse, gain):
    shaped = grad_out * gain
    return (
        shaped
        - jnp.mean(shaped, axis=-1, keepdims=True)
        - normal * jnp.mean(shaped * normal, axis=-1, keepdims=True)
    ) * inverse


def angles(positions):
    ladder = jnp.arange(ROT // 2, dtype=jnp.float32)
    frequency = 10000.0 ** (-2.0 * ladder / ROT)
    phases = positions.astype(jnp.float32)[:, None] * frequency[None, :]
    return (jnp.cos(phases), jnp.sin(phases))


def rotate(values, cos_table, sin_table):
    shaped = values.reshape(values.shape[0], -1, HD)
    rot_half = ROT // 2
    leading = shaped[:, :, :rot_half]
    trailing = shaped[:, :, rot_half:ROT]
    cos_row = cos_table[:, None, :]
    sin_row = sin_table[:, None, :]
    turned = jnp.concatenate(
        [
            leading * cos_row - trailing * sin_row,
            trailing * cos_row + leading * sin_row,
            shaped[:, :, ROT:],
        ],
        axis=-1,
    )
    return turned.reshape(values.shape)


def product(matrix_a, matrix_b):
    return jnp.dot(matrix_a, matrix_b, preferred_element_type=jnp.float32)


def product_t(matrix_a, matrix_b):
    return lax.dot_general(
        matrix_a, matrix_b, (((1,), (1,)), ((), ())), preferred_element_type=jnp.float32
    )


def product_tn(matrix_a, matrix_b):
    return lax.dot_general(
        matrix_a, matrix_b, (((0,), (0,)), ((), ())), preferred_element_type=jnp.float32
    )


def exact_t(matrix_a, matrix_b):
    return lax.dot_general(
        matrix_a,
        matrix_b,
        (((1,), (1,)), ((), ())),
        precision=lax.Precision.HIGHEST,
        preferred_element_type=jnp.float32,
    )


def exact_tn(matrix_a, matrix_b):
    return lax.dot_general(
        matrix_a,
        matrix_b,
        (((0,), (0,)), ((), ())),
        precision=lax.Precision.HIGHEST,
        preferred_element_type=jnp.float32,
    )


def score_parts(query_h, key_parts, score_scale):
    return [
        jnp.where(
            visible[None],
            jnp.einsum("qhd,khd->hqk", query_h, key_h, preferred_element_type=jnp.float32)
            * score_scale,
            NEG,
        )
        for key_h, value_h, visible in key_parts
    ]


def attend_forward(query_h, key_parts, score_scale):
    scores = score_parts(query_h, key_parts, score_scale)
    row_peak = reduce(jnp.maximum, [jnp.max(score_part, axis=-1) for score_part in scores])
    exp_parts = [jnp.exp(score_part - row_peak[:, :, None]) for score_part in scores]
    row_total = reduce(jnp.add, [jnp.sum(exp_part, axis=-1) for exp_part in exp_parts])
    attn_mixed = reduce(
        jnp.add,
        [
            jnp.einsum(
                "hqk,khd->qhd",
                (exp_part / row_total[:, :, None]).astype(jnp.bfloat16),
                key_part[1],
                preferred_element_type=jnp.float32,
            )
            for exp_part, key_part in zip(exp_parts, key_parts)
        ],
    )
    return (attn_mixed, row_peak + jnp.log(row_total))


def attend_backward(query_h, key_parts, score_scale, log_total, grad_h):
    scores = score_parts(query_h, key_parts, score_scale)
    prob_parts = [jnp.exp(score_part - log_total[:, :, None]) for score_part in scores]
    dprob_parts = [
        jnp.einsum("qhd,khd->hqk", grad_h, key_part[1], preferred_element_type=jnp.float32)
        for key_part in key_parts
    ]
    row_dot = reduce(
        jnp.add,
        [
            jnp.sum(prob_part * dprob_part, axis=-1)
            for prob_part, dprob_part in zip(prob_parts, dprob_parts)
        ],
    )
    dscore_parts = [
        (prob_part * (dprob_part - row_dot[:, :, None])).astype(jnp.bfloat16)
        for prob_part, dprob_part in zip(prob_parts, dprob_parts)
    ]
    grad_query = (
        reduce(
            jnp.add,
            [
                jnp.einsum(
                    "hqk,khd->qhd", dscore_part, key_part[0], preferred_element_type=jnp.float32
                )
                for dscore_part, key_part in zip(dscore_parts, key_parts)
            ],
        )
        * score_scale
    )
    grad_keys = [
        jnp.einsum("hqk,qhd->khd", dscore_part, query_h, preferred_element_type=jnp.float32)
        * score_scale
        for dscore_part in dscore_parts
    ]
    grad_values = [
        jnp.einsum(
            "hqk,qhd->khd",
            prob_part.astype(jnp.bfloat16),
            grad_h,
            preferred_element_type=jnp.float32,
        )
        for prob_part in prob_parts
    ]
    return (grad_query, grad_keys, grad_values)


LANES = 128
BLOCK = 256
VMEM_BYTES = 60 * 1024 * 1024
MESH = pl.DeviceIdType.MESH


def ring_place(chip, chips):
    return jnp.where(chip % 2 == 0, chip // 2, chips - 1 - chip // 2)


def ring_chip(place, chips):
    return jnp.where(2 * place < chips, 2 * place, 2 * (chips - 1 - place) + 1)


def static_chip(place, chips):
    return 2 * place if 2 * place < chips else 2 * (chips - 1 - place) + 1


def ring_pairs(chips, step):
    return [
        (2 * static_chip(place, chips) + core, 2 * static_chip((place + step) % chips, chips) + core)
        for place in range(chips)
        for core in range(2)
    ]


def owner_matrix(width, seq_index, seq_count):
    chips = seq_count // 2
    seg = width // seq_count
    core = seq_index % 2
    place = ring_place(seq_index // 2, chips)
    row = jnp.arange(width, dtype=jnp.int32)
    which = row // (width // 2)
    near = row % (width // 2) // seg
    chip = ring_chip((place + near) % chips, chips)
    source = (2 * chip + jnp.where(which == 0, core, 1 - core)) * seg + row % seg
    return (source[:, None] == row[None, :]).astype(jnp.bfloat16)


def over_core(values, seq_count):
    return lax.ppermute(values, "seq", [(index, index ^ 1) for index in range(seq_count)])


class Ring:
    def __init__(self, term, seq_count):
        self.term = term
        self.chips = seq_count // 2
        self.far = self.chips // 2
        self.near = self.far
        self.ahead, self.behind = ring_pairs(self.chips, 1), ring_pairs(self.chips, -1)
        first = term(self.far)
        self.half = first.shape[-1] // 2
        self.send(first[..., : self.half], first[..., self.half :])

    def send(self, onward, backward):
        self.onward = lax.ppermute(onward.astype(jnp.bfloat16), "seq", self.ahead)
        self.backward = lax.ppermute(backward.astype(jnp.bfloat16), "seq", self.behind)

    def joined(self, near, arrived, low_side):
        term = self.term(near).astype(jnp.float32)
        arrived = arrived.astype(jnp.float32)
        if arrived.shape != term.shape:
            pads = (0, self.half) if low_side else (self.half, 0)
            arrived = jnp.pad(arrived, ((0, 0),) * (term.ndim - 1) + (pads,))
        return term + arrived

    def step(self):
        if self.near == 1:
            return
        self.near -= 1
        self.send(
            self.joined(self.near, self.onward, True),
            self.joined(2 * self.far - self.near, self.backward, False),
        )

    def after(self, value):
        value, self.onward, self.backward = lax.optimization_barrier(
            (value, self.onward, self.backward)
        )
        return value

    def finish(self):
        while self.near > 1:
            self.step()
        return (
            self.term(0).astype(jnp.float32)
            + self.onward.astype(jnp.float32)
            + self.backward.astype(jnp.float32)
        )


def core_sum(rows_t, columns, seq_count):
    half = rows_t.shape[0] // 2
    away = product(rows_t[half:], columns).astype(jnp.bfloat16)
    arrived = over_core(away, seq_count)
    return (product(rows_t[:half], columns) + arrived.astype(jnp.float32)).astype(jnp.bfloat16)


def block_of(matrix, near, chips):
    width = matrix.shape[0] // chips
    return matrix[near * width : (near + 1) * width]


def side_by_side(matrices, chips):
    return lambda near: jnp.concatenate([block_of(each, near, chips) for each in matrices], axis=-1)


def all_sum(values, axes):
    for axis in axes:
        count = lax.axis_size(axis)
        bit = 1
        while bit < count:
            values = values + lax.ppermute(
                values, axis, [(index, index ^ bit) for index in range(count)]
            )
            bit *= 2
    return values


def glu_kernel(
    blocks,
    normed,
    normed_t,
    top,
    top_t,
    w_gate,
    w_up,
    w_down,
    b_gate,
    b_up,
    out,
    grad_normed,
    sums,
    bias_grads,
    out_acc,
    grad_acc,
    mine,
    away,
    arrived,
    send_sem,
    recv_sem,
):
    index = pl.program_id(0)
    seq_index = lax.axis_index("seq")
    partner = seq_index + 1 - 2 * (seq_index % 2)
    half = normed_t.shape[0] // 2

    def crossing(block):
        return pltpu.make_async_remote_copy(
            src_ref=away.at[block % 2],
            dst_ref=arrived.at[block],
            send_sem=send_sem.at[block % 2],
            recv_sem=recv_sem.at[block],
            device_id={"seq": partner},
            device_id_type=MESH,
        )

    @pl.when(index == 0)
    def _():
        barrier = pltpu.get_barrier_semaphore()
        pl.semaphore_signal(barrier, inc=1, device_id={"seq": partner}, device_id_type=MESH)
        pl.semaphore_wait(barrier, 1)
        out_acc[...] = jnp.zeros_like(out_acc)
        grad_acc[...] = jnp.zeros_like(grad_acc)

    @pl.when(index < blocks)
    def _():
        gate_pre = product(normed[...], w_gate[...]) + b_gate[...]
        up_pre = product(normed[...], w_up[...]) + b_up[...]
        grad_hidden = product(top[...], w_down[...])
        sigmoid_gate = jax.nn.sigmoid(gate_pre)
        silu_gate = gate_pre * sigmoid_gate
        hidden = (silu_gate * up_pre).astype(jnp.bfloat16)
        grad_up = (grad_hidden * silu_gate).astype(jnp.bfloat16)
        grad_gate = (
            grad_hidden * up_pre * sigmoid_gate * (1.0 + gate_pre * (1.0 - sigmoid_gate))
        ).astype(jnp.bfloat16)
        bias_grads[0:1, :] = jnp.sum(grad_gate.astype(jnp.float32), axis=0, keepdims=True)
        bias_grads[1:2, :] = jnp.sum(grad_up.astype(jnp.float32), axis=0, keepdims=True)
        out_acc[...] += product_t(hidden, w_down[...])
        grad_acc[...] += product_t(grad_gate, w_gate[...]) + product_t(grad_up, w_up[...])

        @pl.when(index >= 2)
        def _():
            crossing(index - 2).wait_send()

        slot = index % 2
        away[slot, 0] = product(normed_t[half:, :], grad_gate).astype(jnp.bfloat16)
        away[slot, 1] = product(normed_t[half:, :], grad_up).astype(jnp.bfloat16)
        away[slot, 2] = product(top_t[half:, :], hidden).astype(jnp.bfloat16)
        crossing(index).start()
        mine[slot, 0] = product(normed_t[:half, :], grad_gate)
        mine[slot, 1] = product(normed_t[:half, :], grad_up)
        mine[slot, 2] = product(top_t[:half, :], hidden)

    @pl.when(index >= 1)
    def _():
        crossing(index - 1).wait_recv()
        prior = index - 1
        sums[...] = (mine[prior % 2] + arrived[prior].astype(jnp.float32)).astype(jnp.bfloat16)

    @pl.when(index == blocks)
    def _():
        crossing(blocks - 2).wait_send()
        crossing(blocks - 1).wait_send()
        out[...] = out_acc[...].astype(jnp.bfloat16)
        grad_normed[...] = grad_acc[...].astype(jnp.bfloat16)


def glu_layer(normed, normed_t, top, top_t, weights, gate_bias, up_bias):
    rows, width = normed.shape
    hidden_width = gate_bias.shape[0]
    blocks = hidden_width // BLOCK
    half = width // 2
    whole = pl.BlockSpec((rows, width), lambda i: (0, 0))
    whole_t = pl.BlockSpec((width, rows), lambda i: (0, 0))

    def weight_spec(which):
        return pl.BlockSpec(
            (width, BLOCK), lambda i: (0, which * blocks + jnp.minimum(i, blocks - 1))
        )

    bias_spec = pl.BlockSpec((1, BLOCK), lambda i: (0, jnp.minimum(i, blocks - 1)))
    work = rows * width * hidden_width
    return pl.pallas_call(
        functools.partial(glu_kernel, blocks),
        grid=(blocks + 1,),
        in_specs=[
            whole,
            whole_t,
            whole,
            whole_t,
            weight_spec(0),
            weight_spec(1),
            weight_spec(2),
            bias_spec,
            bias_spec,
        ],
        out_specs=[
            whole,
            whole,
            pl.BlockSpec((3, half, BLOCK), lambda i: (0, 0, jnp.maximum(i - 1, 0))),
            pl.BlockSpec((2, BLOCK), lambda i: (0, jnp.minimum(i, blocks - 1))),
        ],
        out_shape=[
            jax.ShapeDtypeStruct((rows, width), jnp.bfloat16),
            jax.ShapeDtypeStruct((rows, width), jnp.bfloat16),
            jax.ShapeDtypeStruct((3, half, hidden_width), jnp.bfloat16),
            jax.ShapeDtypeStruct((2, hidden_width), jnp.float32),
        ],
        scratch_shapes=[
            pltpu.VMEM((rows, width), jnp.float32),
            pltpu.VMEM((rows, width), jnp.float32),
            pltpu.VMEM((2, 3, half, BLOCK), jnp.float32),
            pltpu.VMEM((2, 3, half, BLOCK), jnp.bfloat16),
            pltpu.VMEM((blocks, 3, half, BLOCK), jnp.bfloat16),
            pltpu.SemaphoreType.DMA((2,)),
            pltpu.SemaphoreType.DMA((blocks,)),
        ],
        compiler_params=pltpu.CompilerParams(
            collective_id=1, has_side_effects=True, vmem_limit_bytes=VMEM_BYTES
        ),
        cost_estimate=pl.CostEstimate(
            flops=18 * work, bytes_accessed=12 * width * hidden_width, transcendentals=rows * hidden_width
        ),
        name="glu_layer",
    )(
        normed,
        normed_t,
        top,
        top_t,
        weights,
        weights,
        weights,
        gate_bias[None],
        up_bias[None],
    )


def head_total(partial_sum):
    low = partial_sum
    if low.dtype != jnp.bfloat16:
        low = lax.optimization_barrier(partial_sum.astype(jnp.bfloat16))
    count = lax.axis_size("head")
    total = low.astype(jnp.float32)
    for step in range(1, count):
        pairs = [(index, (index + step) % count) for index in range(count)]
        total = total + lax.ppermute(low, "head", pairs).astype(jnp.float32)
    return total


def low_gather(block):
    return lax.all_gather(block.astype(jnp.bfloat16), "seq", axis=0, tiled=True)


def per_device(
    frames,
    time_token,
    prompt,
    clip_ids,
    norm1_gain,
    norm2_gain,
    norm3_gain,
    query_weight,
    key_weight,
    value_weight,
    out_weight,
    cross_query,
    cross_key,
    cross_value,
    cross_out,
    gate_weight,
    up_weight,
    down_weight,
    gate_bias,
    up_bias,
    down_bias,
    out_grad,
):
    local_rows, width = frames.shape
    clip_total = time_token.shape[0]
    ctx_tokens = prompt.shape[1]
    slot_count = local_rows // (2 * HALF) + 2
    seq_count = lax.axis_size("seq")
    seq_index = lax.axis_index("seq")
    head_index = lax.axis_index("head")
    first_row = seq_index * local_rows
    score_scale = HD ** (-0.5)
    part = query_weight.shape[1]
    hidden_width = gate_weight.shape[1]
    gain_rows = norm1_gain.shape[0]
    ctx_rows = cross_key.shape[0]
    ctx_width = prompt.shape[2]
    head_count = part // HD
    chips = seq_count // 2
    order = owner_matrix(width, seq_index, seq_count)

    def ordered(matrix, by=order):
        return product_t(by, matrix).astype(jnp.bfloat16)

    vectors = jnp.stack([norm1_gain, norm2_gain, norm3_gain, down_bias], axis=1)
    vectors = jnp.pad(vectors, ((0, 0), (0, LANES - 4)))
    ctx_pair = jnp.concatenate([cross_key, cross_value], axis=0)
    attn_local = jnp.concatenate(
        [query_weight, key_weight, value_weight, out_weight, cross_query, cross_out, ctx_pair, vectors],
        axis=1,
    )
    attn_weights = low_gather(attn_local)
    glu_weights = low_gather(jnp.concatenate([gate_weight, up_weight, down_weight], axis=1))
    w_qkv = attn_weights[:, : 3 * part]
    w_out = attn_weights[:, 3 * part : 4 * part]
    c_query = attn_weights[:, 4 * part : 5 * part]
    c_out = attn_weights[:, 5 * part : 6 * part]
    ctx_weights = attn_weights[:, 6 * part : 7 * part].reshape(seq_count, 2, ctx_rows, part)
    c_key = ctx_weights[:, 0].reshape(ctx_width, part)
    c_value = ctx_weights[:, 1].reshape(ctx_width, part)
    rows_of = attn_weights[:, 7 * part : 7 * part + 8].astype(jnp.float32).T
    gain_one_f, gain_two_f, gain_three_f, bias_f = rows_of[0], rows_of[1], rows_of[2], rows_of[3]

    positions = first_row + jnp.arange(local_rows, dtype=jnp.int32)
    cos_table, sin_table = angles(positions)
    padded_ids = jnp.pad(clip_ids, (HALF, HALF), constant_values=-1)
    own_ids = lax.dynamic_slice_in_dim(clip_ids, first_row, local_rows)
    near_ids = lax.dynamic_slice_in_dim(padded_ids, first_row, local_rows + 2 * HALF)
    base_clip = jnp.minimum(own_ids[0], clip_total - slot_count)
    own_slot = own_ids - base_clip
    slot_range = jnp.arange(slot_count, dtype=jnp.int32)
    pad_rows = -slot_count % 16
    stamp_end = local_rows + slot_count

    stamp_rows = lax.dynamic_slice_in_dim(time_token, base_clip, slot_count, 0)
    source = jnp.concatenate(
        [frames, jnp.pad(stamp_rows, ((0, pad_rows), (0, 0)))], axis=0
    ).astype(jnp.float32)
    normed_out, normal_one, inverse_one = layer_norm_parts(source, gain_one_f)
    normed_one = normed_out.astype(jnp.bfloat16)
    frames_f = source[:local_rows]
    qkv = product(normed_one, w_qkv)
    query_rows = rotate(qkv[:local_rows, :part], cos_table, sin_table).astype(jnp.bfloat16)
    key_rows = rotate(qkv[:local_rows, part : 2 * part], cos_table, sin_table).astype(jnp.bfloat16)
    value_rows = qkv[:local_rows, 2 * part :].astype(jnp.bfloat16)
    near = extended(jnp.stack([key_rows, value_rows]), (("seq", 1),), HALF)
    window = local_rows + 2 * HALF
    near_key_h = near[0].reshape(window, head_count, HD)
    near_value_h = near[1].reshape(window, head_count, HD)
    query_h = query_rows.reshape(local_rows, head_count, HD)
    stamps = qkv[local_rows:stamp_end].astype(jnp.bfloat16)
    stamp_key_h = stamps[:, part : 2 * part].reshape(slot_count, head_count, HD)
    stamp_value_h = stamps[:, 2 * part :].reshape(slot_count, head_count, HD)

    query_pos = jnp.arange(local_rows, dtype=jnp.int32)
    key_pos = jnp.arange(window, dtype=jnp.int32) - HALF
    visible = (own_ids[:, None] == near_ids[None, :]) & (
        jnp.abs(query_pos[:, None] - key_pos[None, :]) <= HALF
    )
    own_stamp = own_slot[:, None] == slot_range[None, :]
    self_keys = [(near_key_h, near_value_h, visible), (stamp_key_h, stamp_value_h, own_stamp)]
    attn_mix_h, self_logs = attend_forward(query_h, self_keys, score_scale)
    attn_mixed = attn_mix_h.reshape(local_rows, part).astype(jnp.bfloat16)
    h_one = frames_f + head_total(product_t(attn_mixed, w_out))
    middle_out, normal_two, inverse_two = layer_norm_parts(h_one, gain_two_f)
    normed_two = middle_out.astype(jnp.bfloat16)
    cross_h = product(normed_two, c_query).astype(jnp.bfloat16).reshape(local_rows, head_count, HD)
    context_rows = lax.dynamic_slice_in_dim(prompt, base_clip, slot_count, 0).reshape(
        slot_count * ctx_tokens, ctx_width
    )
    ctx_key_h = product(context_rows, c_key).astype(jnp.bfloat16)
    ctx_key_h = ctx_key_h.reshape(slot_count * ctx_tokens, head_count, HD)
    ctx_value_h = product(context_rows, c_value).astype(jnp.bfloat16)
    ctx_value_h = ctx_value_h.reshape(slot_count * ctx_tokens, head_count, HD)
    key_slot = jnp.arange(slot_count * ctx_tokens, dtype=jnp.int32) // ctx_tokens
    cross_keys = [(ctx_key_h, ctx_value_h, own_slot[:, None] == key_slot[None, :])]
    cross_mix_h, cross_logs = attend_forward(cross_h, cross_keys, score_scale)
    cross_mixed = cross_mix_h.reshape(local_rows, part).astype(jnp.bfloat16)
    h_two = h_one + head_total(product_t(cross_mixed, c_out))
    third_out, normal_three, inverse_three = layer_norm_parts(h_two, gain_three_f)
    normed_three = third_out.astype(jnp.bfloat16)

    glu_out, grad_normed_low, glu_sums, bias_local = glu_layer(
        normed_three,
        ordered(normed_three),
        out_grad,
        ordered(out_grad),
        glu_weights,
        gate_bias,
        up_bias,
    )
    grad_normed_three = head_total(grad_normed_low)
    result = (h_two + head_total(glu_out) + bias_f).astype(jnp.bfloat16)
    glu_ring = Ring(
        lambda near: glu_sums[:, near * gain_rows : (near + 1) * gain_rows], seq_count
    )
    grad_top = out_grad.astype(jnp.float32)
    gain_three_term = jnp.sum(grad_normed_three * normal_three, axis=0)
    down_bias_term = jnp.sum(grad_top, axis=0)

    grad_h_two = grad_top + norm_back(grad_normed_three, normal_three, inverse_three, gain_three_f)
    grad_two_low = grad_h_two.astype(jnp.bfloat16)
    grad_cross_h = product(grad_two_low, c_out).astype(jnp.bfloat16)
    grad_cross_h = grad_cross_h.reshape(local_rows, head_count, HD)
    cross_out_sum = core_sum(ordered(grad_two_low), cross_mixed, seq_count)
    grad_cross_h = glu_ring.after(grad_cross_h)
    glu_ring.step()
    grad_cross_q, ctx_key_grads, ctx_value_grads = attend_backward(
        cross_h, cross_keys, score_scale, cross_logs, grad_cross_h
    )
    grad_cross_query = grad_cross_q.reshape(local_rows, part).astype(jnp.bfloat16)
    ctx_grads = jnp.concatenate(
        [ctx_key_grads[0].reshape(-1, part), ctx_value_grads[0].reshape(-1, part)], axis=1
    ).astype(jnp.bfloat16)
    grad_normed_two = head_total(product_t(grad_cross_query, c_query))
    grad_normed_two = glu_ring.after(grad_normed_two)
    glu_ring.step()
    cross_query_sum = core_sum(ordered(normed_two), grad_cross_query, seq_count)
    ctx_order = owner_matrix(ctx_width, seq_index, seq_count)
    ctx_sum = core_sum(ordered(context_rows, ctx_order), ctx_grads, seq_count)
    gain_two_term = jnp.sum(grad_normed_two * normal_two, axis=0)
    grad_h_one = grad_h_two + norm_back(grad_normed_two, normal_two, inverse_two, gain_two_f)
    grad_one_low = grad_h_one.astype(jnp.bfloat16)
    grad_attn_h = product(grad_one_low, w_out).astype(jnp.bfloat16)
    grad_attn_h = grad_attn_h.reshape(local_rows, head_count, HD)
    out_sum = core_sum(ordered(grad_one_low), attn_mixed, seq_count)
    joined_sums = side_by_side([cross_out_sum, cross_query_sum, out_sum], chips)

    def cross_term(near):
        ctx_block = block_of(ctx_sum, near, chips)
        ctx_block = jnp.concatenate([ctx_block[:, :part], ctx_block[:, part:]], axis=0)
        return jnp.concatenate([joined_sums(near), ctx_block], axis=1)

    grad_attn_h = glu_ring.after(grad_attn_h)
    glu_ring.step()

    grad_query, grad_keys, grad_values = attend_backward(
        query_h, self_keys, score_scale, self_logs, grad_attn_h
    )
    near_grads = jnp.stack([grad_keys[0], grad_values[0]]).reshape(2, window, part)
    near_grads = glu_ring.after(near_grads)
    glu_share = glu_ring.finish()
    cross_ring = Ring(cross_term, seq_count)
    cross_share = cross_ring.finish()
    from_above = passed_along(near_grads[:, :HALF].astype(jnp.bfloat16), "seq", -1).astype(
        jnp.float32
    )
    from_below = passed_along(
        near_grads[:, HALF + local_rows :].astype(jnp.bfloat16), "seq", 1
    ).astype(jnp.float32)
    own_grads = (
        near_grads[:, HALF : HALF + local_rows]
        + jnp.pad(from_below, ((0, 0), (0, local_rows - HALF), (0, 0)))
        + jnp.pad(from_above, ((0, 0), (local_rows - HALF, 0), (0, 0)))
    )
    grad_query_rows = rotate(grad_query.reshape(local_rows, part), cos_table, -sin_table)
    grad_key_rows = rotate(own_grads[0], cos_table, -sin_table)
    stamp_grads = jnp.concatenate(
        [
            jnp.zeros((slot_count, part), jnp.float32),
            grad_keys[1].reshape(slot_count, part),
            grad_values[1].reshape(slot_count, part),
        ],
        axis=1,
    )
    frame_grads = jnp.concatenate([grad_query_rows, grad_key_rows, own_grads[1]], axis=1)
    grad_qkv = jnp.concatenate(
        [
            frame_grads.astype(jnp.bfloat16),
            jnp.pad(stamp_grads, ((0, pad_rows), (0, 0))).astype(jnp.bfloat16),
        ],
        axis=0,
    )
    grad_normed_all = product_t(grad_qkv, w_qkv)
    grad_normed_one = head_total(grad_normed_all[:local_rows])
    qkv_ring = Ring(
        side_by_side([core_sum(ordered(normed_one), grad_qkv, seq_count)], chips), seq_count
    )
    qkv_share = qkv_ring.finish()
    cross_out_share = cross_share[:, :part]
    cross_query_share = cross_share[:, part : 2 * part]
    out_share = cross_share[:, 2 * part : 3 * part]
    ctx_share = cross_share[:, 3 * part :]
    gain_one_term = jnp.sum(grad_normed_all[:local_rows] * normal_one[:local_rows], axis=0)
    frames_grad = (
        grad_h_one
        + norm_back(grad_normed_one, normal_one[:local_rows], inverse_one[:local_rows], gain_one_f)
    ).astype(jnp.bfloat16)

    stamp_full = lax.dynamic_update_slice_in_dim(
        jnp.zeros((clip_total, width), jnp.float32), grad_normed_all[local_rows:stamp_end], base_clip, 0
    )
    late = all_sum(jnp.concatenate([stamp_full, gain_one_term[None]], axis=0), ("seq", "head"))
    stamp_sum = late[:clip_total]
    early = all_sum(
        jnp.concatenate(
            [
                bias_local.reshape(-1, width),
                jnp.stack([gain_two_term, gain_three_term, down_bias_term]),
            ],
            axis=0,
        ),
        ("seq",),
    )
    own_bias = early[:-3].reshape(2, hidden_width)
    every_out, every_normal, every_inverse = layer_norm_parts(
        time_token.astype(jnp.float32), gain_one_f
    )
    time_grad = norm_back(stamp_sum, every_normal, every_inverse, gain_one_f)
    time_gain = jnp.sum(stamp_sum * every_normal, axis=0)
    gains_own = lax.dynamic_slice_in_dim(
        jnp.concatenate([late[clip_total:] + time_gain[None], early[-3:]], axis=0),
        seq_index * gain_rows,
        gain_rows,
        1,
    )
    return (
        result,
        frames_grad,
        time_grad,
        gains_own[0],
        gains_own[1],
        gains_own[2],
        qkv_share[:, :part],
        qkv_share[:, part : 2 * part],
        qkv_share[:, 2 * part :],
        out_share,
        cross_query_share,
        ctx_share[:ctx_rows],
        ctx_share[ctx_rows:],
        cross_out_share,
        glu_share[0],
        glu_share[1],
        glu_share[2],
        own_bias[0],
        own_bias[1],
        gains_own[3],
    )


def solution(mesh):
    in_specs = (
        P("seq", None),
        P(),
        P(),
        P(),
        P("seq"),
        P("seq"),
        P("seq"),
        P("seq", "head"),
        P("seq", "head"),
        P("seq", "head"),
        P("seq", "head"),
        P("seq", "head"),
        P("seq", "head"),
        P("seq", "head"),
        P("seq", "head"),
        P("seq", "head"),
        P("seq", "head"),
        P("seq", "head"),
        P("head"),
        P("head"),
        P("seq"),
        P("seq", None),
    )
    out_specs = (
        P("seq", None),
        P("seq", None),
        P(),
        P("seq"),
        P("seq"),
        P("seq"),
        P("seq", "head"),
        P("seq", "head"),
        P("seq", "head"),
        P("seq", "head"),
        P("seq", "head"),
        P("seq", "head"),
        P("seq", "head"),
        P("seq", "head"),
        P("seq", "head"),
        P("seq", "head"),
        P("seq", "head"),
        P("head"),
        P("head"),
        P("seq"),
    )
    return jax.shard_map(
        per_device, mesh=mesh, in_specs=in_specs, out_specs=out_specs, check_vma=False
    )
```

```python
import functools
from functools import reduce

import jax
import jax.numpy as jnp
from jax import lax
from jax.experimental import pallas as pl
from jax.experimental.pallas import tpu as pltpu
from jax.sharding import PartitionSpec as P

HD = 64
ROT = 32
HALF = 256


EPS = 1e-05
NEG = -1e30


def extended(block, sides, width):
    for axis, dim in sides:
        count = lax.axis_size(axis)
        forward = [(i, i + 1) for i in range(count - 1)]
        backward = [(target, source) for source, target in forward]
        low = lax.ppermute(
            lax.slice_in_dim(block, block.shape[dim] - width, None, axis=dim), axis, forward
        )
        high = lax.ppermute(lax.slice_in_dim(block, 0, width, axis=dim), axis, backward)
        block = jnp.concatenate([low, block, high], axis=dim)
    return block


def passed_along(value, axis, steps):
    count = lax.axis_size(axis)
    first, last = (max(0, -steps), min(count, count - steps))
    return lax.ppermute(value, axis, [(source, source + steps) for source in range(first, last)])


def layer_norm_parts(values, gain):
    average = jnp.mean(values, axis=-1, keepdims=True)
    centered = values - average
    spread = jnp.mean(centered * centered, axis=-1, keepdims=True)
    inverse = lax.rsqrt(spread + EPS)
    normal = centered * inverse
    return (normal * gain, normal, inverse)


def norm_back(grad_out, normal, inverse, gain):
    shaped = grad_out * gain
    return (
        shaped
        - jnp.mean(shaped, axis=-1, keepdims=True)
        - normal * jnp.mean(shaped * normal, axis=-1, keepdims=True)
    ) * inverse


def angles(positions):
    ladder = jnp.arange(ROT // 2, dtype=jnp.float32)
    frequency = 10000.0 ** (-2.0 * ladder / ROT)
    phases = positions.astype(jnp.float32)[:, None] * frequency[None, :]
    return (jnp.cos(phases), jnp.sin(phases))


def rotate(values, cos_table, sin_table):
    shaped = values.reshape(values.shape[0], -1, HD)
    rot_half = ROT // 2
    leading = shaped[:, :, :rot_half]
    trailing = shaped[:, :, rot_half:ROT]
    cos_row = cos_table[:, None, :]
    sin_row = sin_table[:, None, :]
    turned = jnp.concatenate(
        [
            leading * cos_row - trailing * sin_row,
            trailing * cos_row + leading * sin_row,
            shaped[:, :, ROT:],
        ],
        axis=-1,
    )
    return turned.reshape(values.shape)


def product(matrix_a, matrix_b):
    return jnp.dot(matrix_a, matrix_b, preferred_element_type=jnp.float32)


def product_t(matrix_a, matrix_b):
    return lax.dot_general(
        matrix_a, matrix_b, (((1,), (1,)), ((), ())), preferred_element_type=jnp.float32
    )


def product_tn(matrix_a, matrix_b):
    return lax.dot_general(
        matrix_a, matrix_b, (((0,), (0,)), ((), ())), preferred_element_type=jnp.float32
    )


def exact_t(matrix_a, matrix_b):
    return lax.dot_general(
        matrix_a,
        matrix_b,
        (((1,), (1,)), ((), ())),
        precision=lax.Precision.HIGHEST,
        preferred_element_type=jnp.float32,
    )


def exact_tn(matrix_a, matrix_b):
    return lax.dot_general(
        matrix_a,
        matrix_b,
        (((0,), (0,)), ((), ())),
        precision=lax.Precision.HIGHEST,
        preferred_element_type=jnp.float32,
    )


def score_parts(query_h, key_parts, score_scale):
    return [
        jnp.where(
            visible[None],
            jnp.einsum("qhd,khd->hqk", query_h, key_h, preferred_element_type=jnp.float32)
            * score_scale,
            NEG,
        )
        for key_h, value_h, visible in key_parts
    ]


def attend_forward(query_h, key_parts, score_scale):
    scores = score_parts(query_h, key_parts, score_scale)
    row_peak = reduce(jnp.maximum, [jnp.max(score_part, axis=-1) for score_part in scores])
    exp_parts = [jnp.exp(score_part - row_peak[:, :, None]) for score_part in scores]
    row_total = reduce(jnp.add, [jnp.sum(exp_part, axis=-1) for exp_part in exp_parts])
    attn_mixed = reduce(
        jnp.add,
        [
            jnp.einsum(
                "hqk,khd->qhd",
                (exp_part / row_total[:, :, None]).astype(jnp.bfloat16),
                key_part[1],
                preferred_element_type=jnp.float32,
            )
            for exp_part, key_part in zip(exp_parts, key_parts)
        ],
    )
    return (attn_mixed, row_peak + jnp.log(row_total))


def attend_backward(query_h, key_parts, score_scale, log_total, grad_h):
    scores = score_parts(query_h, key_parts, score_scale)
    prob_parts = [jnp.exp(score_part - log_total[:, :, None]) for score_part in scores]
    dprob_parts = [
        jnp.einsum("qhd,khd->hqk", grad_h, key_part[1], preferred_element_type=jnp.float32)
        for key_part in key_parts
    ]
    row_dot = reduce(
        jnp.add,
        [
            jnp.sum(prob_part * dprob_part, axis=-1)
            for prob_part, dprob_part in zip(prob_parts, dprob_parts)
        ],
    )
    dscore_parts = [
        (prob_part * (dprob_part - row_dot[:, :, None])).astype(jnp.bfloat16)
        for prob_part, dprob_part in zip(prob_parts, dprob_parts)
    ]
    grad_query = (
        reduce(
            jnp.add,
            [
                jnp.einsum(
                    "hqk,khd->qhd", dscore_part, key_part[0], preferred_element_type=jnp.float32
                )
                for dscore_part, key_part in zip(dscore_parts, key_parts)
            ],
        )
        * score_scale
    )
    grad_keys = [
        jnp.einsum("hqk,qhd->khd", dscore_part, query_h, preferred_element_type=jnp.float32)
        * score_scale
        for dscore_part in dscore_parts
    ]
    grad_values = [
        jnp.einsum(
            "hqk,qhd->khd",
            prob_part.astype(jnp.bfloat16),
            grad_h,
            preferred_element_type=jnp.float32,
        )
        for prob_part in prob_parts
    ]
    return (grad_query, grad_keys, grad_values)


LANES = 128
BLOCK = 256
TAIL_WIDTH = 768
SELF_PIECES = 3
QUERY_BLOCK = 128
VMEM_BYTES = 60 * 1024 * 1024
MESH = pl.DeviceIdType.MESH


def ring_place(chip, chips):
    return jnp.where(chip % 2 == 0, chip // 2, chips - 1 - chip // 2)


def ring_chip(place, chips):
    return jnp.where(2 * place < chips, 2 * place, 2 * (chips - 1 - place) + 1)


def static_chip(place, chips):
    return 2 * place if 2 * place < chips else 2 * (chips - 1 - place) + 1


def ring_pairs(chips, step):
    return [
        (2 * static_chip(place, chips) + core, 2 * static_chip((place + step) % chips, chips) + core)
        for place in range(chips)
        for core in range(2)
    ]


def owner_matrix(width, seq_index, seq_count):
    chips = seq_count // 2
    seg = width // seq_count
    core = seq_index % 2
    place = ring_place(seq_index // 2, chips)
    row = jnp.arange(width, dtype=jnp.int32)
    which = row // (width // 2)
    near = row % (width // 2) // seg
    chip = ring_chip((place + near) % chips, chips)
    source = (2 * chip + jnp.where(which == 0, core, 1 - core)) * seg + row % seg
    return (source[:, None] == row[None, :]).astype(jnp.bfloat16)


def over_core(values, seq_count):
    return lax.ppermute(values, "seq", [(index, index ^ 1) for index in range(seq_count)])


class Ring:
    def __init__(self, term, seq_count):
        self.term = term
        self.chips = seq_count // 2
        self.far = self.chips // 2
        self.near = self.far
        self.ahead, self.behind = ring_pairs(self.chips, 1), ring_pairs(self.chips, -1)
        first = term(self.far)
        self.half = first.shape[-1] // 2
        self.send(first[..., : self.half], first[..., self.half :])

    def send(self, onward, backward):
        self.onward = lax.ppermute(onward.astype(jnp.bfloat16), "seq", self.ahead)
        self.backward = lax.ppermute(backward.astype(jnp.bfloat16), "seq", self.behind)

    def joined(self, near, arrived, low_side):
        term = self.term(near).astype(jnp.float32)
        arrived = arrived.astype(jnp.float32)
        if arrived.shape != term.shape:
            pads = (0, self.half) if low_side else (self.half, 0)
            arrived = jnp.pad(arrived, ((0, 0),) * (term.ndim - 1) + (pads,))
        return term + arrived

    def step(self):
        if self.near == 1:
            return
        self.near -= 1
        self.send(
            self.joined(self.near, self.onward, True),
            self.joined(2 * self.far - self.near, self.backward, False),
        )

    def after(self, value):
        value, self.onward, self.backward = lax.optimization_barrier(
            (value, self.onward, self.backward)
        )
        return value

    def finish(self):
        while self.near > 1:
            self.step()
        return (
            self.term(0).astype(jnp.float32)
            + self.onward.astype(jnp.float32)
            + self.backward.astype(jnp.float32)
        )


def core_sum(rows_t, columns, seq_count):
    half = rows_t.shape[0] // 2
    away = product(rows_t[half:], columns).astype(jnp.bfloat16)
    arrived = over_core(away, seq_count)
    return (product(rows_t[:half], columns) + arrived.astype(jnp.float32)).astype(jnp.bfloat16)


def block_of(matrix, near, chips):
    width = matrix.shape[0] // chips
    return matrix[near * width : (near + 1) * width]


def side_by_side(matrices, chips):
    return lambda near: jnp.concatenate([block_of(each, near, chips) for each in matrices], axis=-1)


def all_sum(values, axes):
    for axis in axes:
        count = lax.axis_size(axis)
        bit = 1
        while bit < count:
            values = values + lax.ppermute(
                values, axis, [(index, index ^ bit) for index in range(count)]
            )
            bit *= 2
    return values


def glu_kernel(
    blocks,
    normed,
    normed_t,
    top,
    top_t,
    w_gate,
    w_up,
    w_down,
    b_gate,
    b_up,
    out,
    grad_normed,
    sums,
    bias_grads,
    out_acc,
    grad_acc,
    mine,
    away,
    arrived,
    send_sem,
    recv_sem,
):
    index = pl.program_id(0)
    seq_index = lax.axis_index("seq")
    partner = seq_index + 1 - 2 * (seq_index % 2)
    half = normed_t.shape[0] // 2

    def crossing(block):
        return pltpu.make_async_remote_copy(
            src_ref=away.at[block % 2],
            dst_ref=arrived.at[block],
            send_sem=send_sem.at[block % 2],
            recv_sem=recv_sem.at[block],
            device_id={"seq": partner},
            device_id_type=MESH,
        )

    @pl.when(index == 0)
    def _():
        barrier = pltpu.get_barrier_semaphore()
        pl.semaphore_signal(barrier, inc=1, device_id={"seq": partner}, device_id_type=MESH)
        pl.semaphore_wait(barrier, 1)
        out_acc[...] = jnp.zeros_like(out_acc)
        grad_acc[...] = jnp.zeros_like(grad_acc)

    @pl.when(index < blocks)
    def _():
        gate_pre = product(normed[...], w_gate[...]) + b_gate[...]
        up_pre = product(normed[...], w_up[...]) + b_up[...]
        grad_hidden = product(top[...], w_down[...])
        sigmoid_gate = jax.nn.sigmoid(gate_pre)
        silu_gate = gate_pre * sigmoid_gate
        hidden = (silu_gate * up_pre).astype(jnp.bfloat16)
        grad_up = (grad_hidden * silu_gate).astype(jnp.bfloat16)
        grad_gate = (
            grad_hidden * up_pre * sigmoid_gate * (1.0 + gate_pre * (1.0 - sigmoid_gate))
        ).astype(jnp.bfloat16)
        bias_grads[0:1, :] = jnp.sum(grad_gate.astype(jnp.float32), axis=0, keepdims=True)
        bias_grads[1:2, :] = jnp.sum(grad_up.astype(jnp.float32), axis=0, keepdims=True)
        out_acc[...] += product_t(hidden, w_down[...])
        grad_acc[...] += product_t(grad_gate, w_gate[...]) + product_t(grad_up, w_up[...])

        @pl.when(index >= 2)
        def _():
            crossing(index - 2).wait_send()

        slot = index % 2
        away[slot, 0] = product(normed_t[half:, :], grad_gate).astype(jnp.bfloat16)
        away[slot, 1] = product(normed_t[half:, :], grad_up).astype(jnp.bfloat16)
        away[slot, 2] = product(top_t[half:, :], hidden).astype(jnp.bfloat16)
        crossing(index).start()
        mine[slot, 0] = product(normed_t[:half, :], grad_gate)
        mine[slot, 1] = product(normed_t[:half, :], grad_up)
        mine[slot, 2] = product(top_t[:half, :], hidden)

    @pl.when(index >= 1)
    def _():
        crossing(index - 1).wait_recv()
        prior = index - 1
        sums[...] = (mine[prior % 2] + arrived[prior].astype(jnp.float32)).astype(jnp.bfloat16)

    @pl.when(index == blocks)
    def _():
        crossing(blocks - 2).wait_send()
        crossing(blocks - 1).wait_send()
        out[...] = out_acc[...].astype(jnp.bfloat16)
        grad_normed[...] = grad_acc[...].astype(jnp.bfloat16)


def glu_layer(normed, normed_t, top, top_t, weights, gate_bias, up_bias):
    rows, width = normed.shape
    hidden_width = gate_bias.shape[0]
    blocks = hidden_width // BLOCK
    half = width // 2
    whole = pl.BlockSpec((rows, width), lambda i: (0, 0))
    whole_t = pl.BlockSpec((width, rows), lambda i: (0, 0))

    def weight_spec(which):
        return pl.BlockSpec(
            (width, BLOCK), lambda i: (0, which * blocks + jnp.minimum(i, blocks - 1))
        )

    bias_spec = pl.BlockSpec((1, BLOCK), lambda i: (0, jnp.minimum(i, blocks - 1)))
    work = rows * width * hidden_width
    return pl.pallas_call(
        functools.partial(glu_kernel, blocks),
        grid=(blocks + 1,),
        in_specs=[
            whole,
            whole_t,
            whole,
            whole_t,
            weight_spec(0),
            weight_spec(1),
            weight_spec(2),
            bias_spec,
            bias_spec,
        ],
        out_specs=[
            whole,
            whole,
            pl.BlockSpec((3, half, BLOCK), lambda i: (0, 0, jnp.maximum(i - 1, 0))),
            pl.BlockSpec((2, BLOCK), lambda i: (0, jnp.minimum(i, blocks - 1))),
        ],
        out_shape=[
            jax.ShapeDtypeStruct((rows, width), jnp.bfloat16),
            jax.ShapeDtypeStruct((rows, width), jnp.bfloat16),
            jax.ShapeDtypeStruct((3, half, hidden_width), jnp.bfloat16),
            jax.ShapeDtypeStruct((2, hidden_width), jnp.float32),
        ],
        scratch_shapes=[
            pltpu.VMEM((rows, width), jnp.float32),
            pltpu.VMEM((rows, width), jnp.float32),
            pltpu.VMEM((2, 3, half, BLOCK), jnp.float32),
            pltpu.VMEM((2, 3, half, BLOCK), jnp.bfloat16),
            pltpu.VMEM((blocks, 3, half, BLOCK), jnp.bfloat16),
            pltpu.SemaphoreType.DMA((2,)),
            pltpu.SemaphoreType.DMA((blocks,)),
        ],
        compiler_params=pltpu.CompilerParams(
            collective_id=1, has_side_effects=True, vmem_limit_bytes=VMEM_BYTES
        ),
        cost_estimate=pl.CostEstimate(
            flops=18 * work, bytes_accessed=12 * width * hidden_width, transcendentals=rows * hidden_width
        ),
        name="glu_layer",
    )(
        normed,
        normed_t,
        top,
        top_t,
        weights,
        weights,
        weights,
        gate_bias[None],
        up_bias[None],
    )


def xor_place(index, bit):
    return index + bit * (1 - 2 * (index // bit % 2))


def ring_neighbours(seq_index, seq_count):
    chips = seq_count // 2
    chip, core = seq_index // 2, seq_index % 2
    odd = chip % 2
    place = (1 - odd) * (chip // 2) + odd * (chips - 1 - chip // 2)
    found = []
    for step in (1, chips - 1):
        there = (place + step) % chips
        upper = there // (chips // 2)
        found.append(2 * ((1 - upper) * 2 * there + upper * (2 * (chips - 1 - there) + 1)) + core)
    return found


class ChipRing:
    def __init__(self, seq_count, pieces, sends, lands, send_sem, recv_sem):
        self.chips = seq_count // 2
        self.far = self.chips // 2
        self.pieces = pieces
        self.sends, self.lands = sends, lands
        self.send_sem, self.recv_sem = send_sem, recv_sem
        self.sides = ring_neighbours(lax.axis_index("seq"), seq_count)
        self.greeted = [{"seq": side} for side in self.sides]
        half, width = pieces[0].shape
        self.seg = half // self.chips
        self.width, self.mid = width, width // 2

    def copy(self, piece, side, hop):
        mid, seg = self.mid, self.seg
        if hop == 0:
            source = self.pieces[piece].at[pl.ds(self.far * seg, seg), pl.ds(side * mid, mid)]
            target = self.lands.at[piece, side, 0, :, pl.ds(0, mid)]
        else:
            source = self.sends.at[piece, side, hop - 1]
            target = self.lands.at[piece, side, hop]
        return pltpu.make_async_remote_copy(
            src_ref=source,
            dst_ref=target,
            send_sem=self.send_sem.at[piece, side, hop],
            recv_sem=self.recv_sem.at[piece, side, hop],
            device_id={"seq": self.sides[side]},
            device_id_type=MESH,
        )

    def start(self, piece):
        for side in range(2):
            self.copy(piece, side, 0).start()

    def advance(self, piece, hop):
        mid, seg = self.mid, self.seg
        for side in range(2):
            near = self.far - hop if side == 0 else self.far + hop
            term = self.pieces[piece][near * seg : (near + 1) * seg, :].astype(jnp.float32)
            self.copy(piece, side, hop - 1).wait_recv()
            if hop == 1:
                land = self.lands[piece, side, 0, :, :mid].astype(jnp.float32)
                low = term[:, :mid] + land if side == 0 else term[:, :mid]
                high = term[:, mid:] if side == 0 else term[:, mid:] + land
                self.sends[piece, side, 0, :, :mid] = low.astype(jnp.bfloat16)
                self.sends[piece, side, 0, :, mid:] = high.astype(jnp.bfloat16)
            else:
                land = self.lands[piece, side, hop - 1].astype(jnp.float32)
                self.sends[piece, side, hop - 1] = (term + land).astype(jnp.bfloat16)
            self.copy(piece, side, hop).start()

    def total(self, piece):
        total = self.pieces[piece][: self.seg, :].astype(jnp.float32)
        for side in range(2):
            self.copy(piece, side, self.far - 1).wait_recv()
            total = total + self.lands[piece, side, self.far - 1].astype(jnp.float32)
        return total

    def close(self):
        for piece in range(len(self.pieces)):
            for side in range(2):
                for hop in range(self.far):
                    self.copy(piece, side, hop).wait_send()


def ring_scratch(seq_count, pieces, seg, width):
    far = seq_count // 4
    return [
        pltpu.VMEM((pieces, 2, far - 1, seg, width), jnp.bfloat16),
        pltpu.VMEM((pieces, 2, far, seg, width), jnp.bfloat16),
        pltpu.SemaphoreType.DMA((pieces, 2, far)),
        pltpu.SemaphoreType.DMA((pieces, 2, far)),
    ]


def greet(devices):
    barrier = pltpu.get_barrier_semaphore()
    for device in devices:
        pl.semaphore_signal(barrier, inc=1, device_id=device, device_id_type=MESH)
    pl.semaphore_wait(barrier, len(devices))


def tail_kernel(seq_count, head_count, ready_count, made_count, *refs):
    ready = refs[:ready_count]
    rows_t, columns, small, out, small_out = refs[ready_count : ready_count + 5]
    (
        mine,
        away,
        arrived,
        small_send,
        small_land,
        core_send,
        core_recv,
        step_send,
        step_recv,
        *ring_refs,
    ) = refs[ready_count + 5 :]
    half = rows_t.shape[0] // 2
    width = columns.shape[1] // made_count
    pieces = [*ready, *(mine.at[made] for made in range(made_count))]
    ring = ChipRing(seq_count, pieces, *ring_refs)
    seq_index = lax.axis_index("seq")
    head_index = lax.axis_index("head")
    partners = []
    bit = 1
    while bit < seq_count:
        partners.append({"seq": xor_place(seq_index, bit)})
        bit *= 2
    seq_steps = len(partners)
    bit = 1
    while bit < head_count:
        partners.append({"head": xor_place(head_index, bit)})
        bit *= 2
    greet(ring.greeted + partners)

    def core_copy(made):
        return pltpu.make_async_remote_copy(
            src_ref=away.at[made],
            dst_ref=arrived.at[made],
            send_sem=core_send.at[made],
            recv_sem=core_recv.at[made],
            device_id=partners[0],
            device_id_type=MESH,
        )

    def step_copy(step):
        rows = small.shape[0] if step < seq_steps else small.shape[0] // 2
        return pltpu.make_async_remote_copy(
            src_ref=small_send.at[step, pl.ds(0, rows)],
            dst_ref=small_land.at[step, pl.ds(0, rows)],
            send_sem=step_send.at[step],
            recv_sem=step_recv.at[step],
            device_id=partners[step],
            device_id_type=MESH,
        )

    def step_on(step):
        late = small.shape[0] // 2
        if step == 0:
            small_send[0] = small[...]
        else:
            step_copy(step - 1).wait_recv()
            if step <= seq_steps:
                total = small_send[step - 1] + small_land[step - 1]
                if step == seq_steps:
                    small_out[late:, :] = total[late:]
                if step < len(partners):
                    small_send[step] = total
                else:
                    small_out[:late, :] = total[:late]
            else:
                total = small_send[step - 1, :late] + small_land[step - 1, :late]
                if step < len(partners):
                    small_send[step, :late] = total
                else:
                    small_out[:late, :] = total
        if step < len(partners):
            step_copy(step).start()

    for piece in range(ready_count):
        ring.start(piece)
    step_on(0)
    for made in range(made_count):
        cols = slice(made * width, (made + 1) * width)
        away[made] = product(rows_t[half:, :], columns[:, cols]).astype(jnp.bfloat16)
        core_copy(made).start()
    for made in range(made_count):
        cols = slice(made * width, (made + 1) * width)
        term = product(rows_t[:half, :], columns[:, cols])
        core_copy(made).wait_recv()
        mine[made] = (term + arrived[made].astype(jnp.float32)).astype(jnp.bfloat16)
        ring.start(ready_count + made)
    done = 1
    for hop in range(1, ring.far):
        for piece in range(len(pieces)):
            ring.advance(piece, hop)
        while done <= len(partners) * hop // (ring.far - 1):
            step_on(done)
            done += 1
    for piece in range(len(pieces)):
        out[:, piece * width : (piece + 1) * width] = ring.total(piece)
    for made in range(made_count):
        core_copy(made).wait_send()
    ring.close()
    for step in range(len(partners)):
        step_copy(step).wait_send()


def tail_sums(ready, rows_t, columns, small, seq_count):
    head_count = lax.axis_size("head")
    chips = seq_count // 2
    half = rows_t.shape[0] // 2
    seg = half // chips
    width = TAIL_WIDTH
    made_count = columns.shape[1] // width
    pieces = len(ready) + made_count
    steps = (seq_count - 1).bit_length() + (head_count - 1).bit_length()
    bf = jnp.bfloat16
    return pl.pallas_call(
        functools.partial(tail_kernel, seq_count, head_count, len(ready), made_count),
        in_specs=[pl.BlockSpec(memory_space=pltpu.VMEM)] * (len(ready) + 3),
        out_specs=[pl.BlockSpec(memory_space=pltpu.VMEM)] * 2,
        out_shape=[
            jax.ShapeDtypeStruct((seg, pieces * width), jnp.float32),
            jax.ShapeDtypeStruct(small.shape, jnp.float32),
        ],
        scratch_shapes=[
            pltpu.VMEM((made_count, half, width), bf),
            pltpu.VMEM((made_count, half, width), bf),
            pltpu.VMEM((made_count, half, width), bf),
            pltpu.VMEM((steps, *small.shape), jnp.float32),
            pltpu.VMEM((steps, *small.shape), jnp.float32),
            pltpu.SemaphoreType.DMA((made_count,)),
            pltpu.SemaphoreType.DMA((made_count,)),
            pltpu.SemaphoreType.DMA((steps,)),
            pltpu.SemaphoreType.DMA((steps,)),
            *ring_scratch(seq_count, pieces, seg, width),
        ],
        compiler_params=pltpu.CompilerParams(
            collective_id=2, has_side_effects=True, vmem_limit_bytes=VMEM_BYTES
        ),
        cost_estimate=pl.CostEstimate(
            flops=2 * rows_t.shape[0] * rows_t.shape[1] * columns.shape[1],
            bytes_accessed=16 * pieces * half * width,
            transcendentals=0,
        ),
        name="tail_sums",
    )(*ready, rows_t, columns, small)


def turned_back(values, tables):
    shift = ROT // 2
    return (
        values * tables[0]
        + pltpu.roll(values, LANES - shift, 1) * tables[1]
        - pltpu.roll(values, shift, 1) * tables[2]
    )


def self_back_kernel(seq_count, pairs, score_scale, ready_count, *refs):
    (
        query,
        keys,
        values,
        stamp_key,
        stamp_value,
        grad_out,
        logs,
        key_ids,
        query_ids,
        query_slots,
        tables,
    ) = refs[:11]
    ready = refs[11 : 11 + ready_count]
    out, shares = refs[11 + ready_count : 13 + ready_count]
    (
        bias,
        acc,
        own,
        halo,
        halo_land,
        halo_send_sem,
        halo_recv_sem,
        *ring_refs,
    ) = refs[13 + ready_count :]
    pair = pl.program_id(0)
    rows = query.shape[0]
    slots = stamp_key.shape[0]
    span = QUERY_BLOCK + 2 * HALF
    seq_index = lax.axis_index("seq")
    before = (seq_index + seq_count - 1) % seq_count
    behind = (seq_index + 1) % seq_count
    ring = ChipRing(seq_count, list(ready), *ring_refs) if ready else None
    hops = ring.far if ready else 1

    def halo_copy(which, side):
        return pltpu.make_async_remote_copy(
            src_ref=halo.at[which, side],
            dst_ref=halo_land.at[which, side],
            send_sem=halo_send_sem.at[which, side],
            recv_sem=halo_recv_sem.at[which, side],
            device_id={"seq": before if side == 0 else behind},
            device_id_type=MESH,
        )

    @pl.when(pair == 0)
    def _():
        greet((ring.greeted if ready else []) + [{"seq": before}, {"seq": behind}])
        for piece in range(ready_count):
            ring.start(piece)
        for block in range(rows // QUERY_BLOCK):
            start = block * QUERY_BLOCK
            asked = query_ids[:, start : start + QUERY_BLOCK]
            key_row = lax.broadcasted_iota(jnp.int32, (span, QUERY_BLOCK), 0)
            query_row = lax.broadcasted_iota(jnp.int32, (span, QUERY_BLOCK), 1)
            away = key_row - HALF - query_row
            seen = (key_ids[start : start + span, :] == asked) & (jnp.abs(away) <= HALF)
            bias[block, :span, :] = jnp.where(seen, 0.0, NEG)
            slot_row = lax.broadcasted_iota(jnp.int32, (slots, QUERY_BLOCK), 0)
            bias[block, span:, :] = jnp.where(
                slot_row == query_slots[:, start : start + QUERY_BLOCK], 0.0, NEG
            )

    for hop in range(1, hops):

        @pl.when(pair == hop)
        def _():
            for piece in range(ready_count):
                ring.advance(piece, hop)

    @pl.when(pair < pairs)
    def _():
        acc[...] = jnp.zeros_like(acc)
        lane = lax.broadcasted_iota(jnp.int32, (1, LANES), 1)
        stamp_k, stamp_v = stamp_key[...], stamp_value[...]
        grad_queries = []
        for block in range(rows // QUERY_BLOCK):
            start = block * QUERY_BLOCK
            near_k = jnp.concatenate([keys[0, start : start + span, :], stamp_k], axis=0)
            near_v = jnp.concatenate([values[0, start : start + span, :], stamp_v], axis=0)
            block_q = query[start : start + QUERY_BLOCK, :]
            block_g = grad_out[start : start + QUERY_BLOCK, :]
            grad_q = jnp.zeros((QUERY_BLOCK, LANES), jnp.float32)
            grad_k = jnp.zeros((span + slots, LANES), jnp.float32)
            grad_v = jnp.zeros((span + slots, LANES), jnp.float32)
            for head in range(LANES // HD):
                here = lane // HD == head
                head_q = jnp.where(here, block_q, jnp.zeros_like(block_q))
                head_g = jnp.where(here, block_g, jnp.zeros_like(block_g))
                head_k = jnp.where(here, near_k, jnp.zeros_like(near_k))
                scores = product_t(near_k, head_q) * score_scale + bias[block]
                probs = jnp.exp(scores - logs[0, head : head + 1, start : start + QUERY_BLOCK])
                grad_p = product_t(near_v, head_g)
                dot = jnp.sum(probs * grad_p, axis=0, keepdims=True)
                grad_s = (probs * (grad_p - dot)).astype(jnp.bfloat16)
                grad_k = grad_k + product(grad_s, head_q)
                grad_v = grad_v + product(probs.astype(jnp.bfloat16), head_g)
                grad_q = grad_q + product_tn(grad_s, head_k)
            grad_queries.append(grad_q)
            acc[0, start : start + span, :] += grad_k[:span]
            acc[1, start : start + span, :] += grad_v[:span]
            acc[0, 2 * HALF + rows :, :] += grad_k[span:]
            acc[1, 2 * HALF + rows :, :] += grad_v[span:]
        column = pl.multiple_of(pair * LANES, LANES)
        grad_q = jnp.concatenate(grad_queries, axis=0) * score_scale
        out[:rows, pl.ds(column, LANES)] = turned_back(grad_q, tables).astype(jnp.bfloat16)
        out[rows:, pl.ds(column, LANES)] = jnp.zeros((slots, LANES), jnp.bfloat16)
        for which in range(2):
            scale = score_scale if which == 0 else 1.0
            shift = (which + 1) * pairs * LANES
            halo[pair, 0, which] = (acc[which, :HALF, :] * scale).astype(jnp.bfloat16)
            halo[pair, 1, which] = (acc[which, HALF + rows : 2 * HALF + rows, :] * scale).astype(
                jnp.bfloat16
            )
            own[pair, which] = acc[which, HALF : HALF + rows, :] * scale
            out[rows:, pl.ds(column + shift, LANES)] = (
                acc[which, 2 * HALF + rows :, :] * scale
            ).astype(jnp.bfloat16)
        halo_copy(pair, 0).start()
        halo_copy(pair, 1).start()

    @pl.when(pair == pairs)
    def _():
        for which in range(pairs):
            halo_copy(which, 0).wait_recv()
            halo_copy(which, 1).wait_recv()
            own[which, :, rows - HALF :, :] += halo_land[which, 0].astype(jnp.float32)
            own[which, :, :HALF, :] += halo_land[which, 1].astype(jnp.float32)
            column = (pairs + which) * LANES
            out[:rows, column : column + LANES] = turned_back(own[which, 0], tables).astype(
                jnp.bfloat16
            )
            column = (2 * pairs + which) * LANES
            out[:rows, column : column + LANES] = own[which, 1].astype(jnp.bfloat16)
        if not ready:
            shares[...] = jnp.zeros_like(shares)
        for piece in range(ready_count):
            shares[:, piece * ring.width : (piece + 1) * ring.width] = ring.total(piece)
        if ready:
            ring.close()
        for which in range(pairs):
            halo_copy(which, 0).wait_send()
            halo_copy(which, 1).wait_send()


def self_back(
    query, near, stamps, grad_out, logs, key_ids, query_ids, query_slots, tables, ready, score_scale, seq_count
):
    rows, part = query.shape
    slots = stamps.shape[0]
    pairs = part // LANES
    window = near.shape[1]
    half, width = ready[0].shape if ready else (8 * seq_count // 2, LANES)
    seg = half // (seq_count // 2)
    share_width = max(len(ready), 1) * width
    span = QUERY_BLOCK + 2 * HALF
    blocks = rows // QUERY_BLOCK
    last = pairs - 1

    def at(first, shape, lead=()):
        return pl.BlockSpec(shape, lambda i: (*lead, 0, first + jnp.minimum(i, last)))

    def whole(shape):
        return pl.BlockSpec(shape, lambda i: (0,) * len(shape), pipeline_mode=pl.Buffered(1))

    return pl.pallas_call(
        functools.partial(self_back_kernel, seq_count, pairs, score_scale, len(ready)),
        grid=(pairs + 1,),
        in_specs=[
            at(0, (rows, LANES)),
            at(0, (1, window, LANES), (0,)),
            at(0, (1, window, LANES), (1,)),
            at(pairs, (slots, LANES)),
            at(2 * pairs, (slots, LANES)),
            at(0, (rows, LANES)),
            pl.BlockSpec((1, LANES // HD, rows), lambda i: (jnp.minimum(i, last), 0, 0)),
            whole((window, 1)),
            whole((1, rows)),
            whole((1, rows)),
            whole((3, rows, LANES)),
            *(whole((half, width)) for _ in ready),
        ],
        out_specs=[
            pl.BlockSpec((rows + slots, 3 * part), lambda i: (0, 0)),
            pl.BlockSpec((seg, share_width), lambda i: (0, 0)),
        ],
        out_shape=[
            jax.ShapeDtypeStruct((rows + slots, 3 * part), jnp.bfloat16),
            jax.ShapeDtypeStruct((seg, share_width), jnp.float32),
        ],
        scratch_shapes=[
            pltpu.VMEM((blocks, span + slots, QUERY_BLOCK), jnp.float32),
            pltpu.VMEM((2, window + slots, LANES), jnp.float32),
            pltpu.VMEM((pairs, 2, rows, LANES), jnp.float32),
            pltpu.VMEM((pairs, 2, 2, HALF, LANES), jnp.bfloat16),
            pltpu.VMEM((pairs, 2, 2, HALF, LANES), jnp.bfloat16),
            pltpu.SemaphoreType.DMA((pairs, 2)),
            pltpu.SemaphoreType.DMA((pairs, 2)),
            *(ring_scratch(seq_count, len(ready), seg, width) if ready else []),
        ],
        compiler_params=pltpu.CompilerParams(
            collective_id=3, has_side_effects=True, vmem_limit_bytes=VMEM_BYTES
        ),
        cost_estimate=pl.CostEstimate(
            flops=10 * rows * window * part,
            bytes_accessed=16 * len(ready) * half * width,
            transcendentals=rows * window * part // HD,
        ),
        name="self_back",
    )(
        query,
        near,
        near,
        stamps,
        stamps,
        grad_out,
        logs.reshape(pairs, LANES // HD, rows),
        key_ids[:, None],
        query_ids[None],
        query_slots[None],
        tables,
        *ready,
    )


def tail_or_rings(ready, rows_t, columns, small, seq_count):
    if rows_t.shape[0] // seq_count % 16 == 0:
        return tail_sums(ready, rows_t, columns, small, seq_count)
    made = core_sum(rows_t, columns, seq_count)
    ring = Ring(side_by_side([*ready, made], seq_count // 2), seq_count)
    late = small.shape[0] // 2
    small = all_sum(small, ("seq",))
    small = jnp.concatenate([all_sum(small[:late], ("head",)), small[late:]], axis=0)
    return ring.finish(), small


def head_total(partial_sum):
    low = partial_sum
    if low.dtype != jnp.bfloat16:
        low = lax.optimization_barrier(partial_sum.astype(jnp.bfloat16))
    count = lax.axis_size("head")
    total = low.astype(jnp.float32)
    for step in range(1, count):
        pairs = [(index, (index + step) % count) for index in range(count)]
        total = total + lax.ppermute(low, "head", pairs).astype(jnp.float32)
    return total


def low_gather(block):
    return lax.all_gather(block.astype(jnp.bfloat16), "seq", axis=0, tiled=True)


def per_device(
    frames,
    time_token,
    prompt,
    clip_ids,
    norm1_gain,
    norm2_gain,
    norm3_gain,
    query_weight,
    key_weight,
    value_weight,
    out_weight,
    cross_query,
    cross_key,
    cross_value,
    cross_out,
    gate_weight,
    up_weight,
    down_weight,
    gate_bias,
    up_bias,
    down_bias,
    out_grad,
):
    local_rows, width = frames.shape
    clip_total = time_token.shape[0]
    ctx_tokens = prompt.shape[1]
    slot_count = local_rows // (2 * HALF) + 2
    seq_count = lax.axis_size("seq")
    seq_index = lax.axis_index("seq")
    head_index = lax.axis_index("head")
    first_row = seq_index * local_rows
    score_scale = HD ** (-0.5)
    part = query_weight.shape[1]
    hidden_width = gate_weight.shape[1]
    gain_rows = norm1_gain.shape[0]
    ctx_rows = cross_key.shape[0]
    ctx_width = prompt.shape[2]
    head_count = part // HD
    chips = seq_count // 2
    bias_rows = 2 * hidden_width // width
    small_rows = -(-max(clip_total + 1, bias_rows + 3) // 8) * 8
    order = owner_matrix(width, seq_index, seq_count)

    def ordered(matrix, by=order):
        return product_t(by, matrix).astype(jnp.bfloat16)

    vectors = jnp.stack([norm1_gain, norm2_gain, norm3_gain, down_bias], axis=1)
    vectors = jnp.pad(vectors, ((0, 0), (0, LANES - 4)))
    ctx_pair = jnp.concatenate([cross_key, cross_value], axis=0)
    attn_local = jnp.concatenate(
        [query_weight, key_weight, value_weight, out_weight, cross_query, cross_out, ctx_pair, vectors],
        axis=1,
    )
    attn_weights = low_gather(attn_local)
    glu_weights = low_gather(jnp.concatenate([gate_weight, up_weight, down_weight], axis=1))
    w_qkv = attn_weights[:, : 3 * part]
    w_out = attn_weights[:, 3 * part : 4 * part]
    c_query = attn_weights[:, 4 * part : 5 * part]
    c_out = attn_weights[:, 5 * part : 6 * part]
    ctx_weights = attn_weights[:, 6 * part : 7 * part].reshape(seq_count, 2, ctx_rows, part)
    c_key = ctx_weights[:, 0].reshape(ctx_width, part)
    c_value = ctx_weights[:, 1].reshape(ctx_width, part)
    rows_of = attn_weights[:, 7 * part : 7 * part + 8].astype(jnp.float32).T
    gain_one_f, gain_two_f, gain_three_f, bias_f = rows_of[0], rows_of[1], rows_of[2], rows_of[3]

    positions = first_row + jnp.arange(local_rows, dtype=jnp.int32)
    cos_table, sin_table = angles(positions)
    padded_ids = jnp.pad(clip_ids, (HALF, HALF), constant_values=-1)
    own_ids = lax.dynamic_slice_in_dim(clip_ids, first_row, local_rows)
    near_ids = lax.dynamic_slice_in_dim(padded_ids, first_row, local_rows + 2 * HALF)
    base_clip = jnp.minimum(own_ids[0], clip_total - slot_count)
    own_slot = own_ids - base_clip
    slot_range = jnp.arange(slot_count, dtype=jnp.int32)
    pad_rows = -slot_count % 16
    stamp_end = local_rows + slot_count

    stamp_rows = lax.dynamic_slice_in_dim(time_token, base_clip, slot_count, 0)
    source = jnp.concatenate(
        [frames, jnp.pad(stamp_rows, ((0, pad_rows), (0, 0)))], axis=0
    ).astype(jnp.float32)
    normed_out, normal_one, inverse_one = layer_norm_parts(source, gain_one_f)
    normed_one = normed_out.astype(jnp.bfloat16)
    frames_f = source[:local_rows]
    qkv = product(normed_one, w_qkv)
    query_rows = rotate(qkv[:local_rows, :part], cos_table, sin_table).astype(jnp.bfloat16)
    key_rows = rotate(qkv[:local_rows, part : 2 * part], cos_table, sin_table).astype(jnp.bfloat16)
    value_rows = qkv[:local_rows, 2 * part :].astype(jnp.bfloat16)
    near = extended(jnp.stack([key_rows, value_rows]), (("seq", 1),), HALF)
    window = local_rows + 2 * HALF
    near_key_h = near[0].reshape(window, head_count, HD)
    near_value_h = near[1].reshape(window, head_count, HD)
    query_h = query_rows.reshape(local_rows, head_count, HD)
    stamps = qkv[local_rows:].astype(jnp.bfloat16)
    stamp_key_h = stamps[:slot_count, part : 2 * part].reshape(slot_count, head_count, HD)
    stamp_value_h = stamps[:slot_count, 2 * part :].reshape(slot_count, head_count, HD)

    query_pos = jnp.arange(local_rows, dtype=jnp.int32)
    key_pos = jnp.arange(window, dtype=jnp.int32) - HALF
    visible = (own_ids[:, None] == near_ids[None, :]) & (
        jnp.abs(query_pos[:, None] - key_pos[None, :]) <= HALF
    )
    own_stamp = own_slot[:, None] == slot_range[None, :]
    self_keys = [(near_key_h, near_value_h, visible), (stamp_key_h, stamp_value_h, own_stamp)]
    attn_mix_h, self_logs = attend_forward(query_h, self_keys, score_scale)
    attn_mixed = attn_mix_h.reshape(local_rows, part).astype(jnp.bfloat16)
    h_one = frames_f + head_total(product_t(attn_mixed, w_out))
    middle_out, normal_two, inverse_two = layer_norm_parts(h_one, gain_two_f)
    normed_two = middle_out.astype(jnp.bfloat16)
    cross_h = product(normed_two, c_query).astype(jnp.bfloat16).reshape(local_rows, head_count, HD)
    context_rows = lax.dynamic_slice_in_dim(prompt, base_clip, slot_count, 0).reshape(
        slot_count * ctx_tokens, ctx_width
    )
    ctx_key_h = product(context_rows, c_key).astype(jnp.bfloat16)
    ctx_key_h = ctx_key_h.reshape(slot_count * ctx_tokens, head_count, HD)
    ctx_value_h = product(context_rows, c_value).astype(jnp.bfloat16)
    ctx_value_h = ctx_value_h.reshape(slot_count * ctx_tokens, head_count, HD)
    key_slot = jnp.arange(slot_count * ctx_tokens, dtype=jnp.int32) // ctx_tokens
    cross_keys = [(ctx_key_h, ctx_value_h, own_slot[:, None] == key_slot[None, :])]
    cross_mix_h, cross_logs = attend_forward(cross_h, cross_keys, score_scale)
    cross_mixed = cross_mix_h.reshape(local_rows, part).astype(jnp.bfloat16)
    h_two = h_one + head_total(product_t(cross_mixed, c_out))
    third_out, normal_three, inverse_three = layer_norm_parts(h_two, gain_three_f)
    normed_three = third_out.astype(jnp.bfloat16)

    glu_out, grad_normed_low, glu_sums, bias_local = glu_layer(
        normed_three,
        ordered(normed_three),
        out_grad,
        ordered(out_grad),
        glu_weights,
        gate_bias,
        up_bias,
    )
    grad_normed_three = head_total(grad_normed_low)
    grad_normed_three, glu_out = lax.optimization_barrier((grad_normed_three, glu_out))
    result = (h_two + head_total(glu_out) + bias_f).astype(jnp.bfloat16)
    glu_ring = Ring(
        lambda near: glu_sums[:, near * gain_rows : (near + 1) * gain_rows], seq_count
    )
    grad_normed_three = glu_ring.after(grad_normed_three)
    glu_ring.step()
    grad_top = out_grad.astype(jnp.float32)
    gain_three_term = jnp.sum(grad_normed_three * normal_three, axis=0)
    down_bias_term = jnp.sum(grad_top, axis=0)

    grad_h_two = grad_top + norm_back(grad_normed_three, normal_three, inverse_three, gain_three_f)
    grad_two_low = grad_h_two.astype(jnp.bfloat16)
    grad_cross_h = product(grad_two_low, c_out).astype(jnp.bfloat16)
    grad_cross_h = grad_cross_h.reshape(local_rows, head_count, HD)
    cross_out_sum = core_sum(ordered(grad_two_low), cross_mixed, seq_count)
    grad_cross_q, ctx_key_grads, ctx_value_grads = attend_backward(
        cross_h, cross_keys, score_scale, cross_logs, grad_cross_h
    )
    grad_cross_query = grad_cross_q.reshape(local_rows, part).astype(jnp.bfloat16)
    ctx_grads = jnp.concatenate(
        [ctx_key_grads[0].reshape(-1, part), ctx_value_grads[0].reshape(-1, part)], axis=1
    ).astype(jnp.bfloat16)
    grad_cross_query = glu_ring.after(grad_cross_query)
    glu_ring.step()
    grad_normed_two = head_total(product_t(grad_cross_query, c_query))
    cross_query_sum = core_sum(ordered(normed_two), grad_cross_query, seq_count)
    ctx_order = owner_matrix(ctx_width, seq_index, seq_count)
    ctx_sum = core_sum(ordered(context_rows, ctx_order), ctx_grads, seq_count)
    gain_two_term = jnp.sum(grad_normed_two * normal_two, axis=0)
    grad_h_one = grad_h_two + norm_back(grad_normed_two, normal_two, inverse_two, gain_two_f)
    grad_one_low = grad_h_one.astype(jnp.bfloat16)
    grad_attn = product(grad_one_low, w_out).astype(jnp.bfloat16)
    out_sum = core_sum(ordered(grad_one_low), attn_mixed, seq_count)
    ctx_sum = jnp.transpose(ctx_sum.reshape(chips, ctx_rows, 2, part), (0, 2, 1, 3))
    ready_sums = [cross_out_sum, cross_query_sum, out_sum, ctx_sum.reshape(width // 2, part)]

    grad_attn = glu_ring.after(grad_attn)
    glu_ring.step()
    if gain_rows % 16 == 0:
        early_sums, ready_sums = ready_sums[:SELF_PIECES], ready_sums[SELF_PIECES:]
    else:
        early_sums = []
    ones = jnp.ones((local_rows, HD - ROT), jnp.float32)
    flat = jnp.zeros((local_rows, ROT // 2), jnp.float32)
    low_side = [sin_table, flat, 0 * ones]
    high_side = [flat, sin_table, 0 * ones]
    tables = jnp.stack(
        [
            jnp.tile(jnp.concatenate(each, axis=1), (1, LANES // HD))
            for each in ([cos_table, cos_table, ones], low_side, high_side)
        ]
    )
    grad_qkv, early_share = self_back(
        query_rows,
        near,
        stamps,
        grad_attn,
        self_logs,
        near_ids,
        own_ids,
        own_slot,
        tables,
        early_sums,
        score_scale,
        seq_count,
    )
    grad_qkv = glu_ring.after(grad_qkv)
    glu_share = glu_ring.finish()
    grad_normed_all = product_t(grad_qkv, w_qkv)
    grad_normed_one = head_total(grad_normed_all[:local_rows])
    gain_one_term = jnp.sum(grad_normed_all[:local_rows] * normal_one[:local_rows], axis=0)
    frames_grad = (
        grad_h_one
        + norm_back(grad_normed_one, normal_one[:local_rows], inverse_one[:local_rows], gain_one_f)
    ).astype(jnp.bfloat16)

    stamp_full = lax.dynamic_update_slice_in_dim(
        jnp.zeros((clip_total, width), jnp.float32), grad_normed_all[local_rows:stamp_end], base_clip, 0
    )
    small = jnp.concatenate(
        [
            jnp.pad(
                jnp.concatenate([stamp_full, gain_one_term[None]], axis=0),
                ((0, small_rows - clip_total - 1), (0, 0)),
            ),
            jnp.pad(
                jnp.concatenate(
                    [
                        bias_local.reshape(-1, width),
                        jnp.stack([gain_two_term, gain_three_term, down_bias_term]),
                    ],
                    axis=0,
                ),
                ((0, small_rows - bias_rows - 3), (0, 0)),
            ),
        ],
        axis=0,
    )
    shares, small = tail_or_rings(ready_sums, ordered(normed_one), grad_qkv, small, seq_count)
    if gain_rows % 16 == 0:
        shares = jnp.concatenate([early_share, shares], axis=1)
    cross_out_share = shares[:, :part]
    cross_query_share = shares[:, part : 2 * part]
    out_share = shares[:, 2 * part : 3 * part]
    ctx_share = shares[:, 3 * part : 4 * part]
    qkv_share = shares[:, 4 * part :]
    late = small[: clip_total + 1]
    early = small[small_rows : small_rows + bias_rows + 3]
    stamp_sum = late[:clip_total]
    own_bias = early[:-3].reshape(2, hidden_width)
    every_out, every_normal, every_inverse = layer_norm_parts(
        time_token.astype(jnp.float32), gain_one_f
    )
    time_grad = norm_back(stamp_sum, every_normal, every_inverse, gain_one_f)
    time_gain = jnp.sum(stamp_sum * every_normal, axis=0)
    gains_own = lax.dynamic_slice_in_dim(
        jnp.concatenate([late[clip_total:] + time_gain[None], early[-3:]], axis=0),
        seq_index * gain_rows,
        gain_rows,
        1,
    )
    return (
        result,
        frames_grad,
        time_grad,
        gains_own[0],
        gains_own[1],
        gains_own[2],
        qkv_share[:, :part],
        qkv_share[:, part : 2 * part],
        qkv_share[:, 2 * part :],
        out_share,
        cross_query_share,
        ctx_share[:ctx_rows],
        ctx_share[ctx_rows:],
        cross_out_share,
        glu_share[0],
        glu_share[1],
        glu_share[2],
        own_bias[0],
        own_bias[1],
        gains_own[3],
    )


def solution(mesh):
    in_specs = (
        P("seq", None),
        P(),
        P(),
        P(),
        P("seq"),
        P("seq"),
        P("seq"),
        P("seq", "head"),
        P("seq", "head"),
        P("seq", "head"),
        P("seq", "head"),
        P("seq", "head"),
        P("seq", "head"),
        P("seq", "head"),
        P("seq", "head"),
        P("seq", "head"),
        P("seq", "head"),
        P("seq", "head"),
        P("head"),
        P("head"),
        P("seq"),
        P("seq", None),
    )
    out_specs = (
        P("seq", None),
        P("seq", None),
        P(),
        P("seq"),
        P("seq"),
        P("seq"),
        P("seq", "head"),
        P("seq", "head"),
        P("seq", "head"),
        P("seq", "head"),
        P("seq", "head"),
        P("seq", "head"),
        P("seq", "head"),
        P("seq", "head"),
        P("seq", "head"),
        P("seq", "head"),
        P("seq", "head"),
        P("head"),
        P("head"),
        P("seq"),
    )
    return jax.shard_map(
        per_device, mesh=mesh, in_specs=in_specs, out_specs=out_specs, check_vma=False
    )
```

```python
import functools
from functools import reduce

import jax
import jax.numpy as jnp
from jax import lax
from jax.experimental import pallas as pl
from jax.experimental.pallas import tpu as pltpu
from jax.sharding import PartitionSpec as P

HD = 64
ROT = 32
HALF = 256


EPS = 1e-05
NEG = -1e30


def extended(block, sides, width):
    for axis, dim in sides:
        count = lax.axis_size(axis)
        forward = [(i, i + 1) for i in range(count - 1)]
        backward = [(target, source) for source, target in forward]
        low = lax.ppermute(
            lax.slice_in_dim(block, block.shape[dim] - width, None, axis=dim), axis, forward
        )
        high = lax.ppermute(lax.slice_in_dim(block, 0, width, axis=dim), axis, backward)
        block = jnp.concatenate([low, block, high], axis=dim)
    return block


def passed_along(value, axis, steps):
    count = lax.axis_size(axis)
    first, last = (max(0, -steps), min(count, count - steps))
    return lax.ppermute(value, axis, [(source, source + steps) for source in range(first, last)])


def layer_norm_parts(values, gain):
    average = jnp.mean(values, axis=-1, keepdims=True)
    centered = values - average
    spread = jnp.mean(centered * centered, axis=-1, keepdims=True)
    inverse = lax.rsqrt(spread + EPS)
    normal = centered * inverse
    return (normal * gain, normal, inverse)


def norm_back(grad_out, normal, inverse, gain):
    shaped = grad_out * gain
    return (
        shaped
        - jnp.mean(shaped, axis=-1, keepdims=True)
        - normal * jnp.mean(shaped * normal, axis=-1, keepdims=True)
    ) * inverse


def angles(positions):
    ladder = jnp.arange(ROT // 2, dtype=jnp.float32)
    frequency = 10000.0 ** (-2.0 * ladder / ROT)
    phases = positions.astype(jnp.float32)[:, None] * frequency[None, :]
    return (jnp.cos(phases), jnp.sin(phases))


def rotate(values, cos_table, sin_table):
    shaped = values.reshape(values.shape[0], -1, HD)
    rot_half = ROT // 2
    leading = shaped[:, :, :rot_half]
    trailing = shaped[:, :, rot_half:ROT]
    cos_row = cos_table[:, None, :]
    sin_row = sin_table[:, None, :]
    turned = jnp.concatenate(
        [
            leading * cos_row - trailing * sin_row,
            trailing * cos_row + leading * sin_row,
            shaped[:, :, ROT:],
        ],
        axis=-1,
    )
    return turned.reshape(values.shape)


def product(matrix_a, matrix_b):
    return jnp.dot(matrix_a, matrix_b, preferred_element_type=jnp.float32)


def product_t(matrix_a, matrix_b):
    return lax.dot_general(
        matrix_a, matrix_b, (((1,), (1,)), ((), ())), preferred_element_type=jnp.float32
    )


def product_tn(matrix_a, matrix_b):
    return lax.dot_general(
        matrix_a, matrix_b, (((0,), (0,)), ((), ())), preferred_element_type=jnp.float32
    )


def exact_t(matrix_a, matrix_b):
    return lax.dot_general(
        matrix_a,
        matrix_b,
        (((1,), (1,)), ((), ())),
        precision=lax.Precision.HIGHEST,
        preferred_element_type=jnp.float32,
    )


def exact_tn(matrix_a, matrix_b):
    return lax.dot_general(
        matrix_a,
        matrix_b,
        (((0,), (0,)), ((), ())),
        precision=lax.Precision.HIGHEST,
        preferred_element_type=jnp.float32,
    )


def score_parts(query_h, key_parts, score_scale):
    return [
        jnp.where(
            visible[None],
            jnp.einsum("qhd,khd->hqk", query_h, key_h, preferred_element_type=jnp.float32)
            * score_scale,
            NEG,
        )
        for key_h, value_h, visible in key_parts
    ]


def attend_forward(query_h, key_parts, score_scale):
    scores = score_parts(query_h, key_parts, score_scale)
    row_peak = reduce(jnp.maximum, [jnp.max(score_part, axis=-1) for score_part in scores])
    exp_parts = [jnp.exp(score_part - row_peak[:, :, None]) for score_part in scores]
    row_total = reduce(jnp.add, [jnp.sum(exp_part, axis=-1) for exp_part in exp_parts])
    attn_mixed = reduce(
        jnp.add,
        [
            jnp.einsum(
                "hqk,khd->qhd",
                (exp_part / row_total[:, :, None]).astype(jnp.bfloat16),
                key_part[1],
                preferred_element_type=jnp.float32,
            )
            for exp_part, key_part in zip(exp_parts, key_parts)
        ],
    )
    return (attn_mixed, row_peak + jnp.log(row_total))


def attend_backward(query_h, key_parts, score_scale, log_total, grad_h):
    scores = score_parts(query_h, key_parts, score_scale)
    prob_parts = [jnp.exp(score_part - log_total[:, :, None]) for score_part in scores]
    dprob_parts = [
        jnp.einsum("qhd,khd->hqk", grad_h, key_part[1], preferred_element_type=jnp.float32)
        for key_part in key_parts
    ]
    row_dot = reduce(
        jnp.add,
        [
            jnp.sum(prob_part * dprob_part, axis=-1)
            for prob_part, dprob_part in zip(prob_parts, dprob_parts)
        ],
    )
    dscore_parts = [
        (prob_part * (dprob_part - row_dot[:, :, None])).astype(jnp.bfloat16)
        for prob_part, dprob_part in zip(prob_parts, dprob_parts)
    ]
    grad_query = (
        reduce(
            jnp.add,
            [
                jnp.einsum(
                    "hqk,khd->qhd", dscore_part, key_part[0], preferred_element_type=jnp.float32
                )
                for dscore_part, key_part in zip(dscore_parts, key_parts)
            ],
        )
        * score_scale
    )
    grad_keys = [
        jnp.einsum("hqk,qhd->khd", dscore_part, query_h, preferred_element_type=jnp.float32)
        * score_scale
        for dscore_part in dscore_parts
    ]
    grad_values = [
        jnp.einsum(
            "hqk,qhd->khd",
            prob_part.astype(jnp.bfloat16),
            grad_h,
            preferred_element_type=jnp.float32,
        )
        for prob_part in prob_parts
    ]
    return (grad_query, grad_keys, grad_values)


LANES = 128
BLOCK = 256
TAIL_WIDTH = 768
SELF_PIECES = 4
QUERY_BLOCK = 128
VMEM_BYTES = 60 * 1024 * 1024
MESH = pl.DeviceIdType.MESH


def ring_place(chip, chips):
    return jnp.where(chip % 2 == 0, chip // 2, chips - 1 - chip // 2)


def ring_chip(place, chips):
    return jnp.where(2 * place < chips, 2 * place, 2 * (chips - 1 - place) + 1)


def static_chip(place, chips):
    return 2 * place if 2 * place < chips else 2 * (chips - 1 - place) + 1


def ring_pairs(chips, step):
    return [
        (2 * static_chip(place, chips) + core, 2 * static_chip((place + step) % chips, chips) + core)
        for place in range(chips)
        for core in range(2)
    ]


def owner_matrix(width, seq_index, seq_count):
    chips = seq_count // 2
    seg = width // seq_count
    core = seq_index % 2
    place = ring_place(seq_index // 2, chips)
    row = jnp.arange(width, dtype=jnp.int32)
    which = row // (width // 2)
    near = row % (width // 2) // seg
    chip = ring_chip((place + near) % chips, chips)
    source = (2 * chip + jnp.where(which == 0, core, 1 - core)) * seg + row % seg
    return (source[:, None] == row[None, :]).astype(jnp.bfloat16)


def over_core(values, seq_count):
    return lax.ppermute(values, "seq", [(index, index ^ 1) for index in range(seq_count)])


class Ring:
    def __init__(self, term, seq_count, moving=None):
        self.term = term
        self.chips = seq_count // 2
        self.far = self.chips // 2
        self.near = self.far
        self.ahead, self.behind = ring_pairs(self.chips, 1), ring_pairs(self.chips, -1)
        if moving is not None:
            self.near = self.far - 2
            self.send(moving[0], moving[1])
            return
        first = term(self.far)
        self.half = first.shape[-1] // 2
        self.send(first[..., : self.half], first[..., self.half :])

    def send(self, onward, backward):
        self.onward = lax.ppermute(onward.astype(jnp.bfloat16), "seq", self.ahead)
        self.backward = lax.ppermute(backward.astype(jnp.bfloat16), "seq", self.behind)

    def joined(self, near, arrived, low_side):
        term = self.term(near).astype(jnp.float32)
        arrived = arrived.astype(jnp.float32)
        if arrived.shape != term.shape:
            pads = (0, self.half) if low_side else (self.half, 0)
            arrived = jnp.pad(arrived, ((0, 0),) * (term.ndim - 1) + (pads,))
        return term + arrived

    def step(self):
        if self.near == 1:
            return
        self.near -= 1
        self.send(
            self.joined(self.near, self.onward, True),
            self.joined(2 * self.far - self.near, self.backward, False),
        )

    def after(self, value):
        value, self.onward, self.backward = lax.optimization_barrier(
            (value, self.onward, self.backward)
        )
        return value

    def last_terms(self):
        while self.near > 1:
            self.step()
        return [self.term(0), self.onward, self.backward]

    def finish(self):
        return sum(each.astype(jnp.float32) for each in self.last_terms())


def core_sum(rows_t, columns, seq_count):
    half = rows_t.shape[0] // 2
    away = product(rows_t[half:], columns).astype(jnp.bfloat16)
    arrived = over_core(away, seq_count)
    return (product(rows_t[:half], columns) + arrived.astype(jnp.float32)).astype(jnp.bfloat16)


def block_of(matrix, near, chips):
    width = matrix.shape[0] // chips
    return matrix[near * width : (near + 1) * width]


def side_by_side(matrices, chips):
    return lambda near: jnp.concatenate([block_of(each, near, chips) for each in matrices], axis=-1)


def all_sum(values, axes):
    for axis in axes:
        count = lax.axis_size(axis)
        bit = 1
        while bit < count:
            values = values + lax.ppermute(
                values, axis, [(index, index ^ bit) for index in range(count)]
            )
            bit *= 2
    return values


def xor_place(index, bit):
    return index + bit * (1 - 2 * (index // bit % 2))


def chip_near(seq_index, seq_count, step):
    chips = seq_count // 2
    chip = seq_index // 2
    odd = chip % 2
    place = (1 - odd) * (chip // 2) + odd * (chips - 1 - chip // 2)
    there = (place + chips + step) % chips
    upper = there // (chips // 2)
    return (1 - upper) * 2 * there + upper * (2 * (chips - 1 - there) + 1)


def ring_neighbours(seq_index, seq_count):
    return [2 * chip_near(seq_index, seq_count, step) + seq_index % 2 for step in (1, -1)]


def gather_kernel(
    seq_count, bounds, local, out, token, own_sem, ring_send, ring_recv, core_send, core_recv
):
    token[...] = jnp.zeros_like(token)
    far = seq_count // 4
    seq_index = lax.axis_index("seq")
    core = seq_index % 2
    partner = {"seq": xor_place(seq_index, 1)}
    sides = ring_neighbours(seq_index, seq_count)
    greet([partner] + [{"seq": side} for side in sides])

    def columns_of(piece, side, hop):
        low, high = bounds[piece], bounds[piece + 1]
        if hop == far - 1:
            mid = low + (high - low) // (2 * LANES) * LANES
            low, high = (low, mid) if side == 0 else (mid, high)
        return pl.ds(low, high - low)

    def ring_copy(piece, side, hop):
        columns = columns_of(piece, side, hop)
        target = out.at[
            chip_near(seq_index, seq_count, -hop if side == 0 else hop), core, :, columns
        ]
        return pltpu.make_async_remote_copy(
            src_ref=local.at[:, columns] if hop == 0 else target,
            dst_ref=target,
            send_sem=ring_send.at[piece, side, hop],
            recv_sem=ring_recv.at[piece, side, hop],
            device_id={"seq": sides[side]},
            device_id_type=MESH,
        )

    def core_copy(piece, side, hop):
        if hop < 0:
            columns = pl.ds(bounds[piece], bounds[piece + 1] - bounds[piece])
            target = out.at[seq_index // 2, core, :, columns]
            source = local.at[:, columns]
        else:
            chip = chip_near(seq_index, seq_count, -1 - hop if side == 0 else 1 + hop)
            target = out.at[chip, core, :, columns_of(piece, side, hop)]
            source = target
        return pltpu.make_async_remote_copy(
            src_ref=source,
            dst_ref=target,
            send_sem=core_send.at[piece, side, hop + 1],
            recv_sem=core_recv.at[piece, side, hop + 1],
            device_id=partner,
            device_id_type=MESH,
        )

    pieces = range(len(bounds) - 1)
    arrivals = [(piece, side, hop) for hop in range(far) for piece in pieces for side in range(2)]
    own_copy = pltpu.make_async_copy(local, out.at[seq_index // 2, core], own_sem)
    for piece in pieces:
        for side in range(2):
            ring_copy(piece, side, 0).start()
    own_copy.start()
    for piece in pieces:
        core_copy(piece, 0, -1).start()
    for piece, side, hop in arrivals:
        ring_copy(piece, side, hop).wait_recv()
        if hop + 1 < far:
            ring_copy(piece, side, hop + 1).start()
        core_copy(piece, side, hop).start()
    crossed = [(piece, 0, -1) for piece in pieces] + arrivals
    for piece, side, hop in crossed:
        core_copy(piece, side, hop).wait_recv()
    own_copy.wait()
    for piece, side, hop in crossed:
        core_copy(piece, side, hop).wait_send()
    for piece, side, hop in arrivals:
        ring_copy(piece, side, hop).wait_send()


def ring_gather(local, bounds, seq_count, collective_id):
    rows, width = local.shape
    local = local.astype(jnp.bfloat16)
    if rows % 16:
        return lax.all_gather(local, "seq", axis=0, tiled=True), jnp.zeros((8, LANES), jnp.float32)
    pieces, far = len(bounds) - 1, seq_count // 4
    gathered, token = pl.pallas_call(
        functools.partial(gather_kernel, seq_count, bounds),
        in_specs=[pl.BlockSpec(memory_space=pl.ANY)],
        out_specs=[
            pl.BlockSpec(memory_space=pl.ANY),
            pl.BlockSpec(memory_space=pltpu.VMEM),
        ],
        out_shape=[
            jax.ShapeDtypeStruct((seq_count // 2, 2, rows, width), jnp.bfloat16),
            jax.ShapeDtypeStruct((8, LANES), jnp.float32),
        ],
        scratch_shapes=[
            pltpu.SemaphoreType.DMA,
            pltpu.SemaphoreType.DMA((pieces, 2, far)),
            pltpu.SemaphoreType.DMA((pieces, 2, far)),
            pltpu.SemaphoreType.DMA((pieces, 2, far + 1)),
            pltpu.SemaphoreType.DMA((pieces, 2, far + 1)),
        ],
        compiler_params=pltpu.CompilerParams(collective_id=collective_id, has_side_effects=True),
        cost_estimate=pl.CostEstimate(
            flops=0, bytes_accessed=32 * rows * seq_count * width, transcendentals=0
        ),
        name="ring_gather",
    )(local)
    return gathered.reshape(seq_count * rows, width), token


def kept_places(seq_count):
    chips = seq_count // 2
    far = chips // 2
    return [*range(far - 2), *range(far + 3, chips)]


def glu_kernel(
    blocks,
    seq_count,
    ringed,
    normed,
    normed_t,
    top,
    top_t,
    w_gate,
    w_up,
    w_down,
    b_gate,
    b_up,
    out,
    grad_normed,
    bias_grads,
    kept,
    *refs,
):
    index = pl.program_id(0)
    seq_index = lax.axis_index("seq")
    partner = {"seq": xor_place(seq_index, 1)}
    half = normed_t.shape[0] // 2
    chips = seq_count // 2
    far, seg = chips // 2, half // chips
    mid = BLOCK // 2
    if ringed:
        moving, *refs = refs
    out_acc, grad_acc, mine, away, arrived, send_sem, recv_sem, *refs = refs
    sides = ring_neighbours(seq_index, seq_count)
    if ringed:
        sums, first_send, first_land, second_send, second_land, *ring_sems = refs

    def crossing(block):
        return pltpu.make_async_remote_copy(
            src_ref=away.at[block % 2],
            dst_ref=arrived.at[block],
            send_sem=send_sem.at[block % 2],
            recv_sem=recv_sem.at[block],
            device_id=partner,
            device_id_type=MESH,
        )

    def hop(block, side, which):
        source, target = (first_send, first_land) if which == 0 else (second_send, second_land)
        return pltpu.make_async_remote_copy(
            src_ref=source.at[block, side],
            dst_ref=target.at[block, side],
            send_sem=ring_sems[2 * which].at[block, side],
            recv_sem=ring_sems[2 * which + 1].at[block, side],
            device_id={"seq": sides[side]},
            device_id_type=MESH,
        )

    @pl.when(index == 0)
    def _():
        greet([partner] + ([{"seq": side} for side in sides] if ringed else []))
        out_acc[...] = jnp.zeros_like(out_acc)
        grad_acc[...] = jnp.zeros_like(grad_acc)

    @pl.when(index < blocks)
    def _():
        gate_pre = product(normed[...], w_gate[...]) + b_gate[...]
        up_pre = product(normed[...], w_up[...]) + b_up[...]
        grad_hidden = product(top[...], w_down[...])
        sigmoid_gate = jax.nn.sigmoid(gate_pre)
        silu_gate = gate_pre * sigmoid_gate
        hidden = (silu_gate * up_pre).astype(jnp.bfloat16)
        grad_up = (grad_hidden * silu_gate).astype(jnp.bfloat16)
        grad_gate = (
            grad_hidden * up_pre * sigmoid_gate * (1.0 + gate_pre * (1.0 - sigmoid_gate))
        ).astype(jnp.bfloat16)
        bias_grads[0:1, :] = jnp.sum(grad_gate.astype(jnp.float32), axis=0, keepdims=True)
        bias_grads[1:2, :] = jnp.sum(grad_up.astype(jnp.float32), axis=0, keepdims=True)
        out_acc[...] += product_t(hidden, w_down[...])
        grad_acc[...] += product_t(grad_gate, w_gate[...]) + product_t(grad_up, w_up[...])

        @pl.when(index >= 2)
        def _():
            crossing(index - 2).wait_send()

        slot = index % 2
        away[slot, 0] = product(normed_t[half:, :], grad_gate).astype(jnp.bfloat16)
        away[slot, 1] = product(normed_t[half:, :], grad_up).astype(jnp.bfloat16)
        away[slot, 2] = product(top_t[half:, :], hidden).astype(jnp.bfloat16)
        crossing(index).start()
        mine[slot, 0] = product(normed_t[:half, :], grad_gate).astype(jnp.bfloat16)
        mine[slot, 1] = product(normed_t[:half, :], grad_up).astype(jnp.bfloat16)
        mine[slot, 2] = product(top_t[:half, :], hidden).astype(jnp.bfloat16)

    def chunk(block, near):
        return sums[block % 3, :, near * seg : (near + 1) * seg, :].astype(jnp.float32)

    @pl.when((index >= 1) & (index <= blocks))
    def _():
        block = index - 1
        crossing(block).wait_recv()
        total = mine[block % 2].astype(jnp.float32) + arrived[block].astype(jnp.float32)
        total = total.astype(jnp.bfloat16)
        if ringed:
            sums[block % 3] = total
            for side in range(2):
                first_send[block, side] = total[
                    :, far * seg : (far + 1) * seg, side * mid : (side + 1) * mid
                ]
                hop(block, side, 0).start()
            for at, near in enumerate(kept_places(seq_count)):
                kept[at] = total[:, near * seg : (near + 1) * seg, :]
        else:
            kept[...] = total

    if ringed:

        @pl.when((index >= 2) & (index <= blocks + 1))
        def _():
            block = index - 2
            for side in range(2):
                term = chunk(block, far - 1 if side == 0 else far + 1)
                hop(block, side, 0).wait_recv()
                land = first_land[block, side].astype(jnp.float32)
                low = term[:, :, :mid] + land if side == 0 else term[:, :, :mid]
                high = term[:, :, mid:] if side == 0 else term[:, :, mid:] + land
                second_send[block, side, :, :, :mid] = low.astype(jnp.bfloat16)
                second_send[block, side, :, :, mid:] = high.astype(jnp.bfloat16)
                hop(block, side, 1).start()

        @pl.when(index >= 3)
        def _():
            block = index - 3
            for side in range(2):
                term = chunk(block, far - 2 if side == 0 else far + 2)
                hop(block, side, 1).wait_recv()
                land = second_land[block, side].astype(jnp.float32)
                moving[side] = (term + land).astype(jnp.bfloat16)

    @pl.when(index == blocks)
    def _():
        crossing(blocks - 2).wait_send()
        crossing(blocks - 1).wait_send()
        out[...] = out_acc[...].astype(jnp.bfloat16)
        grad_normed[...] = grad_acc[...].astype(jnp.bfloat16)

    if ringed:

        @pl.when(index == blocks + 2)
        def _():
            for block in range(blocks):
                for side in range(2):
                    hop(block, side, 0).wait_send()
                    hop(block, side, 1).wait_send()


def glu_layer(normed, normed_t, top, top_t, weights, gate_bias, up_bias, seq_count):
    rows, width = normed.shape
    hidden_width = gate_bias.shape[0]
    blocks = hidden_width // BLOCK
    half = width // 2
    seg = width // seq_count
    ringed = seg % 16 == 0
    kept = len(kept_places(seq_count))
    bf = jnp.bfloat16

    def whole(shape):
        return pl.BlockSpec(shape, lambda i: (0, 0), pipeline_mode=pl.Buffered(1))

    def at(lag):
        return lambda i: jnp.clip(i - lag, 0, blocks - 1)

    def weight_spec(which):
        return pl.BlockSpec((width, BLOCK), lambda i: (0, which * blocks + at(0)(i)))

    bias_spec = pl.BlockSpec((1, BLOCK), lambda i: (0, at(0)(i)))
    work = rows * width * hidden_width
    if ringed:
        term_specs = [
            pl.BlockSpec((kept, 3, seg, BLOCK), lambda i: (0, 0, 0, at(1)(i))),
            pl.BlockSpec((2, 3, seg, BLOCK), lambda i: (0, 0, 0, at(3)(i))),
        ]
        term_shapes = [
            jax.ShapeDtypeStruct((kept, 3, seg, hidden_width), bf),
            jax.ShapeDtypeStruct((2, 3, seg, hidden_width), bf),
        ]
        ring_scratches = [
            pltpu.VMEM((3, 3, half, BLOCK), bf),
            pltpu.VMEM((blocks, 2, 3, seg, BLOCK // 2), bf),
            pltpu.VMEM((blocks, 2, 3, seg, BLOCK // 2), bf),
            pltpu.VMEM((blocks, 2, 3, seg, BLOCK), bf),
            pltpu.VMEM((blocks, 2, 3, seg, BLOCK), bf),
            *(pltpu.SemaphoreType.DMA((blocks, 2)) for _ in range(4)),
        ]
    else:
        term_specs = [pl.BlockSpec((3, half, BLOCK), lambda i: (0, 0, at(1)(i)))]
        term_shapes = [jax.ShapeDtypeStruct((3, half, hidden_width), bf)]
        ring_scratches = []
    return pl.pallas_call(
        functools.partial(glu_kernel, blocks, seq_count, ringed),
        grid=(blocks + (3 if ringed else 1),),
        in_specs=[
            whole((rows, width)),
            whole((width, rows)),
            whole((rows, width)),
            whole((width, rows)),
            weight_spec(0),
            weight_spec(1),
            weight_spec(2),
            bias_spec,
            bias_spec,
        ],
        out_specs=[
            pl.BlockSpec((rows, width), lambda i: (0, 0)),
            pl.BlockSpec((rows, width), lambda i: (0, 0)),
            pl.BlockSpec((2, BLOCK), lambda i: (0, at(0)(i))),
            *term_specs,
        ],
        out_shape=[
            jax.ShapeDtypeStruct((rows, width), bf),
            jax.ShapeDtypeStruct((rows, width), bf),
            jax.ShapeDtypeStruct((2, hidden_width), jnp.float32),
            *term_shapes,
        ],
        scratch_shapes=[
            pltpu.VMEM((rows, width), jnp.float32),
            pltpu.VMEM((rows, width), jnp.float32),
            pltpu.VMEM((2, 3, half, BLOCK), bf),
            pltpu.VMEM((2, 3, half, BLOCK), bf),
            pltpu.VMEM((blocks, 3, half, BLOCK), bf),
            pltpu.SemaphoreType.DMA((2,)),
            pltpu.SemaphoreType.DMA((blocks,)),
            *ring_scratches,
        ],
        compiler_params=pltpu.CompilerParams(
            collective_id=1, has_side_effects=True, vmem_limit_bytes=VMEM_BYTES
        ),
        cost_estimate=pl.CostEstimate(
            flops=18 * work, bytes_accessed=12 * width * hidden_width, transcendentals=rows * hidden_width
        ),
        name="glu_layer",
    )(
        normed,
        normed_t,
        top,
        top_t,
        weights,
        weights,
        weights,
        gate_bias[None],
        up_bias[None],
    )


class ChipRing:
    def __init__(self, seq_count, pieces, sends, lands, send_sem, recv_sem):
        self.chips = seq_count // 2
        self.far = self.chips // 2
        self.pieces = pieces
        self.sends, self.lands = sends, lands
        self.send_sem, self.recv_sem = send_sem, recv_sem
        self.sides = ring_neighbours(lax.axis_index("seq"), seq_count)
        self.greeted = [{"seq": side} for side in self.sides]
        half, width = pieces[0].shape
        self.seg = half // self.chips
        self.width, self.mid = width, width // 2

    def copy(self, piece, side, hop):
        mid, seg = self.mid, self.seg
        if hop == 0:
            source = self.pieces[piece].at[pl.ds(self.far * seg, seg), pl.ds(side * mid, mid)]
            target = self.lands.at[piece, side, 0, :, pl.ds(0, mid)]
        else:
            source = self.sends.at[piece, side, hop - 1]
            target = self.lands.at[piece, side, hop]
        return pltpu.make_async_remote_copy(
            src_ref=source,
            dst_ref=target,
            send_sem=self.send_sem.at[piece, side, hop],
            recv_sem=self.recv_sem.at[piece, side, hop],
            device_id={"seq": self.sides[side]},
            device_id_type=MESH,
        )

    def start(self, piece):
        for side in range(2):
            self.copy(piece, side, 0).start()

    def advance(self, piece, hop):
        mid, seg = self.mid, self.seg
        for side in range(2):
            near = self.far - hop if side == 0 else self.far + hop
            term = self.pieces[piece][near * seg : (near + 1) * seg, :].astype(jnp.float32)
            self.copy(piece, side, hop - 1).wait_recv()
            if hop == 1:
                land = self.lands[piece, side, 0, :, :mid].astype(jnp.float32)
                low = term[:, :mid] + land if side == 0 else term[:, :mid]
                high = term[:, mid:] if side == 0 else term[:, mid:] + land
                self.sends[piece, side, 0, :, :mid] = low.astype(jnp.bfloat16)
                self.sends[piece, side, 0, :, mid:] = high.astype(jnp.bfloat16)
            else:
                land = self.lands[piece, side, hop - 1].astype(jnp.float32)
                self.sends[piece, side, hop - 1] = (term + land).astype(jnp.bfloat16)
            self.copy(piece, side, hop).start()

    def total(self, piece):
        total = self.pieces[piece][: self.seg, :].astype(jnp.float32)
        for side in range(2):
            self.copy(piece, side, self.far - 1).wait_recv()
            total = total + self.lands[piece, side, self.far - 1].astype(jnp.float32)
        return total

    def close(self):
        for piece in range(len(self.pieces)):
            for side in range(2):
                for hop in range(self.far):
                    self.copy(piece, side, hop).wait_send()


def ring_scratch(seq_count, pieces, seg, width):
    far = seq_count // 4
    return [
        pltpu.VMEM((pieces, 2, far - 1, seg, width), jnp.bfloat16),
        pltpu.VMEM((pieces, 2, far, seg, width), jnp.bfloat16),
        pltpu.SemaphoreType.DMA((pieces, 2, far)),
        pltpu.SemaphoreType.DMA((pieces, 2, far)),
    ]


def greet(devices):
    barrier = pltpu.get_barrier_semaphore()
    for device in devices:
        pl.semaphore_signal(barrier, inc=1, device_id=device, device_id_type=MESH)
    pl.semaphore_wait(barrier, len(devices))


def tail_kernel(seq_count, head_count, ready_count, made_count, *refs):
    ready = refs[:ready_count]
    rows_t, columns, small, split, *refs = refs[ready_count:]
    last_terms, refs = refs[:3], refs[3:]
    out, small_out, joint, last_out, *refs = refs
    (
        mine,
        away,
        arrived,
        small_send,
        small_land,
        core_send,
        core_recv,
        step_send,
        step_recv,
        split_land,
        split_send,
        split_recv,
        *ring_refs,
    ) = refs
    half = rows_t.shape[0] // 2
    width = columns.shape[1] // made_count
    pieces = [*ready, *(mine.at[made] for made in range(made_count))]
    ring = ChipRing(seq_count, pieces, *ring_refs)
    seq_index = lax.axis_index("seq")
    head_index = lax.axis_index("head")
    partners = []
    bit = 1
    while bit < seq_count:
        partners.append({"seq": xor_place(seq_index, bit)})
        bit *= 2
    seq_steps = len(partners)
    bit = 1
    while bit < head_count:
        partners.append({"head": xor_place(head_index, bit)})
        bit *= 2
    greet(ring.greeted + partners)

    def core_copy(made):
        return pltpu.make_async_remote_copy(
            src_ref=away.at[made],
            dst_ref=arrived.at[made],
            send_sem=core_send.at[made],
            recv_sem=core_recv.at[made],
            device_id=partners[0],
            device_id_type=MESH,
        )

    def step_copy(step):
        rows = small.shape[0] if step < seq_steps else small.shape[0] // 2
        return pltpu.make_async_remote_copy(
            src_ref=small_send.at[step, pl.ds(0, rows)],
            dst_ref=small_land.at[step, pl.ds(0, rows)],
            send_sem=step_send.at[step],
            recv_sem=step_recv.at[step],
            device_id=partners[step],
            device_id_type=MESH,
        )

    def step_on(step):
        late = small.shape[0] // 2
        if step == 0:
            small_send[0] = small[...]
        else:
            step_copy(step - 1).wait_recv()
            if step <= seq_steps:
                total = small_send[step - 1] + small_land[step - 1]
                if step == seq_steps:
                    small_out[late:, :] = total[late:]
                if step < len(partners):
                    small_send[step] = total
                else:
                    small_out[:late, :] = total[:late]
            else:
                total = small_send[step - 1, :late] + small_land[step - 1, :late]
                if step < len(partners):
                    small_send[step, :late] = total
                else:
                    small_out[:late, :] = total
        if step < len(partners):
            step_copy(step).start()

    def split_copy(step):
        return pltpu.make_async_remote_copy(
            src_ref=split,
            dst_ref=split_land.at[step],
            send_sem=split_send.at[step],
            recv_sem=split_recv.at[step],
            device_id={"head": (head_index + 1 + step) % head_count},
            device_id_type=MESH,
        )

    for step in range(head_count - 1):
        split_copy(step).start()
    for piece in range(ready_count):
        ring.start(piece)
    step_on(0)
    for made in range(made_count):
        cols = slice(made * width, (made + 1) * width)
        away[made] = product(rows_t[half:, :], columns[:, cols]).astype(jnp.bfloat16)
        core_copy(made).start()
    for made in range(made_count):
        cols = slice(made * width, (made + 1) * width)
        term = product(rows_t[:half, :], columns[:, cols])
        core_copy(made).wait_recv()
        mine[made] = (term + arrived[made].astype(jnp.float32)).astype(jnp.bfloat16)
        ring.start(ready_count + made)
    last_total = last_terms[0][...].astype(jnp.float32)
    for term in last_terms[1:]:
        last_total = last_total + term[...].astype(jnp.float32)
    last_out[...] = last_total
    done = 1
    for hop in range(1, ring.far):
        for piece in range(len(pieces)):
            ring.advance(piece, hop)
        while done <= len(partners) * hop // (ring.far - 1):
            step_on(done)
            done += 1
    total = split[...].astype(jnp.float32)
    for step in range(head_count - 1):
        split_copy(step).wait_recv()
        total = total + split_land[step].astype(jnp.float32)
    joint[...] = total
    for piece in range(len(pieces)):
        out[:, piece * width : (piece + 1) * width] = ring.total(piece)
    for step in range(head_count - 1):
        split_copy(step).wait_send()
    for made in range(made_count):
        core_copy(made).wait_send()
    ring.close()
    for step in range(len(partners)):
        step_copy(step).wait_send()


def tail_sums(ready, rows_t, columns, small, split, last_terms, seq_count):
    head_count = lax.axis_size("head")
    chips = seq_count // 2
    half = rows_t.shape[0] // 2
    seg = half // chips
    width = TAIL_WIDTH
    made_count = columns.shape[1] // width
    pieces = len(ready) + made_count
    steps = (seq_count - 1).bit_length() + (head_count - 1).bit_length()
    bf = jnp.bfloat16
    return pl.pallas_call(
        functools.partial(tail_kernel, seq_count, head_count, len(ready), made_count),
        in_specs=[pl.BlockSpec(memory_space=pltpu.VMEM)] * (len(ready) + 7),
        out_specs=[pl.BlockSpec(memory_space=pltpu.VMEM)] * 4,
        out_shape=[
            jax.ShapeDtypeStruct((seg, pieces * width), jnp.float32),
            jax.ShapeDtypeStruct(small.shape, jnp.float32),
            jax.ShapeDtypeStruct(split.shape, jnp.float32),
            jax.ShapeDtypeStruct(last_terms[0].shape, jnp.float32),
        ],
        scratch_shapes=[
            pltpu.VMEM((made_count, half, width), bf),
            pltpu.VMEM((made_count, half, width), bf),
            pltpu.VMEM((made_count, half, width), bf),
            pltpu.VMEM((steps, *small.shape), jnp.float32),
            pltpu.VMEM((steps, *small.shape), jnp.float32),
            pltpu.SemaphoreType.DMA((made_count,)),
            pltpu.SemaphoreType.DMA((made_count,)),
            pltpu.SemaphoreType.DMA((steps,)),
            pltpu.SemaphoreType.DMA((steps,)),
            pltpu.VMEM((head_count - 1, *split.shape), bf),
            pltpu.SemaphoreType.DMA((head_count - 1,)),
            pltpu.SemaphoreType.DMA((head_count - 1,)),
            *ring_scratch(seq_count, pieces, seg, width),
        ],
        compiler_params=pltpu.CompilerParams(
            collective_id=2, has_side_effects=True, vmem_limit_bytes=VMEM_BYTES
        ),
        cost_estimate=pl.CostEstimate(
            flops=2 * rows_t.shape[0] * rows_t.shape[1] * columns.shape[1],
            bytes_accessed=16 * pieces * half * width,
            transcendentals=0,
        ),
        name="tail_sums",
    )(*ready, rows_t, columns, small, split, *last_terms)


def turned_back(values, tables):
    shift = ROT // 2
    return (
        values * tables[0]
        + pltpu.roll(values, LANES - shift, 1) * tables[1]
        - pltpu.roll(values, shift, 1) * tables[2]
    )


def self_back_kernel(seq_count, pairs, score_scale, ready_count, *refs):
    (
        query,
        keys,
        values,
        stamp_key,
        stamp_value,
        grad_out,
        logs,
        key_ids,
        query_ids,
        query_slots,
        tables,
    ) = refs[:11]
    ready = refs[11 : 11 + ready_count]
    out, shares = refs[11 + ready_count : 13 + ready_count]
    (
        bias,
        acc,
        own,
        halo,
        halo_land,
        halo_send_sem,
        halo_recv_sem,
        *ring_refs,
    ) = refs[13 + ready_count :]
    pair = pl.program_id(0)
    rows = query.shape[0]
    slots = stamp_key.shape[0]
    span = QUERY_BLOCK + 2 * HALF
    seq_index = lax.axis_index("seq")
    before = (seq_index + seq_count - 1) % seq_count
    behind = (seq_index + 1) % seq_count
    ring = ChipRing(seq_count, list(ready), *ring_refs) if ready else None
    hops = ring.far if ready else 1

    def halo_copy(which, side):
        return pltpu.make_async_remote_copy(
            src_ref=halo.at[which, side],
            dst_ref=halo_land.at[which, side],
            send_sem=halo_send_sem.at[which, side],
            recv_sem=halo_recv_sem.at[which, side],
            device_id={"seq": before if side == 0 else behind},
            device_id_type=MESH,
        )

    @pl.when(pair == 0)
    def _():
        greet((ring.greeted if ready else []) + [{"seq": before}, {"seq": behind}])
        for piece in range(ready_count):
            ring.start(piece)
        for block in range(rows // QUERY_BLOCK):
            start = block * QUERY_BLOCK
            asked = query_ids[:, start : start + QUERY_BLOCK]
            key_row = lax.broadcasted_iota(jnp.int32, (span, QUERY_BLOCK), 0)
            query_row = lax.broadcasted_iota(jnp.int32, (span, QUERY_BLOCK), 1)
            away = key_row - HALF - query_row
            seen = (key_ids[start : start + span, :] == asked) & (jnp.abs(away) <= HALF)
            bias[block, :span, :] = jnp.where(seen, 0.0, NEG)
            slot_row = lax.broadcasted_iota(jnp.int32, (slots, QUERY_BLOCK), 0)
            bias[block, span:, :] = jnp.where(
                slot_row == query_slots[:, start : start + QUERY_BLOCK], 0.0, NEG
            )

    for hop in range(1, hops):

        @pl.when(pair == hop)
        def _():
            for piece in range(ready_count):
                ring.advance(piece, hop)

    @pl.when(pair < pairs)
    def _():
        acc[...] = jnp.zeros_like(acc)
        lane = lax.broadcasted_iota(jnp.int32, (1, LANES), 1)
        stamp_k, stamp_v = stamp_key[...], stamp_value[...]
        grad_queries = []
        for block in range(rows // QUERY_BLOCK):
            start = block * QUERY_BLOCK
            near_k = jnp.concatenate([keys[0, start : start + span, :], stamp_k], axis=0)
            near_v = jnp.concatenate([values[0, start : start + span, :], stamp_v], axis=0)
            block_q = query[start : start + QUERY_BLOCK, :]
            block_g = grad_out[start : start + QUERY_BLOCK, :]
            grad_q = jnp.zeros((QUERY_BLOCK, LANES), jnp.float32)
            grad_k = jnp.zeros((span + slots, LANES), jnp.float32)
            grad_v = jnp.zeros((span + slots, LANES), jnp.float32)
            for head in range(LANES // HD):
                here = lane // HD == head
                head_q = jnp.where(here, block_q, jnp.zeros_like(block_q))
                head_g = jnp.where(here, block_g, jnp.zeros_like(block_g))
                head_k = jnp.where(here, near_k, jnp.zeros_like(near_k))
                scores = product_t(near_k, head_q) * score_scale + bias[block]
                probs = jnp.exp(scores - logs[0, head : head + 1, start : start + QUERY_BLOCK])
                grad_p = product_t(near_v, head_g)
                dot = jnp.sum(probs * grad_p, axis=0, keepdims=True)
                grad_s = (probs * (grad_p - dot)).astype(jnp.bfloat16)
                grad_k = grad_k + product(grad_s, head_q)
                grad_v = grad_v + product(probs.astype(jnp.bfloat16), head_g)
                grad_q = grad_q + product_tn(grad_s, head_k)
            grad_queries.append(grad_q)
            acc[0, start : start + span, :] += grad_k[:span]
            acc[1, start : start + span, :] += grad_v[:span]
            acc[0, 2 * HALF + rows :, :] += grad_k[span:]
            acc[1, 2 * HALF + rows :, :] += grad_v[span:]
        column = pl.multiple_of(pair * LANES, LANES)
        grad_q = jnp.concatenate(grad_queries, axis=0) * score_scale
        out[:rows, pl.ds(column, LANES)] = turned_back(grad_q, tables).astype(jnp.bfloat16)
        out[rows:, pl.ds(column, LANES)] = jnp.zeros((slots, LANES), jnp.bfloat16)
        for which in range(2):
            scale = score_scale if which == 0 else 1.0
            shift = (which + 1) * pairs * LANES
            halo[pair, 0, which] = (acc[which, :HALF, :] * scale).astype(jnp.bfloat16)
            halo[pair, 1, which] = (acc[which, HALF + rows : 2 * HALF + rows, :] * scale).astype(
                jnp.bfloat16
            )
            own[pair, which] = acc[which, HALF : HALF + rows, :] * scale
            out[rows:, pl.ds(column + shift, LANES)] = (
                acc[which, 2 * HALF + rows :, :] * scale
            ).astype(jnp.bfloat16)
        halo_copy(pair, 0).start()
        halo_copy(pair, 1).start()

    @pl.when(pair == pairs)
    def _():
        for which in range(pairs):
            halo_copy(which, 0).wait_recv()
            halo_copy(which, 1).wait_recv()
            own[which, :, rows - HALF :, :] += halo_land[which, 0].astype(jnp.float32)
            own[which, :, :HALF, :] += halo_land[which, 1].astype(jnp.float32)
            column = (pairs + which) * LANES
            out[:rows, column : column + LANES] = turned_back(own[which, 0], tables).astype(
                jnp.bfloat16
            )
            column = (2 * pairs + which) * LANES
            out[:rows, column : column + LANES] = own[which, 1].astype(jnp.bfloat16)
        if not ready:
            shares[...] = jnp.zeros_like(shares)
        for piece in range(ready_count):
            shares[:, piece * ring.width : (piece + 1) * ring.width] = ring.total(piece)
        if ready:
            ring.close()
        for which in range(pairs):
            halo_copy(which, 0).wait_send()
            halo_copy(which, 1).wait_send()


def self_back(
    query, near, stamps, grad_out, logs, key_ids, query_ids, query_slots, tables, ready, score_scale, seq_count
):
    rows, part = query.shape
    slots = stamps.shape[0]
    pairs = part // LANES
    window = near.shape[1]
    half, width = ready[0].shape if ready else (8 * seq_count // 2, LANES)
    seg = half // (seq_count // 2)
    share_width = max(len(ready), 1) * width
    span = QUERY_BLOCK + 2 * HALF
    blocks = rows // QUERY_BLOCK
    last = pairs - 1

    def at(first, shape, lead=()):
        return pl.BlockSpec(shape, lambda i: (*lead, 0, first + jnp.minimum(i, last)))

    def whole(shape):
        return pl.BlockSpec(shape, lambda i: (0,) * len(shape), pipeline_mode=pl.Buffered(1))

    return pl.pallas_call(
        functools.partial(self_back_kernel, seq_count, pairs, score_scale, len(ready)),
        grid=(pairs + 1,),
        in_specs=[
            at(0, (rows, LANES)),
            at(0, (1, window, LANES), (0,)),
            at(0, (1, window, LANES), (1,)),
            at(pairs, (slots, LANES)),
            at(2 * pairs, (slots, LANES)),
            at(0, (rows, LANES)),
            pl.BlockSpec((1, LANES // HD, rows), lambda i: (jnp.minimum(i, last), 0, 0)),
            whole((window, 1)),
            whole((1, rows)),
            whole((1, rows)),
            whole((3, rows, LANES)),
            *(whole((half, width)) for _ in ready),
        ],
        out_specs=[
            pl.BlockSpec((rows + slots, 3 * part), lambda i: (0, 0)),
            pl.BlockSpec((seg, share_width), lambda i: (0, 0)),
        ],
        out_shape=[
            jax.ShapeDtypeStruct((rows + slots, 3 * part), jnp.bfloat16),
            jax.ShapeDtypeStruct((seg, share_width), jnp.float32),
        ],
        scratch_shapes=[
            pltpu.VMEM((blocks, span + slots, QUERY_BLOCK), jnp.float32),
            pltpu.VMEM((2, window + slots, LANES), jnp.float32),
            pltpu.VMEM((pairs, 2, rows, LANES), jnp.float32),
            pltpu.VMEM((pairs, 2, 2, HALF, LANES), jnp.bfloat16),
            pltpu.VMEM((pairs, 2, 2, HALF, LANES), jnp.bfloat16),
            pltpu.SemaphoreType.DMA((pairs, 2)),
            pltpu.SemaphoreType.DMA((pairs, 2)),
            *(ring_scratch(seq_count, len(ready), seg, width) if ready else []),
        ],
        compiler_params=pltpu.CompilerParams(
            collective_id=3, has_side_effects=True, vmem_limit_bytes=VMEM_BYTES
        ),
        cost_estimate=pl.CostEstimate(
            flops=10 * rows * window * part,
            bytes_accessed=16 * len(ready) * half * width,
            transcendentals=rows * window * part // HD,
        ),
        name="self_back",
    )(
        query,
        near,
        near,
        stamps,
        stamps,
        grad_out,
        logs.reshape(pairs, LANES // HD, rows),
        key_ids[:, None],
        query_ids[None],
        query_slots[None],
        tables,
        *ready,
    )


def tail_or_rings(ready, rows_t, columns, small, split, last_terms, seq_count):
    if rows_t.shape[0] // seq_count % 16 == 0:
        return tail_sums(ready, rows_t, columns, small, split, last_terms, seq_count)
    made = core_sum(rows_t, columns, seq_count)
    ring = Ring(side_by_side([*ready, made], seq_count // 2), seq_count)
    late = small.shape[0] // 2
    small = all_sum(small, ("seq",))
    small = jnp.concatenate([all_sum(small[:late], ("head",)), small[late:]], axis=0)
    return ring.finish(), small, head_total(split), sum(each.astype(jnp.float32) for each in last_terms)


def head_total(partial_sum):
    low = partial_sum
    if low.dtype != jnp.bfloat16:
        low = lax.optimization_barrier(partial_sum.astype(jnp.bfloat16))
    count = lax.axis_size("head")
    total = low.astype(jnp.float32)
    for step in range(1, count):
        pairs = [(index, (index + step) % count) for index in range(count)]
        total = total + lax.ppermute(low, "head", pairs).astype(jnp.float32)
    return total


def low_gather(block):
    return lax.all_gather(block.astype(jnp.bfloat16), "seq", axis=0, tiled=True)


def per_device(
    frames,
    time_token,
    prompt,
    clip_ids,
    norm1_gain,
    norm2_gain,
    norm3_gain,
    query_weight,
    key_weight,
    value_weight,
    out_weight,
    cross_query,
    cross_key,
    cross_value,
    cross_out,
    gate_weight,
    up_weight,
    down_weight,
    gate_bias,
    up_bias,
    down_bias,
    out_grad,
):
    local_rows, width = frames.shape
    clip_total = time_token.shape[0]
    ctx_tokens = prompt.shape[1]
    slot_count = local_rows // (2 * HALF) + 2
    seq_count = lax.axis_size("seq")
    seq_index = lax.axis_index("seq")
    head_index = lax.axis_index("head")
    first_row = seq_index * local_rows
    score_scale = HD ** (-0.5)
    part = query_weight.shape[1]
    hidden_width = gate_weight.shape[1]
    gain_rows = norm1_gain.shape[0]
    ctx_rows = cross_key.shape[0]
    ctx_width = prompt.shape[2]
    head_count = part // HD
    chips = seq_count // 2
    bias_rows = 2 * hidden_width // width
    small_rows = -(-max(clip_total + 1, bias_rows + 3) // 8) * 8
    order = owner_matrix(width, seq_index, seq_count)

    def ordered(matrix, by=order):
        return product_t(by, matrix).astype(jnp.bfloat16)

    vectors = jnp.stack([norm1_gain, norm2_gain, norm3_gain, down_bias], axis=1)
    vectors = jnp.pad(vectors, ((0, 0), (0, LANES - 4)))
    ctx_pair = jnp.concatenate([cross_key, cross_value], axis=0)
    attn_local = jnp.concatenate(
        [
            vectors,
            query_weight,
            key_weight,
            value_weight,
            out_weight,
            cross_query,
            cross_out,
            ctx_pair,
        ],
        axis=1,
    )
    starts = [LANES + each * part for each in range(8)]
    attn_weights, token = ring_gather(
        attn_local, (0, starts[1], *starts[2:]), seq_count, 4
    )
    glu_local = jnp.concatenate([gate_weight, up_weight, down_weight], axis=1).astype(jnp.bfloat16)
    token, glu_local = lax.optimization_barrier((token, glu_local))
    glu_weights = low_gather(glu_local)
    w_qkv = attn_weights[:, LANES : starts[3]]
    w_out = attn_weights[:, starts[3] : starts[4]]
    c_query = attn_weights[:, starts[4] : starts[5]]
    c_out = attn_weights[:, starts[5] : starts[6]]
    ctx_weights = attn_weights[:, starts[6] :].reshape(seq_count, 2, ctx_rows, part)
    c_key = ctx_weights[:, 0].reshape(ctx_width, part)
    c_value = ctx_weights[:, 1].reshape(ctx_width, part)
    rows_of = attn_weights[:, :8].astype(jnp.float32).T + token[0, 0]
    gain_one_f, gain_two_f, gain_three_f, bias_f = rows_of[0], rows_of[1], rows_of[2], rows_of[3]

    positions = first_row + jnp.arange(local_rows, dtype=jnp.int32)
    cos_table, sin_table = angles(positions)
    padded_ids = jnp.pad(clip_ids, (HALF, HALF), constant_values=-1)
    own_ids = lax.dynamic_slice_in_dim(clip_ids, first_row, local_rows)
    near_ids = lax.dynamic_slice_in_dim(padded_ids, first_row, local_rows + 2 * HALF)
    base_clip = jnp.minimum(own_ids[0], clip_total - slot_count)
    own_slot = own_ids - base_clip
    slot_range = jnp.arange(slot_count, dtype=jnp.int32)
    pad_rows = -slot_count % 16
    stamp_end = local_rows + slot_count

    stamp_rows = lax.dynamic_slice_in_dim(time_token, base_clip, slot_count, 0)
    source = jnp.concatenate(
        [frames, jnp.pad(stamp_rows, ((0, pad_rows), (0, 0)))], axis=0
    ).astype(jnp.float32)
    normed_out, normal_one, inverse_one = layer_norm_parts(source, gain_one_f)
    normed_one = normed_out.astype(jnp.bfloat16)
    frames_f = source[:local_rows]
    qkv = product(normed_one, w_qkv)
    query_rows = rotate(qkv[:local_rows, :part], cos_table, sin_table).astype(jnp.bfloat16)
    key_rows = rotate(qkv[:local_rows, part : 2 * part], cos_table, sin_table).astype(jnp.bfloat16)
    value_rows = qkv[:local_rows, 2 * part :].astype(jnp.bfloat16)
    near = extended(jnp.stack([key_rows, value_rows]), (("seq", 1),), HALF)
    window = local_rows + 2 * HALF
    near_key_h = near[0].reshape(window, head_count, HD)
    near_value_h = near[1].reshape(window, head_count, HD)
    query_h = query_rows.reshape(local_rows, head_count, HD)
    stamps = qkv[local_rows:].astype(jnp.bfloat16)
    stamp_key_h = stamps[:slot_count, part : 2 * part].reshape(slot_count, head_count, HD)
    stamp_value_h = stamps[:slot_count, 2 * part :].reshape(slot_count, head_count, HD)

    query_pos = jnp.arange(local_rows, dtype=jnp.int32)
    key_pos = jnp.arange(window, dtype=jnp.int32) - HALF
    visible = (own_ids[:, None] == near_ids[None, :]) & (
        jnp.abs(query_pos[:, None] - key_pos[None, :]) <= HALF
    )
    own_stamp = own_slot[:, None] == slot_range[None, :]
    self_keys = [(near_key_h, near_value_h, visible), (stamp_key_h, stamp_value_h, own_stamp)]
    attn_mix_h, self_logs = attend_forward(query_h, self_keys, score_scale)
    attn_mixed = attn_mix_h.reshape(local_rows, part).astype(jnp.bfloat16)
    h_one = frames_f + head_total(product_t(attn_mixed, w_out))
    middle_out, normal_two, inverse_two = layer_norm_parts(h_one, gain_two_f)
    normed_two = middle_out.astype(jnp.bfloat16)
    cross_h = product(normed_two, c_query).astype(jnp.bfloat16).reshape(local_rows, head_count, HD)
    context_rows = lax.dynamic_slice_in_dim(prompt, base_clip, slot_count, 0).reshape(
        slot_count * ctx_tokens, ctx_width
    )
    ctx_key_h = product(context_rows, c_key).astype(jnp.bfloat16)
    ctx_key_h = ctx_key_h.reshape(slot_count * ctx_tokens, head_count, HD)
    ctx_value_h = product(context_rows, c_value).astype(jnp.bfloat16)
    ctx_value_h = ctx_value_h.reshape(slot_count * ctx_tokens, head_count, HD)
    key_slot = jnp.arange(slot_count * ctx_tokens, dtype=jnp.int32) // ctx_tokens
    cross_keys = [(ctx_key_h, ctx_value_h, own_slot[:, None] == key_slot[None, :])]
    cross_mix_h, cross_logs = attend_forward(cross_h, cross_keys, score_scale)
    cross_mixed = cross_mix_h.reshape(local_rows, part).astype(jnp.bfloat16)
    h_two = h_one + head_total(product_t(cross_mixed, c_out))
    third_out, normal_three, inverse_three = layer_norm_parts(h_two, gain_three_f)
    normed_three = third_out.astype(jnp.bfloat16)

    glu_out, grad_normed_low, bias_local, glu_left, *moving = glu_layer(
        normed_three,
        ordered(normed_three),
        out_grad,
        ordered(out_grad),
        glu_weights,
        gate_bias,
        up_bias,
        seq_count,
    )
    grad_normed_three = head_total(grad_normed_low)
    if moving:
        places = kept_places(seq_count)
        glu_ring = Ring(lambda near: glu_left[places.index(near)], seq_count, moving[0])
    else:
        glu_ring = Ring(
            lambda near: glu_left[:, near * gain_rows : (near + 1) * gain_rows], seq_count
        )
    grad_top = out_grad.astype(jnp.float32)
    gain_three_term = jnp.sum(grad_normed_three * normal_three, axis=0)
    down_bias_term = jnp.sum(grad_top, axis=0)

    grad_h_two = grad_top + norm_back(grad_normed_three, normal_three, inverse_three, gain_three_f)
    grad_two_low = grad_h_two.astype(jnp.bfloat16)
    grad_cross_h = product(grad_two_low, c_out).astype(jnp.bfloat16)
    grad_cross_h = grad_cross_h.reshape(local_rows, head_count, HD)
    cross_out_sum = core_sum(ordered(grad_two_low), cross_mixed, seq_count)
    grad_cross_q, ctx_key_grads, ctx_value_grads = attend_backward(
        cross_h, cross_keys, score_scale, cross_logs, grad_cross_h
    )
    grad_cross_query = grad_cross_q.reshape(local_rows, part).astype(jnp.bfloat16)
    ctx_grads = jnp.concatenate(
        [ctx_key_grads[0].reshape(-1, part), ctx_value_grads[0].reshape(-1, part)], axis=1
    ).astype(jnp.bfloat16)
    grad_cross_query = glu_ring.after(grad_cross_query)
    glu_ring.step()
    grad_normed_two = head_total(product_t(grad_cross_query, c_query))
    cross_query_sum = core_sum(ordered(normed_two), grad_cross_query, seq_count)
    ctx_order = owner_matrix(ctx_width, seq_index, seq_count)
    ctx_sum = core_sum(ordered(context_rows, ctx_order), ctx_grads, seq_count)
    ctx_sum = jnp.transpose(ctx_sum.reshape(chips, ctx_rows, 2, part), (0, 2, 1, 3))
    grad_normed_two, cross_out_sum, cross_query_sum, ctx_sum = lax.optimization_barrier(
        (grad_normed_two, cross_out_sum, cross_query_sum, ctx_sum.reshape(width // 2, part))
    )
    gain_two_term = jnp.sum(grad_normed_two * normal_two, axis=0)
    grad_h_one = grad_h_two + norm_back(grad_normed_two, normal_two, inverse_two, gain_two_f)
    grad_one_low = grad_h_one.astype(jnp.bfloat16)
    grad_attn = product(grad_one_low, w_out).astype(jnp.bfloat16)
    grad_attn, glu_out = lax.optimization_barrier((grad_attn, glu_out))
    glu_total = head_total(glu_out)
    out_sum = core_sum(ordered(grad_one_low), attn_mixed, seq_count)
    ready_sums = [cross_out_sum, cross_query_sum, out_sum, ctx_sum]

    if gain_rows % 16 == 0:
        early_sums, ready_sums = ready_sums[:SELF_PIECES], ready_sums[SELF_PIECES:]
    else:
        early_sums = []
    ones = jnp.ones((local_rows, HD - ROT), jnp.float32)
    flat = jnp.zeros((local_rows, ROT // 2), jnp.float32)
    low_side = [sin_table, flat, 0 * ones]
    high_side = [flat, sin_table, 0 * ones]
    tables = jnp.stack(
        [
            jnp.tile(jnp.concatenate(each, axis=1), (1, LANES // HD))
            for each in ([cos_table, cos_table, ones], low_side, high_side)
        ]
    )
    grad_qkv, early_share = self_back(
        query_rows,
        near,
        stamps,
        grad_attn,
        self_logs,
        near_ids,
        own_ids,
        own_slot,
        tables,
        early_sums,
        score_scale,
        seq_count,
    )
    grad_qkv, glu_total = lax.optimization_barrier((grad_qkv, glu_total))
    result = (h_two + glu_total + bias_f).astype(jnp.bfloat16)
    grad_qkv = glu_ring.after(grad_qkv)
    glu_terms = glu_ring.last_terms()
    grad_normed_all = product_t(grad_qkv, w_qkv)
    gain_one_term = jnp.sum(grad_normed_all[:local_rows] * normal_one[:local_rows], axis=0)
    stamp_full = lax.dynamic_update_slice_in_dim(
        jnp.zeros((clip_total, width), jnp.float32), grad_normed_all[local_rows:stamp_end], base_clip, 0
    )
    small = jnp.concatenate(
        [
            jnp.pad(
                jnp.concatenate([stamp_full, gain_one_term[None]], axis=0),
                ((0, small_rows - clip_total - 1), (0, 0)),
            ),
            jnp.pad(
                jnp.concatenate(
                    [
                        bias_local.reshape(-1, width),
                        jnp.stack([gain_two_term, gain_three_term, down_bias_term]),
                    ],
                    axis=0,
                ),
                ((0, small_rows - bias_rows - 3), (0, 0)),
            ),
        ],
        axis=0,
    )
    shares, small, grad_normed_one, glu_share = tail_or_rings(
        ready_sums,
        ordered(normed_one),
        grad_qkv,
        small,
        grad_normed_all[:local_rows].astype(jnp.bfloat16),
        glu_terms,
        seq_count,
    )
    frames_grad = (
        grad_h_one
        + norm_back(grad_normed_one, normal_one[:local_rows], inverse_one[:local_rows], gain_one_f)
    ).astype(jnp.bfloat16)
    if gain_rows % 16 == 0:
        shares = jnp.concatenate([early_share, shares], axis=1)
    cross_out_share = shares[:, :part]
    cross_query_share = shares[:, part : 2 * part]
    out_share = shares[:, 2 * part : 3 * part]
    ctx_share = shares[:, 3 * part : 4 * part]
    qkv_share = shares[:, 4 * part :]
    late = small[: clip_total + 1]
    early = small[small_rows : small_rows + bias_rows + 3]
    stamp_sum = late[:clip_total]
    own_bias = early[:-3].reshape(2, hidden_width)
    every_out, every_normal, every_inverse = layer_norm_parts(
        time_token.astype(jnp.float32), gain_one_f
    )
    time_grad = norm_back(stamp_sum, every_normal, every_inverse, gain_one_f)
    time_gain = jnp.sum(stamp_sum * every_normal, axis=0)
    gains_own = lax.dynamic_slice_in_dim(
        jnp.concatenate([late[clip_total:] + time_gain[None], early[-3:]], axis=0),
        seq_index * gain_rows,
        gain_rows,
        1,
    )
    return (
        result,
        frames_grad,
        time_grad,
        gains_own[0],
        gains_own[1],
        gains_own[2],
        qkv_share[:, :part],
        qkv_share[:, part : 2 * part],
        qkv_share[:, 2 * part :],
        out_share,
        cross_query_share,
        ctx_share[:ctx_rows],
        ctx_share[ctx_rows:],
        cross_out_share,
        glu_share[0],
        glu_share[1],
        glu_share[2],
        own_bias[0],
        own_bias[1],
        gains_own[3],
    )


def solution(mesh):
    in_specs = (
        P("seq", None),
        P(),
        P(),
        P(),
        P("seq"),
        P("seq"),
        P("seq"),
        P("seq", "head"),
        P("seq", "head"),
        P("seq", "head"),
        P("seq", "head"),
        P("seq", "head"),
        P("seq", "head"),
        P("seq", "head"),
        P("seq", "head"),
        P("seq", "head"),
        P("seq", "head"),
        P("seq", "head"),
        P("head"),
        P("head"),
        P("seq"),
        P("seq", None),
    )
    out_specs = (
        P("seq", None),
        P("seq", None),
        P(),
        P("seq"),
        P("seq"),
        P("seq"),
        P("seq", "head"),
        P("seq", "head"),
        P("seq", "head"),
        P("seq", "head"),
        P("seq", "head"),
        P("seq", "head"),
        P("seq", "head"),
        P("seq", "head"),
        P("seq", "head"),
        P("seq", "head"),
        P("seq", "head"),
        P("head"),
        P("head"),
        P("seq"),
    )
    return jax.shard_map(
        per_device, mesh=mesh, in_specs=in_specs, out_specs=out_specs, check_vma=False
    )
```

```python
import functools
from functools import reduce

import jax
import jax.numpy as jnp
from jax import lax
from jax.experimental import pallas as pl
from jax.experimental.pallas import tpu as pltpu
from jax.sharding import PartitionSpec as P

HD = 64
ROT = 32
HALF = 256


EPS = 1e-05
NEG = -1e30


def extended(block, sides, width):
    for axis, dim in sides:
        count = lax.axis_size(axis)
        forward = [(i, i + 1) for i in range(count - 1)]
        backward = [(target, source) for source, target in forward]
        low = lax.ppermute(
            lax.slice_in_dim(block, block.shape[dim] - width, None, axis=dim), axis, forward
        )
        high = lax.ppermute(lax.slice_in_dim(block, 0, width, axis=dim), axis, backward)
        block = jnp.concatenate([low, block, high], axis=dim)
    return block


def passed_along(value, axis, steps):
    count = lax.axis_size(axis)
    first, last = (max(0, -steps), min(count, count - steps))
    return lax.ppermute(value, axis, [(source, source + steps) for source in range(first, last)])


def layer_norm_parts(values, gain):
    average = jnp.mean(values, axis=-1, keepdims=True)
    centered = values - average
    spread = jnp.mean(centered * centered, axis=-1, keepdims=True)
    inverse = lax.rsqrt(spread + EPS)
    normal = centered * inverse
    return (normal * gain, normal, inverse)


def norm_back(grad_out, normal, inverse, gain):
    shaped = grad_out * gain
    return (
        shaped
        - jnp.mean(shaped, axis=-1, keepdims=True)
        - normal * jnp.mean(shaped * normal, axis=-1, keepdims=True)
    ) * inverse


def angles(positions):
    ladder = jnp.arange(ROT // 2, dtype=jnp.float32)
    frequency = 10000.0 ** (-2.0 * ladder / ROT)
    phases = positions.astype(jnp.float32)[:, None] * frequency[None, :]
    return (jnp.cos(phases), jnp.sin(phases))


def rotate(values, cos_table, sin_table):
    shaped = values.reshape(values.shape[0], -1, HD)
    rot_half = ROT // 2
    leading = shaped[:, :, :rot_half]
    trailing = shaped[:, :, rot_half:ROT]
    cos_row = cos_table[:, None, :]
    sin_row = sin_table[:, None, :]
    turned = jnp.concatenate(
        [
            leading * cos_row - trailing * sin_row,
            trailing * cos_row + leading * sin_row,
            shaped[:, :, ROT:],
        ],
        axis=-1,
    )
    return turned.reshape(values.shape)


def product(matrix_a, matrix_b):
    return jnp.dot(matrix_a, matrix_b, preferred_element_type=jnp.float32)


def product_t(matrix_a, matrix_b):
    return lax.dot_general(
        matrix_a, matrix_b, (((1,), (1,)), ((), ())), preferred_element_type=jnp.float32
    )


def product_tn(matrix_a, matrix_b):
    return lax.dot_general(
        matrix_a, matrix_b, (((0,), (0,)), ((), ())), preferred_element_type=jnp.float32
    )


def exact_t(matrix_a, matrix_b):
    return lax.dot_general(
        matrix_a,
        matrix_b,
        (((1,), (1,)), ((), ())),
        precision=lax.Precision.HIGHEST,
        preferred_element_type=jnp.float32,
    )


def exact_tn(matrix_a, matrix_b):
    return lax.dot_general(
        matrix_a,
        matrix_b,
        (((0,), (0,)), ((), ())),
        precision=lax.Precision.HIGHEST,
        preferred_element_type=jnp.float32,
    )


def score_parts(query_h, key_parts, score_scale):
    return [
        jnp.where(
            visible[None],
            jnp.einsum("qhd,khd->hqk", query_h, key_h, preferred_element_type=jnp.float32)
            * score_scale,
            NEG,
        )
        for key_h, value_h, visible in key_parts
    ]


def attend_forward(query_h, key_parts, score_scale):
    scores = score_parts(query_h, key_parts, score_scale)
    row_peak = reduce(jnp.maximum, [jnp.max(score_part, axis=-1) for score_part in scores])
    exp_parts = [jnp.exp(score_part - row_peak[:, :, None]) for score_part in scores]
    row_total = reduce(jnp.add, [jnp.sum(exp_part, axis=-1) for exp_part in exp_parts])
    attn_mixed = reduce(
        jnp.add,
        [
            jnp.einsum(
                "hqk,khd->qhd",
                (exp_part / row_total[:, :, None]).astype(jnp.bfloat16),
                key_part[1],
                preferred_element_type=jnp.float32,
            )
            for exp_part, key_part in zip(exp_parts, key_parts)
        ],
    )
    return (attn_mixed, row_peak + jnp.log(row_total))


def attend_backward(query_h, key_parts, score_scale, log_total, grad_h):
    scores = score_parts(query_h, key_parts, score_scale)
    prob_parts = [jnp.exp(score_part - log_total[:, :, None]) for score_part in scores]
    dprob_parts = [
        jnp.einsum("qhd,khd->hqk", grad_h, key_part[1], preferred_element_type=jnp.float32)
        for key_part in key_parts
    ]
    row_dot = reduce(
        jnp.add,
        [
            jnp.sum(prob_part * dprob_part, axis=-1)
            for prob_part, dprob_part in zip(prob_parts, dprob_parts)
        ],
    )
    dscore_parts = [
        (prob_part * (dprob_part - row_dot[:, :, None])).astype(jnp.bfloat16)
        for prob_part, dprob_part in zip(prob_parts, dprob_parts)
    ]
    grad_query = (
        reduce(
            jnp.add,
            [
                jnp.einsum(
                    "hqk,khd->qhd", dscore_part, key_part[0], preferred_element_type=jnp.float32
                )
                for dscore_part, key_part in zip(dscore_parts, key_parts)
            ],
        )
        * score_scale
    )
    grad_keys = [
        jnp.einsum("hqk,qhd->khd", dscore_part, query_h, preferred_element_type=jnp.float32)
        * score_scale
        for dscore_part in dscore_parts
    ]
    grad_values = [
        jnp.einsum(
            "hqk,qhd->khd",
            prob_part.astype(jnp.bfloat16),
            grad_h,
            preferred_element_type=jnp.float32,
        )
        for prob_part in prob_parts
    ]
    return (grad_query, grad_keys, grad_values)


def per_device_plain(
    frames,
    time_token,
    prompt,
    clip_ids,
    norm1_gain,
    norm2_gain,
    norm3_gain,
    query_weight,
    key_weight,
    value_weight,
    out_weight,
    cross_query,
    cross_key,
    cross_value,
    cross_out,
    gate_weight,
    up_weight,
    down_weight,
    gate_bias,
    up_bias,
    down_bias,
    out_grad,
):
    local_rows = frames.shape[0]
    clip_total = time_token.shape[0]
    ctx_tokens = prompt.shape[1]
    slot_count = local_rows // (2 * HALF) + 2
    seq_index = lax.axis_index("seq")
    head_index = lax.axis_index("head")
    first_row = seq_index * local_rows
    score_scale = HD ** (-0.5)
    block_rows = min(local_rows, 2 * HALF)
    block_count = local_rows // block_rows
    window = block_rows + 2 * HALF
    block_indices = jnp.arange(block_count, dtype=jnp.int32)

    def branch_total(partial_sum):
        return lax.psum(partial_sum.astype(jnp.bfloat16), "head").astype(jnp.float32)

    def back_total(partial_sum):
        return lax.psum(partial_sum.astype(jnp.bfloat16), "head").astype(jnp.float32)

    (
        gain_one,
        gain_two,
        gain_three,
        w_query,
        w_key,
        w_value,
        w_out,
        c_query,
        c_key,
        c_value,
        c_out,
        w_gate,
        w_up,
        w_down,
        b_down,
    ) = (
        lax.all_gather(norm1_gain.astype(jnp.bfloat16), "seq", axis=0, tiled=True),
        lax.all_gather(norm2_gain.astype(jnp.bfloat16), "seq", axis=0, tiled=True),
        lax.all_gather(norm3_gain.astype(jnp.bfloat16), "seq", axis=0, tiled=True),
        lax.all_gather(query_weight.astype(jnp.bfloat16), "seq", axis=0, tiled=True),
        lax.all_gather(key_weight.astype(jnp.bfloat16), "seq", axis=0, tiled=True),
        lax.all_gather(value_weight.astype(jnp.bfloat16), "seq", axis=0, tiled=True),
        lax.all_gather(out_weight.astype(jnp.bfloat16), "seq", axis=0, tiled=True),
        lax.all_gather(cross_query.astype(jnp.bfloat16), "seq", axis=0, tiled=True),
        lax.all_gather(cross_key.astype(jnp.bfloat16), "seq", axis=0, tiled=True),
        lax.all_gather(cross_value.astype(jnp.bfloat16), "seq", axis=0, tiled=True),
        lax.all_gather(cross_out.astype(jnp.bfloat16), "seq", axis=0, tiled=True),
        lax.all_gather(gate_weight.astype(jnp.bfloat16), "seq", axis=0, tiled=True),
        lax.all_gather(up_weight.astype(jnp.bfloat16), "seq", axis=0, tiled=True),
        lax.all_gather(down_weight.astype(jnp.bfloat16), "seq", axis=0, tiled=True),
        lax.all_gather(down_bias.astype(jnp.bfloat16), "seq", axis=0, tiled=True),
    )
    gain_one_f = gain_one.astype(jnp.float32)
    gain_two_f = gain_two.astype(jnp.float32)
    positions = first_row + jnp.arange(local_rows, dtype=jnp.int32)
    cos_table, sin_table = angles(positions)
    padded_ids = jnp.pad(clip_ids, (HALF, HALF), constant_values=-1)
    own_ids = lax.dynamic_slice_in_dim(clip_ids, first_row, local_rows)
    near_ids = lax.dynamic_slice_in_dim(padded_ids, first_row, local_rows + 2 * HALF)
    base_clip = jnp.minimum(own_ids[0], clip_total - slot_count)
    own_slot = own_ids - base_clip
    slot_range = jnp.arange(slot_count, dtype=jnp.int32)
    frames_f = frames.astype(jnp.float32)
    normed_out, normal_one, inverse_one = layer_norm_parts(frames_f, gain_one_f)
    normed_one = normed_out.astype(jnp.bfloat16)
    query_rows = rotate(product(normed_one, w_query), cos_table, sin_table).astype(jnp.bfloat16)
    key_rows = rotate(product(normed_one, w_key), cos_table, sin_table).astype(jnp.bfloat16)
    value_rows = product(normed_one, w_value).astype(jnp.bfloat16)
    local_width = query_rows.shape[1]
    head_count = local_width // HD
    near = extended(jnp.stack([key_rows, value_rows]), (("seq", 1),), HALF)
    near_key_h = near[0].reshape(local_rows + 2 * HALF, head_count, HD)
    near_value_h = near[1].reshape(local_rows + 2 * HALF, head_count, HD)
    query_all_h = query_rows.reshape(local_rows, head_count, HD)
    stamp_rows = lax.dynamic_slice_in_dim(time_token, base_clip, slot_count, 0).astype(jnp.float32)
    stamp_out, stamp_normal, stamp_inverse = layer_norm_parts(stamp_rows, gain_one_f)
    stamp_normed = stamp_out.astype(jnp.bfloat16)
    stamp_key_h = (
        product(stamp_normed, w_key).astype(jnp.bfloat16).reshape(slot_count, head_count, HD)
    )
    stamp_value_h = (
        product(stamp_normed, w_value).astype(jnp.bfloat16).reshape(slot_count, head_count, HD)
    )

    def self_parts(block_index):
        row_start = block_index * block_rows
        query_pos = row_start + jnp.arange(block_rows, dtype=jnp.int32)
        key_pos = row_start - HALF + jnp.arange(window, dtype=jnp.int32)
        visible = (own_ids[:, None] == near_ids[None, :]) & (
            jnp.abs(query_pos[:, None] - key_pos[None, :]) <= HALF
        )
        own_stamp = own_slot[:, None] == slot_range[None, :]
        return (
            query_all_h,
            [(near_key_h, near_value_h, visible), (stamp_key_h, stamp_value_h, own_stamp)],
        )

    def self_forward(block_index):
        query_h, key_parts = self_parts(block_index)
        attn_mixed, log_total = attend_forward(query_h, key_parts, score_scale)
        return (attn_mixed.reshape(block_rows, local_width).astype(jnp.bfloat16), log_total)

    attn_blocks, self_logs = lax.map(self_forward, block_indices)
    attn_mixed = attn_blocks.reshape(local_rows, local_width)
    h_one = frames_f + branch_total(product_t(attn_mixed, w_out))
    middle_out, normal_two, inverse_two = layer_norm_parts(h_one, gain_two_f)
    normed_two = middle_out.astype(jnp.bfloat16)
    cross_rows = product(normed_two, c_query).astype(jnp.bfloat16)
    cross_all_h = cross_rows.reshape(local_rows, head_count, HD)
    context_rows = lax.dynamic_slice_in_dim(prompt, base_clip, slot_count, 0).reshape(
        slot_count * ctx_tokens, prompt.shape[2]
    )
    ctx_key_h = (
        product(context_rows, c_key)
        .astype(jnp.bfloat16)
        .reshape(slot_count * ctx_tokens, head_count, HD)
    )
    ctx_value_h = (
        product(context_rows, c_value)
        .astype(jnp.bfloat16)
        .reshape(slot_count * ctx_tokens, head_count, HD)
    )
    key_slot = jnp.arange(slot_count * ctx_tokens, dtype=jnp.int32) // ctx_tokens

    def cross_parts(block_index):
        row_start = block_index * block_rows
        visible = own_slot[:, None] == key_slot[None, :]
        return (cross_all_h, [(ctx_key_h, ctx_value_h, visible)])

    def cross_forward(block_index):
        query_h, key_parts = cross_parts(block_index)
        cross_mix, log_total = attend_forward(query_h, key_parts, score_scale)
        return (cross_mix.reshape(block_rows, local_width).astype(jnp.bfloat16), log_total)

    cross_blocks, cross_logs = lax.map(cross_forward, block_indices)
    cross_mixed = cross_blocks.reshape(local_rows, local_width)
    h_two = h_one + branch_total(product_t(cross_mixed, c_out))
    gain_three_f = gain_three.astype(jnp.float32)
    third_out, normal_three, inverse_three = layer_norm_parts(h_two, gain_three_f)
    normed_three = third_out.astype(jnp.bfloat16)
    gate_pre = product(normed_three, w_gate) + gate_bias
    up_pre = product(normed_three, w_up) + up_bias
    hidden = (jax.nn.silu(gate_pre) * up_pre).astype(jnp.bfloat16)
    result = (h_two + branch_total(product_t(hidden, w_down)) + b_down.astype(jnp.float32)).astype(
        jnp.bfloat16
    )
    grad_top = out_grad.astype(jnp.float32)
    grad_hidden = product(out_grad, w_down)
    sigmoid_gate = jax.nn.sigmoid(gate_pre)
    grad_up = (grad_hidden * gate_pre * sigmoid_gate).astype(jnp.bfloat16)
    grad_gate = (
        grad_hidden * up_pre * sigmoid_gate * (1.0 + gate_pre * (1.0 - sigmoid_gate))
    ).astype(jnp.bfloat16)
    gate_bias_local = jnp.sum(grad_gate.astype(jnp.float32), axis=0)
    up_bias_local = jnp.sum(grad_up.astype(jnp.float32), axis=0)
    grad_normed_three = back_total(product_t(grad_gate, w_gate) + product_t(grad_up, w_up))
    glu_terms = (
        product_tn(normed_three, grad_gate),
        product_tn(normed_three, grad_up),
        product_tn(out_grad, hidden),
        jnp.sum(grad_normed_three * normal_three, axis=0),
        jnp.sum(grad_top, axis=0),
    )
    grad_h_two = grad_top + norm_back(grad_normed_three, normal_three, inverse_three, gain_three_f)
    grad_two_low = grad_h_two.astype(jnp.bfloat16)
    grad_cross_mixed = product(grad_two_low, c_out).astype(jnp.bfloat16)
    cross_out_term = product_tn(grad_two_low, cross_mixed)
    grad_cross_h = grad_cross_mixed.reshape(local_rows, head_count, HD)

    def cross_step(ctx_grads, block_index):
        query_h, key_parts = cross_parts(block_index)
        grad_query, grad_keys, grad_values = attend_backward(
            query_h, key_parts, score_scale, cross_logs[block_index], grad_cross_h
        )
        return (ctx_grads + jnp.stack([grad_keys[0], grad_values[0]]), grad_query)

    ctx_grads, grad_cross_q = lax.scan(
        cross_step,
        jnp.zeros((2, slot_count * ctx_tokens, head_count, HD), jnp.float32),
        block_indices,
    )
    grad_cross_query = grad_cross_q.reshape(local_rows, local_width).astype(jnp.bfloat16)
    context_float = context_rows.astype(jnp.float32)
    cross_key_term = exact_tn(context_float, ctx_grads[0].reshape(-1, local_width))
    cross_value_term = exact_tn(context_float, ctx_grads[1].reshape(-1, local_width))
    cross_query_term = product_tn(normed_two, grad_cross_query)
    grad_normed_two = back_total(product_t(grad_cross_query, c_query))
    gain_two_term = jnp.sum(grad_normed_two * normal_two, axis=0)
    grad_h_one = grad_h_two + norm_back(grad_normed_two, normal_two, inverse_two, gain_two_f)
    grad_one_low = grad_h_one.astype(jnp.bfloat16)
    grad_attn = product(grad_one_low, w_out).astype(jnp.bfloat16)
    out_term = product_tn(grad_one_low, attn_mixed)
    grad_attn_h = grad_attn.reshape(local_rows, head_count, HD)

    def self_step(grad_state, block_index):
        near_grads, stamp_grads = grad_state
        query_h, key_parts = self_parts(block_index)
        row_start = block_index * block_rows
        grad_query, grad_keys, grad_values = attend_backward(
            query_h, key_parts, score_scale, self_logs[block_index], grad_attn_h
        )
        prior = near_grads
        near_grads = prior + jnp.stack([grad_keys[0], grad_values[0]])
        stamp_grads = stamp_grads + jnp.stack([grad_keys[1], grad_values[1]])
        return ((near_grads, stamp_grads), grad_query)

    start_state = (
        jnp.zeros((2, local_rows + 2 * HALF, head_count, HD), jnp.float32),
        jnp.zeros((2, slot_count, head_count, HD), jnp.float32),
    )
    (near_grads, stamp_grads), grad_query_blocks = lax.scan(self_step, start_state, block_indices)
    near_grads = near_grads.reshape(2, local_rows + 2 * HALF, local_width)
    from_above = passed_along(near_grads[:, :HALF].astype(jnp.bfloat16), "seq", -1).astype(
        jnp.float32
    )
    from_below = passed_along(
        near_grads[:, HALF + local_rows :].astype(jnp.bfloat16), "seq", 1
    ).astype(jnp.float32)
    own_grads = (
        near_grads[:, HALF : HALF + local_rows]
        + jnp.pad(from_below, ((0, 0), (0, local_rows - HALF), (0, 0)))
        + jnp.pad(from_above, ((0, 0), (local_rows - HALF, 0), (0, 0)))
    )
    grad_query_rows = rotate(
        grad_query_blocks.reshape(local_rows, local_width), cos_table, -sin_table
    ).astype(jnp.bfloat16)
    grad_key_rows = rotate(own_grads[0], cos_table, -sin_table).astype(jnp.bfloat16)
    grad_value_rows = own_grads[1].astype(jnp.bfloat16)
    stamp_key_grad = stamp_grads[0].reshape(slot_count, local_width)
    stamp_value_grad = stamp_grads[1].reshape(slot_count, local_width)
    stamp_float = stamp_normed.astype(jnp.float32)
    query_term = product_tn(normed_one, grad_query_rows)
    key_term = product_tn(normed_one, grad_key_rows) + exact_tn(stamp_float, stamp_key_grad)
    value_term = product_tn(normed_one, grad_value_rows) + exact_tn(stamp_float, stamp_value_grad)
    grad_normed_one = back_total(
        product_t(grad_query_rows, w_query)
        + product_t(grad_key_rows, w_key)
        + product_t(grad_value_rows, w_value)
    )
    gain_one_term = jnp.sum(grad_normed_one * normal_one, axis=0)
    frames_grad = (
        grad_h_one + norm_back(grad_normed_one, normal_one, inverse_one, gain_one_f)
    ).astype(jnp.bfloat16)
    stamp_partial = exact_t(stamp_key_grad, w_key.astype(jnp.float32)) + exact_t(
        stamp_value_grad, w_value.astype(jnp.float32)
    )
    attn_shares = (
        lax.psum_scatter(query_term, "seq", scatter_dimension=0, tiled=True),
        lax.psum_scatter(key_term, "seq", scatter_dimension=0, tiled=True),
        lax.psum_scatter(value_term, "seq", scatter_dimension=0, tiled=True),
        lax.psum_scatter(out_term, "seq", scatter_dimension=0, tiled=True),
        lax.psum_scatter(cross_query_term, "seq", scatter_dimension=0, tiled=True),
        lax.psum_scatter(cross_key_term, "seq", scatter_dimension=0, tiled=True),
        lax.psum_scatter(cross_value_term, "seq", scatter_dimension=0, tiled=True),
        lax.psum_scatter(cross_out_term, "seq", scatter_dimension=0, tiled=True),
        lax.psum_scatter(gain_one_term, "seq", scatter_dimension=0, tiled=True),
        lax.psum_scatter(gain_two_term, "seq", scatter_dimension=0, tiled=True),
    )
    hidden_width = gate_bias.shape[0]
    stamp_full = lax.dynamic_update_slice_in_dim(
        jnp.zeros((clip_total, stamp_partial.shape[1]), jnp.float32), stamp_partial, base_clip, 0
    )
    bias_full = lax.dynamic_update_slice_in_dim(
        jnp.zeros((2, hidden_width * lax.axis_size("head")), jnp.float32),
        jnp.stack([gate_bias_local, up_bias_local]),
        head_index * hidden_width,
        1,
    )
    stamp_sum, bias_sum = lax.psum((stamp_full, bias_full), ("seq", "head"))
    every_out, every_normal, every_inverse = layer_norm_parts(
        time_token.astype(jnp.float32), gain_one_f
    )
    time_grad = norm_back(stamp_sum, every_normal, every_inverse, gain_one_f)
    gain_rows = norm1_gain.shape[0]
    time_gain = lax.dynamic_slice_in_dim(
        jnp.sum(stamp_sum * every_normal, axis=0), seq_index * gain_rows, gain_rows
    )
    own_bias = lax.dynamic_slice_in_dim(bias_sum, head_index * hidden_width, hidden_width, 1)
    return (
        result,
        frames_grad,
        time_grad,
        attn_shares[8] + time_gain,
        attn_shares[9],
        lax.psum_scatter(glu_terms[3], "seq", scatter_dimension=0, tiled=True),
        attn_shares[0],
        attn_shares[1],
        attn_shares[2],
        attn_shares[3],
        attn_shares[4],
        attn_shares[5],
        attn_shares[6],
        attn_shares[7],
        lax.psum_scatter(glu_terms[0], "seq", scatter_dimension=0, tiled=True),
        lax.psum_scatter(glu_terms[1], "seq", scatter_dimension=0, tiled=True),
        lax.psum_scatter(glu_terms[2], "seq", scatter_dimension=0, tiled=True),
        own_bias[0],
        own_bias[1],
        lax.psum_scatter(glu_terms[4], "seq", scatter_dimension=0, tiled=True),
    )


LANES = 128
FAST_SEQ = 16
BLOCK = 256
TAIL_WIDTH = 768
QUERY_BLOCK = 128
HOP_PAIR = 3
MADE_AT = 1
VMEM_BYTES = 60 * 1024 * 1024
MESH = pl.DeviceIdType.MESH


def xor_place(index, bit):
    return index + bit * (1 - 2 * (index // bit % 2))


def chip_near(seq_index, seq_count, step):
    chips = seq_count // 2
    chip = seq_index // 2
    odd = chip % 2
    place = (1 - odd) * (chip // 2) + odd * (chips - 1 - chip // 2)
    there = (place + chips + step) % chips
    upper = there // (chips // 2)
    return (1 - upper) * 2 * there + upper * (2 * (chips - 1 - there) + 1)


def ring_neighbours(seq_index, seq_count):
    return [2 * chip_near(seq_index, seq_count, step) + seq_index % 2 for step in (1, -1)]


def gather_kernel(
    seq_count, bounds, local, out, token, own_sem, ring_send, ring_recv, core_send, core_recv
):
    token[...] = jnp.zeros_like(token)
    far = seq_count // 4
    seq_index = lax.axis_index("seq")
    core = seq_index % 2
    partner = {"seq": xor_place(seq_index, 1)}
    sides = ring_neighbours(seq_index, seq_count)
    greet([partner] + [{"seq": side} for side in sides])

    def columns_of(piece, side, hop):
        low, high = bounds[piece], bounds[piece + 1]
        if hop == far - 1:
            mid = low + (high - low) // (2 * LANES) * LANES
            low, high = (low, mid) if side == 0 else (mid, high)
        return pl.ds(low, high - low)

    def ring_copy(piece, side, hop):
        columns = columns_of(piece, side, hop)
        target = out.at[
            chip_near(seq_index, seq_count, -hop if side == 0 else hop), core, :, columns
        ]
        return pltpu.make_async_remote_copy(
            src_ref=local.at[:, columns] if hop == 0 else target,
            dst_ref=target,
            send_sem=ring_send.at[piece, side, hop],
            recv_sem=ring_recv.at[piece, side, hop],
            device_id={"seq": sides[side]},
            device_id_type=MESH,
        )

    def core_copy(piece, side, hop):
        if hop < 0:
            columns = pl.ds(bounds[piece], bounds[piece + 1] - bounds[piece])
            target = out.at[seq_index // 2, core, :, columns]
            source = local.at[:, columns]
        else:
            chip = chip_near(seq_index, seq_count, -1 - hop if side == 0 else 1 + hop)
            target = out.at[chip, core, :, columns_of(piece, side, hop)]
            source = target
        return pltpu.make_async_remote_copy(
            src_ref=source,
            dst_ref=target,
            send_sem=core_send.at[piece, side, hop + 1],
            recv_sem=core_recv.at[piece, side, hop + 1],
            device_id=partner,
            device_id_type=MESH,
        )

    pieces = range(len(bounds) - 1)
    arrivals = [(piece, side, hop) for hop in range(far) for piece in pieces for side in range(2)]
    own_copy = pltpu.make_async_copy(local, out.at[seq_index // 2, core], own_sem)
    for piece in pieces:
        for side in range(2):
            ring_copy(piece, side, 0).start()
    own_copy.start()
    for piece in pieces:
        core_copy(piece, 0, -1).start()
    for piece, side, hop in arrivals:
        ring_copy(piece, side, hop).wait_recv()
        if hop + 1 < far:
            ring_copy(piece, side, hop + 1).start()
        core_copy(piece, side, hop).start()
    crossed = [(piece, 0, -1) for piece in pieces] + arrivals
    for piece, side, hop in crossed:
        core_copy(piece, side, hop).wait_recv()
    own_copy.wait()
    for piece, side, hop in crossed:
        core_copy(piece, side, hop).wait_send()
    for piece, side, hop in arrivals:
        ring_copy(piece, side, hop).wait_send()


def ring_gather(local, bounds, seq_count, collective_id):
    rows, width = local.shape
    local = local.astype(jnp.bfloat16)
    pieces, far = len(bounds) - 1, seq_count // 4
    gathered, token = pl.pallas_call(
        functools.partial(gather_kernel, seq_count, bounds),
        in_specs=[pl.BlockSpec(memory_space=pl.ANY)],
        out_specs=[
            pl.BlockSpec(memory_space=pl.ANY),
            pl.BlockSpec(memory_space=pltpu.VMEM),
        ],
        out_shape=[
            jax.ShapeDtypeStruct((seq_count // 2, 2, rows, width), jnp.bfloat16),
            jax.ShapeDtypeStruct((8, LANES), jnp.float32),
        ],
        scratch_shapes=[
            pltpu.SemaphoreType.DMA,
            pltpu.SemaphoreType.DMA((pieces, 2, far)),
            pltpu.SemaphoreType.DMA((pieces, 2, far)),
            pltpu.SemaphoreType.DMA((pieces, 2, far + 1)),
            pltpu.SemaphoreType.DMA((pieces, 2, far + 1)),
        ],
        compiler_params=pltpu.CompilerParams(collective_id=collective_id, has_side_effects=True),
        cost_estimate=pl.CostEstimate(
            flops=0, bytes_accessed=32 * rows * seq_count * width, transcendentals=0
        ),
        name="ring_gather",
    )(local)
    return gathered.reshape(seq_count * rows, width), token


def kept_places(seq_count):
    chips = seq_count // 2
    far = chips // 2
    return [*range(far - 2), *range(far + 3, chips)]


def glu_kernel(
    blocks,
    seq_count,
    normed,
    normed_t,
    top,
    top_t,
    w_gate,
    w_up,
    w_down,
    b_gate,
    b_up,
    out,
    grad_normed,
    bias_grads,
    kept,
    *refs,
):
    index = pl.program_id(0)
    seq_index = lax.axis_index("seq")
    partner = {"seq": xor_place(seq_index, 1)}
    core = seq_index % 2
    chips = seq_count // 2
    far = chips // 2
    mid = BLOCK // 2
    moving, out_acc, grad_acc, terms, arrived, send_sem, recv_sem, *refs = refs
    sides = ring_neighbours(seq_index, seq_count)
    sums, first_send, first_land, second_send, second_land, *ring_sems = refs

    def crossing(block):
        return pltpu.make_async_remote_copy(
            src_ref=terms.at[block % 2, :, :, 1 - core],
            dst_ref=arrived.at[block],
            send_sem=send_sem.at[block % 2],
            recv_sem=recv_sem.at[block],
            device_id=partner,
            device_id_type=MESH,
        )

    def hop(block, side, which):
        source, target = (first_send, first_land) if which == 0 else (second_send, second_land)
        return pltpu.make_async_remote_copy(
            src_ref=source.at[block, side],
            dst_ref=target.at[block, side],
            send_sem=ring_sems[2 * which].at[block, side],
            recv_sem=ring_sems[2 * which + 1].at[block, side],
            device_id={"seq": sides[side]},
            device_id_type=MESH,
        )

    @pl.when(index == 0)
    def _():
        greet([partner] + [{"seq": side} for side in sides])
        out_acc[...] = jnp.zeros_like(out_acc)
        grad_acc[...] = jnp.zeros_like(grad_acc)

    @pl.when(index < blocks)
    def _():
        gate_pre = product(normed[...], w_gate[...]) + b_gate[...]
        up_pre = product(normed[...], w_up[...]) + b_up[...]
        grad_hidden = product(top[...], w_down[...])
        sigmoid_gate = jax.nn.sigmoid(gate_pre)
        silu_gate = gate_pre * sigmoid_gate
        hidden = (silu_gate * up_pre).astype(jnp.bfloat16)
        grad_up = (grad_hidden * silu_gate).astype(jnp.bfloat16)
        grad_gate = (
            grad_hidden * up_pre * sigmoid_gate * (1.0 + gate_pre * (1.0 - sigmoid_gate))
        ).astype(jnp.bfloat16)
        bias_grads[0:1, :] = jnp.sum(grad_gate.astype(jnp.float32), axis=0, keepdims=True)
        bias_grads[1:2, :] = jnp.sum(grad_up.astype(jnp.float32), axis=0, keepdims=True)
        out_acc[...] += product_t(hidden, w_down[...])
        grad_acc[...] += product_t(grad_gate, w_gate[...]) + product_t(grad_up, w_up[...])

        @pl.when(index >= 2)
        def _():
            crossing(index - 2).wait_send()

        slot = index % 2
        for which, (rows_t, columns) in enumerate(
            ((normed_t, grad_gate), (normed_t, grad_up), (top_t, hidden))
        ):
            term = product(rows_t[...], columns).astype(jnp.bfloat16)
            terms[slot, which] = term.reshape(terms.shape[2:])
        crossing(index).start()

    def chunk(block, near):
        return sums[block % 3, :, chip_near(seq_index, seq_count, near)]

    @pl.when((index >= 1) & (index <= blocks))
    def _():
        block = index - 1
        crossing(block).wait_recv()
        total = terms[block % 2, :, :, core].astype(jnp.float32) + arrived[block].astype(
            jnp.float32
        )
        sums[block % 3] = total.astype(jnp.bfloat16)
        opposite = chunk(block, far)
        for side in range(2):
            first_send[block, side] = opposite[:, :, side * mid : (side + 1) * mid]
            hop(block, side, 0).start()
        for at, near in enumerate(kept_places(seq_count)):
            kept[at] = chunk(block, near)

    @pl.when((index >= 2) & (index <= blocks + 1))
    def _():
        block = index - 2
        for side in range(2):
            term = chunk(block, far - 1 if side == 0 else far + 1).astype(jnp.float32)
            hop(block, side, 0).wait_recv()
            land = first_land[block, side].astype(jnp.float32)
            low = term[:, :, :mid] + land if side == 0 else term[:, :, :mid]
            high = term[:, :, mid:] if side == 0 else term[:, :, mid:] + land
            second_send[block, side, :, :, :mid] = low.astype(jnp.bfloat16)
            second_send[block, side, :, :, mid:] = high.astype(jnp.bfloat16)
            hop(block, side, 1).start()

    @pl.when(index >= 3)
    def _():
        block = index - 3
        for side in range(2):
            term = chunk(block, far - 2 if side == 0 else far + 2).astype(jnp.float32)
            hop(block, side, 1).wait_recv()
            land = second_land[block, side].astype(jnp.float32)
            moving[side] = (term + land).astype(jnp.bfloat16)

    @pl.when(index == blocks)
    def _():
        crossing(blocks - 2).wait_send()
        crossing(blocks - 1).wait_send()
        out[...] = out_acc[...].astype(jnp.bfloat16)
        grad_normed[...] = grad_acc[...].astype(jnp.bfloat16)

    @pl.when(index == blocks + 2)
    def _():
        for block in range(blocks):
            for side in range(2):
                hop(block, side, 0).wait_send()
                hop(block, side, 1).wait_send()


def glu_layer(normed, normed_t, top, top_t, weights, gate_bias, up_bias, seq_count):
    rows, width = normed.shape
    hidden_width = gate_bias.shape[0]
    blocks = hidden_width // BLOCK
    chips = seq_count // 2
    seg = width // seq_count
    kept = len(kept_places(seq_count))
    bf = jnp.bfloat16

    def whole(shape):
        return pl.BlockSpec(shape, lambda i: (0, 0), pipeline_mode=pl.Buffered(1))

    def at(lag):
        return lambda i: jnp.clip(i - lag, 0, blocks - 1)

    def weight_spec(which):
        return pl.BlockSpec((width, BLOCK), lambda i: (0, which * blocks + at(0)(i)))

    bias_spec = pl.BlockSpec((1, BLOCK), lambda i: (0, at(0)(i)))
    work = rows * width * hidden_width
    term_specs = [
        pl.BlockSpec((kept, 3, seg, BLOCK), lambda i: (0, 0, 0, at(1)(i))),
        pl.BlockSpec((2, 3, seg, BLOCK), lambda i: (0, 0, 0, at(3)(i))),
    ]
    term_shapes = [
        jax.ShapeDtypeStruct((kept, 3, seg, hidden_width), bf),
        jax.ShapeDtypeStruct((2, 3, seg, hidden_width), bf),
    ]
    return pl.pallas_call(
        functools.partial(glu_kernel, blocks, seq_count),
        grid=(blocks + 3,),
        in_specs=[
            whole((rows, width)),
            whole((width, rows)),
            whole((rows, width)),
            whole((width, rows)),
            weight_spec(0),
            weight_spec(1),
            weight_spec(2),
            bias_spec,
            bias_spec,
        ],
        out_specs=[
            pl.BlockSpec((rows, width), lambda i: (0, 0)),
            pl.BlockSpec((rows, width), lambda i: (0, 0)),
            pl.BlockSpec((2, BLOCK), lambda i: (0, at(0)(i))),
            *term_specs,
        ],
        out_shape=[
            jax.ShapeDtypeStruct((rows, width), bf),
            jax.ShapeDtypeStruct((rows, width), bf),
            jax.ShapeDtypeStruct((2, hidden_width), jnp.float32),
            *term_shapes,
        ],
        scratch_shapes=[
            pltpu.VMEM((rows, width), jnp.float32),
            pltpu.VMEM((rows, width), jnp.float32),
            pltpu.VMEM((2, 3, chips, 2, seg, BLOCK), bf),
            pltpu.VMEM((blocks, 3, chips, seg, BLOCK), bf),
            pltpu.SemaphoreType.DMA((2,)),
            pltpu.SemaphoreType.DMA((blocks,)),
            pltpu.VMEM((3, 3, chips, seg, BLOCK), bf),
            pltpu.VMEM((blocks, 2, 3, seg, BLOCK // 2), bf),
            pltpu.VMEM((blocks, 2, 3, seg, BLOCK // 2), bf),
            pltpu.VMEM((blocks, 2, 3, seg, BLOCK), bf),
            pltpu.VMEM((blocks, 2, 3, seg, BLOCK), bf),
            *(pltpu.SemaphoreType.DMA((blocks, 2)) for _ in range(4)),
        ],
        compiler_params=pltpu.CompilerParams(
            collective_id=1, has_side_effects=True, vmem_limit_bytes=VMEM_BYTES
        ),
        cost_estimate=pl.CostEstimate(
            flops=18 * work, bytes_accessed=12 * width * hidden_width, transcendentals=rows * hidden_width
        ),
        name="glu_layer",
    )(
        normed,
        normed_t,
        top,
        top_t,
        weights,
        weights,
        weights,
        gate_bias[None],
        up_bias[None],
    )


class ChipRing:
    def __init__(self, seq_count, pieces, sends, lands, send_sem, recv_sem):
        self.chips = seq_count // 2
        self.far = self.chips // 2
        self.pieces = pieces
        self.sends, self.lands = sends, lands
        self.send_sem, self.recv_sem = send_sem, recv_sem
        self.sides = ring_neighbours(lax.axis_index("seq"), seq_count)
        self.greeted = [{"seq": side} for side in self.sides]
        width = pieces[0].shape[2]
        self.near = [
            chip_near(lax.axis_index("seq"), seq_count, step) for step in range(self.chips)
        ]
        self.width, self.mid = width, width // 2

    def copy(self, piece, side, hop):
        mid = self.mid
        if hop == 0:
            source = self.pieces[piece].at[self.near[self.far], :, pl.ds(side * mid, mid)]
            target = self.lands.at[piece, side, 0, :, pl.ds(0, mid)]
        else:
            source = self.sends.at[piece, side, hop - 1]
            target = self.lands.at[piece, side, hop]
        return pltpu.make_async_remote_copy(
            src_ref=source,
            dst_ref=target,
            send_sem=self.send_sem.at[piece, side, hop],
            recv_sem=self.recv_sem.at[piece, side, hop],
            device_id={"seq": self.sides[side]},
            device_id_type=MESH,
        )

    def start(self, piece):
        for side in range(2):
            self.copy(piece, side, 0).start()

    def advance(self, piece, hop):
        mid = self.mid
        for side in range(2):
            near = self.far - hop if side == 0 else self.far + hop
            term = self.pieces[piece][self.near[near]].astype(jnp.float32)
            self.copy(piece, side, hop - 1).wait_recv()
            if hop == 1:
                land = self.lands[piece, side, 0, :, :mid].astype(jnp.float32)
                low = term[:, :mid] + land if side == 0 else term[:, :mid]
                high = term[:, mid:] if side == 0 else term[:, mid:] + land
                self.sends[piece, side, 0, :, :mid] = low.astype(jnp.bfloat16)
                self.sends[piece, side, 0, :, mid:] = high.astype(jnp.bfloat16)
            else:
                land = self.lands[piece, side, hop - 1].astype(jnp.float32)
                self.sends[piece, side, hop - 1] = (term + land).astype(jnp.bfloat16)
            self.copy(piece, side, hop).start()

    def total(self, piece):
        total = self.pieces[piece][self.near[0]].astype(jnp.float32)
        for side in range(2):
            self.copy(piece, side, self.far - 1).wait_recv()
            total = total + self.lands[piece, side, self.far - 1].astype(jnp.float32)
        return total

    def close(self):
        for piece in range(len(self.pieces)):
            for side in range(2):
                for hop in range(self.far):
                    self.copy(piece, side, hop).wait_send()


def ring_scratch(seq_count, pieces, seg, width):
    far = seq_count // 4
    return [
        pltpu.VMEM((pieces, 2, far - 1, seg, width), jnp.bfloat16),
        pltpu.VMEM((pieces, 2, far, seg, width), jnp.bfloat16),
        pltpu.SemaphoreType.DMA((pieces, 2, far)),
        pltpu.SemaphoreType.DMA((pieces, 2, far)),
    ]


def greet(devices):
    barrier = pltpu.get_barrier_semaphore()
    for device in devices:
        pl.semaphore_signal(barrier, inc=1, device_id=device, device_id_type=MESH)
    pl.semaphore_wait(barrier, len(devices))


class CoreSum:
    def __init__(self, partner, terms, arrived, send_sem, recv_sem):
        self.core = lax.axis_index("seq") % 2
        self.partner = partner
        self.terms, self.arrived = terms, arrived
        self.send_sem, self.recv_sem = send_sem, recv_sem

    def copy(self, piece):
        return pltpu.make_async_remote_copy(
            src_ref=self.terms.at[piece % self.terms.shape[0], :, 1 - self.core],
            dst_ref=self.arrived.at[piece],
            send_sem=self.send_sem.at[piece],
            recv_sem=self.recv_sem.at[piece],
            device_id=self.partner,
            device_id_type=MESH,
        )

    def start(self, piece, term):
        slot = piece % self.terms.shape[0]
        self.terms[slot] = term.astype(jnp.bfloat16).reshape(self.terms.shape[1:])
        self.copy(piece).start()

    def finish(self, piece):
        self.copy(piece).wait_recv()
        total = self.terms[piece % self.terms.shape[0], :, self.core].astype(jnp.float32)
        return (total + self.arrived[piece].astype(jnp.float32)).astype(jnp.bfloat16)

    def close(self, piece):
        self.copy(piece).wait_send()


def core_scratch(pieces, chips, seg, width, slots):
    return [
        pltpu.VMEM((slots, chips, 2, seg, width), jnp.bfloat16),
        pltpu.VMEM((pieces, chips, seg, width), jnp.bfloat16),
        pltpu.SemaphoreType.DMA((pieces,)),
        pltpu.SemaphoreType.DMA((pieces,)),
    ]


def through_norm(total, normal, inverse, gain):
    shaped = total * gain
    return (
        shaped
        - jnp.mean(shaped, axis=-1, keepdims=True)
        - normal * jnp.mean(shaped * normal, axis=-1, keepdims=True)
    ) * inverse


def tail_kernel(seq_count, head_count, made_count, clip_total, *refs):
    (
        rows_t,
        columns,
        weights,
        normal,
        inverse,
        gain,
        grad_h_one,
        placing,
        early,
        h_two,
        glu_own,
        glu_other,
        down_bias,
        out,
        small_out,
        frames_grad,
        result,
        mine,
        small_send,
        small_land,
        step_send,
        step_recv,
        split,
        split_land,
        split_send,
        split_recv,
        *refs,
    ) = refs
    core_refs, ring_refs = refs[:4], refs[4:]
    width = columns.shape[1] // made_count
    rows = grad_h_one.shape[0]
    late = placing.shape[0]
    ring = ChipRing(seq_count, [mine.at[made] for made in range(made_count)], *ring_refs)
    seq_index = lax.axis_index("seq")
    head_index = lax.axis_index("head")
    partners = []
    bit = 1
    while bit < seq_count:
        partners.append({"seq": xor_place(seq_index, bit)})
        bit *= 2
    seq_steps = len(partners)
    bit = 1
    while bit < head_count:
        partners.append({"head": xor_place(head_index, bit)})
        bit *= 2
    greet(ring.greeted + partners)
    cores = CoreSum(partners[0], *core_refs)

    def step_copy(step):
        count = small_out.shape[0] if step < seq_steps else late
        return pltpu.make_async_remote_copy(
            src_ref=small_send.at[step, pl.ds(0, count)],
            dst_ref=small_land.at[step, pl.ds(0, count)],
            send_sem=step_send.at[step],
            recv_sem=step_recv.at[step],
            device_id=partners[step],
            device_id_type=MESH,
        )

    def step_on(step):
        if step > 0:
            step_copy(step - 1).wait_recv()
            if step <= seq_steps:
                total = small_send[step - 1] + small_land[step - 1]
                if step == seq_steps:
                    small_out[late:, :] = total[late:]
                if step < len(partners):
                    small_send[step] = total
                else:
                    small_out[:late, :] = total[:late]
            else:
                total = small_send[step - 1, :late] + small_land[step - 1, :late]
                if step < len(partners):
                    small_send[step, :late] = total
                else:
                    small_out[:late, :] = total
        if step < len(partners):
            step_copy(step).start()

    def split_copy():
        return pltpu.make_async_remote_copy(
            src_ref=split,
            dst_ref=split_land,
            send_sem=split_send,
            recv_sem=split_recv,
            device_id=partners[seq_steps],
            device_id_type=MESH,
        )

    for made in range(made_count):
        cores.start(made, product(rows_t[...], columns[:, made * width : (made + 1) * width]))
    grad_normed = product_t(columns[...], weights[...])
    split[...] = grad_normed[:rows].astype(jnp.bfloat16)
    split_copy().start()
    row = lax.broadcasted_iota(jnp.int32, (late, 1), 0)
    gain_term = jnp.sum(grad_normed[:rows] * normal[...], axis=0, keepdims=True)
    first = jnp.where(row == clip_total, gain_term, 0.0)
    for slot in range(placing.shape[1]):
        first = first + placing[:, slot : slot + 1] * grad_normed[rows + slot : rows + slot + 1]
    small_send[0, :late, :] = first
    small_send[0, late:, :] = early[...]
    step_on(0)
    for made in range(made_count):
        mine[made] = cores.finish(made)
        ring.start(made)
    result[...] = (
        h_two[...]
        + (glu_own[...].astype(jnp.float32) + glu_other[...].astype(jnp.float32))
        + down_bias[...]
    ).astype(jnp.bfloat16)
    done = 1
    for hop in range(1, ring.far):
        for made in range(made_count):
            ring.advance(made, hop)
        while done <= len(partners) * hop // (ring.far - 1):
            step_on(done)
            done += 1
    split_copy().wait_recv()
    total = split[...].astype(jnp.float32) + split_land[...].astype(jnp.float32)
    back = through_norm(total, normal[...], inverse[...], gain[...])
    frames_grad[...] = (grad_h_one[...] + back).astype(jnp.bfloat16)
    for made in range(made_count):
        out[made] = ring.total(made)
    split_copy().wait_send()
    for made in range(made_count):
        cores.close(made)
    ring.close()
    for step in range(len(partners)):
        step_copy(step).wait_send()


def tail_sums(
    rows_t, columns, weights, norm, grad_h_one, placing, early, h_two, glu_terms, down_bias, clip_total, seq_count
):
    head_count = lax.axis_size("head")
    chips = seq_count // 2
    rows, wide = grad_h_one.shape
    seg = rows_t.shape[0] // seq_count
    width = TAIL_WIDTH
    made_count = columns.shape[1] // width
    steps = (seq_count - 1).bit_length() + (head_count - 1).bit_length()
    bf = jnp.bfloat16
    vmem = pl.BlockSpec(memory_space=pltpu.VMEM)
    small = (placing.shape[0] + early.shape[0], wide)
    return pl.pallas_call(
        functools.partial(tail_kernel, seq_count, head_count, made_count, clip_total),
        grid=(1,),
        in_specs=[
            vmem,
            vmem,
            pl.BlockSpec((wide, made_count * width), lambda i: (0, 0), pipeline_mode=pl.Buffered(1)),
            *[vmem] * 10,
        ],
        out_specs=[vmem] * 4,
        out_shape=[
            jax.ShapeDtypeStruct((made_count, seg, width), jnp.float32),
            jax.ShapeDtypeStruct(small, jnp.float32),
            jax.ShapeDtypeStruct((rows, wide), bf),
            jax.ShapeDtypeStruct((rows, wide), bf),
        ],
        scratch_shapes=[
            pltpu.VMEM((made_count, chips, seg, width), bf),
            pltpu.VMEM((steps, *small), jnp.float32),
            pltpu.VMEM((steps, *small), jnp.float32),
            pltpu.SemaphoreType.DMA((steps,)),
            pltpu.SemaphoreType.DMA((steps,)),
            pltpu.VMEM((rows, wide), bf),
            pltpu.VMEM((rows, wide), bf),
            pltpu.SemaphoreType.DMA,
            pltpu.SemaphoreType.DMA,
            *core_scratch(made_count, chips, seg, width, made_count),
            *ring_scratch(seq_count, made_count, seg, width),
        ],
        compiler_params=pltpu.CompilerParams(
            collective_id=2, has_side_effects=True, vmem_limit_bytes=VMEM_BYTES
        ),
        cost_estimate=pl.CostEstimate(
            flops=4 * rows_t.shape[0] * rows_t.shape[1] * columns.shape[1],
            bytes_accessed=32 * made_count * chips * seg * width,
            transcendentals=0,
        ),
        name="tail_sums",
    )(
        rows_t,
        columns,
        weights,
        *norm,
        grad_h_one,
        placing,
        early,
        h_two,
        *glu_terms,
        down_bias,
    )


def turned_back(values, tables):
    shift = ROT // 2
    return (
        values * tables[0]
        + pltpu.roll(values, LANES - shift, 1) * tables[1]
        - pltpu.roll(values, shift, 1) * tables[2]
    )


def self_back_kernel(seq_count, pairs, score_scale, *refs):
    (
        query,
        keys,
        values,
        stamp_key,
        stamp_value,
        grad_out,
        logs,
        key_ids,
        query_ids,
        query_slots,
        tables,
        ready,
        made_rows,
        made_columns,
        out,
        shares,
        mine,
        bias,
        acc,
        own,
        halo,
        halo_land,
        halo_send_sem,
        halo_recv_sem,
        *refs,
    ) = refs
    core_refs, ring_refs = refs[:4], refs[4:]
    ready_count = ready.shape[0]
    pair = pl.program_id(0)
    rows = query.shape[0]
    slots = stamp_key.shape[0]
    span = QUERY_BLOCK + 2 * HALF
    seq_index = lax.axis_index("seq")
    before = (seq_index + seq_count - 1) % seq_count
    behind = (seq_index + 1) % seq_count
    pieces = [*(ready.at[piece] for piece in range(ready_count)), mine]
    ring = ChipRing(seq_count, pieces, *ring_refs)
    partner = {"seq": xor_place(seq_index, 1)}
    cores = CoreSum(partner, *core_refs)

    def halo_copy(which, side):
        return pltpu.make_async_remote_copy(
            src_ref=halo.at[which, side],
            dst_ref=halo_land.at[which, side],
            send_sem=halo_send_sem.at[which, side],
            recv_sem=halo_recv_sem.at[which, side],
            device_id={"seq": before if side == 0 else behind},
            device_id_type=MESH,
        )

    @pl.when(pair == 0)
    def _():
        greet(ring.greeted + [partner, {"seq": before}, {"seq": behind}])
        for piece in range(ready_count):
            ring.start(piece)
        cores.start(0, product_tn(made_rows[...], made_columns[...]))
        for block in range(rows // QUERY_BLOCK):
            start = block * QUERY_BLOCK
            asked = query_ids[:, start : start + QUERY_BLOCK]
            key_row = lax.broadcasted_iota(jnp.int32, (span, QUERY_BLOCK), 0)
            query_row = lax.broadcasted_iota(jnp.int32, (span, QUERY_BLOCK), 1)
            away = key_row - HALF - query_row
            seen = (key_ids[start : start + span, :] == asked) & (jnp.abs(away) <= HALF)
            bias[block, :span, :] = jnp.where(seen, 0.0, NEG)
            slot_row = lax.broadcasted_iota(jnp.int32, (slots, QUERY_BLOCK), 0)
            bias[block, span:, :] = jnp.where(
                slot_row == query_slots[:, start : start + QUERY_BLOCK], 0.0, NEG
            )

    blocks = rows // QUERY_BLOCK
    order = [(piece, hop) for hop in range(1, ring.far) for piece in range(len(pieces))]
    due = [1 + at * (pairs * blocks - 1) // len(order) for at in range(len(order))]

    def ring_work(block):
        @pl.when(pair * blocks + block == MADE_AT)
        def _():
            mine[...] = cores.finish(0)
            ring.start(ready_count)

        for moment, (piece, hop) in zip(due, order):
            if moment % blocks == block:

                @pl.when(pair == moment // blocks)
                def _():
                    ring.advance(piece, hop)

    @pl.when(pair < pairs)
    def _():
        acc[...] = jnp.zeros_like(acc)
        lane = lax.broadcasted_iota(jnp.int32, (1, LANES), 1)
        stamp_k, stamp_v = stamp_key[...], stamp_value[...]
        grad_queries = []
        for block in range(rows // QUERY_BLOCK):
            start = block * QUERY_BLOCK
            near_k = jnp.concatenate([keys[0, start : start + span, :], stamp_k], axis=0)
            near_v = jnp.concatenate([values[0, start : start + span, :], stamp_v], axis=0)
            block_q = query[start : start + QUERY_BLOCK, :]
            block_g = grad_out[start : start + QUERY_BLOCK, :]
            grad_q = jnp.zeros((QUERY_BLOCK, LANES), jnp.float32)
            grad_k = jnp.zeros((span + slots, LANES), jnp.float32)
            grad_v = jnp.zeros((span + slots, LANES), jnp.float32)
            for head in range(LANES // HD):
                here = lane // HD == head
                head_q = jnp.where(here, block_q, jnp.zeros_like(block_q))
                head_g = jnp.where(here, block_g, jnp.zeros_like(block_g))
                head_k = jnp.where(here, near_k, jnp.zeros_like(near_k))
                scores = product_t(near_k, head_q) * score_scale + bias[block]
                probs = jnp.exp(scores - logs[0, head : head + 1, start : start + QUERY_BLOCK])
                grad_p = product_t(near_v, head_g)
                dot = jnp.sum(probs * grad_p, axis=0, keepdims=True)
                grad_s = (probs * (grad_p - dot)).astype(jnp.bfloat16)
                grad_k = grad_k + product(grad_s, head_q)
                grad_v = grad_v + product(probs.astype(jnp.bfloat16), head_g)
                grad_q = grad_q + product_tn(grad_s, head_k)
            grad_queries.append(grad_q)
            ring_work(block)
            acc[0, start : start + span, :] += grad_k[:span]
            acc[1, start : start + span, :] += grad_v[:span]
            acc[0, 2 * HALF + rows :, :] += grad_k[span:]
            acc[1, 2 * HALF + rows :, :] += grad_v[span:]
        column = pl.multiple_of(pair * LANES, LANES)
        grad_q = jnp.concatenate(grad_queries, axis=0) * score_scale
        out[:rows, pl.ds(column, LANES)] = turned_back(grad_q, tables).astype(jnp.bfloat16)
        out[rows:, pl.ds(column, LANES)] = jnp.zeros((slots, LANES), jnp.bfloat16)
        for which in range(2):
            scale = score_scale if which == 0 else 1.0
            shift = (which + 1) * pairs * LANES
            halo[pair, 0, which] = (acc[which, :HALF, :] * scale).astype(jnp.bfloat16)
            halo[pair, 1, which] = (acc[which, HALF + rows : 2 * HALF + rows, :] * scale).astype(
                jnp.bfloat16
            )
            own[pair, which] = acc[which, HALF : HALF + rows, :] * scale
            out[rows:, pl.ds(column + shift, LANES)] = (
                acc[which, 2 * HALF + rows :, :] * scale
            ).astype(jnp.bfloat16)

        @pl.when(seq_index > 0)
        def _():
            halo_copy(pair, 0).start()

        @pl.when(seq_index < seq_count - 1)
        def _():
            halo_copy(pair, 1).start()

    @pl.when(pair == pairs)
    def _():

        @pl.when(seq_index < seq_count - 1)
        def _():
            for which in range(pairs):
                halo_copy(which, 0).wait_recv()
                own[which, :, rows - HALF :, :] += halo_land[which, 0].astype(jnp.float32)

        @pl.when(seq_index > 0)
        def _():
            for which in range(pairs):
                halo_copy(which, 1).wait_recv()
                own[which, :, :HALF, :] += halo_land[which, 1].astype(jnp.float32)

        for which in range(pairs):
            column = (pairs + which) * LANES
            out[:rows, column : column + LANES] = turned_back(own[which, 0], tables).astype(
                jnp.bfloat16
            )
            column = (2 * pairs + which) * LANES
            out[:rows, column : column + LANES] = own[which, 1].astype(jnp.bfloat16)
        for piece in range(len(pieces)):
            shares[piece] = ring.total(piece)
        ring.close()
        cores.close(0)

        @pl.when(seq_index > 0)
        def _():
            for which in range(pairs):
                halo_copy(which, 0).wait_send()

        @pl.when(seq_index < seq_count - 1)
        def _():
            for which in range(pairs):
                halo_copy(which, 1).wait_send()


def self_back(
    query, near, stamps, grad_out, logs, key_ids, query_ids, query_slots, tables, ready, made_rows, made_columns, score_scale, seq_count
):
    rows, part = query.shape
    slots = stamps.shape[0]
    pairs = part // LANES
    window = near.shape[1]
    ready_count, chips, seg, width = ready.shape
    span = QUERY_BLOCK + 2 * HALF
    blocks = rows // QUERY_BLOCK
    last = pairs - 1

    def at(first, shape, lead=()):
        return pl.BlockSpec(shape, lambda i: (*lead, 0, first + jnp.minimum(i, last)))

    def whole(shape):
        return pl.BlockSpec(shape, lambda i: (0,) * len(shape), pipeline_mode=pl.Buffered(1))

    return pl.pallas_call(
        functools.partial(self_back_kernel, seq_count, pairs, score_scale),
        grid=(pairs + 1,),
        in_specs=[
            at(0, (rows, LANES)),
            at(0, (1, window, LANES), (0,)),
            at(0, (1, window, LANES), (1,)),
            at(pairs, (slots, LANES)),
            at(2 * pairs, (slots, LANES)),
            at(0, (rows, LANES)),
            pl.BlockSpec((1, LANES // HD, rows), lambda i: (jnp.minimum(i, last), 0, 0)),
            whole((window, 1)),
            whole((1, rows)),
            whole((1, rows)),
            whole((3, rows, LANES)),
            whole(ready.shape),
            whole(made_rows.shape),
            whole(made_columns.shape),
        ],
        out_specs=[
            pl.BlockSpec((rows + slots, 3 * part), lambda i: (0, 0)),
            pl.BlockSpec((ready_count + 1, seg, width), lambda i: (0, 0, 0)),
        ],
        out_shape=[
            jax.ShapeDtypeStruct((rows + slots, 3 * part), jnp.bfloat16),
            jax.ShapeDtypeStruct((ready_count + 1, seg, width), jnp.float32),
        ],
        scratch_shapes=[
            pltpu.VMEM((chips, seg, width), jnp.bfloat16),
            pltpu.VMEM((blocks, span + slots, QUERY_BLOCK), jnp.float32),
            pltpu.VMEM((2, window + slots, LANES), jnp.float32),
            pltpu.VMEM((pairs, 2, rows, LANES), jnp.float32),
            pltpu.VMEM((pairs, 2, 2, HALF, LANES), jnp.bfloat16),
            pltpu.VMEM((pairs, 2, 2, HALF, LANES), jnp.bfloat16),
            pltpu.SemaphoreType.DMA((pairs, 2)),
            pltpu.SemaphoreType.DMA((pairs, 2)),
            *core_scratch(1, chips, seg, width, 1),
            *ring_scratch(seq_count, ready_count + 1, seg, width),
        ],
        compiler_params=pltpu.CompilerParams(
            collective_id=3, has_side_effects=True, vmem_limit_bytes=VMEM_BYTES
        ),
        cost_estimate=pl.CostEstimate(
            flops=10 * rows * window * part,
            bytes_accessed=16 * chips * seg * width * (ready_count + 1),
            transcendentals=rows * window * part // HD,
        ),
        name="self_back",
    )(
        query,
        near,
        near,
        stamps,
        stamps,
        grad_out,
        logs.reshape(pairs, LANES // HD, rows),
        key_ids[:, None],
        query_ids[None],
        query_slots[None],
        tables,
        ready,
        made_rows,
        made_columns,
    )


def mid_kernel(seq_count, head_count, score_scale, ctx_tokens, *refs):
    (
        grad_low,
        top,
        normal_three,
        inverse_three,
        normal_two,
        inverse_two,
        gains,
        c_out,
        c_query,
        w_out,
        query,
        key,
        value,
        logs,
        query_slots,
        cross_mixed,
        normed_two,
        context,
        kept,
        moving,
        grad_h_one,
        grad_two_low,
        grad_one_low,
        grad_attn,
        grad_query,
        ctx_grads,
        gain_terms,
        share,
        core_sums,
        grad_mix,
        split,
        split_land,
        split_send,
        split_recv,
        third_land,
        fourth_land,
        third_sems,
        fourth_sems,
        keep,
        keep_sems,
        *core_refs,
    ) = refs
    seq_index = lax.axis_index("seq")
    head_index = lax.axis_index("head")
    others = [{"head": (head_index + 1 + step) % head_count} for step in range(head_count - 1)]
    sides = ring_neighbours(seq_index, seq_count)
    partner = {"seq": xor_place(seq_index, 1)}
    cores = CoreSum(partner, *core_refs)
    greet([*others, partner] + [{"seq": side} for side in sides])

    def hop(side, which):
        sems = fourth_sems if which else third_sems
        return pltpu.make_async_remote_copy(
            src_ref=third_land.at[side] if which else moving.at[side],
            dst_ref=(fourth_land if which else third_land).at[side],
            send_sem=sems.at[0, side],
            recv_sem=sems.at[1, side],
            device_id={"seq": sides[side]},
            device_id_type=MESH,
        )

    def keep_copy(which):
        at = (1, kept.shape[0] - 1, 0)[which]
        return pltpu.make_async_copy(kept.at[at], keep.at[which % 2], keep_sems.at[which])

    def third_to_fourth():
        for side in range(2):
            hop(side, 0).wait_recv()
            keep_copy(side).wait()
            term = keep[side].astype(jnp.float32) + third_land[side].astype(jnp.float32)
            third_land[side] = term.astype(jnp.bfloat16)
            hop(side, 1).start()
        keep_copy(2).start()

    def over_heads(which, step):
        return pltpu.make_async_remote_copy(
            src_ref=grad_low if which == 0 else split,
            dst_ref=split_land.at[which, step],
            send_sem=split_send.at[which, step],
            recv_sem=split_recv.at[which, step],
            device_id=others[step],
            device_id_type=MESH,
        )

    def summed(which):
        total = (grad_low if which == 0 else split)[...].astype(jnp.float32)
        for step in range(head_count - 1):
            over_heads(which, step).wait_recv()
            total = total + split_land[which, step].astype(jnp.float32)
        return total

    for step in range(head_count - 1):
        over_heads(0, step).start()
    hop(0, 0).start()
    hop(1, 0).start()
    keep_copy(0).start()
    keep_copy(1).start()
    gain_terms[...] = jnp.zeros_like(gain_terms)
    total = summed(0)
    normal = normal_three[...]
    gain_terms[0:1, :] = jnp.sum(total * normal, axis=0, keepdims=True)
    grad_h_one[...] = top[...].astype(jnp.float32) + through_norm(
        total, normal, inverse_three[...], gains[0:1, :]
    )
    grad_two_low[...] = grad_h_one[...].astype(jnp.bfloat16)
    grad_mix[...] = product(grad_two_low[...], c_out[...]).astype(jnp.bfloat16)
    cores.start(0, product_tn(grad_two_low[...], cross_mixed[...]))
    rows = query.shape[0]
    keys = key.shape[0]
    pairs = query.shape[1] // LANES
    token_slot = lax.broadcasted_iota(jnp.int32, (keys, 1), 0) // ctx_tokens
    bias = jnp.where(token_slot == query_slots[...], 0.0, NEG)
    lane = lax.broadcasted_iota(jnp.int32, (1, LANES), 1)
    for pair in range(pairs):
        columns = slice(pair * LANES, (pair + 1) * LANES)
        pair_q, pair_g = query[:, columns], grad_mix[:, columns]
        pair_k, pair_v = key[:, columns], value[:, columns]
        grad_q = jnp.zeros((rows, LANES), jnp.float32)
        grad_k = jnp.zeros((keys, LANES), jnp.float32)
        grad_v = jnp.zeros((keys, LANES), jnp.float32)
        for head in range(LANES // HD):
            here = lane // HD == head
            head_q = jnp.where(here, pair_q, jnp.zeros_like(pair_q))
            head_g = jnp.where(here, pair_g, jnp.zeros_like(pair_g))
            head_k = jnp.where(here, pair_k, jnp.zeros_like(pair_k))
            at = pair * (LANES // HD) + head
            scores = product_t(pair_k, head_q) * score_scale + bias
            probs = jnp.exp(scores - logs[at : at + 1, :])
            grad_p = product_t(pair_v, head_g)
            dot = jnp.sum(probs * grad_p, axis=0, keepdims=True)
            grad_s = (probs * (grad_p - dot)).astype(jnp.bfloat16)
            grad_k = grad_k + product(grad_s, head_q)
            grad_v = grad_v + product(probs.astype(jnp.bfloat16), head_g)
            grad_q = grad_q + product_tn(grad_s, head_k)
        grad_query[:, columns] = (grad_q * score_scale).astype(jnp.bfloat16)
        ctx_grads[:, columns] = (grad_k * score_scale).astype(jnp.bfloat16)
        second = slice((pairs + pair) * LANES, (pairs + pair + 1) * LANES)
        ctx_grads[:, second] = grad_v.astype(jnp.bfloat16)
        if pair == HOP_PAIR:
            third_to_fourth()
    split[...] = product_t(grad_query[...], c_query[...]).astype(jnp.bfloat16)
    for step in range(head_count - 1):
        over_heads(1, step).start()
    cores.start(1, product_tn(normed_two[...], grad_query[...]))
    part = query.shape[1]
    core_sums[0] = cores.finish(0)
    cores.close(0)
    ctx_rows = cores.terms.shape[3] // 2
    for which in range(2):
        term = product_tn(context[...], ctx_grads[:, which * part : (which + 1) * part])
        term = term.astype(jnp.bfloat16).reshape(-1, 2, ctx_rows, part)
        cores.terms[0, :, :, which * ctx_rows : (which + 1) * ctx_rows, :] = term
    cores.copy(2).start()
    for piece in range(1, 3):
        core_sums[piece] = cores.finish(piece)
    total = summed(1)
    normal = normal_two[...]
    gain_terms[1:2, :] = jnp.sum(total * normal, axis=0, keepdims=True)
    grad_h_one[...] += through_norm(
        total, normal, inverse_two[...], gains[1:2, :]
    )
    grad_one_low[...] = grad_h_one[...].astype(jnp.bfloat16)
    grad_attn[...] = product(grad_one_low[...], w_out[...]).astype(jnp.bfloat16)
    keep_copy(2).wait()
    whole = keep[0].astype(jnp.float32)
    for side in range(2):
        hop(side, 1).wait_recv()
        whole = whole + fourth_land[side].astype(jnp.float32)
    share[...] = whole
    for side in range(2):
        hop(side, 0).wait_send()
        hop(side, 1).wait_send()
    for piece in range(1, 3):
        cores.close(piece)
    for which in range(2):
        for step in range(head_count - 1):
            over_heads(which, step).wait_send()


def mid_layer(
    grad_low, top, thirds, seconds, gains, weights, query, key, value, logs, slots, cross_mixed, normed_two, context, kept, moving, ctx_tokens, seq_count
):
    rows, width = grad_low.shape
    part = query.shape[1]
    keys = key.shape[0]
    head_count = lax.axis_size("head")
    chips, moved = seq_count // 2, moving.shape
    seg = moved[2]
    bf, wide = jnp.bfloat16, jnp.float32
    vmem = pl.BlockSpec(memory_space=pltpu.VMEM)

    def weight_spec(which):
        return pl.BlockSpec((width, part), lambda i: (0, which), pipeline_mode=pl.Buffered(1))

    scratches = [
        pltpu.VMEM((rows, part), bf),
        pltpu.VMEM((rows, width), bf),
        pltpu.VMEM((2, head_count - 1, rows, width), bf),
        pltpu.SemaphoreType.DMA((2, head_count - 1)),
        pltpu.SemaphoreType.DMA((2, head_count - 1)),
    ]
    out_shapes = [
        jax.ShapeDtypeStruct((rows, width), wide),
        jax.ShapeDtypeStruct((rows, width), bf),
        jax.ShapeDtypeStruct((rows, width), bf),
        jax.ShapeDtypeStruct((rows, part), bf),
        jax.ShapeDtypeStruct((rows, part), bf),
        jax.ShapeDtypeStruct((keys, 2 * part), bf),
        jax.ShapeDtypeStruct((8, width), wide),
    ]
    scratches += [
        pltpu.VMEM(moved, bf),
        pltpu.VMEM(moved, bf),
        pltpu.SemaphoreType.DMA((2, 2)),
        pltpu.SemaphoreType.DMA((2, 2)),
        pltpu.VMEM((2, *moved[1:]), bf),
        pltpu.SemaphoreType.DMA((3,)),
        *core_scratch(3, chips, seg, part, 2),
    ]
    out_shapes += [
        jax.ShapeDtypeStruct(moved[1:], wide),
        jax.ShapeDtypeStruct((3, chips, seg, part), bf),
    ]
    return pl.pallas_call(
        functools.partial(
            mid_kernel, seq_count, head_count, HD ** (-0.5), ctx_tokens
        ),
        grid=(1,),
        in_specs=[
            *[vmem] * 7,
            weight_spec(5),
            weight_spec(4),
            weight_spec(3),
            *[vmem] * 8,
            pl.BlockSpec(memory_space=pl.ANY),
            pl.BlockSpec(memory_space=pl.ANY),
        ],
        out_specs=[vmem] * len(out_shapes),
        out_shape=out_shapes,
        scratch_shapes=scratches,
        compiler_params=pltpu.CompilerParams(
            collective_id=6, has_side_effects=True, vmem_limit_bytes=VMEM_BYTES
        ),
        cost_estimate=pl.CostEstimate(
            flops=10 * rows * keys * part + 6 * rows * width * part,
            bytes_accessed=100 * rows * width,
            transcendentals=rows * keys * part // HD,
        ),
        name="mid_layer",
    )(
        grad_low,
        top,
        *thirds,
        *seconds,
        gains,
        weights,
        weights,
        weights,
        query,
        key,
        value,
        logs,
        slots[None],
        cross_mixed,
        normed_two,
        context,
        kept,
        moving,
    )


def head_total(partial_sum):
    low = partial_sum
    if low.dtype != jnp.bfloat16:
        low = lax.optimization_barrier(partial_sum.astype(jnp.bfloat16))
    count = lax.axis_size("head")
    total = low.astype(jnp.float32)
    for step in range(1, count):
        pairs = [(index, (index + step) % count) for index in range(count)]
        total = total + lax.ppermute(low, "head", pairs).astype(jnp.float32)
    return total


def low_gather(block):
    return lax.all_gather(block.astype(jnp.bfloat16), "seq", axis=0, tiled=True)


def per_device(
    frames,
    time_token,
    prompt,
    clip_ids,
    norm1_gain,
    norm2_gain,
    norm3_gain,
    query_weight,
    key_weight,
    value_weight,
    out_weight,
    cross_query,
    cross_key,
    cross_value,
    cross_out,
    gate_weight,
    up_weight,
    down_weight,
    gate_bias,
    up_bias,
    down_bias,
    out_grad,
):
    local_rows, width = frames.shape
    clip_total = time_token.shape[0]
    ctx_tokens = prompt.shape[1]
    slot_count = local_rows // (2 * HALF) + 2
    seq_count = lax.axis_size("seq")
    seq_index = lax.axis_index("seq")
    head_index = lax.axis_index("head")
    first_row = seq_index * local_rows
    score_scale = HD ** (-0.5)
    part = query_weight.shape[1]
    hidden_width = gate_weight.shape[1]
    gain_rows = norm1_gain.shape[0]
    ctx_rows = cross_key.shape[0]
    ctx_width = prompt.shape[2]
    head_count = part // HD
    bias_rows = 2 * hidden_width // width
    small_rows = -(-max(clip_total + 1, bias_rows + 3) // 8) * 8
    vectors = jnp.stack([norm1_gain, norm2_gain, norm3_gain, down_bias], axis=1)
    vectors = jnp.pad(vectors, ((0, 0), (0, LANES - 4)))
    ctx_pair = jnp.concatenate([cross_key, cross_value], axis=0)
    attn_local = jnp.concatenate(
        [
            query_weight,
            key_weight,
            value_weight,
            out_weight,
            cross_query,
            cross_out,
            ctx_pair,
            vectors,
        ],
        axis=1,
    )
    starts = [each * part for each in range(8)]
    attn_weights, token = ring_gather(
        attn_local, (*starts[:7], starts[7] + LANES), seq_count, 4
    )
    glu_local = jnp.concatenate([gate_weight, up_weight, down_weight], axis=1).astype(jnp.bfloat16)
    token, glu_local = lax.optimization_barrier((token, glu_local))
    glu_weights = low_gather(glu_local)
    w_qkv = attn_weights[:, : starts[3]]
    w_out = attn_weights[:, starts[3] : starts[4]]
    c_query = attn_weights[:, starts[4] : starts[5]]
    c_out = attn_weights[:, starts[5] : starts[6]]
    ctx_weights = attn_weights[:, starts[6] : starts[7]].reshape(seq_count, 2, ctx_rows, part)
    c_key = ctx_weights[:, 0].reshape(ctx_width, part)
    c_value = ctx_weights[:, 1].reshape(ctx_width, part)
    rows_of = attn_weights[:, starts[7] : starts[7] + 8].astype(jnp.float32).T + token[0, 0]
    gain_one_f, gain_two_f, gain_three_f, bias_f = rows_of[0], rows_of[1], rows_of[2], rows_of[3]

    positions = first_row + jnp.arange(local_rows, dtype=jnp.int32)
    cos_table, sin_table = angles(positions)
    padded_ids = jnp.pad(clip_ids, (HALF, HALF), constant_values=-1)
    own_ids = lax.dynamic_slice_in_dim(clip_ids, first_row, local_rows)
    near_ids = lax.dynamic_slice_in_dim(padded_ids, first_row, local_rows + 2 * HALF)
    base_clip = jnp.minimum(own_ids[0], clip_total - slot_count)
    own_slot = own_ids - base_clip
    slot_range = jnp.arange(slot_count, dtype=jnp.int32)
    pad_rows = -slot_count % 16
    stamp_end = local_rows + slot_count

    stamp_rows = lax.dynamic_slice_in_dim(time_token, base_clip, slot_count, 0)
    source = jnp.concatenate(
        [frames, jnp.pad(stamp_rows, ((0, pad_rows), (0, 0)))], axis=0
    ).astype(jnp.float32)
    normed_out, normal_one, inverse_one = layer_norm_parts(source, gain_one_f)
    normed_one = normed_out.astype(jnp.bfloat16)
    frames_f = source[:local_rows]
    qkv = product(normed_one, w_qkv)
    query_rows = rotate(qkv[:local_rows, :part], cos_table, sin_table).astype(jnp.bfloat16)
    key_rows = rotate(qkv[:local_rows, part : 2 * part], cos_table, sin_table).astype(jnp.bfloat16)
    value_rows = qkv[:local_rows, 2 * part :].astype(jnp.bfloat16)
    near = extended(jnp.stack([key_rows, value_rows]), (("seq", 1),), HALF)
    window = local_rows + 2 * HALF
    near_key_h = near[0].reshape(window, head_count, HD)
    near_value_h = near[1].reshape(window, head_count, HD)
    query_h = query_rows.reshape(local_rows, head_count, HD)
    stamps = qkv[local_rows:].astype(jnp.bfloat16)
    stamp_key_h = stamps[:slot_count, part : 2 * part].reshape(slot_count, head_count, HD)
    stamp_value_h = stamps[:slot_count, 2 * part :].reshape(slot_count, head_count, HD)

    query_pos = jnp.arange(local_rows, dtype=jnp.int32)
    key_pos = jnp.arange(window, dtype=jnp.int32) - HALF
    visible = (own_ids[:, None] == near_ids[None, :]) & (
        jnp.abs(query_pos[:, None] - key_pos[None, :]) <= HALF
    )
    own_stamp = own_slot[:, None] == slot_range[None, :]
    self_keys = [(near_key_h, near_value_h, visible), (stamp_key_h, stamp_value_h, own_stamp)]
    attn_mix_h, self_logs = attend_forward(query_h, self_keys, score_scale)
    attn_mixed = attn_mix_h.reshape(local_rows, part).astype(jnp.bfloat16)
    h_one = frames_f + head_total(product_t(attn_mixed, w_out))
    middle_out, normal_two, inverse_two = layer_norm_parts(h_one, gain_two_f)
    normed_two = middle_out.astype(jnp.bfloat16)
    cross_rows = product(normed_two, c_query).astype(jnp.bfloat16)
    cross_h = cross_rows.reshape(local_rows, head_count, HD)
    context_rows = lax.dynamic_slice_in_dim(prompt, base_clip, slot_count, 0).reshape(
        slot_count * ctx_tokens, ctx_width
    )
    ctx_keys = product(context_rows, c_key).astype(jnp.bfloat16)
    ctx_key_h = ctx_keys.reshape(slot_count * ctx_tokens, head_count, HD)
    ctx_values = product(context_rows, c_value).astype(jnp.bfloat16)
    ctx_value_h = ctx_values.reshape(slot_count * ctx_tokens, head_count, HD)
    key_slot = jnp.arange(slot_count * ctx_tokens, dtype=jnp.int32) // ctx_tokens
    cross_keys = [(ctx_key_h, ctx_value_h, own_slot[:, None] == key_slot[None, :])]
    cross_mix_h, cross_logs = attend_forward(cross_h, cross_keys, score_scale)
    cross_mixed = cross_mix_h.reshape(local_rows, part).astype(jnp.bfloat16)
    h_two = h_one + head_total(product_t(cross_mixed, c_out))
    third_out, normal_three, inverse_three = layer_norm_parts(h_two, gain_three_f)
    normed_three = third_out.astype(jnp.bfloat16)

    glu_out, grad_normed_low, bias_local, glu_kept, glu_moving = glu_layer(
        normed_three,
        normed_three.T,
        out_grad,
        out_grad.T,
        glu_weights,
        gate_bias,
        up_bias,
        seq_count,
    )
    (
        grad_h_one,
        grad_two_low,
        grad_one_low,
        grad_attn,
        grad_cross_query,
        ctx_grads,
        gain_terms,
        glu_share,
        cross_sums,
    ) = mid_layer(
        grad_normed_low,
        out_grad,
        (normal_three, inverse_three),
        (normal_two, inverse_two),
        jnp.stack([gain_three_f, gain_two_f]),
        attn_weights,
        cross_rows,
        ctx_keys,
        ctx_values,
        cross_logs,
        own_slot,
        cross_mixed,
        normed_two,
        context_rows,
        glu_kept,
        glu_moving,
        ctx_tokens,
        seq_count,
    )
    gain_three_term, gain_two_term = gain_terms[0], gain_terms[1]
    down_bias_term = jnp.sum(out_grad.astype(jnp.float32), axis=0)
    grad_attn, glu_out = lax.optimization_barrier((grad_attn, glu_out))
    head_pairs = [(index, index ^ 1) for index in range(lax.axis_size("head"))]
    glu_other = lax.ppermute(glu_out, "head", head_pairs)
    ones = jnp.ones((local_rows, HD - ROT), jnp.float32)
    flat = jnp.zeros((local_rows, ROT // 2), jnp.float32)
    low_side = [sin_table, flat, 0 * ones]
    high_side = [flat, sin_table, 0 * ones]
    tables = jnp.stack(
        [
            jnp.tile(jnp.concatenate(each, axis=1), (1, LANES // HD))
            for each in ([cos_table, cos_table, ones], low_side, high_side)
        ]
    )
    grad_qkv, early_share = self_back(
        query_rows,
        near,
        stamps,
        grad_attn,
        self_logs,
        near_ids,
        own_ids,
        own_slot,
        tables,
        cross_sums,
        grad_one_low,
        attn_mixed,
        score_scale,
        seq_count,
    )
    early_rows = jnp.concatenate(
        [
            bias_local.reshape(-1, width),
            jnp.stack([gain_two_term, gain_three_term, down_bias_term]),
        ],
        axis=0,
    )
    early_rows = jnp.pad(early_rows, ((0, small_rows - bias_rows - 3), (0, 0)))
    clip_range = jnp.arange(small_rows, dtype=jnp.int32)
    placing = (clip_range[:, None] - base_clip == slot_range[None, :]).astype(jnp.float32)
    qkv_share, small, frames_grad, result = tail_sums(
        normed_one.T,
        grad_qkv,
        attn_weights,
        (normal_one[:local_rows], inverse_one[:local_rows], gain_one_f[None]),
        grad_h_one,
        placing,
        early_rows,
        h_two,
        (glu_out, glu_other),
        bias_f[None],
        clip_total,
        seq_count,
    )
    cross_out_share, cross_query_share, ctx_share, out_share = early_share
    late = small[: clip_total + 1]
    early = small[small_rows : small_rows + bias_rows + 3]
    stamp_sum = late[:clip_total]
    own_bias = early[:-3].reshape(2, hidden_width)
    every_out, every_normal, every_inverse = layer_norm_parts(
        time_token.astype(jnp.float32), gain_one_f
    )
    time_grad = norm_back(stamp_sum, every_normal, every_inverse, gain_one_f)
    time_gain = jnp.sum(stamp_sum * every_normal, axis=0)
    gains_own = lax.dynamic_slice_in_dim(
        jnp.concatenate([late[clip_total:] + time_gain[None], early[-3:]], axis=0),
        seq_index * gain_rows,
        gain_rows,
        1,
    )
    return (
        result,
        frames_grad,
        time_grad,
        gains_own[0],
        gains_own[1],
        gains_own[2],
        qkv_share[0],
        qkv_share[1],
        qkv_share[2],
        out_share,
        cross_query_share,
        ctx_share[:ctx_rows],
        ctx_share[ctx_rows:],
        cross_out_share,
        glu_share[0],
        glu_share[1],
        glu_share[2],
        own_bias[0],
        own_bias[1],
        gains_own[3],
    )


def solution(mesh):
    in_specs = (
        P("seq", None),
        P(),
        P(),
        P(),
        P("seq"),
        P("seq"),
        P("seq"),
        P("seq", "head"),
        P("seq", "head"),
        P("seq", "head"),
        P("seq", "head"),
        P("seq", "head"),
        P("seq", "head"),
        P("seq", "head"),
        P("seq", "head"),
        P("seq", "head"),
        P("seq", "head"),
        P("seq", "head"),
        P("head"),
        P("head"),
        P("seq"),
        P("seq", None),
    )
    out_specs = (
        P("seq", None),
        P("seq", None),
        P(),
        P("seq"),
        P("seq"),
        P("seq"),
        P("seq", "head"),
        P("seq", "head"),
        P("seq", "head"),
        P("seq", "head"),
        P("seq", "head"),
        P("seq", "head"),
        P("seq", "head"),
        P("seq", "head"),
        P("seq", "head"),
        P("seq", "head"),
        P("seq", "head"),
        P("head"),
        P("head"),
        P("seq"),
    )
    fast = mesh.shape["seq"] == FAST_SEQ
    return jax.shard_map(
        per_device if fast else per_device_plain, mesh=mesh, in_specs=in_specs, out_specs=out_specs, check_vma=False
    )
```

```python
import functools
from functools import reduce

import jax
import jax.numpy as jnp
from jax import lax
from jax.experimental import pallas as pl
from jax.experimental.pallas import tpu as pltpu
from jax.sharding import PartitionSpec as P

HD = 64
ROT = 32
HALF = 256


EPS = 1e-05
NEG = -1e30


def extended(block, sides, width):
    for axis, dim in sides:
        count = lax.axis_size(axis)
        forward = [(i, i + 1) for i in range(count - 1)]
        backward = [(target, source) for source, target in forward]
        low = lax.ppermute(
            lax.slice_in_dim(block, block.shape[dim] - width, None, axis=dim), axis, forward
        )
        high = lax.ppermute(lax.slice_in_dim(block, 0, width, axis=dim), axis, backward)
        block = jnp.concatenate([low, block, high], axis=dim)
    return block


def passed_along(value, axis, steps):
    count = lax.axis_size(axis)
    first, last = (max(0, -steps), min(count, count - steps))
    return lax.ppermute(value, axis, [(source, source + steps) for source in range(first, last)])


def layer_norm_parts(values, gain):
    average = jnp.mean(values, axis=-1, keepdims=True)
    centered = values - average
    spread = jnp.mean(centered * centered, axis=-1, keepdims=True)
    inverse = lax.rsqrt(spread + EPS)
    normal = centered * inverse
    return (normal * gain, normal, inverse)


def norm_back(grad_out, normal, inverse, gain):
    shaped = grad_out * gain
    return (
        shaped
        - jnp.mean(shaped, axis=-1, keepdims=True)
        - normal * jnp.mean(shaped * normal, axis=-1, keepdims=True)
    ) * inverse


def angles(positions):
    ladder = jnp.arange(ROT // 2, dtype=jnp.float32)
    frequency = 10000.0 ** (-2.0 * ladder / ROT)
    phases = positions.astype(jnp.float32)[:, None] * frequency[None, :]
    return (jnp.cos(phases), jnp.sin(phases))


def rotate(values, cos_table, sin_table):
    shaped = values.reshape(values.shape[0], -1, HD)
    rot_half = ROT // 2
    leading = shaped[:, :, :rot_half]
    trailing = shaped[:, :, rot_half:ROT]
    cos_row = cos_table[:, None, :]
    sin_row = sin_table[:, None, :]
    turned = jnp.concatenate(
        [
            leading * cos_row - trailing * sin_row,
            trailing * cos_row + leading * sin_row,
            shaped[:, :, ROT:],
        ],
        axis=-1,
    )
    return turned.reshape(values.shape)


def product(matrix_a, matrix_b):
    return jnp.dot(matrix_a, matrix_b, preferred_element_type=jnp.float32)


def product_t(matrix_a, matrix_b):
    return lax.dot_general(
        matrix_a, matrix_b, (((1,), (1,)), ((), ())), preferred_element_type=jnp.float32
    )


def product_tn(matrix_a, matrix_b):
    return lax.dot_general(
        matrix_a, matrix_b, (((0,), (0,)), ((), ())), preferred_element_type=jnp.float32
    )


def exact_t(matrix_a, matrix_b):
    return lax.dot_general(
        matrix_a,
        matrix_b,
        (((1,), (1,)), ((), ())),
        precision=lax.Precision.HIGHEST,
        preferred_element_type=jnp.float32,
    )


def exact_tn(matrix_a, matrix_b):
    return lax.dot_general(
        matrix_a,
        matrix_b,
        (((0,), (0,)), ((), ())),
        precision=lax.Precision.HIGHEST,
        preferred_element_type=jnp.float32,
    )


def score_parts(query_h, key_parts, score_scale):
    return [
        jnp.where(
            visible[None],
            jnp.einsum("qhd,khd->hqk", query_h, key_h, preferred_element_type=jnp.float32)
            * score_scale,
            NEG,
        )
        for key_h, value_h, visible in key_parts
    ]


def attend_forward(query_h, key_parts, score_scale):
    scores = score_parts(query_h, key_parts, score_scale)
    row_peak = reduce(jnp.maximum, [jnp.max(score_part, axis=-1) for score_part in scores])
    exp_parts = [jnp.exp(score_part - row_peak[:, :, None]) for score_part in scores]
    row_total = reduce(jnp.add, [jnp.sum(exp_part, axis=-1) for exp_part in exp_parts])
    attn_mixed = reduce(
        jnp.add,
        [
            jnp.einsum(
                "hqk,khd->qhd",
                (exp_part / row_total[:, :, None]).astype(jnp.bfloat16),
                key_part[1],
                preferred_element_type=jnp.float32,
            )
            for exp_part, key_part in zip(exp_parts, key_parts)
        ],
    )
    return (attn_mixed, row_peak + jnp.log(row_total))


def attend_backward(query_h, key_parts, score_scale, log_total, grad_h):
    scores = score_parts(query_h, key_parts, score_scale)
    prob_parts = [jnp.exp(score_part - log_total[:, :, None]) for score_part in scores]
    dprob_parts = [
        jnp.einsum("qhd,khd->hqk", grad_h, key_part[1], preferred_element_type=jnp.float32)
        for key_part in key_parts
    ]
    row_dot = reduce(
        jnp.add,
        [
            jnp.sum(prob_part * dprob_part, axis=-1)
            for prob_part, dprob_part in zip(prob_parts, dprob_parts)
        ],
    )
    dscore_parts = [
        (prob_part * (dprob_part - row_dot[:, :, None])).astype(jnp.bfloat16)
        for prob_part, dprob_part in zip(prob_parts, dprob_parts)
    ]
    grad_query = (
        reduce(
            jnp.add,
            [
                jnp.einsum(
                    "hqk,khd->qhd", dscore_part, key_part[0], preferred_element_type=jnp.float32
                )
                for dscore_part, key_part in zip(dscore_parts, key_parts)
            ],
        )
        * score_scale
    )
    grad_keys = [
        jnp.einsum("hqk,qhd->khd", dscore_part, query_h, preferred_element_type=jnp.float32)
        * score_scale
        for dscore_part in dscore_parts
    ]
    grad_values = [
        jnp.einsum(
            "hqk,qhd->khd",
            prob_part.astype(jnp.bfloat16),
            grad_h,
            preferred_element_type=jnp.float32,
        )
        for prob_part in prob_parts
    ]
    return (grad_query, grad_keys, grad_values)


def per_device_plain(
    frames,
    time_token,
    prompt,
    clip_ids,
    norm1_gain,
    norm2_gain,
    norm3_gain,
    query_weight,
    key_weight,
    value_weight,
    out_weight,
    cross_query,
    cross_key,
    cross_value,
    cross_out,
    gate_weight,
    up_weight,
    down_weight,
    gate_bias,
    up_bias,
    down_bias,
    out_grad,
):
    local_rows = frames.shape[0]
    clip_total = time_token.shape[0]
    ctx_tokens = prompt.shape[1]
    slot_count = local_rows // (2 * HALF) + 2
    seq_index = lax.axis_index("seq")
    head_index = lax.axis_index("head")
    first_row = seq_index * local_rows
    score_scale = HD ** (-0.5)
    block_rows = min(local_rows, 2 * HALF)
    block_count = local_rows // block_rows
    window = block_rows + 2 * HALF
    block_indices = jnp.arange(block_count, dtype=jnp.int32)

    def branch_total(partial_sum):
        return lax.psum(partial_sum.astype(jnp.bfloat16), "head").astype(jnp.float32)

    def back_total(partial_sum):
        return lax.psum(partial_sum.astype(jnp.bfloat16), "head").astype(jnp.float32)

    (
        gain_one,
        gain_two,
        gain_three,
        w_query,
        w_key,
        w_value,
        w_out,
        c_query,
        c_key,
        c_value,
        c_out,
        w_gate,
        w_up,
        w_down,
        b_down,
    ) = (
        lax.all_gather(norm1_gain.astype(jnp.bfloat16), "seq", axis=0, tiled=True),
        lax.all_gather(norm2_gain.astype(jnp.bfloat16), "seq", axis=0, tiled=True),
        lax.all_gather(norm3_gain.astype(jnp.bfloat16), "seq", axis=0, tiled=True),
        lax.all_gather(query_weight.astype(jnp.bfloat16), "seq", axis=0, tiled=True),
        lax.all_gather(key_weight.astype(jnp.bfloat16), "seq", axis=0, tiled=True),
        lax.all_gather(value_weight.astype(jnp.bfloat16), "seq", axis=0, tiled=True),
        lax.all_gather(out_weight.astype(jnp.bfloat16), "seq", axis=0, tiled=True),
        lax.all_gather(cross_query.astype(jnp.bfloat16), "seq", axis=0, tiled=True),
        lax.all_gather(cross_key.astype(jnp.bfloat16), "seq", axis=0, tiled=True),
        lax.all_gather(cross_value.astype(jnp.bfloat16), "seq", axis=0, tiled=True),
        lax.all_gather(cross_out.astype(jnp.bfloat16), "seq", axis=0, tiled=True),
        lax.all_gather(gate_weight.astype(jnp.bfloat16), "seq", axis=0, tiled=True),
        lax.all_gather(up_weight.astype(jnp.bfloat16), "seq", axis=0, tiled=True),
        lax.all_gather(down_weight.astype(jnp.bfloat16), "seq", axis=0, tiled=True),
        lax.all_gather(down_bias.astype(jnp.bfloat16), "seq", axis=0, tiled=True),
    )
    gain_one_f = gain_one.astype(jnp.float32)
    gain_two_f = gain_two.astype(jnp.float32)
    positions = first_row + jnp.arange(local_rows, dtype=jnp.int32)
    cos_table, sin_table = angles(positions)
    padded_ids = jnp.pad(clip_ids, (HALF, HALF), constant_values=-1)
    own_ids = lax.dynamic_slice_in_dim(clip_ids, first_row, local_rows)
    near_ids = lax.dynamic_slice_in_dim(padded_ids, first_row, local_rows + 2 * HALF)
    base_clip = jnp.minimum(own_ids[0], clip_total - slot_count)
    own_slot = own_ids - base_clip
    slot_range = jnp.arange(slot_count, dtype=jnp.int32)
    frames_f = frames.astype(jnp.float32)
    normed_out, normal_one, inverse_one = layer_norm_parts(frames_f, gain_one_f)
    normed_one = normed_out.astype(jnp.bfloat16)
    query_rows = rotate(product(normed_one, w_query), cos_table, sin_table).astype(jnp.bfloat16)
    key_rows = rotate(product(normed_one, w_key), cos_table, sin_table).astype(jnp.bfloat16)
    value_rows = product(normed_one, w_value).astype(jnp.bfloat16)
    local_width = query_rows.shape[1]
    head_count = local_width // HD
    near = extended(jnp.stack([key_rows, value_rows]), (("seq", 1),), HALF)
    near_key_h = near[0].reshape(local_rows + 2 * HALF, head_count, HD)
    near_value_h = near[1].reshape(local_rows + 2 * HALF, head_count, HD)
    query_all_h = query_rows.reshape(local_rows, head_count, HD)
    stamp_rows = lax.dynamic_slice_in_dim(time_token, base_clip, slot_count, 0).astype(jnp.float32)
    stamp_out, stamp_normal, stamp_inverse = layer_norm_parts(stamp_rows, gain_one_f)
    stamp_normed = stamp_out.astype(jnp.bfloat16)
    stamp_key_h = (
        product(stamp_normed, w_key).astype(jnp.bfloat16).reshape(slot_count, head_count, HD)
    )
    stamp_value_h = (
        product(stamp_normed, w_value).astype(jnp.bfloat16).reshape(slot_count, head_count, HD)
    )

    def self_parts(block_index):
        row_start = block_index * block_rows
        query_pos = row_start + jnp.arange(block_rows, dtype=jnp.int32)
        key_pos = row_start - HALF + jnp.arange(window, dtype=jnp.int32)
        visible = (own_ids[:, None] == near_ids[None, :]) & (
            jnp.abs(query_pos[:, None] - key_pos[None, :]) <= HALF
        )
        own_stamp = own_slot[:, None] == slot_range[None, :]
        return (
            query_all_h,
            [(near_key_h, near_value_h, visible), (stamp_key_h, stamp_value_h, own_stamp)],
        )

    def self_forward(block_index):
        query_h, key_parts = self_parts(block_index)
        attn_mixed, log_total = attend_forward(query_h, key_parts, score_scale)
        return (attn_mixed.reshape(block_rows, local_width).astype(jnp.bfloat16), log_total)

    attn_blocks, self_logs = lax.map(self_forward, block_indices)
    attn_mixed = attn_blocks.reshape(local_rows, local_width)
    h_one = frames_f + branch_total(product_t(attn_mixed, w_out))
    middle_out, normal_two, inverse_two = layer_norm_parts(h_one, gain_two_f)
    normed_two = middle_out.astype(jnp.bfloat16)
    cross_rows = product(normed_two, c_query).astype(jnp.bfloat16)
    cross_all_h = cross_rows.reshape(local_rows, head_count, HD)
    context_rows = lax.dynamic_slice_in_dim(prompt, base_clip, slot_count, 0).reshape(
        slot_count * ctx_tokens, prompt.shape[2]
    )
    ctx_key_h = (
        product(context_rows, c_key)
        .astype(jnp.bfloat16)
        .reshape(slot_count * ctx_tokens, head_count, HD)
    )
    ctx_value_h = (
        product(context_rows, c_value)
        .astype(jnp.bfloat16)
        .reshape(slot_count * ctx_tokens, head_count, HD)
    )
    key_slot = jnp.arange(slot_count * ctx_tokens, dtype=jnp.int32) // ctx_tokens

    def cross_parts(block_index):
        row_start = block_index * block_rows
        visible = own_slot[:, None] == key_slot[None, :]
        return (cross_all_h, [(ctx_key_h, ctx_value_h, visible)])

    def cross_forward(block_index):
        query_h, key_parts = cross_parts(block_index)
        cross_mix, log_total = attend_forward(query_h, key_parts, score_scale)
        return (cross_mix.reshape(block_rows, local_width).astype(jnp.bfloat16), log_total)

    cross_blocks, cross_logs = lax.map(cross_forward, block_indices)
    cross_mixed = cross_blocks.reshape(local_rows, local_width)
    h_two = h_one + branch_total(product_t(cross_mixed, c_out))
    gain_three_f = gain_three.astype(jnp.float32)
    third_out, normal_three, inverse_three = layer_norm_parts(h_two, gain_three_f)
    normed_three = third_out.astype(jnp.bfloat16)
    gate_pre = product(normed_three, w_gate) + gate_bias
    up_pre = product(normed_three, w_up) + up_bias
    hidden = (jax.nn.silu(gate_pre) * up_pre).astype(jnp.bfloat16)
    result = (h_two + branch_total(product_t(hidden, w_down)) + b_down.astype(jnp.float32)).astype(
        jnp.bfloat16
    )
    grad_top = out_grad.astype(jnp.float32)
    grad_hidden = product(out_grad, w_down)
    sigmoid_gate = jax.nn.sigmoid(gate_pre)
    grad_up = (grad_hidden * gate_pre * sigmoid_gate).astype(jnp.bfloat16)
    grad_gate = (
        grad_hidden * up_pre * sigmoid_gate * (1.0 + gate_pre * (1.0 - sigmoid_gate))
    ).astype(jnp.bfloat16)
    gate_bias_local = jnp.sum(grad_gate.astype(jnp.float32), axis=0)
    up_bias_local = jnp.sum(grad_up.astype(jnp.float32), axis=0)
    grad_normed_three = back_total(product_t(grad_gate, w_gate) + product_t(grad_up, w_up))
    glu_terms = (
        product_tn(normed_three, grad_gate),
        product_tn(normed_three, grad_up),
        product_tn(out_grad, hidden),
        jnp.sum(grad_normed_three * normal_three, axis=0),
        jnp.sum(grad_top, axis=0),
    )
    grad_h_two = grad_top + norm_back(grad_normed_three, normal_three, inverse_three, gain_three_f)
    grad_two_low = grad_h_two.astype(jnp.bfloat16)
    grad_cross_mixed = product(grad_two_low, c_out).astype(jnp.bfloat16)
    cross_out_term = product_tn(grad_two_low, cross_mixed)
    grad_cross_h = grad_cross_mixed.reshape(local_rows, head_count, HD)

    def cross_step(ctx_grads, block_index):
        query_h, key_parts = cross_parts(block_index)
        grad_query, grad_keys, grad_values = attend_backward(
            query_h, key_parts, score_scale, cross_logs[block_index], grad_cross_h
        )
        return (ctx_grads + jnp.stack([grad_keys[0], grad_values[0]]), grad_query)

    ctx_grads, grad_cross_q = lax.scan(
        cross_step,
        jnp.zeros((2, slot_count * ctx_tokens, head_count, HD), jnp.float32),
        block_indices,
    )
    grad_cross_query = grad_cross_q.reshape(local_rows, local_width).astype(jnp.bfloat16)
    context_float = context_rows.astype(jnp.float32)
    cross_key_term = exact_tn(context_float, ctx_grads[0].reshape(-1, local_width))
    cross_value_term = exact_tn(context_float, ctx_grads[1].reshape(-1, local_width))
    cross_query_term = product_tn(normed_two, grad_cross_query)
    grad_normed_two = back_total(product_t(grad_cross_query, c_query))
    gain_two_term = jnp.sum(grad_normed_two * normal_two, axis=0)
    grad_h_one = grad_h_two + norm_back(grad_normed_two, normal_two, inverse_two, gain_two_f)
    grad_one_low = grad_h_one.astype(jnp.bfloat16)
    grad_attn = product(grad_one_low, w_out).astype(jnp.bfloat16)
    out_term = product_tn(grad_one_low, attn_mixed)
    grad_attn_h = grad_attn.reshape(local_rows, head_count, HD)

    def self_step(grad_state, block_index):
        near_grads, stamp_grads = grad_state
        query_h, key_parts = self_parts(block_index)
        row_start = block_index * block_rows
        grad_query, grad_keys, grad_values = attend_backward(
            query_h, key_parts, score_scale, self_logs[block_index], grad_attn_h
        )
        prior = near_grads
        near_grads = prior + jnp.stack([grad_keys[0], grad_values[0]])
        stamp_grads = stamp_grads + jnp.stack([grad_keys[1], grad_values[1]])
        return ((near_grads, stamp_grads), grad_query)

    start_state = (
        jnp.zeros((2, local_rows + 2 * HALF, head_count, HD), jnp.float32),
        jnp.zeros((2, slot_count, head_count, HD), jnp.float32),
    )
    (near_grads, stamp_grads), grad_query_blocks = lax.scan(self_step, start_state, block_indices)
    near_grads = near_grads.reshape(2, local_rows + 2 * HALF, local_width)
    from_above = passed_along(near_grads[:, :HALF].astype(jnp.bfloat16), "seq", -1).astype(
        jnp.float32
    )
    from_below = passed_along(
        near_grads[:, HALF + local_rows :].astype(jnp.bfloat16), "seq", 1
    ).astype(jnp.float32)
    own_grads = (
        near_grads[:, HALF : HALF + local_rows]
        + jnp.pad(from_below, ((0, 0), (0, local_rows - HALF), (0, 0)))
        + jnp.pad(from_above, ((0, 0), (local_rows - HALF, 0), (0, 0)))
    )
    grad_query_rows = rotate(
        grad_query_blocks.reshape(local_rows, local_width), cos_table, -sin_table
    ).astype(jnp.bfloat16)
    grad_key_rows = rotate(own_grads[0], cos_table, -sin_table).astype(jnp.bfloat16)
    grad_value_rows = own_grads[1].astype(jnp.bfloat16)
    stamp_key_grad = stamp_grads[0].reshape(slot_count, local_width)
    stamp_value_grad = stamp_grads[1].reshape(slot_count, local_width)
    stamp_float = stamp_normed.astype(jnp.float32)
    query_term = product_tn(normed_one, grad_query_rows)
    key_term = product_tn(normed_one, grad_key_rows) + exact_tn(stamp_float, stamp_key_grad)
    value_term = product_tn(normed_one, grad_value_rows) + exact_tn(stamp_float, stamp_value_grad)
    grad_normed_one = back_total(
        product_t(grad_query_rows, w_query)
        + product_t(grad_key_rows, w_key)
        + product_t(grad_value_rows, w_value)
    )
    gain_one_term = jnp.sum(grad_normed_one * normal_one, axis=0)
    frames_grad = (
        grad_h_one + norm_back(grad_normed_one, normal_one, inverse_one, gain_one_f)
    ).astype(jnp.bfloat16)
    stamp_partial = exact_t(stamp_key_grad, w_key.astype(jnp.float32)) + exact_t(
        stamp_value_grad, w_value.astype(jnp.float32)
    )
    attn_shares = (
        lax.psum_scatter(query_term, "seq", scatter_dimension=0, tiled=True),
        lax.psum_scatter(key_term, "seq", scatter_dimension=0, tiled=True),
        lax.psum_scatter(value_term, "seq", scatter_dimension=0, tiled=True),
        lax.psum_scatter(out_term, "seq", scatter_dimension=0, tiled=True),
        lax.psum_scatter(cross_query_term, "seq", scatter_dimension=0, tiled=True),
        lax.psum_scatter(cross_key_term, "seq", scatter_dimension=0, tiled=True),
        lax.psum_scatter(cross_value_term, "seq", scatter_dimension=0, tiled=True),
        lax.psum_scatter(cross_out_term, "seq", scatter_dimension=0, tiled=True),
        lax.psum_scatter(gain_one_term, "seq", scatter_dimension=0, tiled=True),
        lax.psum_scatter(gain_two_term, "seq", scatter_dimension=0, tiled=True),
    )
    hidden_width = gate_bias.shape[0]
    stamp_full = lax.dynamic_update_slice_in_dim(
        jnp.zeros((clip_total, stamp_partial.shape[1]), jnp.float32), stamp_partial, base_clip, 0
    )
    bias_full = lax.dynamic_update_slice_in_dim(
        jnp.zeros((2, hidden_width * lax.axis_size("head")), jnp.float32),
        jnp.stack([gate_bias_local, up_bias_local]),
        head_index * hidden_width,
        1,
    )
    stamp_sum, bias_sum = lax.psum((stamp_full, bias_full), ("seq", "head"))
    every_out, every_normal, every_inverse = layer_norm_parts(
        time_token.astype(jnp.float32), gain_one_f
    )
    time_grad = norm_back(stamp_sum, every_normal, every_inverse, gain_one_f)
    gain_rows = norm1_gain.shape[0]
    time_gain = lax.dynamic_slice_in_dim(
        jnp.sum(stamp_sum * every_normal, axis=0), seq_index * gain_rows, gain_rows
    )
    own_bias = lax.dynamic_slice_in_dim(bias_sum, head_index * hidden_width, hidden_width, 1)
    return (
        result,
        frames_grad,
        time_grad,
        attn_shares[8] + time_gain,
        attn_shares[9],
        lax.psum_scatter(glu_terms[3], "seq", scatter_dimension=0, tiled=True),
        attn_shares[0],
        attn_shares[1],
        attn_shares[2],
        attn_shares[3],
        attn_shares[4],
        attn_shares[5],
        attn_shares[6],
        attn_shares[7],
        lax.psum_scatter(glu_terms[0], "seq", scatter_dimension=0, tiled=True),
        lax.psum_scatter(glu_terms[1], "seq", scatter_dimension=0, tiled=True),
        lax.psum_scatter(glu_terms[2], "seq", scatter_dimension=0, tiled=True),
        own_bias[0],
        own_bias[1],
        lax.psum_scatter(glu_terms[4], "seq", scatter_dimension=0, tiled=True),
    )


LANES = 128
FAST_SEQ = 16
BLOCK = 256
TAIL_WIDTH = 768
QUERY_BLOCK = 128
HOP_CHUNK = 1
MADE_AT = 1
VMEM_BYTES = 60 * 1024 * 1024
MESH = pl.DeviceIdType.MESH


def xor_place(index, bit):
    return index + bit * (1 - 2 * (index // bit % 2))


def chip_near(seq_index, seq_count, step):
    chips = seq_count // 2
    chip = seq_index // 2
    odd = chip % 2
    place = (1 - odd) * (chip // 2) + odd * (chips - 1 - chip // 2)
    there = (place + chips + step) % chips
    upper = there // (chips // 2)
    return (1 - upper) * 2 * there + upper * (2 * (chips - 1 - there) + 1)


def ring_neighbours(seq_index, seq_count):
    return [2 * chip_near(seq_index, seq_count, step) + seq_index % 2 for step in (1, -1)]


def gather_kernel(seq_count, bounds, count, later_count, *refs):
    wides, refs = refs[:count], refs[count:]
    later, refs = refs[:later_count], refs[later_count:]
    out, later_out, refs = refs[0], refs[1], refs[2:]
    wide_bufs, later_bufs, refs = refs[:count], refs[count : count + later_count], refs[count + later_count :]
    (
        local,
        later_local,
        in_sems,
        later_sem,
        own_sem,
        ring_send,
        ring_recv,
        core_send,
        core_recv,
    ) = refs
    loads = [
        pltpu.make_async_copy(source, target, in_sems.at[at])
        for at, (source, target) in enumerate(
            zip([*wides, *later], [*wide_bufs, *later_bufs])
        )
    ]
    for load in loads:
        load.start()
    far = seq_count // 4
    seq_index = lax.axis_index("seq")
    core = seq_index % 2
    partner = {"seq": xor_place(seq_index, 1)}
    sides = ring_neighbours(seq_index, seq_count)
    greet([partner] + [{"seq": side} for side in sides])

    def columns_of(piece, side, hop):
        low, high = bounds[piece], bounds[piece + 1]
        if hop == far - 1:
            mid = low + (high - low) // (2 * LANES) * LANES
            low, high = (low, mid) if side == 0 else (mid, high)
        return pl.ds(low, high - low)

    def ring_copy(piece, side, hop):
        columns = columns_of(piece, side, hop)
        target = out.at[
            chip_near(seq_index, seq_count, -hop if side == 0 else hop), core, :, columns
        ]
        return pltpu.make_async_remote_copy(
            src_ref=local.at[:, columns] if hop == 0 else target,
            dst_ref=target,
            send_sem=ring_send.at[piece, side, hop],
            recv_sem=ring_recv.at[piece, side, hop],
            device_id={"seq": sides[side]},
            device_id_type=MESH,
        )

    def core_copy(piece, side, hop):
        if hop < 0:
            columns = pl.ds(bounds[piece], bounds[piece + 1] - bounds[piece])
            target = out.at[seq_index // 2, core, :, columns]
            source = local.at[:, columns]
        else:
            chip = chip_near(seq_index, seq_count, -1 - hop if side == 0 else 1 + hop)
            target = out.at[chip, core, :, columns_of(piece, side, hop)]
            source = target
        return pltpu.make_async_remote_copy(
            src_ref=source,
            dst_ref=target,
            send_sem=core_send.at[piece, side, hop + 1],
            recv_sem=core_recv.at[piece, side, hop + 1],
            device_id=partner,
            device_id_type=MESH,
        )

    def wides_of(piece):
        if piece < len(bounds) - 2:
            return [(0, 0, piece)]
        height, width = wides[piece].shape
        return [(0, 0, piece), (height, 0, piece + 1), (0, width, piece + 2)]

    pieces = range(len(bounds) - 1)
    arrivals = [(piece, side, hop) for hop in range(far) for piece in pieces for side in range(2)]
    own_copy = pltpu.make_async_copy(local, out.at[seq_index // 2, core], own_sem)
    for piece in pieces:
        for row, column, at in wides_of(piece):
            height, width = wides[at].shape
            column += bounds[piece]
            loads[at].wait()
            local[row : row + height, column : column + width] = wide_bufs[at][...].astype(
                jnp.bfloat16
            )
        for side in range(2):
            ring_copy(piece, side, 0).start()
        core_copy(piece, 0, -1).start()
    own_copy.start()
    for at, wide in enumerate(later_bufs):
        width = wide.shape[1]
        loads[count + at].wait()
        later_local[:, at * width : (at + 1) * width] = wide[...].astype(jnp.bfloat16)
    later_copy = pltpu.make_async_copy(later_local, later_out, later_sem)
    later_copy.start()
    for piece, side, hop in arrivals:
        ring_copy(piece, side, hop).wait_recv()
        if hop + 1 < far:
            ring_copy(piece, side, hop + 1).start()
        core_copy(piece, side, hop).start()
    crossed = [(piece, 0, -1) for piece in pieces] + arrivals
    for piece, side, hop in crossed:
        core_copy(piece, side, hop).wait_recv()
    own_copy.wait()
    later_copy.wait()
    for piece, side, hop in crossed:
        core_copy(piece, side, hop).wait_send()
    for piece, side, hop in arrivals:
        ring_copy(piece, side, hop).wait_send()


def ring_gather(wides, later, bounds, seq_count, collective_id):
    rows, width = wides[0].shape[0], bounds[-1]
    pieces, far = len(bounds) - 1, seq_count // 4
    later_width = sum(each.shape[1] for each in later)
    hbm = pl.BlockSpec(memory_space=pltpu.HBM)
    gathered, later = pl.pallas_call(
        functools.partial(gather_kernel, seq_count, bounds, len(wides), len(later)),
        in_specs=[hbm] * (len(wides) + len(later)),
        out_specs=[hbm, hbm],
        out_shape=[
            jax.ShapeDtypeStruct((seq_count // 2, 2, rows, width), jnp.bfloat16),
            jax.ShapeDtypeStruct((rows, later_width), jnp.bfloat16),
        ],
        scratch_shapes=[
            *(pltpu.VMEM(each.shape, jnp.float32) for each in (*wides, *later)),
            pltpu.VMEM((rows, width), jnp.bfloat16),
            pltpu.VMEM((rows, later_width), jnp.bfloat16),
            pltpu.SemaphoreType.DMA((len(wides) + len(later),)),
            pltpu.SemaphoreType.DMA,
            pltpu.SemaphoreType.DMA,
            pltpu.SemaphoreType.DMA((pieces, 2, far)),
            pltpu.SemaphoreType.DMA((pieces, 2, far)),
            pltpu.SemaphoreType.DMA((pieces, 2, far + 1)),
            pltpu.SemaphoreType.DMA((pieces, 2, far + 1)),
        ],
        compiler_params=pltpu.CompilerParams(
            collective_id=collective_id, has_side_effects=True, vmem_limit_bytes=VMEM_BYTES
        ),
        cost_estimate=pl.CostEstimate(
            flops=0, bytes_accessed=32 * rows * seq_count * width, transcendentals=0
        ),
        name="ring_gather",
    )(*wides, *later)
    return gathered.reshape(seq_count * rows, width), later


def kept_places(seq_count):
    chips = seq_count // 2
    far = chips // 2
    return [*range(far - 2), *range(far + 3, chips)]


def glu_kernel(
    blocks,
    seq_count,
    normed,
    normed_t,
    top,
    top_t,
    w_gate,
    w_up,
    w_down,
    b_gate,
    b_up,
    out,
    grad_normed,
    bias_grads,
    kept,
    *refs,
):
    index = pl.program_id(0)
    seq_index = lax.axis_index("seq")
    partner = {"seq": xor_place(seq_index, 1)}
    core = seq_index % 2
    chips = seq_count // 2
    far = chips // 2
    mid = BLOCK // 2
    moving, out_acc, grad_acc, terms, arrived, send_sem, recv_sem, *refs = refs
    sides = ring_neighbours(seq_index, seq_count)
    sums, first_send, first_land, second_send, second_land, *ring_sems = refs

    def crossing(block):
        return pltpu.make_async_remote_copy(
            src_ref=terms.at[block % 2, :, :, 1 - core],
            dst_ref=arrived.at[block],
            send_sem=send_sem.at[block % 2],
            recv_sem=recv_sem.at[block],
            device_id=partner,
            device_id_type=MESH,
        )

    def hop(block, side, which):
        source, target = (first_send, first_land) if which == 0 else (second_send, second_land)
        return pltpu.make_async_remote_copy(
            src_ref=source.at[block, side],
            dst_ref=target.at[block, side],
            send_sem=ring_sems[2 * which].at[block, side],
            recv_sem=ring_sems[2 * which + 1].at[block, side],
            device_id={"seq": sides[side]},
            device_id_type=MESH,
        )

    @pl.when(index == 0)
    def _():
        greet([partner] + [{"seq": side} for side in sides])
        out_acc[...] = jnp.zeros_like(out_acc)
        grad_acc[...] = jnp.zeros_like(grad_acc)

    @pl.when(index < blocks)
    def _():
        gate_pre = product(normed[...], w_gate[...]) + b_gate[...]
        up_pre = product(normed[...], w_up[...]) + b_up[...]
        grad_hidden = product(top[...], w_down[...])
        sigmoid_gate = jax.nn.sigmoid(gate_pre)
        silu_gate = gate_pre * sigmoid_gate
        hidden = (silu_gate * up_pre).astype(jnp.bfloat16)
        grad_up = (grad_hidden * silu_gate).astype(jnp.bfloat16)
        grad_gate = (
            grad_hidden * up_pre * sigmoid_gate * (1.0 + gate_pre * (1.0 - sigmoid_gate))
        ).astype(jnp.bfloat16)
        bias_grads[0:1, :] = jnp.sum(grad_gate.astype(jnp.float32), axis=0, keepdims=True)
        bias_grads[1:2, :] = jnp.sum(grad_up.astype(jnp.float32), axis=0, keepdims=True)
        out_acc[...] += product_t(hidden, w_down[...])
        grad_acc[...] += product_t(grad_gate, w_gate[...]) + product_t(grad_up, w_up[...])

        @pl.when(index >= 2)
        def _():
            crossing(index - 2).wait_send()

        slot = index % 2
        for which, (rows_t, columns) in enumerate(
            ((normed_t, grad_gate), (normed_t, grad_up), (top_t, hidden))
        ):
            term = product(rows_t[...], columns).astype(jnp.bfloat16)
            terms[slot, which] = term.reshape(terms.shape[2:])
        crossing(index).start()

    def chunk(block, near):
        return sums[block % 3, :, chip_near(seq_index, seq_count, near)]

    @pl.when((index >= 1) & (index <= blocks))
    def _():
        block = index - 1
        crossing(block).wait_recv()
        total = terms[block % 2, :, :, core].astype(jnp.float32) + arrived[block].astype(
            jnp.float32
        )
        sums[block % 3] = total.astype(jnp.bfloat16)
        opposite = chunk(block, far)
        for side in range(2):
            first_send[block, side] = opposite[:, :, side * mid : (side + 1) * mid]
            hop(block, side, 0).start()
        for at, near in enumerate(kept_places(seq_count)):
            kept[at] = chunk(block, near)

    @pl.when((index >= 2) & (index <= blocks + 1))
    def _():
        block = index - 2
        for side in range(2):
            term = chunk(block, far - 1 if side == 0 else far + 1).astype(jnp.float32)
            hop(block, side, 0).wait_recv()
            land = first_land[block, side].astype(jnp.float32)
            low = term[:, :, :mid] + land if side == 0 else term[:, :, :mid]
            high = term[:, :, mid:] if side == 0 else term[:, :, mid:] + land
            second_send[block, side, :, :, :mid] = low.astype(jnp.bfloat16)
            second_send[block, side, :, :, mid:] = high.astype(jnp.bfloat16)
            hop(block, side, 1).start()

    @pl.when(index >= 3)
    def _():
        block = index - 3
        for side in range(2):
            term = chunk(block, far - 2 if side == 0 else far + 2).astype(jnp.float32)
            hop(block, side, 1).wait_recv()
            land = second_land[block, side].astype(jnp.float32)
            moving[side] = (term + land).astype(jnp.bfloat16)

    @pl.when(index == blocks)
    def _():
        crossing(blocks - 2).wait_send()
        crossing(blocks - 1).wait_send()
        out[...] = out_acc[...].astype(jnp.bfloat16)
        grad_normed[...] = grad_acc[...].astype(jnp.bfloat16)

    @pl.when(index == blocks + 2)
    def _():
        for block in range(blocks):
            for side in range(2):
                hop(block, side, 0).wait_send()
                hop(block, side, 1).wait_send()


def glu_layer(normed, normed_t, top, top_t, weights, gate_bias, up_bias, seq_count):
    rows, width = normed.shape
    hidden_width = gate_bias.shape[0]
    blocks = hidden_width // BLOCK
    chips = seq_count // 2
    seg = width // seq_count
    kept = len(kept_places(seq_count))
    bf = jnp.bfloat16

    def whole(shape):
        return pl.BlockSpec(shape, lambda i: (0, 0), pipeline_mode=pl.Buffered(1))

    def at(lag):
        return lambda i: jnp.clip(i - lag, 0, blocks - 1)

    def weight_spec(which):
        return pl.BlockSpec((width, BLOCK), lambda i: (0, which * blocks + at(0)(i)))

    bias_spec = pl.BlockSpec((1, BLOCK), lambda i: (0, at(0)(i)))
    work = rows * width * hidden_width
    term_specs = [
        pl.BlockSpec((kept, 3, seg, BLOCK), lambda i: (0, 0, 0, at(1)(i))),
        pl.BlockSpec((2, 3, seg, BLOCK), lambda i: (0, 0, 0, at(3)(i))),
    ]
    term_shapes = [
        jax.ShapeDtypeStruct((kept, 3, seg, hidden_width), bf),
        jax.ShapeDtypeStruct((2, 3, seg, hidden_width), bf),
    ]
    return pl.pallas_call(
        functools.partial(glu_kernel, blocks, seq_count),
        grid=(blocks + 3,),
        in_specs=[
            whole((rows, width)),
            whole((width, rows)),
            whole((rows, width)),
            whole((width, rows)),
            weight_spec(0),
            weight_spec(1),
            weight_spec(2),
            bias_spec,
            bias_spec,
        ],
        out_specs=[
            pl.BlockSpec((rows, width), lambda i: (0, 0)),
            pl.BlockSpec((rows, width), lambda i: (0, 0)),
            pl.BlockSpec((2, BLOCK), lambda i: (0, at(0)(i))),
            *term_specs,
        ],
        out_shape=[
            jax.ShapeDtypeStruct((rows, width), bf),
            jax.ShapeDtypeStruct((rows, width), bf),
            jax.ShapeDtypeStruct((2, hidden_width), jnp.float32),
            *term_shapes,
        ],
        scratch_shapes=[
            pltpu.VMEM((rows, width), jnp.float32),
            pltpu.VMEM((rows, width), jnp.float32),
            pltpu.VMEM((2, 3, chips, 2, seg, BLOCK), bf),
            pltpu.VMEM((blocks, 3, chips, seg, BLOCK), bf),
            pltpu.SemaphoreType.DMA((2,)),
            pltpu.SemaphoreType.DMA((blocks,)),
            pltpu.VMEM((3, 3, chips, seg, BLOCK), bf),
            pltpu.VMEM((blocks, 2, 3, seg, BLOCK // 2), bf),
            pltpu.VMEM((blocks, 2, 3, seg, BLOCK // 2), bf),
            pltpu.VMEM((blocks, 2, 3, seg, BLOCK), bf),
            pltpu.VMEM((blocks, 2, 3, seg, BLOCK), bf),
            *(pltpu.SemaphoreType.DMA((blocks, 2)) for _ in range(4)),
        ],
        compiler_params=pltpu.CompilerParams(
            collective_id=1, has_side_effects=True, vmem_limit_bytes=VMEM_BYTES
        ),
        cost_estimate=pl.CostEstimate(
            flops=18 * work, bytes_accessed=12 * width * hidden_width, transcendentals=rows * hidden_width
        ),
        name="glu_layer",
    )(
        normed,
        normed_t,
        top,
        top_t,
        weights,
        weights,
        weights,
        gate_bias[None],
        up_bias[None],
    )


class ChipRing:
    def __init__(self, seq_count, pieces, sends, lands, send_sem, recv_sem):
        self.chips = seq_count // 2
        self.far = self.chips // 2
        self.pieces = pieces
        self.sends, self.lands = sends, lands
        self.send_sem, self.recv_sem = send_sem, recv_sem
        self.sides = ring_neighbours(lax.axis_index("seq"), seq_count)
        self.greeted = [{"seq": side} for side in self.sides]
        width = pieces[0].shape[2]
        self.near = [
            chip_near(lax.axis_index("seq"), seq_count, step) for step in range(self.chips)
        ]
        self.width, self.mid = width, width // 2

    def copy(self, piece, side, hop):
        mid = self.mid
        if hop == 0:
            source = self.pieces[piece].at[self.near[self.far], :, pl.ds(side * mid, mid)]
            target = self.lands.at[piece, side, 0, :, pl.ds(0, mid)]
        else:
            source = self.sends.at[piece, side, hop - 1]
            target = self.lands.at[piece, side, hop]
        return pltpu.make_async_remote_copy(
            src_ref=source,
            dst_ref=target,
            send_sem=self.send_sem.at[piece, side, hop],
            recv_sem=self.recv_sem.at[piece, side, hop],
            device_id={"seq": self.sides[side]},
            device_id_type=MESH,
        )

    def start(self, piece):
        for side in range(2):
            self.copy(piece, side, 0).start()

    def advance(self, piece, hop):
        mid = self.mid
        for side in range(2):
            near = self.far - hop if side == 0 else self.far + hop
            term = self.pieces[piece][self.near[near]].astype(jnp.float32)
            self.copy(piece, side, hop - 1).wait_recv()
            if hop == 1:
                land = self.lands[piece, side, 0, :, :mid].astype(jnp.float32)
                low = term[:, :mid] + land if side == 0 else term[:, :mid]
                high = term[:, mid:] if side == 0 else term[:, mid:] + land
                self.sends[piece, side, 0, :, :mid] = low.astype(jnp.bfloat16)
                self.sends[piece, side, 0, :, mid:] = high.astype(jnp.bfloat16)
            else:
                land = self.lands[piece, side, hop - 1].astype(jnp.float32)
                self.sends[piece, side, hop - 1] = (term + land).astype(jnp.bfloat16)
            self.copy(piece, side, hop).start()

    def total(self, piece):
        total = self.pieces[piece][self.near[0]].astype(jnp.float32)
        for side in range(2):
            self.copy(piece, side, self.far - 1).wait_recv()
            total = total + self.lands[piece, side, self.far - 1].astype(jnp.float32)
        return total

    def close(self):
        for piece in range(len(self.pieces)):
            for side in range(2):
                for hop in range(self.far):
                    self.copy(piece, side, hop).wait_send()


def ring_scratch(seq_count, pieces, seg, width):
    far = seq_count // 4
    return [
        pltpu.VMEM((pieces, 2, far - 1, seg, width), jnp.bfloat16),
        pltpu.VMEM((pieces, 2, far, seg, width), jnp.bfloat16),
        pltpu.SemaphoreType.DMA((pieces, 2, far)),
        pltpu.SemaphoreType.DMA((pieces, 2, far)),
    ]


def greet(devices):
    barrier = pltpu.get_barrier_semaphore()
    for device in devices:
        pl.semaphore_signal(barrier, inc=1, device_id=device, device_id_type=MESH)
    pl.semaphore_wait(barrier, len(devices))


class CoreSum:
    def __init__(self, partner, terms, arrived, send_sem, recv_sem):
        self.core = lax.axis_index("seq") % 2
        self.partner = partner
        self.terms, self.arrived = terms, arrived
        self.send_sem, self.recv_sem = send_sem, recv_sem

    def copy(self, piece):
        return pltpu.make_async_remote_copy(
            src_ref=self.terms.at[piece % self.terms.shape[0], :, 1 - self.core],
            dst_ref=self.arrived.at[piece],
            send_sem=self.send_sem.at[piece],
            recv_sem=self.recv_sem.at[piece],
            device_id=self.partner,
            device_id_type=MESH,
        )

    def start(self, piece, term):
        slot = piece % self.terms.shape[0]
        self.terms[slot] = term.astype(jnp.bfloat16).reshape(self.terms.shape[1:])
        self.copy(piece).start()

    def finish(self, piece):
        self.copy(piece).wait_recv()
        total = self.terms[piece % self.terms.shape[0], :, self.core].astype(jnp.float32)
        return (total + self.arrived[piece].astype(jnp.float32)).astype(jnp.bfloat16)

    def close(self, piece):
        self.copy(piece).wait_send()


def core_scratch(pieces, chips, seg, width, slots):
    return [
        pltpu.VMEM((slots, chips, 2, seg, width), jnp.bfloat16),
        pltpu.VMEM((pieces, chips, seg, width), jnp.bfloat16),
        pltpu.SemaphoreType.DMA((pieces,)),
        pltpu.SemaphoreType.DMA((pieces,)),
    ]


def through_norm(total, normal, inverse, gain):
    shaped = total * gain
    return (
        shaped
        - jnp.mean(shaped, axis=-1, keepdims=True)
        - normal * jnp.mean(shaped * normal, axis=-1, keepdims=True)
    ) * inverse


def tail_kernel(seq_count, head_count, made_count, clip_total, *refs):
    (
        rows_t,
        columns,
        weights,
        normal,
        inverse,
        gain,
        grad_h_one,
        placing,
        early,
        h_two,
        glu_own,
        glu_other,
        down_bias,
        ready,
        out,
        small_out,
        frames_grad,
        result,
        mine,
        small_send,
        small_land,
        step_send,
        step_recv,
        split,
        split_land,
        split_send,
        split_recv,
        *refs,
    ) = refs
    core_refs, ring_refs = refs[:4], refs[4:]
    width = columns.shape[1] // made_count
    rows = grad_h_one.shape[0]
    late = placing.shape[0]
    pieces = [ready, *(mine.at[made] for made in range(made_count))]
    ring = ChipRing(seq_count, pieces, *ring_refs)
    seq_index = lax.axis_index("seq")
    head_index = lax.axis_index("head")
    partners = []
    bit = 1
    while bit < seq_count:
        partners.append({"seq": xor_place(seq_index, bit)})
        bit *= 2
    seq_steps = len(partners)
    bit = 1
    while bit < head_count:
        partners.append({"head": xor_place(head_index, bit)})
        bit *= 2
    greet(ring.greeted + partners)
    cores = CoreSum(partners[0], *core_refs)

    def step_copy(step):
        count = small_out.shape[0] if step < seq_steps else late
        return pltpu.make_async_remote_copy(
            src_ref=small_send.at[step, pl.ds(0, count)],
            dst_ref=small_land.at[step, pl.ds(0, count)],
            send_sem=step_send.at[step],
            recv_sem=step_recv.at[step],
            device_id=partners[step],
            device_id_type=MESH,
        )

    def step_on(step):
        if step > 0:
            step_copy(step - 1).wait_recv()
            if step <= seq_steps:
                total = small_send[step - 1] + small_land[step - 1]
                if step == seq_steps:
                    small_out[late:, :] = total[late:]
                if step < len(partners):
                    small_send[step] = total
                else:
                    small_out[:late, :] = total[:late]
            else:
                total = small_send[step - 1, :late] + small_land[step - 1, :late]
                if step < len(partners):
                    small_send[step, :late] = total
                else:
                    small_out[:late, :] = total
        if step < len(partners):
            step_copy(step).start()

    def split_copy():
        return pltpu.make_async_remote_copy(
            src_ref=split,
            dst_ref=split_land,
            send_sem=split_send,
            recv_sem=split_recv,
            device_id=partners[seq_steps],
            device_id_type=MESH,
        )

    ring.start(0)
    for made in range(made_count):
        cores.start(made, product(rows_t[...], columns[:, made * width : (made + 1) * width]))
    grad_normed = product_t(columns[...], weights[...])
    split[...] = grad_normed[:rows].astype(jnp.bfloat16)
    split_copy().start()
    row = lax.broadcasted_iota(jnp.int32, (late, 1), 0)
    gain_term = jnp.sum(grad_normed[:rows] * normal[...], axis=0, keepdims=True)
    first = jnp.where(row == clip_total, gain_term, 0.0)
    for slot in range(placing.shape[1]):
        first = first + placing[:, slot : slot + 1] * grad_normed[rows + slot : rows + slot + 1]
    small_send[0, :late, :] = first
    small_send[0, late:, :] = early[...]
    step_on(0)
    for made in range(made_count):
        mine[made] = cores.finish(made)
        ring.start(made + 1)
    result[...] = (
        h_two[...]
        + (glu_own[...].astype(jnp.float32) + glu_other[...].astype(jnp.float32))
        + down_bias[...]
    ).astype(jnp.bfloat16)
    done = 1
    for hop in range(1, ring.far):
        for piece in range(len(pieces)):
            ring.advance(piece, hop)
        while done <= len(partners) * hop // (ring.far - 1):
            step_on(done)
            done += 1
    split_copy().wait_recv()
    total = split[...].astype(jnp.float32) + split_land[...].astype(jnp.float32)
    back = through_norm(total, normal[...], inverse[...], gain[...])
    frames_grad[...] = (grad_h_one[...] + back).astype(jnp.bfloat16)
    for piece in range(len(pieces)):
        out[piece] = ring.total(piece)
    split_copy().wait_send()
    for made in range(made_count):
        cores.close(made)
    ring.close()
    for step in range(len(partners)):
        step_copy(step).wait_send()


def tail_sums(
    rows_t, columns, weights, norm, grad_h_one, placing, early, h_two, glu_terms, down_bias, ready, clip_total, seq_count
):
    head_count = lax.axis_size("head")
    chips = seq_count // 2
    rows, wide = grad_h_one.shape
    seg = rows_t.shape[0] // seq_count
    width = TAIL_WIDTH
    made_count = columns.shape[1] // width
    steps = (seq_count - 1).bit_length() + (head_count - 1).bit_length()
    bf = jnp.bfloat16
    vmem = pl.BlockSpec(memory_space=pltpu.VMEM)
    small = (placing.shape[0] + early.shape[0], wide)
    return pl.pallas_call(
        functools.partial(tail_kernel, seq_count, head_count, made_count, clip_total),
        grid=(1,),
        in_specs=[
            vmem,
            vmem,
            pl.BlockSpec((wide, made_count * width), lambda i: (0, 0), pipeline_mode=pl.Buffered(1)),
            *[vmem] * 11,
        ],
        out_specs=[vmem] * 4,
        out_shape=[
            jax.ShapeDtypeStruct((made_count + 1, seg, width), jnp.float32),
            jax.ShapeDtypeStruct(small, jnp.float32),
            jax.ShapeDtypeStruct((rows, wide), bf),
            jax.ShapeDtypeStruct((rows, wide), bf),
        ],
        scratch_shapes=[
            pltpu.VMEM((made_count, chips, seg, width), bf),
            pltpu.VMEM((steps, *small), jnp.float32),
            pltpu.VMEM((steps, *small), jnp.float32),
            pltpu.SemaphoreType.DMA((steps,)),
            pltpu.SemaphoreType.DMA((steps,)),
            pltpu.VMEM((rows, wide), bf),
            pltpu.VMEM((rows, wide), bf),
            pltpu.SemaphoreType.DMA,
            pltpu.SemaphoreType.DMA,
            *core_scratch(made_count, chips, seg, width, made_count),
            *ring_scratch(seq_count, made_count + 1, seg, width),
        ],
        compiler_params=pltpu.CompilerParams(
            collective_id=2, has_side_effects=True, vmem_limit_bytes=VMEM_BYTES
        ),
        cost_estimate=pl.CostEstimate(
            flops=4 * rows_t.shape[0] * rows_t.shape[1] * columns.shape[1],
            bytes_accessed=32 * made_count * chips * seg * width,
            transcendentals=0,
        ),
        name="tail_sums",
    )(
        rows_t,
        columns,
        weights,
        *norm,
        grad_h_one,
        placing,
        early,
        h_two,
        *glu_terms,
        down_bias,
        ready,
    )


def turned_back(values, tables):
    shift = ROT // 2
    return (
        values * tables[0]
        + pltpu.roll(values, LANES - shift, 1) * tables[1]
        - pltpu.roll(values, shift, 1) * tables[2]
    )


def self_back_kernel(seq_count, pairs, score_scale, *refs):
    (
        query,
        keys,
        values,
        stamp_key,
        stamp_value,
        grad_out,
        logs,
        key_ids,
        query_ids,
        query_slots,
        tables,
        ready,
        made_rows,
        made_columns,
        out,
        shares,
        mine,
        bias,
        acc,
        own,
        halo,
        halo_land,
        halo_send_sem,
        halo_recv_sem,
        *refs,
    ) = refs
    core_refs, ring_refs = refs[:4], refs[4:]
    ready_count = ready.shape[0]
    pair = pl.program_id(0)
    rows = query.shape[0]
    slots = stamp_key.shape[0]
    span = QUERY_BLOCK + 2 * HALF
    seq_index = lax.axis_index("seq")
    before = (seq_index + seq_count - 1) % seq_count
    behind = (seq_index + 1) % seq_count
    pieces = [ready.at[piece] for piece in range(ready_count)]
    ring = ChipRing(seq_count, pieces, *ring_refs)
    partner = {"seq": xor_place(seq_index, 1)}
    cores = CoreSum(partner, *core_refs)

    def halo_copy(which, side):
        return pltpu.make_async_remote_copy(
            src_ref=halo.at[which, side],
            dst_ref=halo_land.at[which, side],
            send_sem=halo_send_sem.at[which, side],
            recv_sem=halo_recv_sem.at[which, side],
            device_id={"seq": before if side == 0 else behind},
            device_id_type=MESH,
        )

    @pl.when(pair == 0)
    def _():
        greet(ring.greeted + [partner, {"seq": before}, {"seq": behind}])
        for piece in range(ready_count):
            ring.start(piece)
        cores.start(0, product_tn(made_rows[...], made_columns[...]))
        for block in range(rows // QUERY_BLOCK):
            start = block * QUERY_BLOCK
            asked = query_ids[:, start : start + QUERY_BLOCK]
            key_row = lax.broadcasted_iota(jnp.int32, (span, QUERY_BLOCK), 0)
            query_row = lax.broadcasted_iota(jnp.int32, (span, QUERY_BLOCK), 1)
            away = key_row - HALF - query_row
            seen = (key_ids[start : start + span, :] == asked) & (jnp.abs(away) <= HALF)
            bias[block, :span, :] = jnp.where(seen, 0.0, NEG)
            slot_row = lax.broadcasted_iota(jnp.int32, (slots, QUERY_BLOCK), 0)
            bias[block, span:, :] = jnp.where(
                slot_row == query_slots[:, start : start + QUERY_BLOCK], 0.0, NEG
            )

    blocks = rows // QUERY_BLOCK
    order = [(piece, hop) for hop in range(1, ring.far) for piece in range(len(pieces))]
    due = [1 + at * (pairs * blocks - 1) // len(order) for at in range(len(order))]

    def ring_work(block):
        @pl.when(pair * blocks + block == MADE_AT)
        def _():
            mine[...] = cores.finish(0)

        for moment, (piece, hop) in zip(due, order):
            if moment % blocks == block:

                @pl.when(pair == moment // blocks)
                def _():
                    ring.advance(piece, hop)

    @pl.when(pair < pairs)
    def _():
        acc[...] = jnp.zeros_like(acc)
        lane = lax.broadcasted_iota(jnp.int32, (1, LANES), 1)
        stamp_k, stamp_v = stamp_key[...], stamp_value[...]
        grad_queries = []
        for block in range(rows // QUERY_BLOCK):
            start = block * QUERY_BLOCK
            near_k = jnp.concatenate([keys[0, start : start + span, :], stamp_k], axis=0)
            near_v = jnp.concatenate([values[0, start : start + span, :], stamp_v], axis=0)
            block_q = query[start : start + QUERY_BLOCK, :]
            block_g = grad_out[start : start + QUERY_BLOCK, :]
            grad_q = jnp.zeros((QUERY_BLOCK, LANES), jnp.float32)
            grad_k = jnp.zeros((span + slots, LANES), jnp.float32)
            grad_v = jnp.zeros((span + slots, LANES), jnp.float32)
            for head in range(LANES // HD):
                here = lane // HD == head
                head_q = jnp.where(here, block_q, jnp.zeros_like(block_q))
                head_g = jnp.where(here, block_g, jnp.zeros_like(block_g))
                head_k = jnp.where(here, near_k, jnp.zeros_like(near_k))
                scores = product_t(near_k, head_q) * score_scale + bias[block]
                probs = jnp.exp(scores - logs[0, head : head + 1, start : start + QUERY_BLOCK])
                grad_p = product_t(near_v, head_g)
                dot = jnp.sum(probs * grad_p, axis=0, keepdims=True)
                grad_s = (probs * (grad_p - dot)).astype(jnp.bfloat16)
                grad_k = grad_k + product(grad_s, head_q)
                grad_v = grad_v + product(probs.astype(jnp.bfloat16), head_g)
                grad_q = grad_q + product_tn(grad_s, head_k)
            grad_queries.append(grad_q)
            ring_work(block)
            acc[0, start : start + span, :] += grad_k[:span]
            acc[1, start : start + span, :] += grad_v[:span]
            acc[0, 2 * HALF + rows :, :] += grad_k[span:]
            acc[1, 2 * HALF + rows :, :] += grad_v[span:]
        column = pl.multiple_of(pair * LANES, LANES)
        grad_q = jnp.concatenate(grad_queries, axis=0) * score_scale
        out[:rows, pl.ds(column, LANES)] = turned_back(grad_q, tables).astype(jnp.bfloat16)
        out[rows:, pl.ds(column, LANES)] = jnp.zeros((slots, LANES), jnp.bfloat16)
        for which in range(2):
            scale = score_scale if which == 0 else 1.0
            shift = (which + 1) * pairs * LANES
            halo[pair, 0, which] = (acc[which, :HALF, :] * scale).astype(jnp.bfloat16)
            halo[pair, 1, which] = (acc[which, HALF + rows : 2 * HALF + rows, :] * scale).astype(
                jnp.bfloat16
            )
            own[pair, which] = acc[which, HALF : HALF + rows, :] * scale
            out[rows:, pl.ds(column + shift, LANES)] = (
                acc[which, 2 * HALF + rows :, :] * scale
            ).astype(jnp.bfloat16)

        @pl.when(seq_index > 0)
        def _():
            halo_copy(pair, 0).start()

        @pl.when(seq_index < seq_count - 1)
        def _():
            halo_copy(pair, 1).start()

    @pl.when(pair == pairs)
    def _():

        @pl.when(seq_index < seq_count - 1)
        def _():
            for which in range(pairs):
                halo_copy(which, 0).wait_recv()
                own[which, :, rows - HALF :, :] += halo_land[which, 0].astype(jnp.float32)

        @pl.when(seq_index > 0)
        def _():
            for which in range(pairs):
                halo_copy(which, 1).wait_recv()
                own[which, :, :HALF, :] += halo_land[which, 1].astype(jnp.float32)

        for which in range(pairs):
            column = (pairs + which) * LANES
            out[:rows, column : column + LANES] = turned_back(own[which, 0], tables).astype(
                jnp.bfloat16
            )
            column = (2 * pairs + which) * LANES
            out[:rows, column : column + LANES] = own[which, 1].astype(jnp.bfloat16)
        for piece in range(len(pieces)):
            shares[piece] = ring.total(piece)
        ring.close()
        cores.close(0)

        @pl.when(seq_index > 0)
        def _():
            for which in range(pairs):
                halo_copy(which, 0).wait_send()

        @pl.when(seq_index < seq_count - 1)
        def _():
            for which in range(pairs):
                halo_copy(which, 1).wait_send()


def self_back(
    query, near, stamps, grad_out, logs, key_ids, query_ids, query_slots, tables, ready, made_rows, made_columns, score_scale, seq_count
):
    rows, part = query.shape
    slots = stamps.shape[0]
    pairs = part // LANES
    window = near.shape[1]
    ready_count, chips, seg, width = ready.shape
    span = QUERY_BLOCK + 2 * HALF
    blocks = rows // QUERY_BLOCK
    last = pairs - 1

    def at(first, shape, lead=()):
        return pl.BlockSpec(shape, lambda i: (*lead, 0, first + jnp.minimum(i, last)))

    def whole(shape):
        return pl.BlockSpec(shape, lambda i: (0,) * len(shape), pipeline_mode=pl.Buffered(1))

    return pl.pallas_call(
        functools.partial(self_back_kernel, seq_count, pairs, score_scale),
        grid=(pairs + 1,),
        in_specs=[
            at(0, (rows, LANES)),
            at(0, (1, window, LANES), (0,)),
            at(0, (1, window, LANES), (1,)),
            at(pairs, (slots, LANES)),
            at(2 * pairs, (slots, LANES)),
            at(0, (rows, LANES)),
            pl.BlockSpec((1, LANES // HD, rows), lambda i: (jnp.minimum(i, last), 0, 0)),
            whole((window, 1)),
            whole((1, rows)),
            whole((1, rows)),
            whole((3, rows, LANES)),
            whole(ready.shape),
            whole(made_rows.shape),
            whole(made_columns.shape),
        ],
        out_specs=[
            pl.BlockSpec((rows + slots, 3 * part), lambda i: (0, 0)),
            pl.BlockSpec((ready_count, seg, width), lambda i: (0, 0, 0)),
            pl.BlockSpec((chips, seg, width), lambda i: (0, 0, 0)),
        ],
        out_shape=[
            jax.ShapeDtypeStruct((rows + slots, 3 * part), jnp.bfloat16),
            jax.ShapeDtypeStruct((ready_count, seg, width), jnp.float32),
            jax.ShapeDtypeStruct((chips, seg, width), jnp.bfloat16),
        ],
        scratch_shapes=[
            pltpu.VMEM((blocks, span + slots, QUERY_BLOCK), jnp.float32),
            pltpu.VMEM((2, window + slots, LANES), jnp.float32),
            pltpu.VMEM((pairs, 2, rows, LANES), jnp.float32),
            pltpu.VMEM((pairs, 2, 2, HALF, LANES), jnp.bfloat16),
            pltpu.VMEM((pairs, 2, 2, HALF, LANES), jnp.bfloat16),
            pltpu.SemaphoreType.DMA((pairs, 2)),
            pltpu.SemaphoreType.DMA((pairs, 2)),
            *core_scratch(1, chips, seg, width, 1),
            *ring_scratch(seq_count, ready_count, seg, width),
        ],
        compiler_params=pltpu.CompilerParams(
            collective_id=3, has_side_effects=True, vmem_limit_bytes=VMEM_BYTES
        ),
        cost_estimate=pl.CostEstimate(
            flops=10 * rows * window * part,
            bytes_accessed=16 * chips * seg * width * ready_count,
            transcendentals=rows * window * part // HD,
        ),
        name="self_back",
    )(
        query,
        near,
        near,
        stamps,
        stamps,
        grad_out,
        logs.reshape(pairs, LANES // HD, rows),
        key_ids[:, None],
        query_ids[None],
        query_slots[None],
        tables,
        ready,
        made_rows,
        made_columns,
    )


def mid_kernel(seq_count, head_count, score_scale, ctx_tokens, *refs):
    (
        grad_low,
        top,
        normal_three,
        inverse_three,
        normal_two,
        inverse_two,
        gains,
        c_out,
        c_query,
        w_out,
        query,
        key,
        value,
        logs,
        query_slots,
        cross_mixed,
        normed_two,
        context,
        kept,
        moving,
        grad_h_one,
        grad_two_low,
        grad_one_low,
        grad_attn,
        grad_query,
        ctx_grads,
        gain_terms,
        share,
        core_sums,
        ctx_acc,
        split,
        split_land,
        split_send,
        split_recv,
        third_land,
        fourth_land,
        third_sems,
        fourth_sems,
        keep,
        keep_sems,
        *core_refs,
    ) = refs
    seq_index = lax.axis_index("seq")
    head_index = lax.axis_index("head")
    others = [{"head": (head_index + 1 + step) % head_count} for step in range(head_count - 1)]
    sides = ring_neighbours(seq_index, seq_count)
    partner = {"seq": xor_place(seq_index, 1)}
    cores = CoreSum(partner, *core_refs)
    greet([*others, partner] + [{"seq": side} for side in sides])

    def hop(side, which, slab):
        sems = fourth_sems if which else third_sems
        return pltpu.make_async_remote_copy(
            src_ref=third_land.at[side, slab] if which else moving.at[side, slab],
            dst_ref=(fourth_land if which else third_land).at[side, slab],
            send_sem=sems.at[0, side, slab],
            recv_sem=sems.at[1, side, slab],
            device_id={"seq": sides[side]},
            device_id_type=MESH,
        )

    def keep_copy(which):
        at = (1, kept.shape[0] - 1, 0)[which]
        return pltpu.make_async_copy(kept.at[at], keep.at[which % 2], keep_sems.at[which])

    def third_to_fourth():
        for side in range(2):
            keep_copy(side).wait()
        for slab in range(3):
            for side in range(2):
                hop(side, 0, slab).wait_recv()
                term = keep[side, slab].astype(jnp.float32)
                term = term + third_land[side, slab].astype(jnp.float32)
                third_land[side, slab] = term.astype(jnp.bfloat16)
                hop(side, 1, slab).start()
        keep_copy(2).start()

    def over_heads(which, chunk):
        part = pl.ds(chunk * QUERY_BLOCK, QUERY_BLOCK)
        return pltpu.make_async_remote_copy(
            src_ref=(grad_low if which == 0 else split).at[part],
            dst_ref=split_land.at[which, part],
            send_sem=split_send.at[which, chunk],
            recv_sem=split_recv.at[which, chunk],
            device_id=others[0],
            device_id_type=MESH,
        )

    rows = query.shape[0]
    keys = key.shape[0]
    part = query.shape[1]
    pairs = part // LANES
    chunks = range(rows // QUERY_BLOCK)

    def chunk_rows(chunk):
        return slice(chunk * QUERY_BLOCK, (chunk + 1) * QUERY_BLOCK)

    def summed(which, chunk):
        over_heads(which, chunk).wait_recv()
        here = chunk_rows(chunk)
        own = (grad_low if which == 0 else split)[here, :].astype(jnp.float32)
        return own + split_land[which, here, :].astype(jnp.float32)

    for chunk in chunks:
        over_heads(0, chunk).start()
    for slab in range(3):
        hop(0, 0, slab).start()
        hop(1, 0, slab).start()
    keep_copy(0).start()
    keep_copy(1).start()
    gain_terms[...] = jnp.zeros_like(gain_terms)
    ctx_acc[...] = jnp.zeros_like(ctx_acc)
    token_slot = lax.broadcasted_iota(jnp.int32, (keys, 1), 0) // ctx_tokens
    lane = lax.broadcasted_iota(jnp.int32, (1, LANES), 1)
    for chunk in chunks:
        here = chunk_rows(chunk)
        total = summed(0, chunk)
        normal = normal_three[here, :]
        gain_terms[0:1, :] += jnp.sum(total * normal, axis=0, keepdims=True)
        grad_two = top[here, :].astype(jnp.float32) + through_norm(
            total, normal, inverse_three[here, :], gains[0:1, :]
        )
        grad_h_one[here, :] = grad_two
        grad_two_low[here, :] = grad_two.astype(jnp.bfloat16)
        grad_mix = product(grad_two_low[here, :], c_out[...]).astype(jnp.bfloat16)
        bias = jnp.where(token_slot == query_slots[:, here], 0.0, NEG)
        for pair in range(pairs):
            columns = slice(pair * LANES, (pair + 1) * LANES)
            second = slice((pairs + pair) * LANES, (pairs + pair + 1) * LANES)
            pair_q, pair_g = query[here, columns], grad_mix[:, columns]
            pair_k, pair_v = key[:, columns], value[:, columns]
            grad_q = jnp.zeros((QUERY_BLOCK, LANES), jnp.float32)
            grad_k = jnp.zeros((keys, LANES), jnp.float32)
            grad_v = jnp.zeros((keys, LANES), jnp.float32)
            for head in range(LANES // HD):
                mine = lane // HD == head
                head_q = jnp.where(mine, pair_q, jnp.zeros_like(pair_q))
                head_g = jnp.where(mine, pair_g, jnp.zeros_like(pair_g))
                head_k = jnp.where(mine, pair_k, jnp.zeros_like(pair_k))
                at = pair * (LANES // HD) + head
                scores = product_t(pair_k, head_q) * score_scale + bias
                probs = jnp.exp(scores - logs[at : at + 1, here])
                grad_p = product_t(pair_v, head_g)
                dot = jnp.sum(probs * grad_p, axis=0, keepdims=True)
                grad_s = (probs * (grad_p - dot)).astype(jnp.bfloat16)
                grad_k = grad_k + product(grad_s, head_q)
                grad_v = grad_v + product(probs.astype(jnp.bfloat16), head_g)
                grad_q = grad_q + product_tn(grad_s, head_k)
            grad_query[here, columns] = (grad_q * score_scale).astype(jnp.bfloat16)
            ctx_acc[:, columns] += grad_k * score_scale
            ctx_acc[:, second] += grad_v
        split[here, :] = product_t(grad_query[here, :], c_query[...]).astype(jnp.bfloat16)
        over_heads(1, chunk).start()
        if chunk == HOP_CHUNK:
            third_to_fourth()
    ctx_grads[...] = ctx_acc[...].astype(jnp.bfloat16)
    cores.start(0, product_tn(grad_two_low[...], cross_mixed[...]))
    cores.start(1, product_tn(normed_two[...], grad_query[...]))
    for chunk in chunks:
        here = chunk_rows(chunk)
        total = summed(1, chunk)
        normal = normal_two[here, :]
        gain_terms[1:2, :] += jnp.sum(total * normal, axis=0, keepdims=True)
        grad_one = grad_h_one[here, :] + through_norm(
            total, normal, inverse_two[here, :], gains[1:2, :]
        )
        grad_h_one[here, :] = grad_one
        grad_one_low[here, :] = grad_one.astype(jnp.bfloat16)
        grad_attn[here, :] = product(grad_one_low[here, :], w_out[...]).astype(jnp.bfloat16)
    core_sums[0] = cores.finish(0)
    cores.close(0)
    ctx_rows = cores.terms.shape[3] // 2
    for which in range(2):
        term = product_tn(context[...], ctx_grads[:, which * part : (which + 1) * part])
        term = term.astype(jnp.bfloat16).reshape(-1, 2, ctx_rows, part)
        cores.terms[0, :, :, which * ctx_rows : (which + 1) * ctx_rows, :] = term
    cores.copy(2).start()
    for piece in range(1, 3):
        core_sums[piece] = cores.finish(piece)
    keep_copy(2).wait()
    whole = keep[0].astype(jnp.float32)
    for side in range(2):
        for slab in range(3):
            hop(side, 1, slab).wait_recv()
        whole = whole + fourth_land[side].astype(jnp.float32)
    share[...] = whole
    for side in range(2):
        for slab in range(3):
            hop(side, 0, slab).wait_send()
            hop(side, 1, slab).wait_send()
    for piece in range(1, 3):
        cores.close(piece)
    for chunk in chunks:
        over_heads(0, chunk).wait_send()
        over_heads(1, chunk).wait_send()


def mid_layer(
    grad_low, top, thirds, seconds, gains, weights, query, key, value, logs, slots, cross_mixed, normed_two, context, kept, moving, ctx_tokens, seq_count
):
    rows, width = grad_low.shape
    part = query.shape[1]
    keys = key.shape[0]
    head_count = lax.axis_size("head")
    chips, moved = seq_count // 2, moving.shape
    seg = moved[2]
    bf, wide = jnp.bfloat16, jnp.float32
    vmem = pl.BlockSpec(memory_space=pltpu.VMEM)

    def weight_spec(which):
        return pl.BlockSpec((width, part), lambda i: (0, which), pipeline_mode=pl.Buffered(1))

    scratches = [
        pltpu.VMEM((keys, 2 * part), wide),
        pltpu.VMEM((rows, width), bf),
        pltpu.VMEM((2, rows, width), bf),
        pltpu.SemaphoreType.DMA((2, rows // QUERY_BLOCK)),
        pltpu.SemaphoreType.DMA((2, rows // QUERY_BLOCK)),
    ]
    out_shapes = [
        jax.ShapeDtypeStruct((rows, width), wide),
        jax.ShapeDtypeStruct((rows, width), bf),
        jax.ShapeDtypeStruct((rows, width), bf),
        jax.ShapeDtypeStruct((rows, part), bf),
        jax.ShapeDtypeStruct((rows, part), bf),
        jax.ShapeDtypeStruct((keys, 2 * part), bf),
        jax.ShapeDtypeStruct((8, width), wide),
    ]
    scratches += [
        pltpu.VMEM(moved, bf),
        pltpu.VMEM(moved, bf),
        pltpu.SemaphoreType.DMA((2, 2, 3)),
        pltpu.SemaphoreType.DMA((2, 2, 3)),
        pltpu.VMEM((2, *moved[1:]), bf),
        pltpu.SemaphoreType.DMA((3,)),
        *core_scratch(3, chips, seg, part, 2),
    ]
    out_shapes += [
        jax.ShapeDtypeStruct(moved[1:], wide),
        jax.ShapeDtypeStruct((3, chips, seg, part), bf),
    ]
    return pl.pallas_call(
        functools.partial(
            mid_kernel, seq_count, head_count, HD ** (-0.5), ctx_tokens
        ),
        grid=(1,),
        in_specs=[
            *[vmem] * 7,
            weight_spec(5),
            weight_spec(4),
            weight_spec(3),
            *[vmem] * 8,
            pl.BlockSpec(memory_space=pl.ANY),
            pl.BlockSpec(memory_space=pl.ANY),
        ],
        out_specs=[vmem] * len(out_shapes),
        out_shape=out_shapes,
        scratch_shapes=scratches,
        compiler_params=pltpu.CompilerParams(
            collective_id=6, has_side_effects=True, vmem_limit_bytes=VMEM_BYTES
        ),
        cost_estimate=pl.CostEstimate(
            flops=10 * rows * keys * part + 6 * rows * width * part,
            bytes_accessed=100 * rows * width,
            transcendentals=rows * keys * part // HD,
        ),
        name="mid_layer",
    )(
        grad_low,
        top,
        *thirds,
        *seconds,
        gains,
        weights,
        weights,
        weights,
        query,
        key,
        value,
        logs,
        slots[None],
        cross_mixed,
        normed_two,
        context,
        kept,
        moving,
    )


def head_total(partial_sum):
    low = partial_sum
    if low.dtype != jnp.bfloat16:
        low = lax.optimization_barrier(partial_sum.astype(jnp.bfloat16))
    count = lax.axis_size("head")
    total = low.astype(jnp.float32)
    for step in range(1, count):
        pairs = [(index, (index + step) % count) for index in range(count)]
        total = total + lax.ppermute(low, "head", pairs).astype(jnp.float32)
    return total


def low_gather(block):
    return lax.all_gather(block.astype(jnp.bfloat16), "seq", axis=0, tiled=True)


def per_device(
    frames,
    time_token,
    prompt,
    clip_ids,
    norm1_gain,
    norm2_gain,
    norm3_gain,
    query_weight,
    key_weight,
    value_weight,
    out_weight,
    cross_query,
    cross_key,
    cross_value,
    cross_out,
    gate_weight,
    up_weight,
    down_weight,
    gate_bias,
    up_bias,
    down_bias,
    out_grad,
):
    local_rows, width = frames.shape
    clip_total = time_token.shape[0]
    ctx_tokens = prompt.shape[1]
    slot_count = local_rows // (2 * HALF) + 2
    seq_count = lax.axis_size("seq")
    seq_index = lax.axis_index("seq")
    head_index = lax.axis_index("head")
    first_row = seq_index * local_rows
    score_scale = HD ** (-0.5)
    part = query_weight.shape[1]
    hidden_width = gate_weight.shape[1]
    gain_rows = norm1_gain.shape[0]
    ctx_rows = cross_key.shape[0]
    ctx_width = prompt.shape[2]
    head_count = part // HD
    bias_rows = 2 * hidden_width // width
    small_rows = -(-max(clip_total + 1, bias_rows + 3) // 8) * 8
    vectors = jnp.stack([norm1_gain, norm2_gain, norm3_gain, down_bias], axis=1)
    vectors = jnp.pad(vectors, ((0, 0), (0, LANES - 4)))
    starts = [each * part for each in range(8)]
    attn_weights, glu_local = ring_gather(
        [
            query_weight,
            key_weight,
            value_weight,
            out_weight,
            cross_query,
            cross_out,
            cross_key,
            cross_value,
            vectors,
        ],
        [gate_weight, up_weight, down_weight],
        (*starts[:7], starts[7] + LANES),
        seq_count,
        4,
    )
    glu_weights = low_gather(glu_local)
    w_qkv = attn_weights[:, : starts[3]]
    w_out = attn_weights[:, starts[3] : starts[4]]
    c_query = attn_weights[:, starts[4] : starts[5]]
    c_out = attn_weights[:, starts[5] : starts[6]]
    ctx_weights = attn_weights[:, starts[6] : starts[7]].reshape(seq_count, 2, ctx_rows, part)
    c_key = ctx_weights[:, 0].reshape(ctx_width, part)
    c_value = ctx_weights[:, 1].reshape(ctx_width, part)
    rows_of = attn_weights[:, starts[7] : starts[7] + 8].astype(jnp.float32).T
    gain_one_f, gain_two_f, gain_three_f, bias_f = rows_of[0], rows_of[1], rows_of[2], rows_of[3]

    positions = first_row + jnp.arange(local_rows, dtype=jnp.int32)
    cos_table, sin_table = angles(positions)
    padded_ids = jnp.pad(clip_ids, (HALF, HALF), constant_values=-1)
    own_ids = lax.dynamic_slice_in_dim(clip_ids, first_row, local_rows)
    near_ids = lax.dynamic_slice_in_dim(padded_ids, first_row, local_rows + 2 * HALF)
    base_clip = jnp.minimum(own_ids[0], clip_total - slot_count)
    own_slot = own_ids - base_clip
    slot_range = jnp.arange(slot_count, dtype=jnp.int32)
    pad_rows = -slot_count % 16
    stamp_end = local_rows + slot_count

    stamp_rows = lax.dynamic_slice_in_dim(time_token, base_clip, slot_count, 0)
    source = jnp.concatenate(
        [frames, jnp.pad(stamp_rows, ((0, pad_rows), (0, 0)))], axis=0
    ).astype(jnp.float32)
    normed_out, normal_one, inverse_one = layer_norm_parts(source, gain_one_f)
    normed_one = normed_out.astype(jnp.bfloat16)
    frames_f = source[:local_rows]
    qkv = product(normed_one, w_qkv)
    query_rows = rotate(qkv[:local_rows, :part], cos_table, sin_table).astype(jnp.bfloat16)
    key_rows = rotate(qkv[:local_rows, part : 2 * part], cos_table, sin_table).astype(jnp.bfloat16)
    value_rows = qkv[:local_rows, 2 * part :].astype(jnp.bfloat16)
    near = extended(jnp.stack([key_rows, value_rows]), (("seq", 1),), HALF)
    window = local_rows + 2 * HALF
    near_key_h = near[0].reshape(window, head_count, HD)
    near_value_h = near[1].reshape(window, head_count, HD)
    query_h = query_rows.reshape(local_rows, head_count, HD)
    stamps = qkv[local_rows:].astype(jnp.bfloat16)
    stamp_key_h = stamps[:slot_count, part : 2 * part].reshape(slot_count, head_count, HD)
    stamp_value_h = stamps[:slot_count, 2 * part :].reshape(slot_count, head_count, HD)

    query_pos = jnp.arange(local_rows, dtype=jnp.int32)
    key_pos = jnp.arange(window, dtype=jnp.int32) - HALF
    visible = (own_ids[:, None] == near_ids[None, :]) & (
        jnp.abs(query_pos[:, None] - key_pos[None, :]) <= HALF
    )
    own_stamp = own_slot[:, None] == slot_range[None, :]
    self_keys = [(near_key_h, near_value_h, visible), (stamp_key_h, stamp_value_h, own_stamp)]
    attn_mix_h, self_logs = attend_forward(query_h, self_keys, score_scale)
    attn_mixed = attn_mix_h.reshape(local_rows, part).astype(jnp.bfloat16)
    h_one = frames_f + head_total(product_t(attn_mixed, w_out))
    middle_out, normal_two, inverse_two = layer_norm_parts(h_one, gain_two_f)
    normed_two = middle_out.astype(jnp.bfloat16)
    cross_rows = product(normed_two, c_query).astype(jnp.bfloat16)
    cross_h = cross_rows.reshape(local_rows, head_count, HD)
    context_rows = lax.dynamic_slice_in_dim(prompt, base_clip, slot_count, 0).reshape(
        slot_count * ctx_tokens, ctx_width
    )
    ctx_keys = product(context_rows, c_key).astype(jnp.bfloat16)
    ctx_key_h = ctx_keys.reshape(slot_count * ctx_tokens, head_count, HD)
    ctx_values = product(context_rows, c_value).astype(jnp.bfloat16)
    ctx_value_h = ctx_values.reshape(slot_count * ctx_tokens, head_count, HD)
    key_slot = jnp.arange(slot_count * ctx_tokens, dtype=jnp.int32) // ctx_tokens
    cross_keys = [(ctx_key_h, ctx_value_h, own_slot[:, None] == key_slot[None, :])]
    cross_mix_h, cross_logs = attend_forward(cross_h, cross_keys, score_scale)
    cross_mixed = cross_mix_h.reshape(local_rows, part).astype(jnp.bfloat16)
    h_two = h_one + head_total(product_t(cross_mixed, c_out))
    third_out, normal_three, inverse_three = layer_norm_parts(h_two, gain_three_f)
    normed_three = third_out.astype(jnp.bfloat16)

    glu_out, grad_normed_low, bias_local, glu_kept, glu_moving = glu_layer(
        normed_three,
        normed_three.T,
        out_grad,
        out_grad.T,
        glu_weights,
        gate_bias,
        up_bias,
        seq_count,
    )
    (
        grad_h_one,
        grad_two_low,
        grad_one_low,
        grad_attn,
        grad_cross_query,
        ctx_grads,
        gain_terms,
        glu_share,
        cross_sums,
    ) = mid_layer(
        grad_normed_low,
        out_grad,
        (normal_three, inverse_three),
        (normal_two, inverse_two),
        jnp.stack([gain_three_f, gain_two_f]),
        attn_weights,
        cross_rows,
        ctx_keys,
        ctx_values,
        cross_logs,
        own_slot,
        cross_mixed,
        normed_two,
        context_rows,
        glu_kept,
        glu_moving,
        ctx_tokens,
        seq_count,
    )
    gain_three_term, gain_two_term = gain_terms[0], gain_terms[1]
    down_bias_term = jnp.sum(out_grad.astype(jnp.float32), axis=0)
    grad_attn, glu_out = lax.optimization_barrier((grad_attn, glu_out))
    head_pairs = [(index, index ^ 1) for index in range(lax.axis_size("head"))]
    glu_other = lax.ppermute(glu_out, "head", head_pairs)
    ones = jnp.ones((local_rows, HD - ROT), jnp.float32)
    flat = jnp.zeros((local_rows, ROT // 2), jnp.float32)
    low_side = [sin_table, flat, 0 * ones]
    high_side = [flat, sin_table, 0 * ones]
    tables = jnp.stack(
        [
            jnp.tile(jnp.concatenate(each, axis=1), (1, LANES // HD))
            for each in ([cos_table, cos_table, ones], low_side, high_side)
        ]
    )
    grad_qkv, early_share, out_sum = self_back(
        query_rows,
        near,
        stamps,
        grad_attn,
        self_logs,
        near_ids,
        own_ids,
        own_slot,
        tables,
        cross_sums,
        grad_one_low,
        attn_mixed,
        score_scale,
        seq_count,
    )
    early_rows = jnp.concatenate(
        [
            bias_local.reshape(-1, width),
            jnp.stack([gain_two_term, gain_three_term, down_bias_term]),
        ],
        axis=0,
    )
    early_rows = jnp.pad(early_rows, ((0, small_rows - bias_rows - 3), (0, 0)))
    clip_range = jnp.arange(small_rows, dtype=jnp.int32)
    placing = (clip_range[:, None] - base_clip == slot_range[None, :]).astype(jnp.float32)
    qkv_share, small, frames_grad, result = tail_sums(
        normed_one.T,
        grad_qkv,
        attn_weights,
        (normal_one[:local_rows], inverse_one[:local_rows], gain_one_f[None]),
        grad_h_one,
        placing,
        early_rows,
        h_two,
        (glu_out, glu_other),
        bias_f[None],
        out_sum,
        clip_total,
        seq_count,
    )
    cross_out_share, cross_query_share, ctx_share = early_share
    out_share = qkv_share[0]
    late = small[: clip_total + 1]
    early = small[small_rows : small_rows + bias_rows + 3]
    stamp_sum = late[:clip_total]
    own_bias = early[:-3].reshape(2, hidden_width)
    every_out, every_normal, every_inverse = layer_norm_parts(
        time_token.astype(jnp.float32), gain_one_f
    )
    time_grad = norm_back(stamp_sum, every_normal, every_inverse, gain_one_f)
    time_gain = jnp.sum(stamp_sum * every_normal, axis=0)
    gains_own = lax.dynamic_slice_in_dim(
        jnp.concatenate([late[clip_total:] + time_gain[None], early[-3:]], axis=0),
        seq_index * gain_rows,
        gain_rows,
        1,
    )
    return (
        result,
        frames_grad,
        time_grad,
        gains_own[0],
        gains_own[1],
        gains_own[2],
        qkv_share[1],
        qkv_share[2],
        qkv_share[3],
        out_share,
        cross_query_share,
        ctx_share[:ctx_rows],
        ctx_share[ctx_rows:],
        cross_out_share,
        glu_share[0],
        glu_share[1],
        glu_share[2],
        own_bias[0],
        own_bias[1],
        gains_own[3],
    )


def solution(mesh):
    in_specs = (
        P("seq", None),
        P(),
        P(),
        P(),
        P("seq"),
        P("seq"),
        P("seq"),
        P("seq", "head"),
        P("seq", "head"),
        P("seq", "head"),
        P("seq", "head"),
        P("seq", "head"),
        P("seq", "head"),
        P("seq", "head"),
        P("seq", "head"),
        P("seq", "head"),
        P("seq", "head"),
        P("seq", "head"),
        P("head"),
        P("head"),
        P("seq"),
        P("seq", None),
    )
    out_specs = (
        P("seq", None),
        P("seq", None),
        P(),
        P("seq"),
        P("seq"),
        P("seq"),
        P("seq", "head"),
        P("seq", "head"),
        P("seq", "head"),
        P("seq", "head"),
        P("seq", "head"),
        P("seq", "head"),
        P("seq", "head"),
        P("seq", "head"),
        P("seq", "head"),
        P("seq", "head"),
        P("seq", "head"),
        P("head"),
        P("head"),
        P("seq"),
    )
    fast = mesh.shape["seq"] == FAST_SEQ
    return jax.shard_map(
        per_device if fast else per_device_plain, mesh=mesh, in_specs=in_specs, out_specs=out_specs, check_vma=False
    )
```

```python
import functools
from functools import reduce

import jax
import jax.numpy as jnp
from jax import lax
from jax.experimental import pallas as pl
from jax.experimental.pallas import tpu as pltpu
from jax.sharding import PartitionSpec as P

HD = 64
ROT = 32
HALF = 256


EPS = 1e-05
NEG = -1e30


def extended(block, sides, width):
    for axis, dim in sides:
        count = lax.axis_size(axis)
        forward = [(i, i + 1) for i in range(count - 1)]
        backward = [(target, source) for source, target in forward]
        low = lax.ppermute(
            lax.slice_in_dim(block, block.shape[dim] - width, None, axis=dim), axis, forward
        )
        high = lax.ppermute(lax.slice_in_dim(block, 0, width, axis=dim), axis, backward)
        block = jnp.concatenate([low, block, high], axis=dim)
    return block


def passed_along(value, axis, steps):
    count = lax.axis_size(axis)
    first, last = (max(0, -steps), min(count, count - steps))
    return lax.ppermute(value, axis, [(source, source + steps) for source in range(first, last)])


def layer_norm_parts(values, gain):
    average = jnp.mean(values, axis=-1, keepdims=True)
    centered = values - average
    spread = jnp.mean(centered * centered, axis=-1, keepdims=True)
    inverse = lax.rsqrt(spread + EPS)
    normal = centered * inverse
    return (normal * gain, normal, inverse)


def norm_back(grad_out, normal, inverse, gain):
    shaped = grad_out * gain
    return (
        shaped
        - jnp.mean(shaped, axis=-1, keepdims=True)
        - normal * jnp.mean(shaped * normal, axis=-1, keepdims=True)
    ) * inverse


def angles(positions):
    ladder = jnp.arange(ROT // 2, dtype=jnp.float32)
    frequency = 10000.0 ** (-2.0 * ladder / ROT)
    phases = positions.astype(jnp.float32)[:, None] * frequency[None, :]
    return (jnp.cos(phases), jnp.sin(phases))


def rotate(values, cos_table, sin_table):
    shaped = values.reshape(values.shape[0], -1, HD)
    rot_half = ROT // 2
    leading = shaped[:, :, :rot_half]
    trailing = shaped[:, :, rot_half:ROT]
    cos_row = cos_table[:, None, :]
    sin_row = sin_table[:, None, :]
    turned = jnp.concatenate(
        [
            leading * cos_row - trailing * sin_row,
            trailing * cos_row + leading * sin_row,
            shaped[:, :, ROT:],
        ],
        axis=-1,
    )
    return turned.reshape(values.shape)


def product(matrix_a, matrix_b):
    return jnp.dot(matrix_a, matrix_b, preferred_element_type=jnp.float32)


def product_t(matrix_a, matrix_b):
    return lax.dot_general(
        matrix_a, matrix_b, (((1,), (1,)), ((), ())), preferred_element_type=jnp.float32
    )


def product_tn(matrix_a, matrix_b):
    return lax.dot_general(
        matrix_a, matrix_b, (((0,), (0,)), ((), ())), preferred_element_type=jnp.float32
    )


def exact_t(matrix_a, matrix_b):
    return lax.dot_general(
        matrix_a,
        matrix_b,
        (((1,), (1,)), ((), ())),
        precision=lax.Precision.HIGHEST,
        preferred_element_type=jnp.float32,
    )


def exact_tn(matrix_a, matrix_b):
    return lax.dot_general(
        matrix_a,
        matrix_b,
        (((0,), (0,)), ((), ())),
        precision=lax.Precision.HIGHEST,
        preferred_element_type=jnp.float32,
    )


def score_parts(query_h, key_parts, score_scale):
    return [
        jnp.where(
            visible[None],
            jnp.einsum("qhd,khd->hqk", query_h, key_h, preferred_element_type=jnp.float32)
            * score_scale,
            NEG,
        )
        for key_h, value_h, visible in key_parts
    ]


def attend_forward(query_h, key_parts, score_scale):
    scores = score_parts(query_h, key_parts, score_scale)
    row_peak = reduce(jnp.maximum, [jnp.max(score_part, axis=-1) for score_part in scores])
    exp_parts = [jnp.exp(score_part - row_peak[:, :, None]) for score_part in scores]
    row_total = reduce(jnp.add, [jnp.sum(exp_part, axis=-1) for exp_part in exp_parts])
    attn_mixed = reduce(
        jnp.add,
        [
            jnp.einsum(
                "hqk,khd->qhd",
                (exp_part / row_total[:, :, None]).astype(jnp.bfloat16),
                key_part[1],
                preferred_element_type=jnp.float32,
            )
            for exp_part, key_part in zip(exp_parts, key_parts)
        ],
    )
    return (attn_mixed, row_peak + jnp.log(row_total))


def attend_backward(query_h, key_parts, score_scale, log_total, grad_h):
    scores = score_parts(query_h, key_parts, score_scale)
    prob_parts = [jnp.exp(score_part - log_total[:, :, None]) for score_part in scores]
    dprob_parts = [
        jnp.einsum("qhd,khd->hqk", grad_h, key_part[1], preferred_element_type=jnp.float32)
        for key_part in key_parts
    ]
    row_dot = reduce(
        jnp.add,
        [
            jnp.sum(prob_part * dprob_part, axis=-1)
            for prob_part, dprob_part in zip(prob_parts, dprob_parts)
        ],
    )
    dscore_parts = [
        (prob_part * (dprob_part - row_dot[:, :, None])).astype(jnp.bfloat16)
        for prob_part, dprob_part in zip(prob_parts, dprob_parts)
    ]
    grad_query = (
        reduce(
            jnp.add,
            [
                jnp.einsum(
                    "hqk,khd->qhd", dscore_part, key_part[0], preferred_element_type=jnp.float32
                )
                for dscore_part, key_part in zip(dscore_parts, key_parts)
            ],
        )
        * score_scale
    )
    grad_keys = [
        jnp.einsum("hqk,qhd->khd", dscore_part, query_h, preferred_element_type=jnp.float32)
        * score_scale
        for dscore_part in dscore_parts
    ]
    grad_values = [
        jnp.einsum(
            "hqk,qhd->khd",
            prob_part.astype(jnp.bfloat16),
            grad_h,
            preferred_element_type=jnp.float32,
        )
        for prob_part in prob_parts
    ]
    return (grad_query, grad_keys, grad_values)


def per_device_plain(
    frames,
    time_token,
    prompt,
    clip_ids,
    norm1_gain,
    norm2_gain,
    norm3_gain,
    query_weight,
    key_weight,
    value_weight,
    out_weight,
    cross_query,
    cross_key,
    cross_value,
    cross_out,
    gate_weight,
    up_weight,
    down_weight,
    gate_bias,
    up_bias,
    down_bias,
    out_grad,
):
    local_rows = frames.shape[0]
    clip_total = time_token.shape[0]
    ctx_tokens = prompt.shape[1]
    slot_count = local_rows // (2 * HALF) + 2
    seq_index = lax.axis_index("seq")
    head_index = lax.axis_index("head")
    first_row = seq_index * local_rows
    score_scale = HD ** (-0.5)
    block_rows = min(local_rows, 2 * HALF)
    block_count = local_rows // block_rows
    window = block_rows + 2 * HALF
    block_indices = jnp.arange(block_count, dtype=jnp.int32)

    def branch_total(partial_sum):
        return lax.psum(partial_sum.astype(jnp.bfloat16), "head").astype(jnp.float32)

    def back_total(partial_sum):
        return lax.psum(partial_sum.astype(jnp.bfloat16), "head").astype(jnp.float32)

    (
        gain_one,
        gain_two,
        gain_three,
        w_query,
        w_key,
        w_value,
        w_out,
        c_query,
        c_key,
        c_value,
        c_out,
        w_gate,
        w_up,
        w_down,
        b_down,
    ) = (
        lax.all_gather(norm1_gain.astype(jnp.bfloat16), "seq", axis=0, tiled=True),
        lax.all_gather(norm2_gain.astype(jnp.bfloat16), "seq", axis=0, tiled=True),
        lax.all_gather(norm3_gain.astype(jnp.bfloat16), "seq", axis=0, tiled=True),
        lax.all_gather(query_weight.astype(jnp.bfloat16), "seq", axis=0, tiled=True),
        lax.all_gather(key_weight.astype(jnp.bfloat16), "seq", axis=0, tiled=True),
        lax.all_gather(value_weight.astype(jnp.bfloat16), "seq", axis=0, tiled=True),
        lax.all_gather(out_weight.astype(jnp.bfloat16), "seq", axis=0, tiled=True),
        lax.all_gather(cross_query.astype(jnp.bfloat16), "seq", axis=0, tiled=True),
        lax.all_gather(cross_key.astype(jnp.bfloat16), "seq", axis=0, tiled=True),
        lax.all_gather(cross_value.astype(jnp.bfloat16), "seq", axis=0, tiled=True),
        lax.all_gather(cross_out.astype(jnp.bfloat16), "seq", axis=0, tiled=True),
        lax.all_gather(gate_weight.astype(jnp.bfloat16), "seq", axis=0, tiled=True),
        lax.all_gather(up_weight.astype(jnp.bfloat16), "seq", axis=0, tiled=True),
        lax.all_gather(down_weight.astype(jnp.bfloat16), "seq", axis=0, tiled=True),
        lax.all_gather(down_bias.astype(jnp.bfloat16), "seq", axis=0, tiled=True),
    )
    gain_one_f = gain_one.astype(jnp.float32)
    gain_two_f = gain_two.astype(jnp.float32)
    positions = first_row + jnp.arange(local_rows, dtype=jnp.int32)
    cos_table, sin_table = angles(positions)
    padded_ids = jnp.pad(clip_ids, (HALF, HALF), constant_values=-1)
    own_ids = lax.dynamic_slice_in_dim(clip_ids, first_row, local_rows)
    near_ids = lax.dynamic_slice_in_dim(padded_ids, first_row, local_rows + 2 * HALF)
    base_clip = jnp.minimum(own_ids[0], clip_total - slot_count)
    own_slot = own_ids - base_clip
    slot_range = jnp.arange(slot_count, dtype=jnp.int32)
    frames_f = frames.astype(jnp.float32)
    normed_out, normal_one, inverse_one = layer_norm_parts(frames_f, gain_one_f)
    normed_one = normed_out.astype(jnp.bfloat16)
    query_rows = rotate(product(normed_one, w_query), cos_table, sin_table).astype(jnp.bfloat16)
    key_rows = rotate(product(normed_one, w_key), cos_table, sin_table).astype(jnp.bfloat16)
    value_rows = product(normed_one, w_value).astype(jnp.bfloat16)
    local_width = query_rows.shape[1]
    head_count = local_width // HD
    near = extended(jnp.stack([key_rows, value_rows]), (("seq", 1),), HALF)
    near_key_h = near[0].reshape(local_rows + 2 * HALF, head_count, HD)
    near_value_h = near[1].reshape(local_rows + 2 * HALF, head_count, HD)
    query_all_h = query_rows.reshape(local_rows, head_count, HD)
    stamp_rows = lax.dynamic_slice_in_dim(time_token, base_clip, slot_count, 0).astype(jnp.float32)
    stamp_out, stamp_normal, stamp_inverse = layer_norm_parts(stamp_rows, gain_one_f)
    stamp_normed = stamp_out.astype(jnp.bfloat16)
    stamp_key_h = (
        product(stamp_normed, w_key).astype(jnp.bfloat16).reshape(slot_count, head_count, HD)
    )
    stamp_value_h = (
        product(stamp_normed, w_value).astype(jnp.bfloat16).reshape(slot_count, head_count, HD)
    )

    def self_parts(block_index):
        row_start = block_index * block_rows
        query_pos = row_start + jnp.arange(block_rows, dtype=jnp.int32)
        key_pos = row_start - HALF + jnp.arange(window, dtype=jnp.int32)
        visible = (own_ids[:, None] == near_ids[None, :]) & (
            jnp.abs(query_pos[:, None] - key_pos[None, :]) <= HALF
        )
        own_stamp = own_slot[:, None] == slot_range[None, :]
        return (
            query_all_h,
            [(near_key_h, near_value_h, visible), (stamp_key_h, stamp_value_h, own_stamp)],
        )

    def self_forward(block_index):
        query_h, key_parts = self_parts(block_index)
        attn_mixed, log_total = attend_forward(query_h, key_parts, score_scale)
        return (attn_mixed.reshape(block_rows, local_width).astype(jnp.bfloat16), log_total)

    attn_blocks, self_logs = lax.map(self_forward, block_indices)
    attn_mixed = attn_blocks.reshape(local_rows, local_width)
    h_one = frames_f + branch_total(product_t(attn_mixed, w_out))
    middle_out, normal_two, inverse_two = layer_norm_parts(h_one, gain_two_f)
    normed_two = middle_out.astype(jnp.bfloat16)
    cross_rows = product(normed_two, c_query).astype(jnp.bfloat16)
    cross_all_h = cross_rows.reshape(local_rows, head_count, HD)
    context_rows = lax.dynamic_slice_in_dim(prompt, base_clip, slot_count, 0).reshape(
        slot_count * ctx_tokens, prompt.shape[2]
    )
    ctx_key_h = (
        product(context_rows, c_key)
        .astype(jnp.bfloat16)
        .reshape(slot_count * ctx_tokens, head_count, HD)
    )
    ctx_value_h = (
        product(context_rows, c_value)
        .astype(jnp.bfloat16)
        .reshape(slot_count * ctx_tokens, head_count, HD)
    )
    key_slot = jnp.arange(slot_count * ctx_tokens, dtype=jnp.int32) // ctx_tokens

    def cross_parts(block_index):
        row_start = block_index * block_rows
        visible = own_slot[:, None] == key_slot[None, :]
        return (cross_all_h, [(ctx_key_h, ctx_value_h, visible)])

    def cross_forward(block_index):
        query_h, key_parts = cross_parts(block_index)
        cross_mix, log_total = attend_forward(query_h, key_parts, score_scale)
        return (cross_mix.reshape(block_rows, local_width).astype(jnp.bfloat16), log_total)

    cross_blocks, cross_logs = lax.map(cross_forward, block_indices)
    cross_mixed = cross_blocks.reshape(local_rows, local_width)
    h_two = h_one + branch_total(product_t(cross_mixed, c_out))
    gain_three_f = gain_three.astype(jnp.float32)
    third_out, normal_three, inverse_three = layer_norm_parts(h_two, gain_three_f)
    normed_three = third_out.astype(jnp.bfloat16)
    gate_pre = product(normed_three, w_gate) + gate_bias
    up_pre = product(normed_three, w_up) + up_bias
    hidden = (jax.nn.silu(gate_pre) * up_pre).astype(jnp.bfloat16)
    result = (h_two + branch_total(product_t(hidden, w_down)) + b_down.astype(jnp.float32)).astype(
        jnp.bfloat16
    )
    grad_top = out_grad.astype(jnp.float32)
    grad_hidden = product(out_grad, w_down)
    sigmoid_gate = jax.nn.sigmoid(gate_pre)
    grad_up = (grad_hidden * gate_pre * sigmoid_gate).astype(jnp.bfloat16)
    grad_gate = (
        grad_hidden * up_pre * sigmoid_gate * (1.0 + gate_pre * (1.0 - sigmoid_gate))
    ).astype(jnp.bfloat16)
    gate_bias_local = jnp.sum(grad_gate.astype(jnp.float32), axis=0)
    up_bias_local = jnp.sum(grad_up.astype(jnp.float32), axis=0)
    grad_normed_three = back_total(product_t(grad_gate, w_gate) + product_t(grad_up, w_up))
    glu_terms = (
        product_tn(normed_three, grad_gate),
        product_tn(normed_three, grad_up),
        product_tn(out_grad, hidden),
        jnp.sum(grad_normed_three * normal_three, axis=0),
        jnp.sum(grad_top, axis=0),
    )
    grad_h_two = grad_top + norm_back(grad_normed_three, normal_three, inverse_three, gain_three_f)
    grad_two_low = grad_h_two.astype(jnp.bfloat16)
    grad_cross_mixed = product(grad_two_low, c_out).astype(jnp.bfloat16)
    cross_out_term = product_tn(grad_two_low, cross_mixed)
    grad_cross_h = grad_cross_mixed.reshape(local_rows, head_count, HD)

    def cross_step(ctx_grads, block_index):
        query_h, key_parts = cross_parts(block_index)
        grad_query, grad_keys, grad_values = attend_backward(
            query_h, key_parts, score_scale, cross_logs[block_index], grad_cross_h
        )
        return (ctx_grads + jnp.stack([grad_keys[0], grad_values[0]]), grad_query)

    ctx_grads, grad_cross_q = lax.scan(
        cross_step,
        jnp.zeros((2, slot_count * ctx_tokens, head_count, HD), jnp.float32),
        block_indices,
    )
    grad_cross_query = grad_cross_q.reshape(local_rows, local_width).astype(jnp.bfloat16)
    context_float = context_rows.astype(jnp.float32)
    cross_key_term = exact_tn(context_float, ctx_grads[0].reshape(-1, local_width))
    cross_value_term = exact_tn(context_float, ctx_grads[1].reshape(-1, local_width))
    cross_query_term = product_tn(normed_two, grad_cross_query)
    grad_normed_two = back_total(product_t(grad_cross_query, c_query))
    gain_two_term = jnp.sum(grad_normed_two * normal_two, axis=0)
    grad_h_one = grad_h_two + norm_back(grad_normed_two, normal_two, inverse_two, gain_two_f)
    grad_one_low = grad_h_one.astype(jnp.bfloat16)
    grad_attn = product(grad_one_low, w_out).astype(jnp.bfloat16)
    out_term = product_tn(grad_one_low, attn_mixed)
    grad_attn_h = grad_attn.reshape(local_rows, head_count, HD)

    def self_step(grad_state, block_index):
        near_grads, stamp_grads = grad_state
        query_h, key_parts = self_parts(block_index)
        row_start = block_index * block_rows
        grad_query, grad_keys, grad_values = attend_backward(
            query_h, key_parts, score_scale, self_logs[block_index], grad_attn_h
        )
        prior = near_grads
        near_grads = prior + jnp.stack([grad_keys[0], grad_values[0]])
        stamp_grads = stamp_grads + jnp.stack([grad_keys[1], grad_values[1]])
        return ((near_grads, stamp_grads), grad_query)

    start_state = (
        jnp.zeros((2, local_rows + 2 * HALF, head_count, HD), jnp.float32),
        jnp.zeros((2, slot_count, head_count, HD), jnp.float32),
    )
    (near_grads, stamp_grads), grad_query_blocks = lax.scan(self_step, start_state, block_indices)
    near_grads = near_grads.reshape(2, local_rows + 2 * HALF, local_width)
    from_above = passed_along(near_grads[:, :HALF].astype(jnp.bfloat16), "seq", -1).astype(
        jnp.float32
    )
    from_below = passed_along(
        near_grads[:, HALF + local_rows :].astype(jnp.bfloat16), "seq", 1
    ).astype(jnp.float32)
    own_grads = (
        near_grads[:, HALF : HALF + local_rows]
        + jnp.pad(from_below, ((0, 0), (0, local_rows - HALF), (0, 0)))
        + jnp.pad(from_above, ((0, 0), (local_rows - HALF, 0), (0, 0)))
    )
    grad_query_rows = rotate(
        grad_query_blocks.reshape(local_rows, local_width), cos_table, -sin_table
    ).astype(jnp.bfloat16)
    grad_key_rows = rotate(own_grads[0], cos_table, -sin_table).astype(jnp.bfloat16)
    grad_value_rows = own_grads[1].astype(jnp.bfloat16)
    stamp_key_grad = stamp_grads[0].reshape(slot_count, local_width)
    stamp_value_grad = stamp_grads[1].reshape(slot_count, local_width)
    stamp_float = stamp_normed.astype(jnp.float32)
    query_term = product_tn(normed_one, grad_query_rows)
    key_term = product_tn(normed_one, grad_key_rows) + exact_tn(stamp_float, stamp_key_grad)
    value_term = product_tn(normed_one, grad_value_rows) + exact_tn(stamp_float, stamp_value_grad)
    grad_normed_one = back_total(
        product_t(grad_query_rows, w_query)
        + product_t(grad_key_rows, w_key)
        + product_t(grad_value_rows, w_value)
    )
    gain_one_term = jnp.sum(grad_normed_one * normal_one, axis=0)
    frames_grad = (
        grad_h_one + norm_back(grad_normed_one, normal_one, inverse_one, gain_one_f)
    ).astype(jnp.bfloat16)
    stamp_partial = exact_t(stamp_key_grad, w_key.astype(jnp.float32)) + exact_t(
        stamp_value_grad, w_value.astype(jnp.float32)
    )
    attn_shares = (
        lax.psum_scatter(query_term, "seq", scatter_dimension=0, tiled=True),
        lax.psum_scatter(key_term, "seq", scatter_dimension=0, tiled=True),
        lax.psum_scatter(value_term, "seq", scatter_dimension=0, tiled=True),
        lax.psum_scatter(out_term, "seq", scatter_dimension=0, tiled=True),
        lax.psum_scatter(cross_query_term, "seq", scatter_dimension=0, tiled=True),
        lax.psum_scatter(cross_key_term, "seq", scatter_dimension=0, tiled=True),
        lax.psum_scatter(cross_value_term, "seq", scatter_dimension=0, tiled=True),
        lax.psum_scatter(cross_out_term, "seq", scatter_dimension=0, tiled=True),
        lax.psum_scatter(gain_one_term, "seq", scatter_dimension=0, tiled=True),
        lax.psum_scatter(gain_two_term, "seq", scatter_dimension=0, tiled=True),
    )
    hidden_width = gate_bias.shape[0]
    stamp_full = lax.dynamic_update_slice_in_dim(
        jnp.zeros((clip_total, stamp_partial.shape[1]), jnp.float32), stamp_partial, base_clip, 0
    )
    bias_full = lax.dynamic_update_slice_in_dim(
        jnp.zeros((2, hidden_width * lax.axis_size("head")), jnp.float32),
        jnp.stack([gate_bias_local, up_bias_local]),
        head_index * hidden_width,
        1,
    )
    stamp_sum, bias_sum = lax.psum((stamp_full, bias_full), ("seq", "head"))
    every_out, every_normal, every_inverse = layer_norm_parts(
        time_token.astype(jnp.float32), gain_one_f
    )
    time_grad = norm_back(stamp_sum, every_normal, every_inverse, gain_one_f)
    gain_rows = norm1_gain.shape[0]
    time_gain = lax.dynamic_slice_in_dim(
        jnp.sum(stamp_sum * every_normal, axis=0), seq_index * gain_rows, gain_rows
    )
    own_bias = lax.dynamic_slice_in_dim(bias_sum, head_index * hidden_width, hidden_width, 1)
    return (
        result,
        frames_grad,
        time_grad,
        attn_shares[8] + time_gain,
        attn_shares[9],
        lax.psum_scatter(glu_terms[3], "seq", scatter_dimension=0, tiled=True),
        attn_shares[0],
        attn_shares[1],
        attn_shares[2],
        attn_shares[3],
        attn_shares[4],
        attn_shares[5],
        attn_shares[6],
        attn_shares[7],
        lax.psum_scatter(glu_terms[0], "seq", scatter_dimension=0, tiled=True),
        lax.psum_scatter(glu_terms[1], "seq", scatter_dimension=0, tiled=True),
        lax.psum_scatter(glu_terms[2], "seq", scatter_dimension=0, tiled=True),
        own_bias[0],
        own_bias[1],
        lax.psum_scatter(glu_terms[4], "seq", scatter_dimension=0, tiled=True),
    )


LANES = 128
FAST_SEQ = 16
BLOCK = 256
TAIL_WIDTH = 768
QUERY_BLOCK = 128
HOP_CHUNK = 1
MADE_AT = 1
VMEM_BYTES = 60 * 1024 * 1024
MESH = pl.DeviceIdType.MESH


def xor_place(index, bit):
    return index + bit * (1 - 2 * (index // bit % 2))


def chip_near(seq_index, seq_count, step):
    chips = seq_count // 2
    chip = seq_index // 2
    odd = chip % 2
    place = (1 - odd) * (chip // 2) + odd * (chips - 1 - chip // 2)
    there = (place + chips + step) % chips
    upper = there // (chips // 2)
    return (1 - upper) * 2 * there + upper * (2 * (chips - 1 - there) + 1)


def ring_neighbours(seq_index, seq_count):
    return [2 * chip_near(seq_index, seq_count, step) + seq_index % 2 for step in (1, -1)]


def gather_kernel(seq_count, bounds, count, later_count, *refs):
    wides, refs = refs[:count], refs[count:]
    later, refs = refs[:later_count], refs[later_count:]
    out, later_out, refs = refs[0], refs[1], refs[2:]
    wide_bufs, later_bufs, refs = refs[:count], refs[count : count + later_count], refs[count + later_count :]
    (
        local,
        later_local,
        in_sems,
        later_sem,
        own_sem,
        ring_send,
        ring_recv,
        core_send,
        core_recv,
    ) = refs
    loads = [
        pltpu.make_async_copy(source, target, in_sems.at[at])
        for at, (source, target) in enumerate(
            zip([*wides, *later], [*wide_bufs, *later_bufs])
        )
    ]
    for load in loads:
        load.start()
    far = seq_count // 4
    seq_index = lax.axis_index("seq")
    core = seq_index % 2
    partner = {"seq": xor_place(seq_index, 1)}
    sides = ring_neighbours(seq_index, seq_count)
    greet([partner] + [{"seq": side} for side in sides])

    def columns_of(piece, side, hop):
        low, high = bounds[piece], bounds[piece + 1]
        if hop == far - 1:
            mid = low + (high - low) // (2 * LANES) * LANES
            low, high = (low, mid) if side == 0 else (mid, high)
        return pl.ds(low, high - low)

    def ring_copy(piece, side, hop):
        columns = columns_of(piece, side, hop)
        target = out.at[
            chip_near(seq_index, seq_count, -hop if side == 0 else hop), core, :, columns
        ]
        return pltpu.make_async_remote_copy(
            src_ref=local.at[:, columns] if hop == 0 else target,
            dst_ref=target,
            send_sem=ring_send.at[piece, side, hop],
            recv_sem=ring_recv.at[piece, side, hop],
            device_id={"seq": sides[side]},
            device_id_type=MESH,
        )

    def core_copy(piece, side, hop):
        if hop < 0:
            columns = pl.ds(bounds[piece], bounds[piece + 1] - bounds[piece])
            target = out.at[seq_index // 2, core, :, columns]
            source = local.at[:, columns]
        else:
            chip = chip_near(seq_index, seq_count, -1 - hop if side == 0 else 1 + hop)
            target = out.at[chip, core, :, columns_of(piece, side, hop)]
            source = target
        return pltpu.make_async_remote_copy(
            src_ref=source,
            dst_ref=target,
            send_sem=core_send.at[piece, side, hop + 1],
            recv_sem=core_recv.at[piece, side, hop + 1],
            device_id=partner,
            device_id_type=MESH,
        )

    def wides_of(piece):
        if piece < len(bounds) - 2:
            return [(0, 0, piece)]
        height, width = wides[piece].shape
        return [(0, 0, piece), (height, 0, piece + 1), (0, width, piece + 2)]

    pieces = range(len(bounds) - 1)
    arrivals = [(piece, side, hop) for hop in range(far) for piece in pieces for side in range(2)]
    own_copy = pltpu.make_async_copy(local, out.at[seq_index // 2, core], own_sem)
    for piece in pieces:
        for row, column, at in wides_of(piece):
            height, width = wides[at].shape
            column += bounds[piece]
            loads[at].wait()
            local[row : row + height, column : column + width] = wide_bufs[at][...].astype(
                jnp.bfloat16
            )
        for side in range(2):
            ring_copy(piece, side, 0).start()
        core_copy(piece, 0, -1).start()
    own_copy.start()
    for at, wide in enumerate(later_bufs):
        width = wide.shape[1]
        loads[count + at].wait()
        later_local[:, at * width : (at + 1) * width] = wide[...].astype(jnp.bfloat16)
    later_copy = pltpu.make_async_copy(later_local, later_out, later_sem)
    later_copy.start()
    for piece, side, hop in arrivals:
        ring_copy(piece, side, hop).wait_recv()
        if hop + 1 < far:
            ring_copy(piece, side, hop + 1).start()
        core_copy(piece, side, hop).start()
    crossed = [(piece, 0, -1) for piece in pieces] + arrivals
    for piece, side, hop in crossed:
        core_copy(piece, side, hop).wait_recv()
    own_copy.wait()
    later_copy.wait()
    for piece, side, hop in crossed:
        core_copy(piece, side, hop).wait_send()
    for piece, side, hop in arrivals:
        ring_copy(piece, side, hop).wait_send()


def ring_gather(wides, later, bounds, seq_count, collective_id):
    rows, width = wides[0].shape[0], bounds[-1]
    pieces, far = len(bounds) - 1, seq_count // 4
    later_width = sum(each.shape[1] for each in later)
    hbm = pl.BlockSpec(memory_space=pltpu.HBM)
    gathered, later = pl.pallas_call(
        functools.partial(gather_kernel, seq_count, bounds, len(wides), len(later)),
        in_specs=[hbm] * (len(wides) + len(later)),
        out_specs=[hbm, hbm],
        out_shape=[
            jax.ShapeDtypeStruct((seq_count // 2, 2, rows, width), jnp.bfloat16),
            jax.ShapeDtypeStruct((rows, later_width), jnp.bfloat16),
        ],
        scratch_shapes=[
            *(pltpu.VMEM(each.shape, jnp.float32) for each in (*wides, *later)),
            pltpu.VMEM((rows, width), jnp.bfloat16),
            pltpu.VMEM((rows, later_width), jnp.bfloat16),
            pltpu.SemaphoreType.DMA((len(wides) + len(later),)),
            pltpu.SemaphoreType.DMA,
            pltpu.SemaphoreType.DMA,
            pltpu.SemaphoreType.DMA((pieces, 2, far)),
            pltpu.SemaphoreType.DMA((pieces, 2, far)),
            pltpu.SemaphoreType.DMA((pieces, 2, far + 1)),
            pltpu.SemaphoreType.DMA((pieces, 2, far + 1)),
        ],
        compiler_params=pltpu.CompilerParams(
            collective_id=collective_id, has_side_effects=True, vmem_limit_bytes=VMEM_BYTES
        ),
        cost_estimate=pl.CostEstimate(
            flops=0, bytes_accessed=32 * rows * seq_count * width, transcendentals=0
        ),
        name="ring_gather",
    )(*wides, *later)
    return gathered.reshape(seq_count * rows, width), later


def kept_places(seq_count):
    chips = seq_count // 2
    far = chips // 2
    return [*range(far - 2), *range(far + 3, chips)]


def glu_kernel(
    blocks,
    seq_count,
    normed,
    normed_t,
    top,
    top_t,
    w_gate,
    w_up,
    w_down,
    b_gate,
    b_up,
    out,
    grad_normed,
    bias_grads,
    kept,
    *refs,
):
    index = pl.program_id(0)
    seq_index = lax.axis_index("seq")
    partner = {"seq": xor_place(seq_index, 1)}
    core = seq_index % 2
    chips = seq_count // 2
    far = chips // 2
    mid = BLOCK // 2
    moving, out_acc, grad_acc, terms, arrived, send_sem, recv_sem, *refs = refs
    sides = ring_neighbours(seq_index, seq_count)
    sums, first_send, first_land, second_send, second_land, *ring_sems = refs

    def crossing(block):
        return pltpu.make_async_remote_copy(
            src_ref=terms.at[block % 2, :, :, 1 - core],
            dst_ref=arrived.at[block],
            send_sem=send_sem.at[block % 2],
            recv_sem=recv_sem.at[block],
            device_id=partner,
            device_id_type=MESH,
        )

    def hop(block, side, which):
        source, target = (first_send, first_land) if which == 0 else (second_send, second_land)
        return pltpu.make_async_remote_copy(
            src_ref=source.at[block, side],
            dst_ref=target.at[block, side],
            send_sem=ring_sems[2 * which].at[block, side],
            recv_sem=ring_sems[2 * which + 1].at[block, side],
            device_id={"seq": sides[side]},
            device_id_type=MESH,
        )

    @pl.when(index == 0)
    def _():
        greet([partner] + [{"seq": side} for side in sides])
        out_acc[...] = jnp.zeros_like(out_acc)
        grad_acc[...] = jnp.zeros_like(grad_acc)

    @pl.when(index < blocks)
    def _():
        gate_pre = product(normed[...], w_gate[...]) + b_gate[...]
        up_pre = product(normed[...], w_up[...]) + b_up[...]
        grad_hidden = product(top[...], w_down[...])
        sigmoid_gate = jax.nn.sigmoid(gate_pre)
        silu_gate = gate_pre * sigmoid_gate
        hidden = (silu_gate * up_pre).astype(jnp.bfloat16)
        grad_up = (grad_hidden * silu_gate).astype(jnp.bfloat16)
        grad_gate = (
            grad_hidden * up_pre * sigmoid_gate * (1.0 + gate_pre * (1.0 - sigmoid_gate))
        ).astype(jnp.bfloat16)
        bias_grads[0:1, :] = jnp.sum(grad_gate.astype(jnp.float32), axis=0, keepdims=True)
        bias_grads[1:2, :] = jnp.sum(grad_up.astype(jnp.float32), axis=0, keepdims=True)
        out_acc[...] += product_t(hidden, w_down[...])
        grad_acc[...] += product_t(grad_gate, w_gate[...]) + product_t(grad_up, w_up[...])

        @pl.when(index >= 2)
        def _():
            crossing(index - 2).wait_send()

        slot = index % 2
        for which, (rows_t, columns) in enumerate(
            ((normed_t, grad_gate), (normed_t, grad_up), (top_t, hidden))
        ):
            term = product(rows_t[...], columns).astype(jnp.bfloat16)
            terms[slot, which] = term.reshape(terms.shape[2:])
        crossing(index).start()

    def chunk(block, near):
        return sums[block % 3, :, chip_near(seq_index, seq_count, near)]

    @pl.when((index >= 1) & (index <= blocks))
    def _():
        block = index - 1
        crossing(block).wait_recv()
        total = terms[block % 2, :, :, core].astype(jnp.float32) + arrived[block].astype(
            jnp.float32
        )
        sums[block % 3] = total.astype(jnp.bfloat16)
        opposite = chunk(block, far)
        for side in range(2):
            first_send[block, side] = opposite[:, :, side * mid : (side + 1) * mid]
            hop(block, side, 0).start()
        for at, near in enumerate(kept_places(seq_count)):
            kept[at] = chunk(block, near)

    @pl.when((index >= 2) & (index <= blocks + 1))
    def _():
        block = index - 2
        for side in range(2):
            term = chunk(block, far - 1 if side == 0 else far + 1).astype(jnp.float32)
            hop(block, side, 0).wait_recv()
            land = first_land[block, side].astype(jnp.float32)
            low = term[:, :, :mid] + land if side == 0 else term[:, :, :mid]
            high = term[:, :, mid:] if side == 0 else term[:, :, mid:] + land
            second_send[block, side, :, :, :mid] = low.astype(jnp.bfloat16)
            second_send[block, side, :, :, mid:] = high.astype(jnp.bfloat16)
            hop(block, side, 1).start()

    @pl.when(index >= 3)
    def _():
        block = index - 3
        for side in range(2):
            term = chunk(block, far - 2 if side == 0 else far + 2).astype(jnp.float32)
            hop(block, side, 1).wait_recv()
            land = second_land[block, side].astype(jnp.float32)
            moving[side] = (term + land).astype(jnp.bfloat16)

    @pl.when(index == blocks)
    def _():
        crossing(blocks - 2).wait_send()
        crossing(blocks - 1).wait_send()
        out[...] = out_acc[...].astype(jnp.bfloat16)
        grad_normed[...] = grad_acc[...].astype(jnp.bfloat16)

    @pl.when(index == blocks + 2)
    def _():
        for block in range(blocks):
            for side in range(2):
                hop(block, side, 0).wait_send()
                hop(block, side, 1).wait_send()


def glu_layer(normed, normed_t, top, top_t, weights, gate_bias, up_bias, seq_count):
    rows, width = normed.shape
    hidden_width = gate_bias.shape[0]
    blocks = hidden_width // BLOCK
    chips = seq_count // 2
    seg = width // seq_count
    kept = len(kept_places(seq_count))
    bf = jnp.bfloat16

    def whole(shape):
        return pl.BlockSpec(shape, lambda i: (0, 0), pipeline_mode=pl.Buffered(1))

    def at(lag):
        return lambda i: jnp.clip(i - lag, 0, blocks - 1)

    def weight_spec(which):
        return pl.BlockSpec((width, BLOCK), lambda i: (0, which * blocks + at(0)(i)))

    bias_spec = pl.BlockSpec((1, BLOCK), lambda i: (0, at(0)(i)))
    work = rows * width * hidden_width
    term_specs = [
        pl.BlockSpec((kept, 3, seg, BLOCK), lambda i: (0, 0, 0, at(1)(i))),
        pl.BlockSpec((2, 3, seg, BLOCK), lambda i: (0, 0, 0, at(3)(i))),
    ]
    term_shapes = [
        jax.ShapeDtypeStruct((kept, 3, seg, hidden_width), bf),
        jax.ShapeDtypeStruct((2, 3, seg, hidden_width), bf),
    ]
    return pl.pallas_call(
        functools.partial(glu_kernel, blocks, seq_count),
        grid=(blocks + 3,),
        in_specs=[
            whole((rows, width)),
            whole((width, rows)),
            whole((rows, width)),
            whole((width, rows)),
            weight_spec(0),
            weight_spec(1),
            weight_spec(2),
            bias_spec,
            bias_spec,
        ],
        out_specs=[
            pl.BlockSpec((rows, width), lambda i: (0, 0)),
            pl.BlockSpec((rows, width), lambda i: (0, 0)),
            pl.BlockSpec((2, BLOCK), lambda i: (0, at(0)(i))),
            *term_specs,
        ],
        out_shape=[
            jax.ShapeDtypeStruct((rows, width), bf),
            jax.ShapeDtypeStruct((rows, width), bf),
            jax.ShapeDtypeStruct((2, hidden_width), jnp.float32),
            *term_shapes,
        ],
        scratch_shapes=[
            pltpu.VMEM((rows, width), jnp.float32),
            pltpu.VMEM((rows, width), jnp.float32),
            pltpu.VMEM((2, 3, chips, 2, seg, BLOCK), bf),
            pltpu.VMEM((blocks, 3, chips, seg, BLOCK), bf),
            pltpu.SemaphoreType.DMA((2,)),
            pltpu.SemaphoreType.DMA((blocks,)),
            pltpu.VMEM((3, 3, chips, seg, BLOCK), bf),
            pltpu.VMEM((blocks, 2, 3, seg, BLOCK // 2), bf),
            pltpu.VMEM((blocks, 2, 3, seg, BLOCK // 2), bf),
            pltpu.VMEM((blocks, 2, 3, seg, BLOCK), bf),
            pltpu.VMEM((blocks, 2, 3, seg, BLOCK), bf),
            *(pltpu.SemaphoreType.DMA((blocks, 2)) for _ in range(4)),
        ],
        compiler_params=pltpu.CompilerParams(
            collective_id=1, has_side_effects=True, vmem_limit_bytes=VMEM_BYTES
        ),
        cost_estimate=pl.CostEstimate(
            flops=18 * work, bytes_accessed=12 * width * hidden_width, transcendentals=rows * hidden_width
        ),
        name="glu_layer",
    )(
        normed,
        normed_t,
        top,
        top_t,
        weights,
        weights,
        weights,
        gate_bias[None],
        up_bias[None],
    )


class ChipRing:
    def __init__(self, seq_count, pieces, sends, lands, send_sem, recv_sem):
        self.chips = seq_count // 2
        self.far = self.chips // 2
        self.pieces = pieces
        self.sends, self.lands = sends, lands
        self.send_sem, self.recv_sem = send_sem, recv_sem
        self.sides = ring_neighbours(lax.axis_index("seq"), seq_count)
        self.greeted = [{"seq": side} for side in self.sides]
        width = pieces[0].shape[2]
        self.near = [
            chip_near(lax.axis_index("seq"), seq_count, step) for step in range(self.chips)
        ]
        self.width, self.mid = width, width // 2

    def copy(self, piece, side, hop):
        mid = self.mid
        if hop == 0:
            source = self.pieces[piece].at[self.near[self.far], :, pl.ds(side * mid, mid)]
            target = self.lands.at[piece, side, 0, :, pl.ds(0, mid)]
        else:
            source = self.sends.at[piece, side, hop - 1]
            target = self.lands.at[piece, side, hop]
        return pltpu.make_async_remote_copy(
            src_ref=source,
            dst_ref=target,
            send_sem=self.send_sem.at[piece, side, hop],
            recv_sem=self.recv_sem.at[piece, side, hop],
            device_id={"seq": self.sides[side]},
            device_id_type=MESH,
        )

    def start(self, piece):
        for side in range(2):
            self.copy(piece, side, 0).start()

    def advance(self, piece, hop):
        mid = self.mid
        for side in range(2):
            near = self.far - hop if side == 0 else self.far + hop
            term = self.pieces[piece][self.near[near]].astype(jnp.float32)
            self.copy(piece, side, hop - 1).wait_recv()
            if hop == 1:
                land = self.lands[piece, side, 0, :, :mid].astype(jnp.float32)
                low = term[:, :mid] + land if side == 0 else term[:, :mid]
                high = term[:, mid:] if side == 0 else term[:, mid:] + land
                self.sends[piece, side, 0, :, :mid] = low.astype(jnp.bfloat16)
                self.sends[piece, side, 0, :, mid:] = high.astype(jnp.bfloat16)
            else:
                land = self.lands[piece, side, hop - 1].astype(jnp.float32)
                self.sends[piece, side, hop - 1] = (term + land).astype(jnp.bfloat16)
            self.copy(piece, side, hop).start()

    def total(self, piece):
        total = self.pieces[piece][self.near[0]].astype(jnp.float32)
        for side in range(2):
            self.copy(piece, side, self.far - 1).wait_recv()
            total = total + self.lands[piece, side, self.far - 1].astype(jnp.float32)
        return total

    def close(self):
        for piece in range(len(self.pieces)):
            for side in range(2):
                for hop in range(self.far):
                    self.copy(piece, side, hop).wait_send()


def ring_scratch(seq_count, pieces, seg, width):
    far = seq_count // 4
    return [
        pltpu.VMEM((pieces, 2, far - 1, seg, width), jnp.bfloat16),
        pltpu.VMEM((pieces, 2, far, seg, width), jnp.bfloat16),
        pltpu.SemaphoreType.DMA((pieces, 2, far)),
        pltpu.SemaphoreType.DMA((pieces, 2, far)),
    ]


def greet(devices):
    barrier = pltpu.get_barrier_semaphore()
    for device in devices:
        pl.semaphore_signal(barrier, inc=1, device_id=device, device_id_type=MESH)
    pl.semaphore_wait(barrier, len(devices))


class CoreSum:
    def __init__(self, partner, terms, arrived, send_sem, recv_sem):
        self.core = lax.axis_index("seq") % 2
        self.partner = partner
        self.terms, self.arrived = terms, arrived
        self.send_sem, self.recv_sem = send_sem, recv_sem

    def copy(self, piece):
        return pltpu.make_async_remote_copy(
            src_ref=self.terms.at[piece % self.terms.shape[0], :, 1 - self.core],
            dst_ref=self.arrived.at[piece],
            send_sem=self.send_sem.at[piece],
            recv_sem=self.recv_sem.at[piece],
            device_id=self.partner,
            device_id_type=MESH,
        )

    def start(self, piece, term):
        slot = piece % self.terms.shape[0]
        self.terms[slot] = term.astype(jnp.bfloat16).reshape(self.terms.shape[1:])
        self.copy(piece).start()

    def finish(self, piece):
        self.copy(piece).wait_recv()
        total = self.terms[piece % self.terms.shape[0], :, self.core].astype(jnp.float32)
        return (total + self.arrived[piece].astype(jnp.float32)).astype(jnp.bfloat16)

    def close(self, piece):
        self.copy(piece).wait_send()


def core_scratch(pieces, chips, seg, width, slots):
    return [
        pltpu.VMEM((slots, chips, 2, seg, width), jnp.bfloat16),
        pltpu.VMEM((pieces, chips, seg, width), jnp.bfloat16),
        pltpu.SemaphoreType.DMA((pieces,)),
        pltpu.SemaphoreType.DMA((pieces,)),
    ]


def through_norm(total, normal, inverse, gain):
    shaped = total * gain
    return (
        shaped
        - jnp.mean(shaped, axis=-1, keepdims=True)
        - normal * jnp.mean(shaped * normal, axis=-1, keepdims=True)
    ) * inverse


def tail_kernel(seq_count, head_count, made_count, clip_total, *refs):
    (
        rows_t,
        columns,
        weights,
        normal,
        inverse,
        gain,
        grad_h_one,
        placing,
        early,
        h_two,
        glu_own,
        glu_other,
        down_bias,
        ready,
        out,
        small_out,
        frames_grad,
        result,
        mine,
        small_send,
        small_land,
        step_send,
        step_recv,
        split,
        split_land,
        split_send,
        split_recv,
        *refs,
    ) = refs
    core_refs, ring_refs = refs[:4], refs[4:]
    width = columns.shape[1] // made_count
    rows = grad_h_one.shape[0]
    late = placing.shape[0]
    pieces = [ready, *(mine.at[made] for made in range(made_count))]
    ring = ChipRing(seq_count, pieces, *ring_refs)
    seq_index = lax.axis_index("seq")
    head_index = lax.axis_index("head")
    partners = []
    bit = 1
    while bit < seq_count:
        partners.append({"seq": xor_place(seq_index, bit)})
        bit *= 2
    seq_steps = len(partners)
    bit = 1
    while bit < head_count:
        partners.append({"head": xor_place(head_index, bit)})
        bit *= 2
    greet(ring.greeted + partners)
    cores = CoreSum(partners[0], *core_refs)

    def step_copy(step):
        count = small_out.shape[0] if step < seq_steps else late
        return pltpu.make_async_remote_copy(
            src_ref=small_send.at[step, pl.ds(0, count)],
            dst_ref=small_land.at[step, pl.ds(0, count)],
            send_sem=step_send.at[step],
            recv_sem=step_recv.at[step],
            device_id=partners[step],
            device_id_type=MESH,
        )

    def step_on(step):
        if step > 0:
            step_copy(step - 1).wait_recv()
            if step <= seq_steps:
                total = small_send[step - 1] + small_land[step - 1]
                if step == seq_steps:
                    small_out[late:, :] = total[late:]
                if step < len(partners):
                    small_send[step] = total
                else:
                    small_out[:late, :] = total[:late]
            else:
                total = small_send[step - 1, :late] + small_land[step - 1, :late]
                if step < len(partners):
                    small_send[step, :late] = total
                else:
                    small_out[:late, :] = total
        if step < len(partners):
            step_copy(step).start()

    def split_copy():
        return pltpu.make_async_remote_copy(
            src_ref=split,
            dst_ref=split_land,
            send_sem=split_send,
            recv_sem=split_recv,
            device_id=partners[seq_steps],
            device_id_type=MESH,
        )

    ring.start(0)
    for made in range(made_count):
        cores.start(made, product(rows_t[...], columns[:, made * width : (made + 1) * width]))
    for made in range(made_count):
        mine[made] = cores.finish(made)
        ring.start(made + 1)
    grad_normed = product_t(columns[...], weights[...])
    split[...] = grad_normed[:rows].astype(jnp.bfloat16)
    split_copy().start()
    row = lax.broadcasted_iota(jnp.int32, (late, 1), 0)
    gain_term = jnp.sum(grad_normed[:rows] * normal[...], axis=0, keepdims=True)
    first = jnp.where(row == clip_total, gain_term, 0.0)
    for slot in range(placing.shape[1]):
        first = first + placing[:, slot : slot + 1] * grad_normed[rows + slot : rows + slot + 1]
    small_send[0, :late, :] = first
    small_send[0, late:, :] = early[...]
    step_on(0)
    done = 1
    for hop in range(1, ring.far):
        for piece in range(len(pieces)):
            ring.advance(piece, hop)
        if hop == 1:
            result[...] = (
                h_two[...]
                + (glu_own[...].astype(jnp.float32) + glu_other[...].astype(jnp.float32))
                + down_bias[...]
            ).astype(jnp.bfloat16)
        while done <= len(partners) * hop // (ring.far - 1):
            step_on(done)
            done += 1
    split_copy().wait_recv()
    total = split[...].astype(jnp.float32) + split_land[...].astype(jnp.float32)
    back = through_norm(total, normal[...], inverse[...], gain[...])
    frames_grad[...] = (grad_h_one[...] + back).astype(jnp.bfloat16)
    for piece in range(len(pieces)):
        out[piece] = ring.total(piece)
    split_copy().wait_send()
    for made in range(made_count):
        cores.close(made)
    ring.close()
    for step in range(len(partners)):
        step_copy(step).wait_send()


def tail_sums(
    rows_t, columns, weights, norm, grad_h_one, placing, early, h_two, glu_terms, down_bias, ready, clip_total, seq_count
):
    head_count = lax.axis_size("head")
    chips = seq_count // 2
    rows, wide = grad_h_one.shape
    seg = rows_t.shape[0] // seq_count
    width = TAIL_WIDTH
    made_count = columns.shape[1] // width
    steps = (seq_count - 1).bit_length() + (head_count - 1).bit_length()
    bf = jnp.bfloat16
    vmem = pl.BlockSpec(memory_space=pltpu.VMEM)
    small = (placing.shape[0] + early.shape[0], wide)
    return pl.pallas_call(
        functools.partial(tail_kernel, seq_count, head_count, made_count, clip_total),
        grid=(1,),
        in_specs=[
            vmem,
            vmem,
            pl.BlockSpec((wide, made_count * width), lambda i: (0, 0), pipeline_mode=pl.Buffered(1)),
            *[vmem] * 11,
        ],
        out_specs=[vmem] * 4,
        out_shape=[
            jax.ShapeDtypeStruct((made_count + 1, seg, width), jnp.float32),
            jax.ShapeDtypeStruct(small, jnp.float32),
            jax.ShapeDtypeStruct((rows, wide), bf),
            jax.ShapeDtypeStruct((rows, wide), bf),
        ],
        scratch_shapes=[
            pltpu.VMEM((made_count, chips, seg, width), bf),
            pltpu.VMEM((steps, *small), jnp.float32),
            pltpu.VMEM((steps, *small), jnp.float32),
            pltpu.SemaphoreType.DMA((steps,)),
            pltpu.SemaphoreType.DMA((steps,)),
            pltpu.VMEM((rows, wide), bf),
            pltpu.VMEM((rows, wide), bf),
            pltpu.SemaphoreType.DMA,
            pltpu.SemaphoreType.DMA,
            *core_scratch(made_count, chips, seg, width, made_count),
            *ring_scratch(seq_count, made_count + 1, seg, width),
        ],
        compiler_params=pltpu.CompilerParams(
            collective_id=2, has_side_effects=True, vmem_limit_bytes=VMEM_BYTES
        ),
        cost_estimate=pl.CostEstimate(
            flops=4 * rows_t.shape[0] * rows_t.shape[1] * columns.shape[1],
            bytes_accessed=32 * made_count * chips * seg * width,
            transcendentals=0,
        ),
        name="tail_sums",
    )(
        rows_t,
        columns,
        weights,
        *norm,
        grad_h_one,
        placing,
        early,
        h_two,
        *glu_terms,
        down_bias,
        ready,
    )


def turned_back(values, tables):
    shift = ROT // 2
    return (
        values * tables[0]
        + pltpu.roll(values, LANES - shift, 1) * tables[1]
        - pltpu.roll(values, shift, 1) * tables[2]
    )


def self_back_kernel(seq_count, pairs, score_scale, *refs):
    (
        query,
        keys,
        values,
        stamp_key,
        stamp_value,
        grad_out,
        logs,
        key_ids,
        query_ids,
        query_slots,
        tables,
        ready,
        made_rows,
        made_columns,
        out,
        shares,
        mine,
        bias,
        acc,
        own,
        halo,
        halo_land,
        halo_send_sem,
        halo_recv_sem,
        *refs,
    ) = refs
    core_refs, ring_refs = refs[:4], refs[4:]
    ready_count = ready.shape[0]
    pair = pl.program_id(0)
    rows = query.shape[0]
    slots = stamp_key.shape[0]
    span = QUERY_BLOCK + 2 * HALF
    seq_index = lax.axis_index("seq")
    before = (seq_index + seq_count - 1) % seq_count
    behind = (seq_index + 1) % seq_count
    pieces = [ready.at[piece] for piece in range(ready_count)]
    ring = ChipRing(seq_count, pieces, *ring_refs)
    partner = {"seq": xor_place(seq_index, 1)}
    cores = CoreSum(partner, *core_refs)

    def halo_copy(which, side):
        return pltpu.make_async_remote_copy(
            src_ref=halo.at[which, side],
            dst_ref=halo_land.at[which, side],
            send_sem=halo_send_sem.at[which, side],
            recv_sem=halo_recv_sem.at[which, side],
            device_id={"seq": before if side == 0 else behind},
            device_id_type=MESH,
        )

    @pl.when(pair == 0)
    def _():
        greet(ring.greeted + [partner, {"seq": before}, {"seq": behind}])
        for piece in range(ready_count):
            ring.start(piece)
        cores.start(0, product_tn(made_rows[...], made_columns[...]))
        for block in range(rows // QUERY_BLOCK):
            start = block * QUERY_BLOCK
            asked = query_ids[:, start : start + QUERY_BLOCK]
            key_row = lax.broadcasted_iota(jnp.int32, (span, QUERY_BLOCK), 0)
            query_row = lax.broadcasted_iota(jnp.int32, (span, QUERY_BLOCK), 1)
            away = key_row - HALF - query_row
            seen = (key_ids[start : start + span, :] == asked) & (jnp.abs(away) <= HALF)
            bias[block, :span, :] = jnp.where(seen, 0.0, NEG)
            slot_row = lax.broadcasted_iota(jnp.int32, (slots, QUERY_BLOCK), 0)
            bias[block, span:, :] = jnp.where(
                slot_row == query_slots[:, start : start + QUERY_BLOCK], 0.0, NEG
            )

    blocks = rows // QUERY_BLOCK
    order = [(piece, hop) for hop in range(1, ring.far) for piece in range(len(pieces))]
    due = [1 + at * (pairs * blocks - 1) // len(order) for at in range(len(order))]

    def ring_work(block):
        @pl.when(pair * blocks + block == MADE_AT)
        def _():
            mine[...] = cores.finish(0)

        for moment, (piece, hop) in zip(due, order):
            if moment % blocks == block:

                @pl.when(pair == moment // blocks)
                def _():
                    ring.advance(piece, hop)

    @pl.when(pair < pairs)
    def _():
        acc[...] = jnp.zeros_like(acc)
        lane = lax.broadcasted_iota(jnp.int32, (1, LANES), 1)
        stamp_k, stamp_v = stamp_key[...], stamp_value[...]
        grad_queries = []
        for block in range(rows // QUERY_BLOCK):
            start = block * QUERY_BLOCK
            near_k = jnp.concatenate([keys[0, start : start + span, :], stamp_k], axis=0)
            near_v = jnp.concatenate([values[0, start : start + span, :], stamp_v], axis=0)
            block_q = query[start : start + QUERY_BLOCK, :]
            block_g = grad_out[start : start + QUERY_BLOCK, :]
            grad_q = jnp.zeros((QUERY_BLOCK, LANES), jnp.float32)
            grad_k = jnp.zeros((span + slots, LANES), jnp.float32)
            grad_v = jnp.zeros((span + slots, LANES), jnp.float32)
            for head in range(LANES // HD):
                here = lane // HD == head
                head_q = jnp.where(here, block_q, jnp.zeros_like(block_q))
                head_g = jnp.where(here, block_g, jnp.zeros_like(block_g))
                head_k = jnp.where(here, near_k, jnp.zeros_like(near_k))
                scores = product_t(near_k, head_q) * score_scale + bias[block]
                probs = jnp.exp(scores - logs[0, head : head + 1, start : start + QUERY_BLOCK])
                grad_p = product_t(near_v, head_g)
                dot = jnp.sum(probs * grad_p, axis=0, keepdims=True)
                grad_s = (probs * (grad_p - dot)).astype(jnp.bfloat16)
                grad_k = grad_k + product(grad_s, head_q)
                grad_v = grad_v + product(probs.astype(jnp.bfloat16), head_g)
                grad_q = grad_q + product_tn(grad_s, head_k)
            grad_queries.append(grad_q)
            ring_work(block)
            acc[0, start : start + span, :] += grad_k[:span]
            acc[1, start : start + span, :] += grad_v[:span]
            acc[0, 2 * HALF + rows :, :] += grad_k[span:]
            acc[1, 2 * HALF + rows :, :] += grad_v[span:]
        column = pl.multiple_of(pair * LANES, LANES)
        grad_q = jnp.concatenate(grad_queries, axis=0) * score_scale
        out[:rows, pl.ds(column, LANES)] = turned_back(grad_q, tables).astype(jnp.bfloat16)
        out[rows:, pl.ds(column, LANES)] = jnp.zeros((slots, LANES), jnp.bfloat16)
        for which in range(2):
            scale = score_scale if which == 0 else 1.0
            shift = (which + 1) * pairs * LANES
            halo[pair, 0, which] = (acc[which, :HALF, :] * scale).astype(jnp.bfloat16)
            halo[pair, 1, which] = (acc[which, HALF + rows : 2 * HALF + rows, :] * scale).astype(
                jnp.bfloat16
            )
            own[pair, which] = acc[which, HALF : HALF + rows, :] * scale
            out[rows:, pl.ds(column + shift, LANES)] = (
                acc[which, 2 * HALF + rows :, :] * scale
            ).astype(jnp.bfloat16)

        @pl.when(seq_index > 0)
        def _():
            halo_copy(pair, 0).start()

        @pl.when(seq_index < seq_count - 1)
        def _():
            halo_copy(pair, 1).start()

    @pl.when(pair == pairs)
    def _():

        @pl.when(seq_index < seq_count - 1)
        def _():
            for which in range(pairs):
                halo_copy(which, 0).wait_recv()
                own[which, :, rows - HALF :, :] += halo_land[which, 0].astype(jnp.float32)

        @pl.when(seq_index > 0)
        def _():
            for which in range(pairs):
                halo_copy(which, 1).wait_recv()
                own[which, :, :HALF, :] += halo_land[which, 1].astype(jnp.float32)

        for which in range(pairs):
            column = (pairs + which) * LANES
            out[:rows, column : column + LANES] = turned_back(own[which, 0], tables).astype(
                jnp.bfloat16
            )
            column = (2 * pairs + which) * LANES
            out[:rows, column : column + LANES] = own[which, 1].astype(jnp.bfloat16)
        for piece in range(len(pieces)):
            shares[piece] = ring.total(piece)
        ring.close()
        cores.close(0)

        @pl.when(seq_index > 0)
        def _():
            for which in range(pairs):
                halo_copy(which, 0).wait_send()

        @pl.when(seq_index < seq_count - 1)
        def _():
            for which in range(pairs):
                halo_copy(which, 1).wait_send()


def self_back(
    query, near, stamps, grad_out, logs, key_ids, query_ids, query_slots, tables, ready, made_rows, made_columns, score_scale, seq_count
):
    rows, part = query.shape
    slots = stamps.shape[0]
    pairs = part // LANES
    window = near.shape[1]
    ready_count, chips, seg, width = ready.shape
    span = QUERY_BLOCK + 2 * HALF
    blocks = rows // QUERY_BLOCK
    last = pairs - 1

    def at(first, shape, lead=()):
        return pl.BlockSpec(shape, lambda i: (*lead, 0, first + jnp.minimum(i, last)))

    def whole(shape):
        return pl.BlockSpec(shape, lambda i: (0,) * len(shape), pipeline_mode=pl.Buffered(1))

    return pl.pallas_call(
        functools.partial(self_back_kernel, seq_count, pairs, score_scale),
        grid=(pairs + 1,),
        in_specs=[
            at(0, (rows, LANES)),
            at(0, (1, window, LANES), (0,)),
            at(0, (1, window, LANES), (1,)),
            at(pairs, (slots, LANES)),
            at(2 * pairs, (slots, LANES)),
            at(0, (rows, LANES)),
            pl.BlockSpec((1, LANES // HD, rows), lambda i: (jnp.minimum(i, last), 0, 0)),
            whole((window, 1)),
            whole((1, rows)),
            whole((1, rows)),
            whole((3, rows, LANES)),
            whole(ready.shape),
            whole(made_rows.shape),
            whole(made_columns.shape),
        ],
        out_specs=[
            pl.BlockSpec((rows + slots, 3 * part), lambda i: (0, 0)),
            pl.BlockSpec((ready_count, seg, width), lambda i: (0, 0, 0)),
            pl.BlockSpec((chips, seg, width), lambda i: (0, 0, 0)),
        ],
        out_shape=[
            jax.ShapeDtypeStruct((rows + slots, 3 * part), jnp.bfloat16),
            jax.ShapeDtypeStruct((ready_count, seg, width), jnp.float32),
            jax.ShapeDtypeStruct((chips, seg, width), jnp.bfloat16),
        ],
        scratch_shapes=[
            pltpu.VMEM((blocks, span + slots, QUERY_BLOCK), jnp.float32),
            pltpu.VMEM((2, window + slots, LANES), jnp.float32),
            pltpu.VMEM((pairs, 2, rows, LANES), jnp.float32),
            pltpu.VMEM((pairs, 2, 2, HALF, LANES), jnp.bfloat16),
            pltpu.VMEM((pairs, 2, 2, HALF, LANES), jnp.bfloat16),
            pltpu.SemaphoreType.DMA((pairs, 2)),
            pltpu.SemaphoreType.DMA((pairs, 2)),
            *core_scratch(1, chips, seg, width, 1),
            *ring_scratch(seq_count, ready_count, seg, width),
        ],
        compiler_params=pltpu.CompilerParams(
            collective_id=3, has_side_effects=True, vmem_limit_bytes=VMEM_BYTES
        ),
        cost_estimate=pl.CostEstimate(
            flops=10 * rows * window * part,
            bytes_accessed=16 * chips * seg * width * ready_count,
            transcendentals=rows * window * part // HD,
        ),
        name="self_back",
    )(
        query,
        near,
        near,
        stamps,
        stamps,
        grad_out,
        logs.reshape(pairs, LANES // HD, rows),
        key_ids[:, None],
        query_ids[None],
        query_slots[None],
        tables,
        ready,
        made_rows,
        made_columns,
    )


def mid_kernel(seq_count, head_count, score_scale, ctx_tokens, *refs):
    (
        grad_low,
        top,
        normal_three,
        inverse_three,
        normal_two,
        inverse_two,
        gains,
        c_out,
        c_query,
        w_out,
        query,
        key,
        value,
        logs,
        query_slots,
        cross_mixed,
        normed_two,
        context,
        kept,
        moving,
        grad_h_one,
        grad_two_low,
        grad_one_low,
        grad_attn,
        grad_query,
        ctx_grads,
        gain_terms,
        share,
        core_sums,
        ctx_acc,
        split,
        split_land,
        split_send,
        split_recv,
        third_land,
        fourth_land,
        third_sems,
        fourth_sems,
        keep,
        keep_sems,
        *core_refs,
    ) = refs
    seq_index = lax.axis_index("seq")
    head_index = lax.axis_index("head")
    others = [{"head": (head_index + 1 + step) % head_count} for step in range(head_count - 1)]
    sides = ring_neighbours(seq_index, seq_count)
    partner = {"seq": xor_place(seq_index, 1)}
    cores = CoreSum(partner, *core_refs)
    greet([*others, partner] + [{"seq": side} for side in sides])

    def hop(side, which, slab):
        sems = fourth_sems if which else third_sems
        return pltpu.make_async_remote_copy(
            src_ref=third_land.at[side, slab] if which else moving.at[side, slab],
            dst_ref=(fourth_land if which else third_land).at[side, slab],
            send_sem=sems.at[0, side, slab],
            recv_sem=sems.at[1, side, slab],
            device_id={"seq": sides[side]},
            device_id_type=MESH,
        )

    def keep_copy(which):
        at = (1, kept.shape[0] - 1, 0)[which]
        return pltpu.make_async_copy(kept.at[at], keep.at[which % 2], keep_sems.at[which])

    def third_to_fourth():
        for side in range(2):
            keep_copy(side).wait()
        for slab in range(3):
            for side in range(2):
                hop(side, 0, slab).wait_recv()
                term = keep[side, slab].astype(jnp.float32)
                term = term + third_land[side, slab].astype(jnp.float32)
                third_land[side, slab] = term.astype(jnp.bfloat16)
                hop(side, 1, slab).start()
        keep_copy(2).start()

    def over_heads(which, chunk):
        part = pl.ds(chunk * QUERY_BLOCK, QUERY_BLOCK)
        return pltpu.make_async_remote_copy(
            src_ref=(grad_low if which == 0 else split).at[part],
            dst_ref=split_land.at[which, part],
            send_sem=split_send.at[which, chunk],
            recv_sem=split_recv.at[which, chunk],
            device_id=others[0],
            device_id_type=MESH,
        )

    rows = query.shape[0]
    keys = key.shape[0]
    part = query.shape[1]
    pairs = part // LANES
    chunks = range(rows // QUERY_BLOCK)

    def chunk_rows(chunk):
        return slice(chunk * QUERY_BLOCK, (chunk + 1) * QUERY_BLOCK)

    def summed(which, chunk):
        over_heads(which, chunk).wait_recv()
        here = chunk_rows(chunk)
        own = (grad_low if which == 0 else split)[here, :].astype(jnp.float32)
        return own + split_land[which, here, :].astype(jnp.float32)

    for chunk in chunks:
        over_heads(0, chunk).start()
    for slab in range(3):
        hop(0, 0, slab).start()
        hop(1, 0, slab).start()
    keep_copy(0).start()
    keep_copy(1).start()
    gain_terms[...] = jnp.zeros_like(gain_terms)
    ctx_acc[...] = jnp.zeros_like(ctx_acc)
    token_slot = lax.broadcasted_iota(jnp.int32, (keys, 1), 0) // ctx_tokens
    lane = lax.broadcasted_iota(jnp.int32, (1, LANES), 1)
    for chunk in chunks:
        here = chunk_rows(chunk)
        total = summed(0, chunk)
        normal = normal_three[here, :]
        gain_terms[0:1, :] += jnp.sum(total * normal, axis=0, keepdims=True)
        grad_two = top[here, :].astype(jnp.float32) + through_norm(
            total, normal, inverse_three[here, :], gains[0:1, :]
        )
        grad_h_one[here, :] = grad_two
        grad_two_low[here, :] = grad_two.astype(jnp.bfloat16)
        grad_mix = product(grad_two_low[here, :], c_out[...]).astype(jnp.bfloat16)
        bias = jnp.where(token_slot == query_slots[:, here], 0.0, NEG)
        for pair in range(pairs):
            columns = slice(pair * LANES, (pair + 1) * LANES)
            second = slice((pairs + pair) * LANES, (pairs + pair + 1) * LANES)
            pair_q, pair_g = query[here, columns], grad_mix[:, columns]
            pair_k, pair_v = key[:, columns], value[:, columns]
            grad_q = jnp.zeros((QUERY_BLOCK, LANES), jnp.float32)
            grad_k = jnp.zeros((keys, LANES), jnp.float32)
            grad_v = jnp.zeros((keys, LANES), jnp.float32)
            for head in range(LANES // HD):
                mine = lane // HD == head
                head_q = jnp.where(mine, pair_q, jnp.zeros_like(pair_q))
                head_g = jnp.where(mine, pair_g, jnp.zeros_like(pair_g))
                head_k = jnp.where(mine, pair_k, jnp.zeros_like(pair_k))
                at = pair * (LANES // HD) + head
                scores = product_t(pair_k, head_q) * score_scale + bias
                probs = jnp.exp(scores - logs[at : at + 1, here])
                grad_p = product_t(pair_v, head_g)
                dot = jnp.sum(probs * grad_p, axis=0, keepdims=True)
                grad_s = (probs * (grad_p - dot)).astype(jnp.bfloat16)
                grad_k = grad_k + product(grad_s, head_q)
                grad_v = grad_v + product(probs.astype(jnp.bfloat16), head_g)
                grad_q = grad_q + product_tn(grad_s, head_k)
            grad_query[here, columns] = (grad_q * score_scale).astype(jnp.bfloat16)
            ctx_acc[:, columns] += grad_k * score_scale
            ctx_acc[:, second] += grad_v
        split[here, :] = product_t(grad_query[here, :], c_query[...]).astype(jnp.bfloat16)
        over_heads(1, chunk).start()
        if chunk == HOP_CHUNK:
            third_to_fourth()
    ctx_grads[...] = ctx_acc[...].astype(jnp.bfloat16)
    cores.start(0, product_tn(grad_two_low[...], cross_mixed[...]))
    cores.start(1, product_tn(normed_two[...], grad_query[...]))
    for chunk in chunks:
        here = chunk_rows(chunk)
        total = summed(1, chunk)
        normal = normal_two[here, :]
        gain_terms[1:2, :] += jnp.sum(total * normal, axis=0, keepdims=True)
        grad_one = grad_h_one[here, :] + through_norm(
            total, normal, inverse_two[here, :], gains[1:2, :]
        )
        grad_h_one[here, :] = grad_one
        grad_one_low[here, :] = grad_one.astype(jnp.bfloat16)
        grad_attn[here, :] = product(grad_one_low[here, :], w_out[...]).astype(jnp.bfloat16)
    core_sums[0] = cores.finish(0)
    cores.close(0)
    ctx_rows = cores.terms.shape[3] // 2
    for which in range(2):
        term = product_tn(context[...], ctx_grads[:, which * part : (which + 1) * part])
        term = term.astype(jnp.bfloat16).reshape(-1, 2, ctx_rows, part)
        cores.terms[0, :, :, which * ctx_rows : (which + 1) * ctx_rows, :] = term
    cores.copy(2).start()
    for piece in range(1, 3):
        core_sums[piece] = cores.finish(piece)
    keep_copy(2).wait()
    whole = keep[0].astype(jnp.float32)
    for side in range(2):
        for slab in range(3):
            hop(side, 1, slab).wait_recv()
        whole = whole + fourth_land[side].astype(jnp.float32)
    share[...] = whole
    for side in range(2):
        for slab in range(3):
            hop(side, 0, slab).wait_send()
            hop(side, 1, slab).wait_send()
    for piece in range(1, 3):
        cores.close(piece)
    for chunk in chunks:
        over_heads(0, chunk).wait_send()
        over_heads(1, chunk).wait_send()


def mid_layer(
    grad_low, top, thirds, seconds, gains, weights, query, key, value, logs, slots, cross_mixed, normed_two, context, kept, moving, ctx_tokens, seq_count
):
    rows, width = grad_low.shape
    part = query.shape[1]
    keys = key.shape[0]
    head_count = lax.axis_size("head")
    chips, moved = seq_count // 2, moving.shape
    seg = moved[2]
    bf, wide = jnp.bfloat16, jnp.float32
    vmem = pl.BlockSpec(memory_space=pltpu.VMEM)

    def weight_spec(which):
        return pl.BlockSpec((width, part), lambda i: (0, which), pipeline_mode=pl.Buffered(1))

    scratches = [
        pltpu.VMEM((keys, 2 * part), wide),
        pltpu.VMEM((rows, width), bf),
        pltpu.VMEM((2, rows, width), bf),
        pltpu.SemaphoreType.DMA((2, rows // QUERY_BLOCK)),
        pltpu.SemaphoreType.DMA((2, rows // QUERY_BLOCK)),
    ]
    out_shapes = [
        jax.ShapeDtypeStruct((rows, width), wide),
        jax.ShapeDtypeStruct((rows, width), bf),
        jax.ShapeDtypeStruct((rows, width), bf),
        jax.ShapeDtypeStruct((rows, part), bf),
        jax.ShapeDtypeStruct((rows, part), bf),
        jax.ShapeDtypeStruct((keys, 2 * part), bf),
        jax.ShapeDtypeStruct((8, width), wide),
    ]
    scratches += [
        pltpu.VMEM(moved, bf),
        pltpu.VMEM(moved, bf),
        pltpu.SemaphoreType.DMA((2, 2, 3)),
        pltpu.SemaphoreType.DMA((2, 2, 3)),
        pltpu.VMEM((2, *moved[1:]), bf),
        pltpu.SemaphoreType.DMA((3,)),
        *core_scratch(3, chips, seg, part, 2),
    ]
    out_shapes += [
        jax.ShapeDtypeStruct(moved[1:], wide),
        jax.ShapeDtypeStruct((3, chips, seg, part), bf),
    ]
    return pl.pallas_call(
        functools.partial(
            mid_kernel, seq_count, head_count, HD ** (-0.5), ctx_tokens
        ),
        grid=(1,),
        in_specs=[
            *[vmem] * 7,
            weight_spec(5),
            weight_spec(4),
            weight_spec(3),
            *[vmem] * 8,
            pl.BlockSpec(memory_space=pl.ANY),
            pl.BlockSpec(memory_space=pl.ANY),
        ],
        out_specs=[vmem] * len(out_shapes),
        out_shape=out_shapes,
        scratch_shapes=scratches,
        compiler_params=pltpu.CompilerParams(
            collective_id=6, has_side_effects=True, vmem_limit_bytes=VMEM_BYTES
        ),
        cost_estimate=pl.CostEstimate(
            flops=10 * rows * keys * part + 6 * rows * width * part,
            bytes_accessed=100 * rows * width,
            transcendentals=rows * keys * part // HD,
        ),
        name="mid_layer",
    )(
        grad_low,
        top,
        *thirds,
        *seconds,
        gains,
        weights,
        weights,
        weights,
        query,
        key,
        value,
        logs,
        slots[None],
        cross_mixed,
        normed_two,
        context,
        kept,
        moving,
    )


def head_total(partial_sum):
    low = partial_sum
    if low.dtype != jnp.bfloat16:
        low = lax.optimization_barrier(partial_sum.astype(jnp.bfloat16))
    count = lax.axis_size("head")
    total = low.astype(jnp.float32)
    for step in range(1, count):
        pairs = [(index, (index + step) % count) for index in range(count)]
        total = total + lax.ppermute(low, "head", pairs).astype(jnp.float32)
    return total


def low_gather(block):
    return lax.all_gather(block.astype(jnp.bfloat16), "seq", axis=0, tiled=True)


def per_device(
    frames,
    time_token,
    prompt,
    clip_ids,
    norm1_gain,
    norm2_gain,
    norm3_gain,
    query_weight,
    key_weight,
    value_weight,
    out_weight,
    cross_query,
    cross_key,
    cross_value,
    cross_out,
    gate_weight,
    up_weight,
    down_weight,
    gate_bias,
    up_bias,
    down_bias,
    out_grad,
):
    local_rows, width = frames.shape
    clip_total = time_token.shape[0]
    ctx_tokens = prompt.shape[1]
    slot_count = local_rows // (2 * HALF) + 2
    seq_count = lax.axis_size("seq")
    seq_index = lax.axis_index("seq")
    head_index = lax.axis_index("head")
    first_row = seq_index * local_rows
    score_scale = HD ** (-0.5)
    part = query_weight.shape[1]
    hidden_width = gate_weight.shape[1]
    gain_rows = norm1_gain.shape[0]
    ctx_rows = cross_key.shape[0]
    ctx_width = prompt.shape[2]
    head_count = part // HD
    bias_rows = 2 * hidden_width // width
    small_rows = -(-max(clip_total + 1, bias_rows + 3) // 8) * 8
    vectors = jnp.stack([norm1_gain, norm2_gain, norm3_gain, down_bias], axis=1)
    vectors = jnp.pad(vectors, ((0, 0), (0, LANES - 4)))
    starts = [each * part for each in range(8)]
    attn_weights, glu_local = ring_gather(
        [
            query_weight,
            key_weight,
            value_weight,
            out_weight,
            cross_query,
            cross_out,
            cross_key,
            cross_value,
            vectors,
        ],
        [gate_weight, up_weight, down_weight],
        (*starts[:7], starts[7] + LANES),
        seq_count,
        4,
    )
    glu_weights = low_gather(glu_local)
    w_qkv = attn_weights[:, : starts[3]]
    w_out = attn_weights[:, starts[3] : starts[4]]
    c_query = attn_weights[:, starts[4] : starts[5]]
    c_out = attn_weights[:, starts[5] : starts[6]]
    ctx_weights = attn_weights[:, starts[6] : starts[7]].reshape(seq_count, 2, ctx_rows, part)
    c_key = ctx_weights[:, 0].reshape(ctx_width, part)
    c_value = ctx_weights[:, 1].reshape(ctx_width, part)
    rows_of = attn_weights[:, starts[7] : starts[7] + 8].astype(jnp.float32).T
    gain_one_f, gain_two_f, gain_three_f, bias_f = rows_of[0], rows_of[1], rows_of[2], rows_of[3]

    positions = first_row + jnp.arange(local_rows, dtype=jnp.int32)
    cos_table, sin_table = angles(positions)
    padded_ids = jnp.pad(clip_ids, (HALF, HALF), constant_values=-1)
    own_ids = lax.dynamic_slice_in_dim(clip_ids, first_row, local_rows)
    near_ids = lax.dynamic_slice_in_dim(padded_ids, first_row, local_rows + 2 * HALF)
    base_clip = jnp.minimum(own_ids[0], clip_total - slot_count)
    own_slot = own_ids - base_clip
    slot_range = jnp.arange(slot_count, dtype=jnp.int32)
    pad_rows = -slot_count % 16
    stamp_end = local_rows + slot_count

    stamp_rows = lax.dynamic_slice_in_dim(time_token, base_clip, slot_count, 0)
    source = jnp.concatenate(
        [frames, jnp.pad(stamp_rows, ((0, pad_rows), (0, 0)))], axis=0
    ).astype(jnp.float32)
    normed_out, normal_one, inverse_one = layer_norm_parts(source, gain_one_f)
    normed_one = normed_out.astype(jnp.bfloat16)
    frames_f = source[:local_rows]
    qkv = product(normed_one, w_qkv)
    query_rows = rotate(qkv[:local_rows, :part], cos_table, sin_table).astype(jnp.bfloat16)
    key_rows = rotate(qkv[:local_rows, part : 2 * part], cos_table, sin_table).astype(jnp.bfloat16)
    value_rows = qkv[:local_rows, 2 * part :].astype(jnp.bfloat16)
    near = extended(jnp.stack([key_rows, value_rows]), (("seq", 1),), HALF)
    window = local_rows + 2 * HALF
    near_key_h = near[0].reshape(window, head_count, HD)
    near_value_h = near[1].reshape(window, head_count, HD)
    query_h = query_rows.reshape(local_rows, head_count, HD)
    stamps = qkv[local_rows:].astype(jnp.bfloat16)
    stamp_key_h = stamps[:slot_count, part : 2 * part].reshape(slot_count, head_count, HD)
    stamp_value_h = stamps[:slot_count, 2 * part :].reshape(slot_count, head_count, HD)

    query_pos = jnp.arange(local_rows, dtype=jnp.int32)
    key_pos = jnp.arange(window, dtype=jnp.int32) - HALF
    visible = (own_ids[:, None] == near_ids[None, :]) & (
        jnp.abs(query_pos[:, None] - key_pos[None, :]) <= HALF
    )
    own_stamp = own_slot[:, None] == slot_range[None, :]
    self_keys = [(near_key_h, near_value_h, visible), (stamp_key_h, stamp_value_h, own_stamp)]
    attn_mix_h, self_logs = attend_forward(query_h, self_keys, score_scale)
    attn_mixed = attn_mix_h.reshape(local_rows, part).astype(jnp.bfloat16)
    h_one = frames_f + head_total(product_t(attn_mixed, w_out))
    middle_out, normal_two, inverse_two = layer_norm_parts(h_one, gain_two_f)
    normed_two = middle_out.astype(jnp.bfloat16)
    cross_rows = product(normed_two, c_query).astype(jnp.bfloat16)
    cross_h = cross_rows.reshape(local_rows, head_count, HD)
    context_rows = lax.dynamic_slice_in_dim(prompt, base_clip, slot_count, 0).reshape(
        slot_count * ctx_tokens, ctx_width
    )
    ctx_keys = product(context_rows, c_key).astype(jnp.bfloat16)
    ctx_key_h = ctx_keys.reshape(slot_count * ctx_tokens, head_count, HD)
    ctx_values = product(context_rows, c_value).astype(jnp.bfloat16)
    ctx_value_h = ctx_values.reshape(slot_count * ctx_tokens, head_count, HD)
    key_slot = jnp.arange(slot_count * ctx_tokens, dtype=jnp.int32) // ctx_tokens
    cross_keys = [(ctx_key_h, ctx_value_h, own_slot[:, None] == key_slot[None, :])]
    cross_mix_h, cross_logs = attend_forward(cross_h, cross_keys, score_scale)
    cross_mixed = cross_mix_h.reshape(local_rows, part).astype(jnp.bfloat16)
    h_two = h_one + head_total(product_t(cross_mixed, c_out))
    third_out, normal_three, inverse_three = layer_norm_parts(h_two, gain_three_f)
    normed_three = third_out.astype(jnp.bfloat16)

    glu_out, grad_normed_low, bias_local, glu_kept, glu_moving = glu_layer(
        normed_three,
        normed_three.T,
        out_grad,
        out_grad.T,
        glu_weights,
        gate_bias,
        up_bias,
        seq_count,
    )
    (
        grad_h_one,
        grad_two_low,
        grad_one_low,
        grad_attn,
        grad_cross_query,
        ctx_grads,
        gain_terms,
        glu_share,
        cross_sums,
    ) = mid_layer(
        grad_normed_low,
        out_grad,
        (normal_three, inverse_three),
        (normal_two, inverse_two),
        jnp.stack([gain_three_f, gain_two_f]),
        attn_weights,
        cross_rows,
        ctx_keys,
        ctx_values,
        cross_logs,
        own_slot,
        cross_mixed,
        normed_two,
        context_rows,
        glu_kept,
        glu_moving,
        ctx_tokens,
        seq_count,
    )
    gain_three_term, gain_two_term = gain_terms[0], gain_terms[1]
    down_bias_term = jnp.sum(out_grad.astype(jnp.float32), axis=0)
    grad_attn, glu_out = lax.optimization_barrier((grad_attn, glu_out))
    head_pairs = [(index, index ^ 1) for index in range(lax.axis_size("head"))]
    glu_other = lax.ppermute(glu_out, "head", head_pairs)
    ones = jnp.ones((local_rows, HD - ROT), jnp.float32)
    flat = jnp.zeros((local_rows, ROT // 2), jnp.float32)
    low_side = [sin_table, flat, 0 * ones]
    high_side = [flat, sin_table, 0 * ones]
    tables = jnp.stack(
        [
            jnp.tile(jnp.concatenate(each, axis=1), (1, LANES // HD))
            for each in ([cos_table, cos_table, ones], low_side, high_side)
        ]
    )
    grad_qkv, early_share, out_sum = self_back(
        query_rows,
        near,
        stamps,
        grad_attn,
        self_logs,
        near_ids,
        own_ids,
        own_slot,
        tables,
        cross_sums,
        grad_one_low,
        attn_mixed,
        score_scale,
        seq_count,
    )
    early_rows = jnp.concatenate(
        [
            bias_local.reshape(-1, width),
            jnp.stack([gain_two_term, gain_three_term, down_bias_term]),
        ],
        axis=0,
    )
    early_rows = jnp.pad(early_rows, ((0, small_rows - bias_rows - 3), (0, 0)))
    clip_range = jnp.arange(small_rows, dtype=jnp.int32)
    placing = (clip_range[:, None] - base_clip == slot_range[None, :]).astype(jnp.float32)
    qkv_share, small, frames_grad, result = tail_sums(
        normed_one.T,
        grad_qkv,
        attn_weights,
        (normal_one[:local_rows], inverse_one[:local_rows], gain_one_f[None]),
        grad_h_one,
        placing,
        early_rows,
        h_two,
        (glu_out, glu_other),
        bias_f[None],
        out_sum,
        clip_total,
        seq_count,
    )
    cross_out_share, cross_query_share, ctx_share = early_share
    out_share = qkv_share[0]
    late = small[: clip_total + 1]
    early = small[small_rows : small_rows + bias_rows + 3]
    stamp_sum = late[:clip_total]
    own_bias = early[:-3].reshape(2, hidden_width)
    every_out, every_normal, every_inverse = layer_norm_parts(
        time_token.astype(jnp.float32), gain_one_f
    )
    time_grad = norm_back(stamp_sum, every_normal, every_inverse, gain_one_f)
    time_gain = jnp.sum(stamp_sum * every_normal, axis=0)
    gains_own = lax.dynamic_slice_in_dim(
        jnp.concatenate([late[clip_total:] + time_gain[None], early[-3:]], axis=0),
        seq_index * gain_rows,
        gain_rows,
        1,
    )
    return (
        result,
        frames_grad,
        time_grad,
        gains_own[0],
        gains_own[1],
        gains_own[2],
        qkv_share[1],
        qkv_share[2],
        qkv_share[3],
        out_share,
        cross_query_share,
        ctx_share[:ctx_rows],
        ctx_share[ctx_rows:],
        cross_out_share,
        glu_share[0],
        glu_share[1],
        glu_share[2],
        own_bias[0],
        own_bias[1],
        gains_own[3],
    )


def solution(mesh):
    in_specs = (
        P("seq", None),
        P(),
        P(),
        P(),
        P("seq"),
        P("seq"),
        P("seq"),
        P("seq", "head"),
        P("seq", "head"),
        P("seq", "head"),
        P("seq", "head"),
        P("seq", "head"),
        P("seq", "head"),
        P("seq", "head"),
        P("seq", "head"),
        P("seq", "head"),
        P("seq", "head"),
        P("seq", "head"),
        P("head"),
        P("head"),
        P("seq"),
        P("seq", None),
    )
    out_specs = (
        P("seq", None),
        P("seq", None),
        P(),
        P("seq"),
        P("seq"),
        P("seq"),
        P("seq", "head"),
        P("seq", "head"),
        P("seq", "head"),
        P("seq", "head"),
        P("seq", "head"),
        P("seq", "head"),
        P("seq", "head"),
        P("seq", "head"),
        P("seq", "head"),
        P("seq", "head"),
        P("seq", "head"),
        P("head"),
        P("head"),
        P("seq"),
    )
    fast = mesh.shape["seq"] == FAST_SEQ
    return jax.shard_map(
        per_device if fast else per_device_plain, mesh=mesh, in_specs=in_specs, out_specs=out_specs, check_vma=False
    )
```
